32 devices in a mesh: batch: 8 (over z, y), ctx: 4 (over x, core).
Axes of the slice: x: 2, y: 2, z: 4, core: 2. Of those that a mesh axis runs over, the one named last changes fastest.
Arguments:
- tokens: bfloat16 [16, 256, 2048], P('batch', 'ctx'), may hold values from -50 to 50
- cotangent: bfloat16 [16, 256, 2048], P('batch', 'ctx'), may hold values from -6 to 6
- lengths: int32 [16], replicated, may hold values from 64 to 256, as said below
- slot_sequence: int32 [16], replicated, may hold values from 0 to 15, each once
- proj_in: bfloat16 [2048, 1536], P(('batch', 'ctx')), may hold values from -0.125 to 0.125
- query_up: bfloat16 [1024, 4096], P(('batch', 'ctx')), may hold values from -0.1875 to 0.1875
- proj_out: bfloat16 [4096, 2048], P(('batch', 'ctx')), may hold values from -0.75 to 0.75
- attn_gain: bfloat16 [2048], P(('batch', 'ctx')), may hold values from 0.5 to 1.5
- query_gain: bfloat16 [1024], P(('batch', 'ctx')), may hold values from 0.5 to 1.5
- mlp_gain: bfloat16 [2048], P(('batch', 'ctx')), may hold values from 0.5 to 1.5
- gate_up: bfloat16 [2048, 11264], P(('batch', 'ctx')), may hold values from -0.125 to 0.125
- down_proj: bfloat16 [5632, 2048], P(('batch', 'ctx')), may hold values from -0.109375 to 0.109375
Outputs:
- layer_out: bfloat16 [16, 256, 2048], P('batch', 'ctx')
- tokens_grad: bfloat16 [16, 256, 2048], P('batch', 'ctx')
- grad_proj_in: float32 [2048, 1536], P(('batch', 'ctx'))
- grad_query_up: float32 [1024, 4096], P(('batch', 'ctx'))
- grad_proj_out: float32 [4096, 2048], P(('batch', 'ctx'))
- grad_attn_gain: float32 [2048], P(('batch', 'ctx'))
- grad_query_gain: float32 [1024], P(('batch', 'ctx'))
- grad_mlp_gain: float32 [2048], P(('batch', 'ctx'))
- grad_gate_up: float32 [2048, 11264], P(('batch', 'ctx'))
- grad_down_proj: float32 [5632, 2048], P(('batch', 'ctx'))
The draws below stay inside these ranges and needn't reach their ends.
Inputs may be any that keep to these rules, and one draw needn't show every extreme that they name: `lengths`: valid tokens of each sequence, counted from its start; the longest equals 256 in every draw. Slot s holds the sequence numbered slot_sequence[s]; every sequence fills exactly one slot.
All inputs are finite; a program needn't handle non-finite values.
Results may differ from the reference program's by a relative error of at most 0.017.
Values may be sent and summed in bfloat16 or wider, within the bound.
A program may use at most 448 MiB of HBM per device.

```python
import math
import jax
import jax.numpy as jnp
from jax import lax

D = 2048
H = 16
HD = 256
QR = 1024
FF = 5632
LEN = 256
SLOTS = 16


def draw_tokens(key, part):
    key_main, key_rows, key_cols = jax.random.split(key, 3)
    row_scale = jnp.exp(jax.random.uniform(key_rows, (SLOTS, LEN, 1), jnp.float32, -1.15, 1.15))
    col_scale = jnp.exp(jax.random.uniform(key_cols, (1, 1, D), jnp.float32, -1.15, 1.15))
    drawn_part = jnp.clip(jax.random.normal(key_main, (SLOTS, LEN, D), jnp.float32), -5.0, 5.0)
    values = drawn_part * row_scale * col_scale
    return values.astype(jnp.bfloat16)


def draw_lengths(key, part):
    key_values, key_place = jax.random.split(key)
    drawn_lengths = jax.random.randint(key_values, (SLOTS,), LEN // 4, LEN + 1, dtype=jnp.int32)
    longest_slot = jax.random.randint(key_place, (), 0, SLOTS, dtype=jnp.int32)
    return jnp.where(jnp.arange(SLOTS, dtype=jnp.int32) == longest_slot, LEN, drawn_lengths).astype(jnp.int32)


def steps_of(key, shape, cuts, smallest, largest):
    loudness, own = 1.0, jax.random.fold_in(key, 6)
    for axis_at, parts in cuts:
        heights = jnp.exp(jax.random.uniform(jax.random.fold_in(own, axis_at), (parts,), jnp.float32, smallest / len(cuts), largest / len(cuts)))
        loudness = loudness * jnp.repeat(heights, shape[axis_at] // parts).reshape([-1 if axis == axis_at else 1 for axis in range(len(shape))])
    return loudness


def normal_values(rng, dims, deviation, most, pieces=(), kind=jnp.bfloat16):
    entries = jax.random.normal(rng, dims, jnp.float32) * deviation
    if len(pieces) > 0:
        entries = steps_of(rng, dims, pieces, -0.22, 0.18) * entries
    return jnp.clip(entries, min=-most, max=most).astype(kind)


def setup_inputs(seed: int = 0) -> dict:
    seeds = jax.random.split(jax.random.key(seed), 13)
    return {
        "tokens": draw_tokens(jax.random.fold_in(seeds[12], 71), 0),
        "cotangent": normal_values(seeds[1], (SLOTS, LEN, D), 1.0, 6.0, ((0, 8), (1, 4))),
        "lengths": draw_lengths(jax.random.fold_in(seeds[12], 71), 0),
        "slot_sequence": jax.random.permutation(seeds[3], SLOTS).astype(jnp.int32),
        "proj_in": normal_values(seeds[4], (D, QR + 2 * HD), D ** -0.5, 0.125, ((0, 32),)),
        "query_up": normal_values(seeds[5], (QR, H * HD), QR ** -0.5, 0.1875, ((0, 32),)),
        "proj_out": normal_values(seeds[6], (H * HD, D), (H * HD // 64) ** -0.5, 0.75, ((0, 32),)),
        "attn_gain": jnp.clip(1.0 + 0.1 * jax.random.normal(seeds[7], (D,), jnp.float32), 0.5, 1.5).astype(jnp.bfloat16),
        "query_gain": jnp.clip(1.0 + 0.1 * jax.random.normal(seeds[8], (QR,), jnp.float32), 0.5, 1.5).astype(jnp.bfloat16),
        "mlp_gain": jnp.clip(1.0 + 0.1 * jax.random.normal(seeds[9], (D,), jnp.float32), 0.5, 1.5).astype(jnp.bfloat16),
        "gate_up": normal_values(seeds[10], (D, 2 * FF), D ** -0.5, 0.125, ((0, 32),)),
        "down_proj": normal_values(seeds[11], (FF, D), (FF // 2) ** -0.5, 0.109375, ((0, 32),)),
    }


@jax.custom_vjp
def low(v):
    return lax.optimization_barrier(v.astype(jnp.bfloat16)).astype(jnp.float32)

@jax.custom_vjp
def low_back(v):
    return v

def low_keep(v):
    return (low(v), None)

def low_pass(kept, grad):
    return (grad,)

def back_keep(v):
    return (v, None)

def back_low(kept, grad):
    return (low(grad),)
low.defvjp(low_keep, low_pass)
low_back.defvjp(back_keep, back_low)
EPSILON = 1e-06

def matmul_high(left_side, right_side):
    return jnp.matmul(left_side, right_side, precision=lax.Precision.HIGHEST)

def rms_scaled(values):
    return values * lax.rsqrt(lax.optimization_barrier(jnp.mean(values * values, axis=-1, keepdims=True)) + EPSILON)

def rope_tables(count):
    half_size = HD // 2
    frequency = 10000.0 ** (-(jnp.arange(half_size, dtype=jnp.float32) * 2.0 / HD))
    angles = jnp.arange(count, dtype=jnp.float32)[:, None] * frequency[None, :]
    return (jnp.cos(angles), jnp.sin(angles))

def rotate(values, cosine_table, sine_table):
    half_size = values.shape[-1] // 2
    front_half = values[..., :half_size]
    back_half = values[..., half_size:]
    return jnp.concatenate([front_half * cosine_table - back_half * sine_table, back_half * cosine_table + front_half * sine_table], axis=-1)

def block_forward(tokens, seq_lengths, proj_in, query_up, proj_out, attn_gain, query_gain, mlp_gain, gate_up, down_proj):
    batch_group = tokens.shape[0]
    attn_in = low(rms_scaled(tokens) * attn_gain)
    projected = low_back(matmul_high(attn_in, proj_in))
    q_latent = projected[..., :QR]
    key_raw = projected[..., QR:QR + HD]
    value_raw = projected[..., QR + HD:]
    q_normed = low(rms_scaled(q_latent) * query_gain)
    queries = low_back(matmul_high(q_normed, query_up)).reshape(batch_group, LEN, H, HD)
    cosine_table, sine_table = rope_tables(LEN)
    q_rot = low(rotate(queries, cosine_table[:, None, :], sine_table[:, None, :]))
    k_rot = low(rotate(key_raw, cosine_table, sine_table))
    v_low = low(value_raw)
    score_scale = 1.0 / math.sqrt(HD)
    scores = low_back(jnp.einsum('gthd,gud->ghtu', q_rot, k_rot, precision=lax.Precision.HIGHEST) * score_scale)
    positions = jnp.arange(LEN, dtype=jnp.int32)
    allowed = (positions[None, :] <= positions[:, None])[None, None] & (positions[None, None, None, :] < seq_lengths[:, None, None, None])
    masked = jnp.where(allowed, scores, -1e+30)
    row_max = lax.optimization_barrier(jnp.max(masked, axis=-1, keepdims=True))
    raised = jnp.exp(masked - row_max)
    weights_low = low(raised / lax.optimization_barrier(jnp.sum(raised, axis=-1, keepdims=True)))
    attended_raw = jnp.einsum('ghtu,gud->gthd', weights_low, v_low, precision=lax.Precision.HIGHEST)
    mixed = low(low_back(attended_raw)).reshape(batch_group, LEN, H * HD)
    attended = low_back(matmul_high(mixed, proj_out))
    hidden_res = tokens + attended
    mlp_in = low(rms_scaled(hidden_res) * mlp_gain)
    gate_mix = low_back(matmul_high(mlp_in, gate_up))
    gate_part = gate_mix[..., :FF]
    up_part = gate_mix[..., FF:]
    activated = low(gate_part * jax.nn.sigmoid(gate_part) * up_part)
    return hidden_res + low_back(matmul_high(activated, down_proj))

def reference(tokens, cotangent, lengths, slot_sequence, proj_in, query_up, proj_out, attn_gain, query_gain, mlp_gain, gate_up, down_proj):
    slot_ids = jnp.arange(SLOTS, dtype=jnp.int32)
    seq_lengths = lax.optimization_barrier(jnp.sum(jnp.where(slot_sequence[:, None] == slot_ids[None, :], lengths[None, :], 0), axis=1)).astype(jnp.int32)
    valid_rows = (jnp.arange(LEN, dtype=jnp.int32)[None, :] < seq_lengths[:, None]).astype(jnp.float32)
    together = 4
    checked = jax.checkpoint(block_forward)

    def forward(tokens_f, proj_in_f, query_up_f, proj_out_f, attn_gain_f, query_gain_f, mlp_gain_f, gate_up_f, down_proj_f):
        grouped = tokens_f.reshape(SLOTS // together, together, LEN, D)
        lengths_grouped = seq_lengths.reshape(SLOTS // together, together)

        def one_group(group_pair):
            return checked(group_pair[0], group_pair[1], proj_in_f, query_up_f, proj_out_f, attn_gain_f, query_gain_f, mlp_gain_f, gate_up_f, down_proj_f)
        return lax.map(one_group, (grouped, lengths_grouped)).reshape(SLOTS, LEN, D)
    output, pullback = jax.vjp(forward, tokens.astype(jnp.float32), proj_in.astype(jnp.float32), query_up.astype(jnp.float32), proj_out.astype(jnp.float32), attn_gain.astype(jnp.float32), query_gain.astype(jnp.float32), mlp_gain.astype(jnp.float32), gate_up.astype(jnp.float32), down_proj.astype(jnp.float32))
    gradients = pullback(cotangent.astype(jnp.float32) * valid_rows[:, :, None])
    return (output.astype(jnp.bfloat16), gradients[0].astype(jnp.bfloat16), gradients[1], gradients[2], gradients[3], gradients[4], gradients[5], gradients[6], gradients[7], gradients[8])
```

```python
import math

import jax
import jax.numpy as jnp
from jax import lax
from jax.sharding import PartitionSpec as P

H = 16
HD = 256
QR = 1024
EPSILON = 1e-06
BF = jnp.bfloat16
F32 = jnp.float32


def rms_scale(values):
    return lax.rsqrt(jnp.mean(values * values, axis=-1, keepdims=True) + EPSILON)


def rope_tables(positions):
    half_size = HD // 2
    frequency = 10000.0 ** (-(jnp.arange(half_size, dtype=F32) * 2.0 / HD))
    angles = positions.astype(F32)[:, None] * frequency[None, :]
    return (jnp.cos(angles), jnp.sin(angles))


def rotate(values, cosine_table, sine_table):
    half_size = values.shape[-1] // 2
    front_half = values[..., :half_size]
    back_half = values[..., half_size:]
    return jnp.concatenate(
        [
            front_half * cosine_table - back_half * sine_table,
            back_half * cosine_table + front_half * sine_table,
        ],
        axis=-1,
    )


def rotate_back(values, cosine_table, sine_table):
    return rotate(values, cosine_table, -sine_table)


def dot(left_side, right_side):
    return jnp.dot(left_side, right_side, preferred_element_type=F32)


def dot_right_t(left_side, right_side):
    return lax.dot_general(
        left_side, right_side, (((1,), (1,)), ((), ())), preferred_element_type=F32
    )


def dot_left_t(left_side, right_side):
    return lax.dot_general(
        left_side, right_side, (((0,), (0,)), ((), ())), preferred_element_type=F32
    )


def norm_back(grad_normed, normed, inv_rms):
    return inv_rms * (grad_normed - normed * jnp.mean(grad_normed * normed, axis=-1, keepdims=True))


def pick(array, index, axis=0):
    return lax.dynamic_index_in_dim(array, index, axis, keepdims=False)


def place(array, block, index, axis=0):
    return lax.dynamic_update_index_in_dim(array, block, index, axis)


class Ring:
    def __init__(self):
        self.n = lax.axis_size("batch")
        self.h = self.n // 2
        rank = lax.axis_index("batch")
        self.at = jnp.where(rank % 2 == 0, rank // 2, self.n - 1 - rank // 2)
        order = [2 * i for i in range(self.h)] + [2 * i + 1 for i in reversed(range(self.h))]
        self.up = [(order[i], order[(i + 1) % self.n]) for i in range(self.n)]
        self.down = [(there, here) for here, there in self.up]

    def rank_of(self, step):
        spot = (self.at + step) % self.n
        return jnp.where(spot < self.h, 2 * spot, 2 * (self.n - 1 - spot) + 1)

    def spread(self, block):
        found = {0: block}
        upward = downward = block
        for step in range(1, self.h):
            upward = lax.ppermute(upward, "batch", self.up)
            downward = lax.ppermute(downward, "batch", self.down)
            found[-step] = upward
            found[step] = downward
        cut = block.shape[0] // 2
        found[self.h] = jnp.concatenate(
            [
                lax.ppermute(upward[:cut], "batch", self.up),
                lax.ppermute(downward[cut:], "batch", self.down),
            ],
            axis=0,
        )
        return found

    def gather(self, block):
        found = self.spread(block)
        whole = jnp.zeros((self.n,) + block.shape, block.dtype)
        for step, part in found.items():
            whole = place(whole, part, self.rank_of(step))
        return whole

    def collect(self, term):
        far = term(self.h)
        cut = far.shape[0] // 2
        downward = lax.ppermute(far[:cut].astype(BF), "batch", self.down)
        upward = lax.ppermute(far[cut:].astype(BF), "batch", self.up)
        for step in range(self.h - 1, 0, -1):
            for_lower = term(-step).astype(F32)
            for_upper = term(step).astype(F32)
            if step == self.h - 1:
                for_lower = jnp.concatenate(
                    [for_lower[:cut] + downward.astype(F32), for_lower[cut:]], axis=0
                )
                for_upper = jnp.concatenate(
                    [for_upper[:cut], for_upper[cut:] + upward.astype(F32)], axis=0
                )
            else:
                for_lower = for_lower + downward.astype(F32)
                for_upper = for_upper + upward.astype(F32)
            downward = lax.ppermute(for_lower.astype(BF), "batch", self.down)
            upward = lax.ppermute(for_upper.astype(BF), "batch", self.up)
        own = term(0).astype(F32)
        return own + downward.astype(F32) + upward.astype(F32)

    def collect_rows(self, stacked):
        return self.collect(lambda step: pick(stacked, self.rank_of(step)))


def batch_exchange(stacked):
    n = lax.axis_size("batch")
    rank = lax.axis_index("batch")
    swapped = stacked
    for offset in range(1, n):
        pairs = [(i, i ^ offset) for i in range(n)]
        other = rank ^ offset
        swapped = place(swapped, lax.ppermute(pick(stacked, other), "batch", pairs), other)
    return swapped


FAR = [(0, 2), (1, 3), (2, 0), (3, 1)]
NEAR = [(0, 1), (1, 0), (2, 3), (3, 2)]


def ctx_place():
    rank = lax.axis_index("ctx")
    return rank // 2, rank % 2


def in_order(mine, theirs, at):
    return jnp.where(at == 0, jnp.stack([mine, theirs]), jnp.stack([theirs, mine]))


def ctx_gather(block):
    outer, inner = ctx_place()
    pair = in_order(block, lax.ppermute(block, "ctx", FAR), outer)
    whole = in_order(pair, lax.ppermute(pair, "ctx", NEAR), inner)
    whole = jnp.swapaxes(whole, 0, 1)
    return whole.reshape((4,) + block.shape)


def ctx_collect(stacked):
    outer, inner = ctx_place()
    parts = stacked.reshape((2, 2) + stacked.shape[1:])
    got = lax.ppermute(pick(parts, 1 - inner, 1).astype(BF), "ctx", NEAR)
    half = pick(parts, inner, 1).astype(F32) + got.astype(F32)
    got = lax.ppermute(pick(half, 1 - outer).astype(BF), "ctx", FAR)
    return pick(half, outer) + got.astype(F32)


def ctx_exchange(stacked):
    outer, inner = ctx_place()
    parts = stacked.reshape((2, 2) + stacked.shape[1:])
    got = lax.ppermute(pick(parts, 1 - outer), "ctx", FAR)
    parts = in_order(pick(parts, outer), got, outer)
    got = lax.ppermute(pick(parts, 1 - inner, 1), "ctx", NEAR)
    whole = in_order(pick(parts, inner, 1), got, inner)
    return jnp.swapaxes(whole, 0, 1).reshape(stacked.shape)


def slab_pairs(n_batch, n_ctx):
    return [(i, (i % n_batch) * n_ctx + i // n_batch) for i in range(n_batch * n_ctx)]


def shards(
    tokens,
    cotangent,
    lengths,
    slot_sequence,
    proj_in,
    query_up,
    proj_out,
    attn_gain,
    query_gain,
    mlp_gain,
    gate_up,
    down_proj,
):
    n_ctx = lax.axis_size("ctx")
    n_batch = lax.axis_size("batch")
    ctx_rank = lax.axis_index("ctx")
    batch_rank = lax.axis_index("batch")
    ring = Ring()
    micro, pos_dev, width = tokens.shape
    n_tok = micro * pos_dev
    full_length = pos_dev * n_ctx
    heads = H // n_ctx
    score_scale = 1.0 / math.sqrt(HD)
    in_cols = proj_in.shape[1]

    slot_total = lengths.shape[0]
    slot_ids = jnp.arange(slot_total, dtype=jnp.int32)
    seq_lengths = jnp.sum(
        jnp.where(slot_sequence[:, None] == slot_ids[None, :], lengths[None, :], 0), axis=1
    )
    own_lengths = lax.dynamic_slice_in_dim(seq_lengths, batch_rank * micro, micro)
    query_pos = ctx_rank * pos_dev + jnp.arange(pos_dev, dtype=jnp.int32)
    key_pos = jnp.arange(full_length, dtype=jnp.int32)
    cos_all, sin_all = rope_tables(key_pos)
    cos_own, sin_own = rope_tables(query_pos)

    own_rows = proj_in.shape[0]
    gain_rows = query_gain.shape[0]
    gains = jnp.stack(
        [attn_gain, mlp_gain, jnp.pad(query_gain, (0, own_rows - gain_rows))], axis=1
    )
    packed = jnp.concatenate([proj_in, jnp.pad(gains, ((0, 0), (0, 125)))], axis=1)
    packed = ctx_gather(ring.gather(packed))
    packed = jnp.swapaxes(packed, 0, 1).reshape(width, in_cols + 128)
    full_in = packed[:, :in_cols]
    gains = packed[:, in_cols : in_cols + 3].T.astype(F32)
    gain_norm = gains[0]
    gain_mlp = gains[1]
    gain_query = gains[2].reshape(n_batch * n_ctx, own_rows)[:, :gain_rows].reshape(QR)

    up_parts = query_up.reshape(gain_rows, n_ctx, heads * HD).swapaxes(0, 1)
    up_block = ctx_exchange(up_parts).reshape(n_ctx * gain_rows, heads * HD)
    own_qup = ring.gather(up_block).reshape(QR, heads * HD)
    slabs = slab_pairs(n_batch, n_ctx)
    out_block = lax.ppermute(proj_out, ("batch", "ctx"), slabs)
    own_out = ring.gather(out_block).reshape(heads * HD, width)

    ff_all = gate_up.shape[1] // 2
    ff = ff_all // n_batch
    gu_parts = gate_up.reshape(own_rows, 2, n_batch, ff).transpose(2, 1, 0, 3)
    gu_rows = ctx_gather(batch_exchange(gu_parts))
    gu_rows = gu_rows.transpose(2, 1, 0, 3, 4).reshape(2, width, ff)
    own_gate, own_up = gu_rows[0], gu_rows[1]
    own_down = ctx_gather(down_proj).reshape(ff, width)

    residual = tokens.reshape(n_tok, width).astype(F32)
    valid_rows = (query_pos[None, :] < own_lengths[:, None]).astype(F32).reshape(n_tok, 1)
    grad_out = cotangent.reshape(n_tok, width).astype(F32) * valid_rows
    grad_mo = ring.spread(grad_out.astype(BF))

    scale_one = rms_scale(residual)
    normed_one = residual * scale_one
    attn_in = (normed_one * gain_norm).astype(BF)
    attn_in_all = ctx_gather(attn_in).reshape(n_ctx * n_tok, width)
    projected = dot(attn_in, full_in)
    q_latent = projected[:, :QR]
    scale_query = rms_scale(q_latent)
    normed_query = q_latent * scale_query
    q_normed = (normed_query * gain_query).astype(BF)
    k_rot = rotate(
        projected[:, QR : QR + HD].reshape(micro, pos_dev, HD), cos_own, sin_own
    ).astype(BF)
    v_low = projected[:, QR + HD :].astype(BF)
    qkv_all = ctx_gather(jnp.concatenate([q_normed, k_rot.reshape(n_tok, HD), v_low], axis=1))
    q_normed_all = qkv_all[..., :QR].reshape(n_ctx * n_tok, QR)

    def by_sequence(values):
        return (
            values.reshape(n_ctx, micro, pos_dev, -1)
            .swapaxes(0, 1)
            .reshape(micro, full_length, -1)
        )

    def by_position(values):
        return (
            values.reshape(micro, n_ctx, pos_dev, -1)
            .swapaxes(0, 1)
            .reshape(n_ctx * n_tok, -1)
        )

    def split_heads(values):
        return by_sequence(values).reshape(micro, full_length, heads, HD).swapaxes(1, 2)

    def join_heads(values):
        return by_position(values.swapaxes(1, 2).reshape(micro, full_length, heads * HD))

    kv_all = by_sequence(qkv_all[..., QR:])
    keys_all = kv_all[..., :HD]
    values_all = kv_all[..., HD:]
    queries = split_heads(dot(q_normed_all, own_qup))
    q_rot = rotate(queries, cos_all, sin_all).astype(BF)
    allowed = (key_pos[None, :] <= key_pos[:, None])[None, None] & (
        key_pos[None, None, None, :] < own_lengths[:, None, None, None]
    )
    scores = jnp.einsum("shtd,sud->shtu", q_rot, keys_all, preferred_element_type=F32) * score_scale
    masked = jnp.where(allowed, scores, -1e30)
    row_max = jnp.max(masked, axis=-1, keepdims=True)
    raised = jnp.exp(masked - row_max)
    weights = raised / jnp.sum(raised, axis=-1, keepdims=True)
    weights_low = weights.astype(BF)
    mixed = join_heads(
        jnp.einsum("shtu,sud->shtd", weights_low, values_all, preferred_element_type=F32).astype(BF)
    )
    attended = ctx_collect(dot(mixed, own_out).reshape(n_ctx, n_tok, width))
    hidden_res = residual + attended

    scale_two = rms_scale(hidden_res)
    normed_two = hidden_res * scale_two
    mlp_in = ring.spread((normed_two * gain_mlp).astype(BF))
    far = ring.h
    groups = [[0]] + [[-step, step] for step in range(1, far)] + [[far]]
    out_terms = {}
    in_terms = {}
    kept = []
    for group in groups:
        rows = jnp.concatenate([mlp_in[step] for step in group], axis=0)
        grad_rows = jnp.concatenate([grad_mo[step] for step in group], axis=0)
        gate_part = dot(rows, own_gate)
        up_part = dot(rows, own_up)
        sigmoid_gate = jax.nn.sigmoid(gate_part)
        silu_gate = gate_part * sigmoid_gate
        activated = (silu_gate * up_part).astype(BF)
        grad_act = dot_right_t(grad_rows, own_down)
        grad_gate = (
            grad_act * up_part * (sigmoid_gate * (1.0 + gate_part * (1.0 - sigmoid_gate)))
        ).astype(BF)
        grad_up = (grad_act * silu_gate).astype(BF)
        in_term = dot_right_t(grad_gate, own_gate) + dot_right_t(grad_up, own_up)
        out_term = dot(activated, own_down)
        for place_in, step in enumerate(group):
            cut = slice(place_in * n_tok, (place_in + 1) * n_tok)
            in_terms[step] = in_term[cut]
            out_terms[step] = out_term[cut]
        kept.append((rows, grad_rows, activated, grad_gate, grad_up))
    rows, grad_rows, activated, grad_gate, grad_up = (
        jnp.concatenate(items, axis=0) for items in zip(*kept)
    )
    grad_mlp_in = ring.collect(lambda step: in_terms[step])
    gain_mlp_term = jnp.sum(grad_mlp_in * normed_two, axis=0)
    grad_hidden = grad_out + norm_back(grad_mlp_in * gain_mlp, normed_two, scale_two)
    layer_out = hidden_res + ring.collect(lambda step: out_terms[step])

    grad_gu_own = jnp.stack([dot_left_t(rows, grad_gate), dot_left_t(rows, grad_up)])
    grad_gu_own = grad_gu_own.reshape(2, n_batch, n_ctx, own_rows, ff).transpose(2, 1, 0, 3, 4)
    grad_gu_own = batch_exchange(ctx_collect(grad_gu_own).astype(BF))
    grad_gate_up = grad_gu_own.transpose(2, 1, 0, 3).reshape(own_rows, 2 * ff_all).astype(F32)
    grad_down_own = dot_left_t(activated, grad_rows)
    grad_down = ctx_collect(grad_down_own.reshape(n_ctx, ff // n_ctx, width))

    grad_att_all = ctx_gather(grad_hidden.astype(BF)).reshape(n_ctx * n_tok, width)
    grad_out_own = dot_left_t(mixed, grad_att_all)
    grad_out_own = ring.collect_rows(grad_out_own.reshape(n_batch, -1, width)).astype(BF)
    grad_proj_out = lax.ppermute(
        grad_out_own, ("batch", "ctx"), [(there, here) for here, there in slabs]
    ).astype(F32)
    grad_mixed = split_heads(dot_right_t(grad_att_all, own_out).astype(BF))
    grad_probs = jnp.einsum(
        "shtd,sud->shtu", grad_mixed, values_all, preferred_element_type=F32
    )
    row_dot = jnp.sum(weights * grad_probs, axis=-1, keepdims=True)
    grad_scores = (weights * (grad_probs - row_dot)).astype(BF)
    grad_q_rot = (
        jnp.einsum("shtu,sud->shtd", grad_scores, keys_all, preferred_element_type=F32)
        * score_scale
    )
    grad_keys = (
        jnp.einsum("shtu,shtd->sud", grad_scores, q_rot, preferred_element_type=F32)
        * score_scale
    )
    grad_values = jnp.einsum(
        "shtu,shtd->sud", weights_low, grad_mixed, preferred_element_type=F32
    )
    grad_q = join_heads(rotate_back(grad_q_rot, cos_all, sin_all).astype(BF))
    grad_qn_part = dot_right_t(grad_q, own_qup)
    grad_kv_part = by_position(jnp.concatenate([grad_keys, grad_values], axis=-1))
    back_parts = jnp.concatenate([grad_qn_part, grad_kv_part], axis=1).astype(BF)
    back_own = ctx_collect(back_parts.reshape(n_ctx, n_tok, in_cols))
    grad_qn = back_own[:, :QR]
    gain_query_term = jnp.sum(grad_qn * normed_query, axis=0)
    grad_latent = norm_back(grad_qn * gain_query, normed_query, scale_query)
    grad_key_raw = rotate_back(
        back_own[:, QR : QR + HD].reshape(micro, pos_dev, HD), cos_own, sin_own
    ).reshape(n_tok, HD)
    grad_project = jnp.concatenate(
        [grad_latent, grad_key_raw, back_own[:, QR + HD :]], axis=1
    ).astype(BF)
    grad_attn_in = dot_right_t(grad_project, full_in)
    gain_norm_term = jnp.sum(grad_attn_in * normed_one, axis=0)
    grad_tokens = grad_hidden + norm_back(grad_attn_in * gain_norm, normed_one, scale_one)

    grad_up_own = dot_left_t(q_normed_all, grad_q)
    grad_up_own = ring.collect_rows(grad_up_own.reshape(n_batch, -1, heads * HD)).astype(BF)
    grad_query_up = (
        ctx_exchange(grad_up_own.reshape(n_ctx, gain_rows, heads * HD))
        .swapaxes(0, 1)
        .reshape(gain_rows, H * HD)
        .astype(F32)
    )
    part_cols = in_cols // n_ctx
    project_parts = grad_project.reshape(n_tok, n_ctx, part_cols).swapaxes(0, 1)
    project_all = ctx_exchange(project_parts).reshape(n_ctx * n_tok, part_cols)
    grad_in_own = dot_left_t(attn_in_all, project_all).reshape(
        n_batch, n_ctx, own_rows, part_cols
    )
    gain_terms = jnp.stack(
        [
            gain_norm_term.reshape(n_batch, n_ctx, own_rows),
            gain_mlp_term.reshape(n_batch, n_ctx, own_rows),
            jnp.pad(
                gain_query_term.reshape(n_batch, n_ctx, gain_rows),
                ((0, 0), (0, 0), (0, own_rows - gain_rows)),
            ),
        ],
        axis=2,
    )
    gain_terms = jnp.pad(gain_terms, ((0, 0), (0, 0), (0, 13), (0, part_cols - own_rows)))
    joined = jnp.concatenate([grad_in_own, gain_terms], axis=2).reshape(n_batch, -1, part_cols)
    joined = ring.collect_rows(joined).astype(BF)
    joined = ctx_exchange(joined.reshape(n_ctx, own_rows + 16, part_cols)).astype(F32)
    grad_proj_in = joined[:, :own_rows].swapaxes(0, 1).reshape(own_rows, in_cols)
    gain_sums = jnp.sum(joined[:, own_rows : own_rows + 3, :own_rows], axis=0)

    return (
        layer_out.reshape(tokens.shape).astype(BF),
        grad_tokens.reshape(tokens.shape).astype(BF),
        grad_proj_in,
        grad_query_up,
        grad_proj_out,
        gain_sums[0],
        gain_sums[2, :gain_rows],
        gain_sums[1],
        grad_gate_up,
        grad_down,
    )


def solution(mesh):
    rows = P(("batch", "ctx"), None)
    vector = P(("batch", "ctx"))
    acts = P("batch", "ctx", None)
    return jax.shard_map(
        shards,
        mesh=mesh,
        in_specs=(acts, acts, P(), P(), rows, rows, rows, vector, vector, vector, rows, rows),
        out_specs=(acts, acts, rows, rows, rows, vector, vector, vector, rows, rows),
        check_vma=False,
    )
```

```python
import functools
import math

import jax
import jax.numpy as jnp
from jax import lax
from jax.experimental import pallas as pl
from jax.experimental.pallas import tpu as pltpu
from jax.sharding import PartitionSpec as P

H = 16
HD = 256
QR = 1024
EPSILON = 1e-06
BF = jnp.bfloat16
F32 = jnp.float32


def rms_scale(values):
    return lax.rsqrt(jnp.mean(values * values, axis=-1, keepdims=True) + EPSILON)


def rope_tables(positions):
    half_size = HD // 2
    frequency = 10000.0 ** (-(jnp.arange(half_size, dtype=F32) * 2.0 / HD))
    angles = positions.astype(F32)[:, None] * frequency[None, :]
    return (jnp.cos(angles), jnp.sin(angles))


def rotate(values, cosine_table, sine_table):
    half_size = values.shape[-1] // 2
    front_half = values[..., :half_size]
    back_half = values[..., half_size:]
    return jnp.concatenate(
        [
            front_half * cosine_table - back_half * sine_table,
            back_half * cosine_table + front_half * sine_table,
        ],
        axis=-1,
    )


def rotate_back(values, cosine_table, sine_table):
    return rotate(values, cosine_table, -sine_table)


def dot(left_side, right_side):
    return jnp.dot(left_side, right_side, preferred_element_type=F32)


def dot_right_t(left_side, right_side):
    return lax.dot_general(
        left_side, right_side, (((1,), (1,)), ((), ())), preferred_element_type=F32
    )


def dot_left_t(left_side, right_side):
    return lax.dot_general(
        left_side, right_side, (((0,), (0,)), ((), ())), preferred_element_type=F32
    )


def norm_back(grad_normed, normed, inv_rms):
    return inv_rms * (grad_normed - normed * jnp.mean(grad_normed * normed, axis=-1, keepdims=True))


def pick(array, index, axis=0):
    return lax.dynamic_index_in_dim(array, index, axis, keepdims=False)


def place(array, block, index, axis=0):
    return lax.dynamic_update_index_in_dim(array, block, index, axis)


class Ring:
    def __init__(self):
        self.n = lax.axis_size("batch")
        self.h = self.n // 2
        rank = lax.axis_index("batch")
        self.at = jnp.where(rank % 2 == 0, rank // 2, self.n - 1 - rank // 2)
        order = [2 * i for i in range(self.h)] + [2 * i + 1 for i in reversed(range(self.h))]
        self.up = [(order[i], order[(i + 1) % self.n]) for i in range(self.n)]
        self.down = [(there, here) for here, there in self.up]

    def rank_of(self, step):
        spot = (self.at + step) % self.n
        return jnp.where(spot < self.h, 2 * spot, 2 * (self.n - 1 - spot) + 1)

    def spread(self, block):
        found = {0: block}
        upward = downward = block
        for step in range(1, self.h):
            upward = lax.ppermute(upward, "batch", self.up)
            downward = lax.ppermute(downward, "batch", self.down)
            found[-step] = upward
            found[step] = downward
        cut = block.shape[0] // 2
        found[self.h] = jnp.concatenate(
            [
                lax.ppermute(upward[:cut], "batch", self.up),
                lax.ppermute(downward[cut:], "batch", self.down),
            ],
            axis=0,
        )
        return found

    def gather(self, block):
        found = self.spread(block)
        whole = jnp.zeros((self.n,) + block.shape, block.dtype)
        for step, part in found.items():
            whole = place(whole, part, self.rank_of(step))
        return whole

    def collect(self, term):
        far = term(self.h)
        cut = far.shape[0] // 2
        downward = lax.ppermute(far[:cut].astype(BF), "batch", self.down)
        upward = lax.ppermute(far[cut:].astype(BF), "batch", self.up)
        for step in range(self.h - 1, 0, -1):
            for_lower = term(-step).astype(F32)
            for_upper = term(step).astype(F32)
            if step == self.h - 1:
                for_lower = jnp.concatenate(
                    [for_lower[:cut] + downward.astype(F32), for_lower[cut:]], axis=0
                )
                for_upper = jnp.concatenate(
                    [for_upper[:cut], for_upper[cut:] + upward.astype(F32)], axis=0
                )
            else:
                for_lower = for_lower + downward.astype(F32)
                for_upper = for_upper + upward.astype(F32)
            downward = lax.ppermute(for_lower.astype(BF), "batch", self.down)
            upward = lax.ppermute(for_upper.astype(BF), "batch", self.up)
        own = term(0).astype(F32)
        return own + downward.astype(F32) + upward.astype(F32)

    def collect_rows(self, stacked):
        return self.collect(lambda step: pick(stacked, self.rank_of(step)))


def batch_exchange(stacked):
    n = lax.axis_size("batch")
    rank = lax.axis_index("batch")
    swapped = place(jnp.zeros_like(stacked), pick(stacked, rank), rank)
    for offset in range(1, n):
        pairs = [(i, i ^ offset) for i in range(n)]
        other = rank ^ offset
        swapped = place(swapped, lax.ppermute(pick(stacked, other), "batch", pairs), other)
    return swapped


FAR = [(0, 2), (1, 3), (2, 0), (3, 1)]
NEAR = [(0, 1), (1, 0), (2, 3), (3, 2)]


def ctx_place():
    rank = lax.axis_index("ctx")
    return rank // 2, rank % 2


def in_order(mine, theirs, at):
    return jnp.where(at == 0, jnp.stack([mine, theirs]), jnp.stack([theirs, mine]))


def ctx_gather(block):
    outer, inner = ctx_place()
    pair = in_order(block, lax.ppermute(block, "ctx", FAR), outer)
    whole = in_order(pair, lax.ppermute(pair, "ctx", NEAR), inner)
    whole = jnp.swapaxes(whole, 0, 1)
    return whole.reshape((4,) + block.shape)


def ctx_collect(stacked):
    outer, inner = ctx_place()
    parts = stacked.reshape((2, 2) + stacked.shape[1:])
    got = lax.ppermute(pick(parts, 1 - inner, 1).astype(BF), "ctx", NEAR)
    half = pick(parts, inner, 1).astype(F32) + got.astype(F32)
    got = lax.ppermute(pick(half, 1 - outer).astype(BF), "ctx", FAR)
    return pick(half, outer) + got.astype(F32)


def ctx_exchange(stacked):
    outer, inner = ctx_place()
    parts = stacked.reshape((2, 2) + stacked.shape[1:])
    got = lax.ppermute(pick(parts, 1 - outer), "ctx", FAR)
    parts = in_order(pick(parts, outer), got, outer)
    got = lax.ppermute(pick(parts, 1 - inner, 1), "ctx", NEAR)
    whole = in_order(pick(parts, inner, 1), got, inner)
    return jnp.swapaxes(whole, 0, 1).reshape(stacked.shape)


def slab_pairs(n_batch, n_ctx):
    return [(i, (i % n_batch) * n_ctx + i // n_batch) for i in range(n_batch * n_ctx)]


MESH = pl.DeviceIdType.MESH


class Place:
    def __init__(self, n_batch):
        self.n = n_batch
        self.h = n_batch // 2
        self.b = lax.axis_index("batch")
        self.c = lax.axis_index("ctx")
        self.outer = lax.div(self.c, 2)
        self.inner = lax.rem(self.c, 2)
        self.far = lax.rem(self.c + 2, 4)
        self.near = self.c + 1 - 2 * self.inner
        odd = lax.rem(self.b, 2)
        half = lax.div(self.b, 2)
        self.at = half + odd * (self.n - 1 - 2 * half)

    def rank_of(self, step):
        spot = lax.rem(self.at + step + 2 * self.n, self.n)
        back = lax.div(spot, self.h)
        return (1 - back) * 2 * spot + back * (2 * (self.n - 1 - spot) + 1)

    def up(self):
        return (self.rank_of(1), self.c)

    def down(self):
        return (self.rank_of(-1), self.c)


class Copies:
    def __init__(self, send_sems, recv_sems):
        self.send_sems = send_sems
        self.recv_sems = recv_sems
        self.count = 0
        self.open_sends = []
        self.open_recvs = []

    def remote(self, source, target, device):
        index = self.count
        self.count += 1
        copy = pltpu.make_async_remote_copy(
            src_ref=source,
            dst_ref=target,
            send_sem=self.send_sems.at[index],
            recv_sem=self.recv_sems.at[index],
            device_id=device,
            device_id_type=MESH,
        )
        copy.start()
        self.open_sends.append(copy)
        self.open_recvs.append(copy)
        return copy

    def local(self, source, target):
        index = self.count
        self.count += 1
        copy = pltpu.make_async_copy(source, target, self.recv_sems.at[index])
        copy.start()
        self.open_recvs.append(copy)
        return copy

    def arrive(self, copy):
        if any(copy is other for other in self.open_recvs):
            self.open_recvs = [other for other in self.open_recvs if other is not copy]
            if any(copy is other for other in self.open_sends):
                copy.wait_recv()
            else:
                copy.wait()

    def drain(self):
        for copy in list(self.open_recvs):
            self.arrive(copy)
        for copy in self.open_sends:
            copy.wait_send()


def greet(place, others):
    barrier = pltpu.get_barrier_semaphore()
    for device in others:
        pl.semaphore_signal(barrier, inc=1, device_id=device, device_id_type=MESH)
    return barrier


class RingGather:
    def __init__(self, place, copies, rows, slot):
        self.place, self.copies, self.rows, self.slot = place, copies, rows, slot
        self.step = 0
        self.moving = ()

    def advance(self):
        place, copies = self.place, self.copies
        for copy in self.moving:
            copies.arrive(copy)
        self.moving = ()
        self.step += 1
        cut = self.rows // 2
        if self.step > place.h:
            return
        lower = place.rank_of(1 - self.step)
        upper = place.rank_of(self.step - 1)
        if self.step < place.h:
            whole = pl.ds(0, self.rows)
            pieces = (whole, whole)
        else:
            pieces = (pl.ds(0, cut), pl.ds(cut, self.rows - cut))
        upward, downward = self.slot(lower, pieces[0]), self.slot(upper, pieces[1])
        self.moving = (
            copies.remote(upward, upward, place.up()),
            copies.remote(downward, downward, place.down()),
        )

    def arrived(self):
        step = self.step - 1
        if step == 0:
            return []
        if step == self.place.h:
            return [self.place.rank_of(step)]
        return [self.place.rank_of(-step), self.place.rank_of(step)]


def weights_kernel(
    n_batch,
    packed_ref,
    up_ref,
    out_ref,
    gu_ref,
    down_ref,
    packed_all,
    up_all,
    out_all,
    gu_all,
    down_all,
    send_sems,
    recv_sems,
    out_sems,
):
    place = Place(n_batch)
    copies = Copies(send_sems, recv_sems)
    b, c, n = place.b, place.c, n_batch
    own_rows = packed_ref.shape[0]
    out_rows = out_ref.shape[0]
    index = b * 4 + c
    target = (lax.rem(index, n), lax.div(index, n))
    slab = c * n + b
    source = (lax.div(slab, 4), lax.rem(slab, 4))
    stays = slab == index
    peers = [(lax.rem(b + k, n), c) for k in range(1, n)]
    ctx_peers = [(b, place.far), (b, place.near), (b, lax.rem(place.near + 2, 4))]

    barrier = greet(place, peers + ctx_peers)

    @pl.when(jnp.logical_not(stays))
    def _():
        for device in (target, source):
            pl.semaphore_signal(barrier, inc=1, device_id=device, device_id_type=MESH)

    pl.semaphore_wait(barrier, n + 4 - 2 * stays.astype(jnp.int32))

    own = [
        copies.local(packed_ref, packed_all.at[b, c]),
        copies.local(up_ref.at[c], up_all.at[b, c]),
        copies.local(gu_ref.at[b], gu_all.at[:, b, c]),
        copies.local(down_ref, down_all.at[c]),
    ]
    out_copy = pltpu.make_async_remote_copy(
        src_ref=out_ref,
        dst_ref=out_all.at[target[0]],
        send_sem=out_sems.at[0],
        recv_sem=out_sems.at[1],
        device_id=target,
        device_id_type=MESH,
    )
    out_stay = pltpu.make_async_copy(out_ref, out_all.at[b], out_sems.at[0])

    @pl.when(jnp.logical_not(stays))
    def _():
        out_copy.start()

    @pl.when(stays)
    def _():
        out_stay.start()

    up_copies = [
        copies.remote(up_ref.at[peer[1]], up_all.at[b, c], peer) for peer in ctx_peers
    ]
    far_device, near_device = ctx_peers[0], ctx_peers[1]
    down_far = copies.remote(down_ref, down_all.at[c], far_device)

    copies.arrive(own[0])
    packed_ring = RingGather(
        place, copies, own_rows, lambda rank, rows: packed_all.at[rank, c, rows]
    )
    up_ring = RingGather(
        place, copies, up_ref.shape[1], lambda rank, rows: up_all.at[rank, :, rows]
    )
    out_ring = RingGather(place, copies, out_rows, lambda rank, rows: out_all.at[rank, rows])

    packed_far = []

    def packed_step():
        packed_ring.advance()
        ranks = packed_ring.arrived() if packed_ring.step > 1 else [b]
        for rank in ranks:
            block = packed_all.at[rank, c]
            packed_far.append((rank, copies.remote(block, block, far_device)))

    packed_step()
    gu_copies = [
        (
            lax.rem(b - k + n, n),
            copies.remote(gu_ref.at[peer[0]], gu_all.at[:, b, c], peer),
        )
        for k, peer in zip(range(1, n), peers)
    ]
    for copy in own[1:2] + up_copies:
        copies.arrive(copy)
    up_ring.advance()
    packed_step()

    @pl.when(jnp.logical_not(stays))
    def _():
        out_copy.wait()

    @pl.when(stays)
    def _():
        out_stay.wait()

    out_ring.advance()
    gu_far = []
    copies.arrive(own[2])
    own_gu = gu_all.at[:, b, c]
    gu_far.append(copies.remote(own_gu, own_gu, far_device))
    waiting = list(gu_copies)
    copies.arrive(own[3])
    down_near = [copies.remote(down_all.at[c], down_all.at[c], near_device)]

    def forward_gu(count):
        for _ in range(min(count, len(waiting))):
            rank, copy = waiting.pop(0)
            copies.arrive(copy)
            block = gu_all.at[:, rank, c]
            gu_far.append(copies.remote(block, block, far_device))

    for _ in range(place.h):
        up_ring.advance()
        if packed_ring.step <= place.h:
            packed_step()
        forward_gu(2)
        out_ring.advance()
    copies.arrive(down_far)
    far = place.far
    down_near.append(copies.remote(down_all.at[far], down_all.at[far], near_device))
    forward_gu(n)
    own_packed = packed_all.at[:, c]
    copies.remote(own_packed, own_packed, near_device)
    own_gu = gu_all.at[:, :, c]
    copies.remote(own_gu, own_gu, near_device)
    for _, copy in packed_far:
        copies.arrive(copy)
    far_packed = packed_all.at[:, far]
    copies.remote(far_packed, far_packed, near_device)
    for copy in gu_far:
        copies.arrive(copy)
    far_gu = gu_all.at[:, :, far]
    copies.remote(far_gu, far_gu, near_device)
    copies.drain()


def spread_weights(n_batch, packed, up_parts, out_rows, gu_parts, down_rows):
    own_rows, packed_cols = packed.shape
    _, gain_rows, up_cols = up_parts.shape
    ff = gu_parts.shape[-1]
    shapes = (
        jax.ShapeDtypeStruct((n_batch, 4, own_rows, packed_cols), BF),
        jax.ShapeDtypeStruct((n_batch, 4, gain_rows, up_cols), BF),
        jax.ShapeDtypeStruct((n_batch,) + out_rows.shape, BF),
        jax.ShapeDtypeStruct((2, n_batch, 4, own_rows, ff), BF),
        jax.ShapeDtypeStruct((4,) + down_rows.shape, BF),
    )
    sems = 6 * n_batch + 3 * n_batch + 32
    return pl.pallas_call(
        functools.partial(weights_kernel, n_batch),
        out_shape=shapes,
        in_specs=[pl.BlockSpec(memory_space=pl.ANY)] * 5,
        out_specs=[pl.BlockSpec(memory_space=pl.ANY)] * 5,
        scratch_shapes=[
            pltpu.SemaphoreType.DMA((sems,)),
            pltpu.SemaphoreType.DMA((sems,)),
            pltpu.SemaphoreType.DMA((2,)),
        ],
        compiler_params=pltpu.CompilerParams(collective_id=0, has_side_effects=True),
        name="spread_weights",
    )(packed, up_parts, out_rows, gu_parts, down_rows)


def shards(
    tokens,
    cotangent,
    lengths,
    slot_sequence,
    proj_in,
    query_up,
    proj_out,
    attn_gain,
    query_gain,
    mlp_gain,
    gate_up,
    down_proj,
):
    n_ctx = lax.axis_size("ctx")
    n_batch = lax.axis_size("batch")
    ctx_rank = lax.axis_index("ctx")
    batch_rank = lax.axis_index("batch")
    ring = Ring()
    micro, pos_dev, width = tokens.shape
    n_tok = micro * pos_dev
    full_length = pos_dev * n_ctx
    heads = H // n_ctx
    score_scale = 1.0 / math.sqrt(HD)
    in_cols = proj_in.shape[1]

    slot_total = lengths.shape[0]
    slot_ids = jnp.arange(slot_total, dtype=jnp.int32)
    seq_lengths = jnp.sum(
        jnp.where(slot_sequence[:, None] == slot_ids[None, :], lengths[None, :], 0), axis=1
    )
    own_lengths = lax.dynamic_slice_in_dim(seq_lengths, batch_rank * micro, micro)
    query_pos = ctx_rank * pos_dev + jnp.arange(pos_dev, dtype=jnp.int32)
    key_pos = jnp.arange(full_length, dtype=jnp.int32)
    cos_all, sin_all = rope_tables(key_pos)
    cos_own, sin_own = rope_tables(query_pos)

    own_rows = proj_in.shape[0]
    gain_rows = query_gain.shape[0]
    gains = jnp.stack(
        [attn_gain, mlp_gain, jnp.pad(query_gain, (0, own_rows - gain_rows))], axis=1
    )
    packed = jnp.concatenate([proj_in, jnp.pad(gains, ((0, 0), (0, 125)))], axis=1)
    up_parts = query_up.reshape(gain_rows, n_ctx, heads * HD).swapaxes(0, 1)
    ff_all = gate_up.shape[1] // 2
    ff = ff_all // n_batch
    gu_parts = gate_up.reshape(own_rows, 2, n_batch, ff).transpose(2, 1, 0, 3)
    packed, own_qup, own_out, gu_rows, own_down = spread_weights(
        n_batch, packed, up_parts, proj_out, gu_parts, down_proj
    )
    packed = packed.reshape(width, in_cols + 128)
    own_qup = own_qup.reshape(QR, heads * HD)
    own_out = own_out.reshape(heads * HD, width)
    own_gate, own_up = gu_rows.reshape(2, width, ff)
    own_down = own_down.reshape(ff, width)
    slabs = slab_pairs(n_batch, n_ctx)
    full_in = packed[:, :in_cols]
    gains = packed[:, in_cols : in_cols + 3].T.astype(F32)
    gain_norm = gains[0]
    gain_mlp = gains[1]
    gain_query = gains[2].reshape(n_batch * n_ctx, own_rows)[:, :gain_rows].reshape(QR)

    residual = tokens.reshape(n_tok, width).astype(F32)
    valid_rows = (query_pos[None, :] < own_lengths[:, None]).astype(F32).reshape(n_tok, 1)
    grad_out = cotangent.reshape(n_tok, width).astype(F32) * valid_rows
    with jax.named_scope('cotangent_spread'):
        grad_mo = ring.spread(grad_out.astype(BF))

    scale_one = rms_scale(residual)
    normed_one = residual * scale_one
    attn_in = (normed_one * gain_norm).astype(BF)
    with jax.named_scope('attn_in_gather'):
        attn_in_all = ctx_gather(attn_in).reshape(n_ctx * n_tok, width)
    projected = dot(attn_in, full_in)
    q_latent = projected[:, :QR]
    scale_query = rms_scale(q_latent)
    normed_query = q_latent * scale_query
    q_normed = (normed_query * gain_query).astype(BF)
    k_rot = rotate(
        projected[:, QR : QR + HD].reshape(micro, pos_dev, HD), cos_own, sin_own
    ).astype(BF)
    v_low = projected[:, QR + HD :].astype(BF)
    with jax.named_scope('qkv_gather'):
        qkv_all = ctx_gather(jnp.concatenate([q_normed, k_rot.reshape(n_tok, HD), v_low], axis=1))
    q_normed_all = qkv_all[..., :QR].reshape(n_ctx * n_tok, QR)

    def by_sequence(values):
        return (
            values.reshape(n_ctx, micro, pos_dev, -1)
            .swapaxes(0, 1)
            .reshape(micro, full_length, -1)
        )

    def by_position(values):
        return (
            values.reshape(micro, n_ctx, pos_dev, -1)
            .swapaxes(0, 1)
            .reshape(n_ctx * n_tok, -1)
        )

    def split_heads(values):
        return by_sequence(values).reshape(micro, full_length, heads, HD).swapaxes(1, 2)

    def join_heads(values):
        return by_position(values.swapaxes(1, 2).reshape(micro, full_length, heads * HD))

    kv_all = by_sequence(qkv_all[..., QR:])
    keys_all = kv_all[..., :HD]
    values_all = kv_all[..., HD:]
    queries = split_heads(dot(q_normed_all, own_qup))
    q_rot = rotate(queries, cos_all, sin_all).astype(BF)
    allowed = (key_pos[None, :] <= key_pos[:, None])[None, None] & (
        key_pos[None, None, None, :] < own_lengths[:, None, None, None]
    )
    scores = jnp.einsum("shtd,sud->shtu", q_rot, keys_all, preferred_element_type=F32) * score_scale
    masked = jnp.where(allowed, scores, -1e30)
    row_max = jnp.max(masked, axis=-1, keepdims=True)
    raised = jnp.exp(masked - row_max)
    weights = raised / jnp.sum(raised, axis=-1, keepdims=True)
    weights_low = weights.astype(BF)
    mixed = join_heads(
        jnp.einsum("shtu,sud->shtd", weights_low, values_all, preferred_element_type=F32).astype(BF)
    )
    with jax.named_scope('attended_collect'):
        attended = ctx_collect(dot(mixed, own_out).reshape(n_ctx, n_tok, width))
    hidden_res = residual + attended

    scale_two = rms_scale(hidden_res)
    normed_two = hidden_res * scale_two
    with jax.named_scope('mlp_in_spread'):
        mlp_in = ring.spread((normed_two * gain_mlp).astype(BF))
    far = ring.h
    groups = [[0]] + [[-step, step] for step in range(1, far)] + [[far]]
    out_terms = {}
    in_terms = {}
    kept = []
    for group in groups:
        rows = jnp.concatenate([mlp_in[step] for step in group], axis=0)
        grad_rows = jnp.concatenate([grad_mo[step] for step in group], axis=0)
        gate_part = dot(rows, own_gate)
        up_part = dot(rows, own_up)
        sigmoid_gate = jax.nn.sigmoid(gate_part)
        silu_gate = gate_part * sigmoid_gate
        activated = (silu_gate * up_part).astype(BF)
        grad_act = dot_right_t(grad_rows, own_down)
        grad_gate = (
            grad_act * up_part * (sigmoid_gate * (1.0 + gate_part * (1.0 - sigmoid_gate)))
        ).astype(BF)
        grad_up = (grad_act * silu_gate).astype(BF)
        in_term = dot_right_t(grad_gate, own_gate) + dot_right_t(grad_up, own_up)
        out_term = dot(activated, own_down)
        for place_in, step in enumerate(group):
            cut = slice(place_in * n_tok, (place_in + 1) * n_tok)
            in_terms[step] = in_term[cut]
            out_terms[step] = out_term[cut]
        kept.append((rows, grad_rows, activated, grad_gate, grad_up))
    rows, grad_rows, activated, grad_gate, grad_up = (
        jnp.concatenate(items, axis=0) for items in zip(*kept)
    )
    with jax.named_scope('grad_mlp_in_collect'):
        grad_mlp_in = ring.collect(lambda step: in_terms[step])
    gain_mlp_term = jnp.sum(grad_mlp_in * normed_two, axis=0)
    grad_hidden = grad_out + norm_back(grad_mlp_in * gain_mlp, normed_two, scale_two)
    with jax.named_scope('layer_out_collect'):
        layer_out = hidden_res + ring.collect(lambda step: out_terms[step])

    grad_gu_own = jnp.stack([dot_left_t(rows, grad_gate), dot_left_t(rows, grad_up)])
    grad_gu_own = grad_gu_own.reshape(2, n_batch, n_ctx, own_rows, ff).transpose(2, 1, 0, 3, 4)
    with jax.named_scope('grad_gate_up_collect'):
        grad_gu_own = ctx_collect(grad_gu_own).astype(BF)
    with jax.named_scope('grad_gate_up_exchange'):
        grad_gu_own = batch_exchange(grad_gu_own)
    grad_gate_up = grad_gu_own.transpose(2, 1, 0, 3).reshape(own_rows, 2 * ff_all).astype(F32)
    grad_down_own = dot_left_t(activated, grad_rows)
    with jax.named_scope('grad_down_collect'):
        grad_down = ctx_collect(grad_down_own.reshape(n_ctx, ff // n_ctx, width))

    with jax.named_scope('grad_att_gather'):
        grad_att_all = ctx_gather(grad_hidden.astype(BF)).reshape(n_ctx * n_tok, width)
    grad_out_own = dot_left_t(mixed, grad_att_all)
    with jax.named_scope('grad_proj_out_collect'):
        grad_out_own = ring.collect_rows(grad_out_own.reshape(n_batch, -1, width)).astype(BF)
        grad_proj_out = lax.ppermute(
            grad_out_own, ("batch", "ctx"), [(there, here) for here, there in slabs]
        ).astype(F32)
    grad_mixed = split_heads(dot_right_t(grad_att_all, own_out).astype(BF))
    grad_probs = jnp.einsum(
        "shtd,sud->shtu", grad_mixed, values_all, preferred_element_type=F32
    )
    row_dot = jnp.sum(weights * grad_probs, axis=-1, keepdims=True)
    grad_scores = (weights * (grad_probs - row_dot)).astype(BF)
    grad_q_rot = (
        jnp.einsum("shtu,sud->shtd", grad_scores, keys_all, preferred_element_type=F32)
        * score_scale
    )
    grad_keys = (
        jnp.einsum("shtu,shtd->sud", grad_scores, q_rot, preferred_element_type=F32)
        * score_scale
    )
    grad_values = jnp.einsum(
        "shtu,shtd->sud", weights_low, grad_mixed, preferred_element_type=F32
    )
    grad_q = join_heads(rotate_back(grad_q_rot, cos_all, sin_all).astype(BF))
    grad_qn_part = dot_right_t(grad_q, own_qup)
    grad_kv_part = by_position(jnp.concatenate([grad_keys, grad_values], axis=-1))
    back_parts = jnp.concatenate([grad_qn_part, grad_kv_part], axis=1).astype(BF)
    with jax.named_scope('back_collect'):
        back_own = ctx_collect(back_parts.reshape(n_ctx, n_tok, in_cols))
    grad_qn = back_own[:, :QR]
    gain_query_term = jnp.sum(grad_qn * normed_query, axis=0)
    grad_latent = norm_back(grad_qn * gain_query, normed_query, scale_query)
    grad_key_raw = rotate_back(
        back_own[:, QR : QR + HD].reshape(micro, pos_dev, HD), cos_own, sin_own
    ).reshape(n_tok, HD)
    grad_project = jnp.concatenate(
        [grad_latent, grad_key_raw, back_own[:, QR + HD :]], axis=1
    ).astype(BF)
    grad_attn_in = dot_right_t(grad_project, full_in)
    gain_norm_term = jnp.sum(grad_attn_in * normed_one, axis=0)
    grad_tokens = grad_hidden + norm_back(grad_attn_in * gain_norm, normed_one, scale_one)

    grad_up_own = dot_left_t(q_normed_all, grad_q)
    with jax.named_scope('grad_query_up_collect'):
        grad_up_own = ring.collect_rows(grad_up_own.reshape(n_batch, -1, heads * HD)).astype(BF)
    grad_query_up = (
        ctx_exchange(grad_up_own.reshape(n_ctx, gain_rows, heads * HD))
        .swapaxes(0, 1)
        .reshape(gain_rows, H * HD)
        .astype(F32)
    )
    part_cols = in_cols // n_ctx
    project_parts = grad_project.reshape(n_tok, n_ctx, part_cols).swapaxes(0, 1)
    with jax.named_scope('grad_project_exchange'):
        project_all = ctx_exchange(project_parts).reshape(n_ctx * n_tok, part_cols)
    grad_in_own = dot_left_t(attn_in_all, project_all).reshape(
        n_batch, n_ctx, own_rows, part_cols
    )
    gain_terms = jnp.stack(
        [
            gain_norm_term.reshape(n_batch, n_ctx, own_rows),
            gain_mlp_term.reshape(n_batch, n_ctx, own_rows),
            jnp.pad(
                gain_query_term.reshape(n_batch, n_ctx, gain_rows),
                ((0, 0), (0, 0), (0, own_rows - gain_rows)),
            ),
        ],
        axis=2,
    )
    gain_terms = jnp.pad(gain_terms, ((0, 0), (0, 0), (0, 13), (0, part_cols - own_rows)))
    joined = jnp.concatenate([grad_in_own, gain_terms], axis=2).reshape(n_batch, -1, part_cols)
    with jax.named_scope('grad_proj_in_collect'):
        joined = ring.collect_rows(joined).astype(BF)
    joined = ctx_exchange(joined.reshape(n_ctx, own_rows + 16, part_cols)).astype(F32)
    grad_proj_in = joined[:, :own_rows].swapaxes(0, 1).reshape(own_rows, in_cols)
    gain_sums = jnp.sum(joined[:, own_rows : own_rows + 3, :own_rows], axis=0)

    return (
        layer_out.reshape(tokens.shape).astype(BF),
        grad_tokens.reshape(tokens.shape).astype(BF),
        grad_proj_in,
        grad_query_up,
        grad_proj_out,
        gain_sums[0],
        gain_sums[2, :gain_rows],
        gain_sums[1],
        grad_gate_up,
        grad_down,
    )


def solution(mesh):
    rows = P(("batch", "ctx"), None)
    vector = P(("batch", "ctx"))
    acts = P("batch", "ctx", None)
    return jax.shard_map(
        shards,
        mesh=mesh,
        in_specs=(acts, acts, P(), P(), rows, rows, rows, vector, vector, vector, rows, rows),
        out_specs=(acts, acts, rows, rows, rows, vector, vector, vector, rows, rows),
        check_vma=False,
    )
```

```python
import functools
import math

import jax
import jax.numpy as jnp
from jax import lax
from jax.experimental import pallas as pl
from jax.experimental.pallas import tpu as pltpu
from jax.sharding import PartitionSpec as P

H = 16
HD = 256
QR = 1024
EPSILON = 1e-06
BF = jnp.bfloat16
F32 = jnp.float32


def rms_scale(values):
    return lax.rsqrt(jnp.mean(values * values, axis=-1, keepdims=True) + EPSILON)


def rope_tables(positions):
    half_size = HD // 2
    frequency = 10000.0 ** (-(jnp.arange(half_size, dtype=F32) * 2.0 / HD))
    angles = positions.astype(F32)[:, None] * frequency[None, :]
    return (jnp.cos(angles), jnp.sin(angles))


def rotate(values, cosine_table, sine_table):
    half_size = values.shape[-1] // 2
    front_half = values[..., :half_size]
    back_half = values[..., half_size:]
    return jnp.concatenate(
        [
            front_half * cosine_table - back_half * sine_table,
            back_half * cosine_table + front_half * sine_table,
        ],
        axis=-1,
    )


def rotate_back(values, cosine_table, sine_table):
    return rotate(values, cosine_table, -sine_table)


def dot(left_side, right_side):
    return jnp.dot(left_side, right_side, preferred_element_type=F32)


def dot_right_t(left_side, right_side):
    return lax.dot_general(
        left_side, right_side, (((1,), (1,)), ((), ())), preferred_element_type=F32
    )


def dot_left_t(left_side, right_side):
    return lax.dot_general(
        left_side, right_side, (((0,), (0,)), ((), ())), preferred_element_type=F32
    )


def norm_back(grad_normed, normed, inv_rms):
    return inv_rms * (grad_normed - normed * jnp.mean(grad_normed * normed, axis=-1, keepdims=True))


def pick(array, index, axis=0):
    return lax.dynamic_index_in_dim(array, index, axis, keepdims=False)


def place(array, block, index, axis=0):
    return lax.dynamic_update_index_in_dim(array, block, index, axis)


class Ring:
    def __init__(self):
        self.n = lax.axis_size("batch")
        self.h = self.n // 2
        rank = lax.axis_index("batch")
        self.at = jnp.where(rank % 2 == 0, rank // 2, self.n - 1 - rank // 2)
        order = [2 * i for i in range(self.h)] + [2 * i + 1 for i in reversed(range(self.h))]
        self.up = [(order[i], order[(i + 1) % self.n]) for i in range(self.n)]
        self.down = [(there, here) for here, there in self.up]

    def rank_of(self, step):
        spot = (self.at + step) % self.n
        return jnp.where(spot < self.h, 2 * spot, 2 * (self.n - 1 - spot) + 1)

    def spread(self, block):
        found = {0: block}
        upward = downward = block
        for step in range(1, self.h):
            upward = lax.ppermute(upward, "batch", self.up)
            downward = lax.ppermute(downward, "batch", self.down)
            found[-step] = upward
            found[step] = downward
        cut = block.shape[0] // 2
        found[self.h] = jnp.concatenate(
            [
                lax.ppermute(upward[:cut], "batch", self.up),
                lax.ppermute(downward[cut:], "batch", self.down),
            ],
            axis=0,
        )
        return found

    def gather(self, block):
        found = self.spread(block)
        whole = jnp.zeros((self.n,) + block.shape, block.dtype)
        for step, part in found.items():
            whole = place(whole, part, self.rank_of(step))
        return whole

    def collect(self, term):
        far = term(self.h)
        cut = far.shape[0] // 2
        downward = lax.ppermute(far[:cut].astype(BF), "batch", self.down)
        upward = lax.ppermute(far[cut:].astype(BF), "batch", self.up)
        for step in range(self.h - 1, 0, -1):
            for_lower = term(-step).astype(F32)
            for_upper = term(step).astype(F32)
            if step == self.h - 1:
                for_lower = jnp.concatenate(
                    [for_lower[:cut] + downward.astype(F32), for_lower[cut:]], axis=0
                )
                for_upper = jnp.concatenate(
                    [for_upper[:cut], for_upper[cut:] + upward.astype(F32)], axis=0
                )
            else:
                for_lower = for_lower + downward.astype(F32)
                for_upper = for_upper + upward.astype(F32)
            downward = lax.ppermute(for_lower.astype(BF), "batch", self.down)
            upward = lax.ppermute(for_upper.astype(BF), "batch", self.up)
        own = term(0).astype(F32)
        return own + downward.astype(F32) + upward.astype(F32)

    def collect_rows(self, stacked):
        return self.collect(lambda step: pick(stacked, self.rank_of(step)))


FAR = [(0, 2), (1, 3), (2, 0), (3, 1)]
NEAR = [(0, 1), (1, 0), (2, 3), (3, 2)]


def ctx_place():
    rank = lax.axis_index("ctx")
    return rank // 2, rank % 2


def in_order(mine, theirs, at):
    return jnp.where(at == 0, jnp.stack([mine, theirs]), jnp.stack([theirs, mine]))


def ctx_gather(block):
    outer, inner = ctx_place()
    pair = in_order(block, lax.ppermute(block, "ctx", FAR), outer)
    whole = in_order(pair, lax.ppermute(pair, "ctx", NEAR), inner)
    whole = jnp.swapaxes(whole, 0, 1)
    return whole.reshape((4,) + block.shape)


def ctx_collect(stacked):
    outer, inner = ctx_place()
    parts = stacked.reshape((2, 2) + stacked.shape[1:])
    got = lax.ppermute(pick(parts, 1 - inner, 1).astype(BF), "ctx", NEAR)
    half = pick(parts, inner, 1).astype(F32) + got.astype(F32)
    got = lax.ppermute(pick(half, 1 - outer).astype(BF), "ctx", FAR)
    return pick(half, outer) + got.astype(F32)


def ctx_exchange(stacked):
    outer, inner = ctx_place()
    parts = stacked.reshape((2, 2) + stacked.shape[1:])
    got = lax.ppermute(pick(parts, 1 - outer), "ctx", FAR)
    parts = in_order(pick(parts, outer), got, outer)
    got = lax.ppermute(pick(parts, 1 - inner, 1), "ctx", NEAR)
    whole = in_order(pick(parts, inner, 1), got, inner)
    return jnp.swapaxes(whole, 0, 1).reshape(stacked.shape)


MESH = pl.DeviceIdType.MESH


class Place:
    def __init__(self, n_batch):
        self.n = n_batch
        self.h = n_batch // 2
        self.b = lax.axis_index("batch")
        self.c = lax.axis_index("ctx")
        self.outer = lax.div(self.c, 2)
        self.inner = lax.rem(self.c, 2)
        self.far = lax.rem(self.c + 2, 4)
        self.near = self.c + 1 - 2 * self.inner
        odd = lax.rem(self.b, 2)
        half = lax.div(self.b, 2)
        self.at = half + odd * (self.n - 1 - 2 * half)

    def rank_of(self, step):
        spot = lax.rem(self.at + step + 2 * self.n, self.n)
        back = lax.div(spot, self.h)
        return (1 - back) * 2 * spot + back * (2 * (self.n - 1 - spot) + 1)

    def up(self):
        return (self.rank_of(1), self.c)

    def down(self):
        return (self.rank_of(-1), self.c)


class Copies:
    def __init__(self, send_sems, recv_sems):
        self.send_sems = send_sems
        self.recv_sems = recv_sems
        self.count = 0
        self.open_sends = []
        self.open_recvs = []

    def remote(self, source, target, device):
        index = self.count
        self.count += 1
        copy = pltpu.make_async_remote_copy(
            src_ref=source,
            dst_ref=target,
            send_sem=self.send_sems.at[index],
            recv_sem=self.recv_sems.at[index],
            device_id=device,
            device_id_type=MESH,
        )
        copy.start()
        self.open_sends.append(copy)
        self.open_recvs.append(copy)
        return copy

    def local(self, source, target):
        index = self.count
        self.count += 1
        copy = pltpu.make_async_copy(source, target, self.recv_sems.at[index])
        copy.start()
        self.open_recvs.append(copy)
        return copy

    def arrive(self, copy):
        if any(copy is other for other in self.open_recvs):
            self.open_recvs = [other for other in self.open_recvs if other is not copy]
            if any(copy is other for other in self.open_sends):
                copy.wait_recv()
            else:
                copy.wait()

    def drain(self):
        for copy in list(self.open_recvs):
            self.arrive(copy)
        for copy in self.open_sends:
            copy.wait_send()


def greet(place, others):
    barrier = pltpu.get_barrier_semaphore()
    for device in others:
        pl.semaphore_signal(barrier, inc=1, device_id=device, device_id_type=MESH)
    return barrier


class RingGather:
    def __init__(self, place, copies, rows, slot):
        self.place, self.copies, self.rows, self.slot = place, copies, rows, slot
        self.step = 0
        self.moving = ()

    def advance(self):
        place, copies = self.place, self.copies
        for copy in self.moving:
            copies.arrive(copy)
        self.moving = ()
        self.step += 1
        cut = self.rows // 2
        if self.step > place.h:
            return
        lower = place.rank_of(1 - self.step)
        upper = place.rank_of(self.step - 1)
        if self.step < place.h:
            whole = pl.ds(0, self.rows)
            pieces = (whole, whole)
        else:
            pieces = (pl.ds(0, cut), pl.ds(cut, self.rows - cut))
        upward, downward = self.slot(lower, pieces[0]), self.slot(upper, pieces[1])
        self.moving = (
            copies.remote(upward, upward, place.up()),
            copies.remote(downward, downward, place.down()),
        )

    def arrived(self):
        step = self.step - 1
        if step == 0:
            return []
        if step == self.place.h:
            return [self.place.rank_of(step)]
        return [self.place.rank_of(-step), self.place.rank_of(step)]


def weights_kernel(
    n_batch,
    packed_ref,
    up_ref,
    out_ref,
    gu_ref,
    down_ref,
    packed_all,
    up_all,
    out_all,
    gu_all,
    down_all,
    send_sems,
    recv_sems,
    out_sems,
):
    place = Place(n_batch)
    copies = Copies(send_sems, recv_sems)
    b, c, n = place.b, place.c, n_batch
    own_rows = packed_ref.shape[0]
    out_rows = out_ref.shape[0]
    index = b * 4 + c
    target = (lax.rem(index, n), lax.div(index, n))
    slab = c * n + b
    source = (lax.div(slab, 4), lax.rem(slab, 4))
    stays = slab == index
    peers = [(lax.rem(b + k, n), c) for k in range(1, n)]
    ctx_peers = [(b, place.far), (b, place.near), (b, lax.rem(place.near + 2, 4))]

    barrier = greet(place, peers + ctx_peers)

    @pl.when(jnp.logical_not(stays))
    def _():
        for device in (target, source):
            pl.semaphore_signal(barrier, inc=1, device_id=device, device_id_type=MESH)

    pl.semaphore_wait(barrier, n + 4 - 2 * stays.astype(jnp.int32))

    own = [
        copies.local(packed_ref, packed_all.at[b, c]),
        copies.local(up_ref.at[c], up_all.at[b, c]),
        copies.local(gu_ref.at[b], gu_all.at[:, b, c]),
        copies.local(down_ref, down_all.at[c]),
    ]
    out_copy = pltpu.make_async_remote_copy(
        src_ref=out_ref,
        dst_ref=out_all.at[target[0]],
        send_sem=out_sems.at[0],
        recv_sem=out_sems.at[1],
        device_id=target,
        device_id_type=MESH,
    )
    out_stay = pltpu.make_async_copy(out_ref, out_all.at[b], out_sems.at[0])

    @pl.when(jnp.logical_not(stays))
    def _():
        out_copy.start()

    @pl.when(stays)
    def _():
        out_stay.start()

    up_copies = [
        copies.remote(up_ref.at[peer[1]], up_all.at[b, c], peer) for peer in ctx_peers
    ]
    far_device, near_device = ctx_peers[0], ctx_peers[1]
    down_far = copies.remote(down_ref, down_all.at[c], far_device)

    copies.arrive(own[0])
    packed_ring = RingGather(
        place, copies, own_rows, lambda rank, rows: packed_all.at[rank, c, rows]
    )
    up_ring = RingGather(
        place, copies, up_ref.shape[1], lambda rank, rows: up_all.at[rank, :, rows]
    )
    out_ring = RingGather(place, copies, out_rows, lambda rank, rows: out_all.at[rank, rows])

    packed_far = []

    def packed_step():
        packed_ring.advance()
        ranks = packed_ring.arrived() if packed_ring.step > 1 else [b]
        for rank in ranks:
            block = packed_all.at[rank, c]
            packed_far.append((rank, copies.remote(block, block, far_device)))

    packed_step()
    gu_copies = [
        (
            lax.rem(b - k + n, n),
            copies.remote(gu_ref.at[peer[0]], gu_all.at[:, b, c], peer),
        )
        for k, peer in zip(range(1, n), peers)
    ]
    for copy in own[1:2] + up_copies:
        copies.arrive(copy)
    up_ring.advance()
    packed_step()

    @pl.when(jnp.logical_not(stays))
    def _():
        out_copy.wait()

    @pl.when(stays)
    def _():
        out_stay.wait()

    out_ring.advance()
    gu_far = []
    copies.arrive(own[2])
    own_gu = gu_all.at[:, b, c]
    gu_far.append(copies.remote(own_gu, own_gu, far_device))
    waiting = list(gu_copies)
    copies.arrive(own[3])
    down_near = [copies.remote(down_all.at[c], down_all.at[c], near_device)]

    def forward_gu(count):
        for _ in range(min(count, len(waiting))):
            rank, copy = waiting.pop(0)
            copies.arrive(copy)
            block = gu_all.at[:, rank, c]
            gu_far.append(copies.remote(block, block, far_device))

    for _ in range(place.h):
        up_ring.advance()
        if packed_ring.step <= place.h:
            packed_step()
        forward_gu(2)
        out_ring.advance()
    copies.arrive(down_far)
    far = place.far
    down_near.append(copies.remote(down_all.at[far], down_all.at[far], near_device))
    forward_gu(n)
    own_packed = packed_all.at[:, c]
    copies.remote(own_packed, own_packed, near_device)
    own_gu = gu_all.at[:, :, c]
    copies.remote(own_gu, own_gu, near_device)
    for _, copy in packed_far:
        copies.arrive(copy)
    far_packed = packed_all.at[:, far]
    copies.remote(far_packed, far_packed, near_device)
    for copy in gu_far:
        copies.arrive(copy)
    far_gu = gu_all.at[:, :, far]
    copies.remote(far_gu, far_gu, near_device)
    copies.drain()


def spread_weights(n_batch, packed, up_parts, out_rows, gu_parts, down_rows):
    own_rows, packed_cols = packed.shape
    _, gain_rows, up_cols = up_parts.shape
    ff = gu_parts.shape[-1]
    shapes = (
        jax.ShapeDtypeStruct((n_batch, 4, own_rows, packed_cols), BF),
        jax.ShapeDtypeStruct((n_batch, 4, gain_rows, up_cols), BF),
        jax.ShapeDtypeStruct((n_batch,) + out_rows.shape, BF),
        jax.ShapeDtypeStruct((2, n_batch, 4, own_rows, ff), BF),
        jax.ShapeDtypeStruct((4,) + down_rows.shape, BF),
    )
    sems = 6 * n_batch + 3 * n_batch + 32
    return pl.pallas_call(
        functools.partial(weights_kernel, n_batch),
        out_shape=shapes,
        in_specs=[pl.BlockSpec(memory_space=pl.ANY)] * 5,
        out_specs=[pl.BlockSpec(memory_space=pl.ANY)] * 5,
        scratch_shapes=[
            pltpu.SemaphoreType.DMA((sems,)),
            pltpu.SemaphoreType.DMA((sems,)),
            pltpu.SemaphoreType.DMA((2,)),
        ],
        compiler_params=pltpu.CompilerParams(collective_id=0, has_side_effects=True),
        name="spread_weights",
    )(packed, up_parts, out_rows, gu_parts, down_rows)


def mlp_kernel(
    n_batch,
    rows_ref,
    gate_ref,
    up_ref,
    down_ref,
    *refs,
):
    cot_refs = refs[:n_batch]
    (
        sum_ref,
        down_grad,
        term_out,
        gu_out,
        rows_v,
        cot_v,
        gate_v,
        up_v,
        down_v,
        act_v,
        ggate_v,
        gup_v,
        in_v,
        term_v,
        got_v,
        gu_got,
        gu_last,
        down_got,
        down_last,
        send_sems,
        recv_sems,
        back_send,
        back_recv,
        load_sems,
        store_sems,
        part_send,
        part_recv,
    ) = refs[n_batch:]
    place = Place(n_batch)
    far = place.h
    n_tok = rows_ref.shape[0]
    cut = n_tok // 2
    width = rows_ref.shape[1]
    ff = gate_ref.shape[-1]
    up_device, down_device = place.up(), place.down()
    far_device, near_device = (place.b, place.far), (place.b, place.near)
    barrier = greet(place, [up_device, down_device, far_device, near_device])
    parts = Copies(part_send, part_recv)
    own_rows = gate_v.shape[2]
    block = 4 * own_rows

    load_rows = pltpu.make_async_copy(rows_ref, rows_v.at[0, pl.ds(0, n_tok)], load_sems.at[0])
    load_rows.start()
    loads = [
        pltpu.make_async_copy(source, target, load_sems.at[1 + i])
        for i, (source, target) in enumerate(
            [(gate_ref, gate_v), (up_ref, up_v), (down_ref, down_v)]
        )
    ]
    spots = [(0, 0)] + [(s, k) for s in range(1, far) for k in (0, 1)] + [(0, 1)]
    for i, (source, (group, side)) in enumerate(zip(cot_refs, spots)):
        loads.append(
            pltpu.make_async_copy(
                source, cot_v.at[group, pl.ds(side * n_tok, n_tok)], load_sems.at[4 + i]
            )
        )
    for copy in loads:
        copy.start()
    load_rows.wait()
    pl.semaphore_wait(barrier, 4)

    def piece(side, half):
        return pl.ds(side * n_tok + half * cut, cut)

    def hop(step, side, half):
        source_group, source_side = step - 1, side
        target_group, target_side = step, side
        if isinstance(step, int) and step == 1:
            source_side = 0
        if isinstance(step, int) and step == far:
            target_group, target_side = 0, 1
        return pltpu.make_async_remote_copy(
            src_ref=rows_v.at[source_group, piece(source_side, half)],
            dst_ref=rows_v.at[target_group, piece(target_side, half)],
            send_sem=send_sems.at[step, side, half],
            recv_sem=recv_sems.at[step, side, half],
            device_id=down_device if side else up_device,
            device_id_type=MESH,
        )

    both = [(side, half) for half in (0, 1) for side in (0, 1)]
    ends = [(0, 0), (1, 1)]
    for side, half in both:
        hop(1, side, half).start()
    for copy in loads:
        copy.wait()

    def stores(group):
        return [
            pltpu.make_async_copy(term_v.at[group], term_out.at[group], store_sems.at[0, group])
        ]

    def compute(group):
        rows = rows_v[group]
        cots = cot_v[group]
        down_all = down_v[...].reshape(ff, width)
        start = 0
        while start < ff:
            size = min(256, ff - start)
            tile = slice(start, start + size)
            gate = dot(rows, gate_v[..., tile].reshape(width, size))
            up = dot(rows, up_v[..., tile].reshape(width, size))
            grad_act = dot_right_t(cots, down_all[tile])
            sigmoid = 1.0 / (1.0 + jnp.exp(-gate))
            silu = gate * sigmoid
            act_v[group, :, tile] = (silu * up).astype(BF)
            slope = sigmoid * (1.0 + gate * (1.0 - sigmoid))
            ggate_v[group, :, tile] = (grad_act * up * slope).astype(BF)
            gup_v[group, :, tile] = (grad_act * silu).astype(BF)
            start += size
        ggate = ggate_v[group]
        gup = gup_v[group]
        act = act_v[group]
        tile_cols = 2 * block

        @pl.loop(0, width // tile_cols)
        def _(t):
            cols = pl.ds(pl.multiple_of(t * tile_cols, tile_cols), tile_cols)
            back = dot_right_t(ggate, gate_v[pl.ds(2 * t, 2)].reshape(tile_cols, ff))
            back += dot_right_t(gup, up_v[pl.ds(2 * t, 2)].reshape(tile_cols, ff))
            in_v[group, :, cols] = back.astype(BF)
            down = down_v[:, :, cols].reshape(ff, tile_cols)
            term_v[group, :, cols] = dot(act, down).astype(BF)

        for copy in stores(group):
            copy.start()

    @pl.loop(1, far)
    def _(step):
        for side, half in both:
            hop(step, side, half).wait_recv()

        @pl.when(step < far - 1)
        def _():
            for side, half in both:
                hop(step + 1, side, half).start()

        @pl.when(step == far - 1)
        def _():
            for side, half in ends:
                hop(far, side, half).start()

        compute(step)

    for side, half in ends:
        hop(far, side, half).wait_recv()
    compute(0)

    def back_hop(step, side, half, source):
        return pltpu.make_async_remote_copy(
            src_ref=source,
            dst_ref=got_v.at[step, side, half],
            send_sem=back_send.at[step, side, half],
            recv_sem=back_recv.at[step, side, half],
            device_id=up_device if side else down_device,
            device_id_type=MESH,
        )

    def held(step, side, half):
        return in_v.at[step, piece(side, half)]

    for side, half in ends:
        back_hop(far - 1, side, half, held(0, 1, half)).start()

    def pass_on(step, side, half, added):
        own = held(step, side, half)
        if added:
            back_hop(step, side, half, own).wait_recv()
            own[...] = (own[...].astype(F32) + got_v[step, side, half].astype(F32)).astype(BF)
        back_hop(step - 1, side, half, own).start()

    for side, half in both:
        if (side, half) not in ends:
            pass_on(far - 1, side, half, False)

    def gate_up_terms(first, last):
        @pl.loop(first, last)
        def _(t):
            cols = pl.ds(pl.multiple_of(t * 2 * block, 2 * block), 2 * block)
            rows = rows_v[:, :, cols].reshape(n_batch * n_tok, 2 * block)
            for target, grads in ((gate_v, ggate_v), (up_v, gup_v)):
                term = dot_left_t(rows, grads[...].reshape(n_batch * n_tok, ff))
                target[pl.ds(2 * t, 2)] = term.astype(BF).reshape(2, 4, own_rows, ff)

    def down_terms():
        @pl.loop(0, width // (2 * block))
        def _(t):
            cols = pl.ds(pl.multiple_of(t * 2 * block, 2 * block), 2 * block)
            grads = cot_v[:, :, cols].reshape(n_batch * n_tok, 2 * block)
            term = dot_left_t(act_v[...].reshape(n_batch * n_tok, ff), grads)
            down_v[:, :, cols] = term.astype(BF).reshape(4, ff // 4, 2 * block)

    def pass_all(step):
        for side, half in [(1, 0), (0, 1), (0, 0), (1, 1)]:
            if step < far - 1 or (side, half) in ends:
                pass_on(step, side, half, True)

    steps = iter(range(far - 1, 0, -1))
    tiles = width // (2 * block)
    outer, inner = place.outer, place.inner

    gate_up_terms(0, tiles // 2)
    pass_all(next(steps))
    gate_up_terms(tiles // 2, tiles)
    near_copies = [
        parts.remote(
            target.at[:, 2 * side + 1 - inner], gu_got.at[kind, side], near_device
        )
        for side in (0, 1)
        for kind, target in enumerate((gate_v, up_v))
    ]
    for step in steps:
        pass_all(step)
        if step > 1:
            down_terms()
    down_copies = [
        parts.remote(down_v.at[2 * side + 1 - inner], down_got.at[side], near_device)
        for side in (0, 1)
    ]
    for copy in near_copies:
        parts.arrive(copy)
    far_copies = []
    for kind, target in enumerate((gate_v, up_v)):
        for side in (1 - outer, outer):
            kept = target.at[:, 2 * side + inner]
            kept[...] = (kept[...].astype(F32) + gu_got[kind, side].astype(F32)).astype(BF)
            if side is not outer:
                far_copies.append(parts.remote(kept, gu_last.at[kind], far_device))
    for copy in down_copies:
        parts.arrive(copy)
    other = down_v.at[2 * (1 - outer) + inner]
    other[...] = (other[...].astype(F32) + down_got[1 - outer].astype(F32)).astype(BF)
    down_far = parts.remote(other, down_last, far_device)
    for half in (0, 1):
        for side in (0, 1):
            back_hop(0, side, half, held(0, 0, half)).wait_recv()
        rows = slice(half * cut, (half + 1) * cut)
        sum_ref[rows, :] = (
            in_v[0, rows, :].astype(F32)
            + got_v[0, 0, half].astype(F32)
            + got_v[0, 1, half].astype(F32)
        )
    for kind, target in enumerate((gate_v, up_v)):
        parts.arrive(far_copies[kind])
        kept = target.at[:, 2 * outer + inner]
        kept[...] = (kept[...].astype(F32) + gu_last[kind].astype(F32)).astype(BF)
        parts.local(kept, gu_out.at[:, kind])
    parts.arrive(down_far)
    down_grad[...] = (
        down_v[2 * outer + inner].astype(F32)
        + down_got[outer].astype(F32)
        + down_last[...].astype(F32)
    )
    parts.drain()

    for step in range(1, far + 1):
        for side, half in both if step < far else ends:
            hop(step, side, half).wait_send()
    for side, half in ends:
        back_hop(far - 1, side, half, held(0, 1, half)).wait_send()
    for step in range(far - 1, 0, -1):
        for side, half in both:
            back_hop(step - 1, side, half, held(step, side, half)).wait_send()
    for group in range(far):
        for copy in stores(group):
            copy.wait()


def fused_mlp(n_batch, rows, cots, own_gate, own_up, own_down):
    n_tok, width = rows.shape
    ff = own_gate.shape[-1]
    own_rows = own_gate.shape[2]
    far = n_batch // 2
    pair = 2 * n_tok
    flops = 18 * n_batch * n_tok * width * ff
    return pl.pallas_call(
        functools.partial(mlp_kernel, n_batch),
        out_shape=(
            jax.ShapeDtypeStruct((n_tok, width), F32),
            jax.ShapeDtypeStruct((ff // 4, width), F32),
            jax.ShapeDtypeStruct((far, pair, width), BF),
            jax.ShapeDtypeStruct((n_batch, 2, own_rows, ff), BF),
        ),
        in_specs=[pl.BlockSpec(memory_space=pl.ANY)] * (4 + n_batch),
        out_specs=[pl.BlockSpec(memory_space=pltpu.VMEM)] * 2
        + [pl.BlockSpec(memory_space=pl.ANY)] * 2,
        scratch_shapes=[
            pltpu.VMEM((far, pair, width), BF),
            pltpu.VMEM((far, pair, width), BF),
            pltpu.VMEM((n_batch, 4, own_rows, ff), BF),
            pltpu.VMEM((n_batch, 4, own_rows, ff), BF),
            pltpu.VMEM((4, ff // 4, width), BF),
            pltpu.VMEM((far, pair, ff), BF),
            pltpu.VMEM((far, pair, ff), BF),
            pltpu.VMEM((far, pair, ff), BF),
            pltpu.VMEM((far, pair, width), BF),
            pltpu.VMEM((far, pair, width), BF),
            pltpu.VMEM((far, 2, 2, n_tok // 2, width), BF),
            pltpu.VMEM((2, 2, n_batch, own_rows, ff), BF),
            pltpu.VMEM((2, n_batch, own_rows, ff), BF),
            pltpu.VMEM((2, ff // 4, width), BF),
            pltpu.VMEM((ff // 4, width), BF),
            pltpu.SemaphoreType.DMA((far + 1, 2, 2)),
            pltpu.SemaphoreType.DMA((far + 1, 2, 2)),
            pltpu.SemaphoreType.DMA((far, 2, 2)),
            pltpu.SemaphoreType.DMA((far, 2, 2)),
            pltpu.SemaphoreType.DMA((4 + n_batch,)),
            pltpu.SemaphoreType.DMA((1, far)),
            pltpu.SemaphoreType.DMA((16,)),
            pltpu.SemaphoreType.DMA((16,)),
        ],
        compiler_params=pltpu.CompilerParams(
            collective_id=1, has_side_effects=True, vmem_limit_bytes=60 * 1024 * 1024
        ),
        cost_estimate=pl.CostEstimate(
            flops=flops, bytes_accessed=24 * 1024 * 1024, transcendentals=n_batch * n_tok * ff
        ),
        name="fused_mlp",
    )(rows, own_gate, own_up, own_down, *cots)


class RingCollect:
    def __init__(self, place, block, got, send_sems, recv_sems):
        self.place, self.block, self.got = place, block, got
        self.send_sems, self.recv_sems = send_sems, recv_sems
        self.cut = got.shape[3]
        self.step = place.h
        self.sent = []

    def held(self, step, half):
        return self.block(self.place.rank_of(step)).at[pl.ds(half * self.cut, self.cut)]

    def hop(self, step, side, half, source):
        place = self.place
        return pltpu.make_async_remote_copy(
            src_ref=source,
            dst_ref=self.got.at[step, side, half],
            send_sem=self.send_sems.at[step, side, half],
            recv_sem=self.recv_sems.at[step, side, half],
            device_id=place.up() if side else place.down(),
            device_id_type=MESH,
        )

    def send(self, step, side, half, source):
        copy = self.hop(step, side, half, source)
        copy.start()
        self.sent.append(copy)

    def advance(self):
        far = self.place.h
        step = self.step
        self.step -= 1
        if step == far:
            for side in (0, 1):
                self.send(far - 1, side, side, self.held(far, side))
            for side in (0, 1):
                half = 1 - side
                self.send(far - 2, side, half, self.held((2 * side - 1) * (far - 1), half))
            return
        pieces = [(0, 0), (1, 1)] if step == far - 1 else [(1, 0), (0, 1), (0, 0), (1, 1)]
        for side, half in pieces:
            own = self.held((2 * side - 1) * step, half)
            self.hop(step, side, half, own).wait_recv()
            own[...] = (own[...].astype(F32) + self.got[step, side, half].astype(F32)).astype(BF)
            self.send(step - 1, side, half, own)

    def finish(self, half):
        own = self.held(0, half)
        for side in (0, 1):
            self.hop(0, side, half, own).wait_recv()
        return (
            own[...].astype(F32)
            + self.got[0, 0, half].astype(F32)
            + self.got[0, 1, half].astype(F32)
        )

    def drain(self):
        for copy in self.sent:
            copy.wait_send()


def tail_kernel(
    n_batch,
    gain_rows,
    out_ref,
    up_ref,
    in_ref,
    gu_ref,
    out_grad,
    up_grad,
    in_grad,
    gain_grad,
    gu_grad,
    out_v,
    up_v,
    in_v,
    out_got,
    up_got,
    in_got,
    out_sum,
    out_all,
    up_sum,
    up_all,
    in_sum,
    in_all,
    ring_send,
    ring_recv,
    send_sems,
    recv_sems,
    load_sems,
    out_sems,
):
    place = Place(n_batch)
    copies = Copies(send_sems, recv_sems)
    b, c, n = place.b, place.c, n_batch
    own_rows = in_grad.shape[0]
    index = b * 4 + c
    slab = c * n + b
    target = (lax.div(slab, 4), lax.rem(slab, 4))
    source = (lax.rem(index, n), lax.div(index, n))
    stays = slab == index
    peers = [(lax.rem(b + k, n), c) for k in range(1, n)]
    ctx_peers = [(b, place.far), (b, place.near), (b, lax.rem(place.near + 2, 4))]

    loads = [
        pltpu.make_async_copy(held, kept, load_sems.at[i])
        for i, (held, kept) in enumerate([(out_ref, out_v), (up_ref, up_v), (in_ref, in_v)])
    ]
    for copy in loads:
        copy.start()
    barrier = greet(place, peers + ctx_peers)

    @pl.when(jnp.logical_not(stays))
    def _():
        for device in (target, source):
            pl.semaphore_signal(barrier, inc=1, device_id=device, device_id_type=MESH)

    pl.semaphore_wait(barrier, n + 4 - 2 * stays.astype(jnp.int32))

    rings = []
    for i, (kept, got) in enumerate([(out_v, out_got), (up_v, up_got), (in_v, in_got)]):
        rings.append(
            RingCollect(
                place,
                lambda rank, kept=kept: kept.at[rank],
                got,
                ring_send.at[i],
                ring_recv.at[i],
            )
        )
    for copy, ring in zip(loads, rings):
        copy.wait()
        ring.advance()
    copies.local(gu_ref.at[b], gu_grad.at[b])
    for peer in peers:
        copies.remote(gu_ref.at[peer[0]], gu_grad.at[b], peer)
    for _ in range(place.h - 1):
        for ring in rings:
            ring.advance()

    in_ring, up_ring, out_ring = rings[2], rings[1], rings[0]
    out_cut, up_cut, in_cut = out_ring.cut, up_ring.cut, in_ring.cut
    for half in (0, 1):
        out_sum[pl.ds(half * out_cut, out_cut), :] = out_ring.finish(half).astype(BF)
    out_copy = pltpu.make_async_remote_copy(
        src_ref=out_sum,
        dst_ref=out_all,
        send_sem=out_sems.at[0],
        recv_sem=out_sems.at[1],
        device_id=target,
        device_id_type=MESH,
    )
    out_stay = pltpu.make_async_copy(out_sum, out_all, out_sems.at[0])

    @pl.when(jnp.logical_not(stays))
    def _():
        out_copy.start()

    @pl.when(stays)
    def _():
        out_stay.start()

    for half in (0, 1):
        up_sum[pl.ds(half * up_cut, up_cut), :] = up_ring.finish(half).astype(BF)
    up_copies = [
        copies.remote(
            up_sum.at[pl.ds(peer[1] * gain_rows, gain_rows)], up_all.at[c], peer
        )
        for peer in ctx_peers
    ]
    up_copies.append(
        copies.local(up_sum.at[pl.ds(c * gain_rows, gain_rows)], up_all.at[c])
    )
    for half in (0, 1):
        in_sum[pl.ds(half * in_cut, in_cut), :] = in_ring.finish(half).astype(BF)
    part_rows = own_rows + 16
    in_copies = [
        copies.remote(in_sum.at[pl.ds(peer[1] * part_rows, part_rows)], in_all.at[c], peer)
        for peer in ctx_peers
    ]
    in_copies.append(copies.local(in_sum.at[pl.ds(c * part_rows, part_rows)], in_all.at[c]))

    @pl.when(jnp.logical_not(stays))
    def _():
        out_copy.wait()

    @pl.when(stays)
    def _():
        out_stay.wait()

    out_grad[...] = out_all[...].astype(F32)
    for copy in up_copies:
        copies.arrive(copy)
    cols = up_all.shape[2]
    for part in range(4):
        up_grad[:, part * cols : (part + 1) * cols] = up_all[part].astype(F32)
    for copy in in_copies:
        copies.arrive(copy)
    cols = in_all.shape[2]
    gains = jnp.zeros(gain_grad.shape, F32)
    for part in range(4):
        in_grad[:, part * cols : (part + 1) * cols] = in_all[part, :own_rows, :].astype(F32)
        gains = gains + in_all[part, own_rows:, :].astype(F32)
    gain_grad[...] = gains
    copies.drain()
    for ring in rings:
        ring.drain()


def collect_weights(n_batch, gain_rows, out_terms, up_terms, in_terms, gu_terms):
    far = n_batch // 2
    out_rows, width = out_terms.shape[1:]
    up_rows, up_cols = up_terms.shape[1:]
    in_rows, in_cols = in_terms.shape[1:]
    own_rows = in_rows // 4 - 16
    shapes = [out_terms.shape[1:], up_terms.shape[1:], in_terms.shape[1:]]
    sems = 2 * n_batch + 16
    return pl.pallas_call(
        functools.partial(tail_kernel, n_batch, gain_rows),
        out_shape=(
            jax.ShapeDtypeStruct((out_rows, width), F32),
            jax.ShapeDtypeStruct((gain_rows, 4 * up_cols), F32),
            jax.ShapeDtypeStruct((own_rows, 4 * in_cols), F32),
            jax.ShapeDtypeStruct((16, in_cols), F32),
            jax.ShapeDtypeStruct(gu_terms.shape, BF),
        ),
        in_specs=[pl.BlockSpec(memory_space=pl.ANY)] * 4,
        out_specs=[pl.BlockSpec(memory_space=pltpu.VMEM)] * 4
        + [pl.BlockSpec(memory_space=pl.ANY)],
        scratch_shapes=[pltpu.VMEM((n_batch,) + shape, BF) for shape in shapes]
        + [pltpu.VMEM((far, 2, 2, rows // 2, cols), BF) for rows, cols in shapes]
        + [
            pltpu.VMEM((out_rows, width), BF),
            pltpu.VMEM((out_rows, width), BF),
            pltpu.VMEM((up_rows, up_cols), BF),
            pltpu.VMEM((4, gain_rows, up_cols), BF),
            pltpu.VMEM((in_rows, in_cols), BF),
            pltpu.VMEM((4, own_rows + 16, in_cols), BF),
            pltpu.SemaphoreType.DMA((3, far, 2, 2)),
            pltpu.SemaphoreType.DMA((3, far, 2, 2)),
            pltpu.SemaphoreType.DMA((sems,)),
            pltpu.SemaphoreType.DMA((sems,)),
            pltpu.SemaphoreType.DMA((3,)),
            pltpu.SemaphoreType.DMA((2,)),
        ],
        compiler_params=pltpu.CompilerParams(
            collective_id=2, has_side_effects=True, vmem_limit_bytes=48 * 1024 * 1024
        ),
        name="collect_weights",
    )(out_terms, up_terms, in_terms, gu_terms)


def permuted_mlp(ring, rows_own, grad_mo, gu_rows, own_down):
    mlp_in = ring.spread(rows_own)
    n_tok, width = rows_own.shape
    _, n_batch, n_ctx, own_rows, ff = gu_rows.shape
    own_gate, own_up = gu_rows.reshape(2, width, ff)
    own_down = own_down.reshape(ff, width)
    far = ring.h
    groups = [[0]] + [[-step, step] for step in range(1, far)] + [[far]]
    out_terms = {}
    in_terms = {}
    kept = []
    for group in groups:
        rows = jnp.concatenate([mlp_in[step] for step in group], axis=0)
        grad_rows = jnp.concatenate([grad_mo[step] for step in group], axis=0)
        gate_part = dot(rows, own_gate)
        up_part = dot(rows, own_up)
        sigmoid_gate = jax.nn.sigmoid(gate_part)
        silu_gate = gate_part * sigmoid_gate
        activated = (silu_gate * up_part).astype(BF)
        grad_act = dot_right_t(grad_rows, own_down)
        grad_gate = (
            grad_act * up_part * (sigmoid_gate * (1.0 + gate_part * (1.0 - sigmoid_gate)))
        ).astype(BF)
        grad_up = (grad_act * silu_gate).astype(BF)
        in_term = dot_right_t(grad_gate, own_gate) + dot_right_t(grad_up, own_up)
        out_term = dot(activated, own_down)
        for place_in, step in enumerate(group):
            cut = slice(place_in * n_tok, (place_in + 1) * n_tok)
            in_terms[step] = in_term[cut]
            out_terms[step] = out_term[cut]
        kept.append((rows, grad_rows, activated, grad_gate, grad_up))
    rows, grad_rows, activated, grad_gate, grad_up = (
        jnp.concatenate(items, axis=0) for items in zip(*kept)
    )
    grad_gu = jnp.stack([dot_left_t(rows, grad_gate), dot_left_t(rows, grad_up)])
    grad_gu = grad_gu.reshape(2, n_batch, n_ctx, own_rows, ff).transpose(2, 1, 0, 3, 4)
    grad_down = dot_left_t(activated, grad_rows)
    return (
        ring.collect(lambda step: in_terms[step]),
        ctx_collect(grad_down.reshape(n_ctx, ff // n_ctx, width)),
        out_terms,
        ctx_collect(grad_gu).astype(BF),
    )


def shards(
    tokens,
    cotangent,
    lengths,
    slot_sequence,
    proj_in,
    query_up,
    proj_out,
    attn_gain,
    query_gain,
    mlp_gain,
    gate_up,
    down_proj,
):
    n_ctx = lax.axis_size("ctx")
    n_batch = lax.axis_size("batch")
    ctx_rank = lax.axis_index("ctx")
    batch_rank = lax.axis_index("batch")
    ring = Ring()
    micro, pos_dev, width = tokens.shape
    n_tok = micro * pos_dev
    full_length = pos_dev * n_ctx
    heads = H // n_ctx
    score_scale = 1.0 / math.sqrt(HD)
    in_cols = proj_in.shape[1]

    slot_total = lengths.shape[0]
    slot_ids = jnp.arange(slot_total, dtype=jnp.int32)
    seq_lengths = jnp.sum(
        jnp.where(slot_sequence[:, None] == slot_ids[None, :], lengths[None, :], 0), axis=1
    )
    own_lengths = lax.dynamic_slice_in_dim(seq_lengths, batch_rank * micro, micro)
    query_pos = ctx_rank * pos_dev + jnp.arange(pos_dev, dtype=jnp.int32)
    key_pos = jnp.arange(full_length, dtype=jnp.int32)
    cos_all, sin_all = rope_tables(key_pos)
    cos_own, sin_own = rope_tables(query_pos)

    own_rows = proj_in.shape[0]
    gain_rows = query_gain.shape[0]
    gains = jnp.stack(
        [attn_gain, mlp_gain, jnp.pad(query_gain, (0, own_rows - gain_rows))], axis=1
    )
    packed = jnp.concatenate([proj_in, jnp.pad(gains, ((0, 0), (0, 125)))], axis=1)
    up_parts = query_up.reshape(gain_rows, n_ctx, heads * HD).swapaxes(0, 1)
    ff_all = gate_up.shape[1] // 2
    ff = ff_all // n_batch
    gu_parts = gate_up.reshape(own_rows, 2, n_batch, ff).transpose(2, 1, 0, 3)
    packed, own_qup, own_out, gu_rows, own_down = spread_weights(
        n_batch, packed, up_parts, proj_out, gu_parts, down_proj
    )
    packed = packed.reshape(width, in_cols + 128)
    own_qup = own_qup.reshape(QR, heads * HD)
    own_out = own_out.reshape(heads * HD, width)
    full_in = packed[:, :in_cols]
    gains = packed[:, in_cols : in_cols + 3].T.astype(F32)
    gain_norm = gains[0]
    gain_mlp = gains[1]
    gain_query = gains[2].reshape(n_batch * n_ctx, own_rows)[:, :gain_rows].reshape(QR)

    residual = tokens.reshape(n_tok, width).astype(F32)
    valid_rows = (query_pos[None, :] < own_lengths[:, None]).astype(F32).reshape(n_tok, 1)
    grad_out = cotangent.reshape(n_tok, width).astype(F32) * valid_rows
    with jax.named_scope('cotangent_spread'):
        grad_mo = ring.spread(grad_out.astype(BF))

    scale_one = rms_scale(residual)
    normed_one = residual * scale_one
    attn_in = (normed_one * gain_norm).astype(BF)
    with jax.named_scope('attn_in_gather'):
        attn_in_all = ctx_gather(attn_in).reshape(n_ctx * n_tok, width)
    projected = dot(attn_in, full_in)
    q_latent = projected[:, :QR]
    scale_query = rms_scale(q_latent)
    normed_query = q_latent * scale_query
    q_normed = (normed_query * gain_query).astype(BF)
    k_rot = rotate(
        projected[:, QR : QR + HD].reshape(micro, pos_dev, HD), cos_own, sin_own
    ).astype(BF)
    v_low = projected[:, QR + HD :].astype(BF)
    with jax.named_scope('qkv_gather'):
        qkv_all = ctx_gather(jnp.concatenate([q_normed, k_rot.reshape(n_tok, HD), v_low], axis=1))
    q_normed_all = qkv_all[..., :QR].reshape(n_ctx * n_tok, QR)

    def by_sequence(values):
        return (
            values.reshape(n_ctx, micro, pos_dev, -1)
            .swapaxes(0, 1)
            .reshape(micro, full_length, -1)
        )

    def by_position(values):
        return (
            values.reshape(micro, n_ctx, pos_dev, -1)
            .swapaxes(0, 1)
            .reshape(n_ctx * n_tok, -1)
        )

    def split_heads(values):
        return by_sequence(values).reshape(micro, full_length, heads, HD).swapaxes(1, 2)

    def join_heads(values):
        return by_position(values.swapaxes(1, 2).reshape(micro, full_length, heads * HD))

    kv_all = by_sequence(qkv_all[..., QR:])
    keys_all = kv_all[..., :HD]
    values_all = kv_all[..., HD:]
    queries = split_heads(dot(q_normed_all, own_qup))
    q_rot = rotate(queries, cos_all, sin_all).astype(BF)
    allowed = (key_pos[None, :] <= key_pos[:, None])[None, None] & (
        key_pos[None, None, None, :] < own_lengths[:, None, None, None]
    )
    scores = jnp.einsum("shtd,sud->shtu", q_rot, keys_all, preferred_element_type=F32) * score_scale
    masked = jnp.where(allowed, scores, -1e30)
    row_max = jnp.max(masked, axis=-1, keepdims=True)
    raised = jnp.exp(masked - row_max)
    weights = raised / jnp.sum(raised, axis=-1, keepdims=True)
    weights_low = weights.astype(BF)
    mixed = join_heads(
        jnp.einsum("shtu,sud->shtd", weights_low, values_all, preferred_element_type=F32).astype(BF)
    )
    with jax.named_scope('attended_collect'):
        attended = ctx_collect(dot(mixed, own_out).reshape(n_ctx, n_tok, width))
    hidden_res = residual + attended

    scale_two = rms_scale(hidden_res)
    normed_two = hidden_res * scale_two
    mlp_in = (normed_two * gain_mlp).astype(BF)
    far = ring.h
    order = [0] + [side * step for step in range(1, far) for side in (-1, 1)] + [far]
    resident = 10 * n_batch * n_tok * width <= 24 * 1024 * 1024
    if resident:
        grad_mlp_in, grad_down, terms, grad_gu_own = fused_mlp(
            n_batch, mlp_in, [grad_mo[step] for step in order], gu_rows[0], gu_rows[1], own_down
        )
        terms = terms.reshape(n_batch, n_tok, width)
        spots = [0, far] + [side * step for step in range(1, far) for side in (-1, 1)]
        out_terms = {step: terms[i] for i, step in enumerate(spots)}
    else:
        grad_mlp_in, grad_down, out_terms, grad_gu_own = permuted_mlp(
            ring, mlp_in, grad_mo, gu_rows, own_down
        )
    gain_mlp_term = jnp.sum(grad_mlp_in * normed_two, axis=0)
    grad_hidden = grad_out + norm_back(grad_mlp_in * gain_mlp, normed_two, scale_two)
    with jax.named_scope('layer_out_collect'):
        layer_out = hidden_res + ring.collect(lambda step: out_terms[step])

    with jax.named_scope('grad_att_gather'):
        grad_att_all = ctx_gather(grad_hidden.astype(BF)).reshape(n_ctx * n_tok, width)
    grad_out_own = dot_left_t(mixed, grad_att_all)
    grad_mixed = split_heads(dot_right_t(grad_att_all, own_out).astype(BF))
    grad_probs = jnp.einsum(
        "shtd,sud->shtu", grad_mixed, values_all, preferred_element_type=F32
    )
    row_dot = jnp.sum(weights * grad_probs, axis=-1, keepdims=True)
    grad_scores = (weights * (grad_probs - row_dot)).astype(BF)
    grad_q_rot = (
        jnp.einsum("shtu,sud->shtd", grad_scores, keys_all, preferred_element_type=F32)
        * score_scale
    )
    grad_keys = (
        jnp.einsum("shtu,shtd->sud", grad_scores, q_rot, preferred_element_type=F32)
        * score_scale
    )
    grad_values = jnp.einsum(
        "shtu,shtd->sud", weights_low, grad_mixed, preferred_element_type=F32
    )
    grad_q = join_heads(rotate_back(grad_q_rot, cos_all, sin_all).astype(BF))
    grad_qn_part = dot_right_t(grad_q, own_qup)
    grad_kv_part = by_position(jnp.concatenate([grad_keys, grad_values], axis=-1))
    back_parts = jnp.concatenate([grad_qn_part, grad_kv_part], axis=1).astype(BF)
    with jax.named_scope('back_collect'):
        back_own = ctx_collect(back_parts.reshape(n_ctx, n_tok, in_cols))
    grad_qn = back_own[:, :QR]
    gain_query_term = jnp.sum(grad_qn * normed_query, axis=0)
    grad_latent = norm_back(grad_qn * gain_query, normed_query, scale_query)
    grad_key_raw = rotate_back(
        back_own[:, QR : QR + HD].reshape(micro, pos_dev, HD), cos_own, sin_own
    ).reshape(n_tok, HD)
    grad_project = jnp.concatenate(
        [grad_latent, grad_key_raw, back_own[:, QR + HD :]], axis=1
    ).astype(BF)
    grad_attn_in = dot_right_t(grad_project, full_in)
    gain_norm_term = jnp.sum(grad_attn_in * normed_one, axis=0)
    grad_tokens = grad_hidden + norm_back(grad_attn_in * gain_norm, normed_one, scale_one)

    grad_up_own = dot_left_t(q_normed_all, grad_q)
    part_cols = in_cols // n_ctx
    project_parts = grad_project.reshape(n_tok, n_ctx, part_cols).swapaxes(0, 1)
    with jax.named_scope('grad_project_exchange'):
        project_all = ctx_exchange(project_parts).reshape(n_ctx * n_tok, part_cols)
    grad_in_own = dot_left_t(attn_in_all, project_all).reshape(
        n_batch, n_ctx, own_rows, part_cols
    )
    gain_terms = jnp.stack(
        [
            gain_norm_term.reshape(n_batch, n_ctx, own_rows),
            gain_mlp_term.reshape(n_batch, n_ctx, own_rows),
            jnp.pad(
                gain_query_term.reshape(n_batch, n_ctx, gain_rows),
                ((0, 0), (0, 0), (0, own_rows - gain_rows)),
            ),
        ],
        axis=2,
    )
    gain_terms = jnp.pad(gain_terms, ((0, 0), (0, 0), (0, 13), (0, part_cols - own_rows)))
    joined = jnp.concatenate([grad_in_own, gain_terms], axis=2).reshape(n_batch, -1, part_cols)
    grad_proj_out, grad_query_up, grad_proj_in, gain_sums, grad_gu_own = collect_weights(
        n_batch,
        gain_rows,
        grad_out_own.reshape(n_batch, -1, width).astype(BF),
        grad_up_own.reshape(n_batch, -1, heads * HD).astype(BF),
        joined.astype(BF),
        grad_gu_own,
    )
    grad_gate_up = grad_gu_own.transpose(2, 1, 0, 3).reshape(own_rows, 2 * ff_all).astype(F32)
    gain_sums = gain_sums[:, :own_rows]

    return (
        layer_out.reshape(tokens.shape).astype(BF),
        grad_tokens.reshape(tokens.shape).astype(BF),
        grad_proj_in,
        grad_query_up,
        grad_proj_out,
        gain_sums[0],
        gain_sums[2, :gain_rows],
        gain_sums[1],
        grad_gate_up,
        grad_down,
    )


def solution(mesh):
    rows = P(("batch", "ctx"), None)
    vector = P(("batch", "ctx"))
    acts = P("batch", "ctx", None)
    return jax.shard_map(
        shards,
        mesh=mesh,
        in_specs=(acts, acts, P(), P(), rows, rows, rows, vector, vector, vector, rows, rows),
        out_specs=(acts, acts, rows, rows, rows, vector, vector, vector, rows, rows),
        check_vma=False,
    )
```

```python
import functools
import math

import jax
import jax.numpy as jnp
from jax import lax
from jax.experimental import pallas as pl
from jax.experimental.pallas import tpu as pltpu
from jax.sharding import PartitionSpec as P

H = 16
HD = 256
QR = 1024
EPSILON = 1e-06
BF = jnp.bfloat16
F32 = jnp.float32


def rms_scale(values):
    return lax.rsqrt(jnp.mean(values * values, axis=-1, keepdims=True) + EPSILON)


def rope_tables(positions):
    half_size = HD // 2
    frequency = 10000.0 ** (-(jnp.arange(half_size, dtype=F32) * 2.0 / HD))
    angles = positions.astype(F32)[:, None] * frequency[None, :]
    return (jnp.cos(angles), jnp.sin(angles))


def rotate(values, cosine_table, sine_table):
    half_size = values.shape[-1] // 2
    front_half = values[..., :half_size]
    back_half = values[..., half_size:]
    return jnp.concatenate(
        [
            front_half * cosine_table - back_half * sine_table,
            back_half * cosine_table + front_half * sine_table,
        ],
        axis=-1,
    )


def rotate_back(values, cosine_table, sine_table):
    return rotate(values, cosine_table, -sine_table)


def dot(left_side, right_side):
    return jnp.dot(left_side, right_side, preferred_element_type=F32)


def dot_right_t(left_side, right_side):
    return lax.dot_general(
        left_side, right_side, (((1,), (1,)), ((), ())), preferred_element_type=F32
    )


def dot_left_t(left_side, right_side):
    return lax.dot_general(
        left_side, right_side, (((0,), (0,)), ((), ())), preferred_element_type=F32
    )


def norm_back(grad_normed, normed, inv_rms):
    return inv_rms * (grad_normed - normed * jnp.mean(grad_normed * normed, axis=-1, keepdims=True))


def pick(array, index, axis=0):
    return lax.dynamic_index_in_dim(array, index, axis, keepdims=False)


def place(array, block, index, axis=0):
    return lax.dynamic_update_index_in_dim(array, block, index, axis)


class Ring:
    def __init__(self):
        self.n = lax.axis_size("batch")
        self.h = self.n // 2
        rank = lax.axis_index("batch")
        self.at = jnp.where(rank % 2 == 0, rank // 2, self.n - 1 - rank // 2)
        order = [2 * i for i in range(self.h)] + [2 * i + 1 for i in reversed(range(self.h))]
        self.up = [(order[i], order[(i + 1) % self.n]) for i in range(self.n)]
        self.down = [(there, here) for here, there in self.up]

    def rank_of(self, step):
        spot = (self.at + step) % self.n
        return jnp.where(spot < self.h, 2 * spot, 2 * (self.n - 1 - spot) + 1)

    def spread(self, block):
        found = {0: block}
        upward = downward = block
        for step in range(1, self.h):
            upward = lax.ppermute(upward, "batch", self.up)
            downward = lax.ppermute(downward, "batch", self.down)
            found[-step] = upward
            found[step] = downward
        cut = block.shape[0] // 2
        found[self.h] = jnp.concatenate(
            [
                lax.ppermute(upward[:cut], "batch", self.up),
                lax.ppermute(downward[cut:], "batch", self.down),
            ],
            axis=0,
        )
        return found

    def gather(self, block):
        found = self.spread(block)
        whole = jnp.zeros((self.n,) + block.shape, block.dtype)
        for step, part in found.items():
            whole = place(whole, part, self.rank_of(step))
        return whole

    def collect(self, term):
        far = term(self.h)
        cut = far.shape[0] // 2
        downward = lax.ppermute(far[:cut].astype(BF), "batch", self.down)
        upward = lax.ppermute(far[cut:].astype(BF), "batch", self.up)
        for step in range(self.h - 1, 0, -1):
            for_lower = term(-step).astype(F32)
            for_upper = term(step).astype(F32)
            if step == self.h - 1:
                for_lower = jnp.concatenate(
                    [for_lower[:cut] + downward.astype(F32), for_lower[cut:]], axis=0
                )
                for_upper = jnp.concatenate(
                    [for_upper[:cut], for_upper[cut:] + upward.astype(F32)], axis=0
                )
            else:
                for_lower = for_lower + downward.astype(F32)
                for_upper = for_upper + upward.astype(F32)
            downward = lax.ppermute(for_lower.astype(BF), "batch", self.down)
            upward = lax.ppermute(for_upper.astype(BF), "batch", self.up)
        own = term(0).astype(F32)
        return own + downward.astype(F32) + upward.astype(F32)

    def collect_rows(self, stacked):
        return self.collect(lambda step: pick(stacked, self.rank_of(step)))


FAR = [(0, 2), (1, 3), (2, 0), (3, 1)]
NEAR = [(0, 1), (1, 0), (2, 3), (3, 2)]


def ctx_place():
    rank = lax.axis_index("ctx")
    return rank // 2, rank % 2


def in_order(mine, theirs, at):
    return jnp.where(at == 0, jnp.stack([mine, theirs]), jnp.stack([theirs, mine]))


def ctx_gather(block):
    outer, inner = ctx_place()
    pair = in_order(block, lax.ppermute(block, "ctx", FAR), outer)
    whole = in_order(pair, lax.ppermute(pair, "ctx", NEAR), inner)
    whole = jnp.swapaxes(whole, 0, 1)
    return whole.reshape((4,) + block.shape)


def ctx_collect(stacked):
    outer, inner = ctx_place()
    parts = stacked.reshape((2, 2) + stacked.shape[1:])
    got = lax.ppermute(pick(parts, 1 - inner, 1).astype(BF), "ctx", NEAR)
    half = pick(parts, inner, 1).astype(F32) + got.astype(F32)
    got = lax.ppermute(pick(half, 1 - outer).astype(BF), "ctx", FAR)
    return pick(half, outer) + got.astype(F32)


def ctx_exchange(stacked):
    outer, inner = ctx_place()
    parts = stacked.reshape((2, 2) + stacked.shape[1:])
    got = lax.ppermute(pick(parts, 1 - outer), "ctx", FAR)
    parts = in_order(pick(parts, outer), got, outer)
    got = lax.ppermute(pick(parts, 1 - inner, 1), "ctx", NEAR)
    whole = in_order(pick(parts, inner, 1), got, inner)
    return jnp.swapaxes(whole, 0, 1).reshape(stacked.shape)


MESH = pl.DeviceIdType.MESH


class Place:
    def __init__(self, n_batch):
        self.n = n_batch
        self.h = n_batch // 2
        self.b = lax.axis_index("batch")
        self.c = lax.axis_index("ctx")
        self.outer = lax.div(self.c, 2)
        self.inner = lax.rem(self.c, 2)
        self.far = lax.rem(self.c + 2, 4)
        self.near = self.c + 1 - 2 * self.inner
        odd = lax.rem(self.b, 2)
        half = lax.div(self.b, 2)
        self.at = half + odd * (self.n - 1 - 2 * half)

    def rank_of(self, step):
        spot = lax.rem(self.at + step + 2 * self.n, self.n)
        back = lax.div(spot, self.h)
        return (1 - back) * 2 * spot + back * (2 * (self.n - 1 - spot) + 1)

    def up(self):
        return (self.rank_of(1), self.c)

    def down(self):
        return (self.rank_of(-1), self.c)


class Copies:
    def __init__(self, send_sems, recv_sems):
        self.send_sems = send_sems
        self.recv_sems = recv_sems
        self.count = 0
        self.open_sends = []
        self.open_recvs = []

    def remote(self, source, target, device):
        index = self.count
        self.count += 1
        copy = pltpu.make_async_remote_copy(
            src_ref=source,
            dst_ref=target,
            send_sem=self.send_sems.at[index],
            recv_sem=self.recv_sems.at[index],
            device_id=device,
            device_id_type=MESH,
        )
        copy.start()
        self.open_sends.append(copy)
        self.open_recvs.append(copy)
        return copy

    def local(self, source, target):
        index = self.count
        self.count += 1
        copy = pltpu.make_async_copy(source, target, self.recv_sems.at[index])
        copy.start()
        self.open_recvs.append(copy)
        return copy

    def arrive(self, copy):
        if any(copy is other for other in self.open_recvs):
            self.open_recvs = [other for other in self.open_recvs if other is not copy]
            if any(copy is other for other in self.open_sends):
                copy.wait_recv()
            else:
                copy.wait()

    def drain(self):
        for copy in list(self.open_recvs):
            self.arrive(copy)
        for copy in self.open_sends:
            copy.wait_send()


def greet(place, others):
    barrier = pltpu.get_barrier_semaphore()
    for device in others:
        pl.semaphore_signal(barrier, inc=1, device_id=device, device_id_type=MESH)
    return barrier


class RingGather:
    def __init__(self, place, copies, rows, slot):
        self.place, self.copies, self.rows, self.slot = place, copies, rows, slot
        self.step = 0
        self.moving = ()

    def advance(self):
        place, copies = self.place, self.copies
        for copy in self.moving:
            copies.arrive(copy)
        self.moving = ()
        self.step += 1
        cut = self.rows // 2
        if self.step > place.h:
            return
        lower = place.rank_of(1 - self.step)
        upper = place.rank_of(self.step - 1)
        if self.step < place.h:
            whole = pl.ds(0, self.rows)
            pieces = (whole, whole)
        else:
            pieces = (pl.ds(0, cut), pl.ds(cut, self.rows - cut))
        upward, downward = self.slot(lower, pieces[0]), self.slot(upper, pieces[1])
        self.moving = (
            copies.remote(upward, upward, place.up()),
            copies.remote(downward, downward, place.down()),
        )

    def arrived(self):
        step = self.step - 1
        if step == 0:
            return []
        if step == self.place.h:
            return [self.place.rank_of(step)]
        return [self.place.rank_of(-step), self.place.rank_of(step)]


def weights_kernel(
    n_batch,
    packed_ref,
    up_ref,
    out_ref,
    gu_ref,
    down_ref,
    packed_all,
    up_all,
    out_all,
    gu_all,
    down_all,
    send_sems,
    recv_sems,
    out_sems,
):
    place = Place(n_batch)
    copies = Copies(send_sems, recv_sems)
    b, c, n = place.b, place.c, n_batch
    own_rows = packed_ref.shape[0]
    out_rows = out_ref.shape[0]
    index = b * 4 + c
    target = (lax.rem(index, n), lax.div(index, n))
    slab = c * n + b
    source = (lax.div(slab, 4), lax.rem(slab, 4))
    stays = slab == index
    peers = [(lax.rem(b + k, n), c) for k in range(1, n)]
    ctx_peers = [(b, place.far), (b, place.near), (b, lax.rem(place.near + 2, 4))]

    barrier = greet(place, peers + ctx_peers)

    @pl.when(jnp.logical_not(stays))
    def _():
        for device in (target, source):
            pl.semaphore_signal(barrier, inc=1, device_id=device, device_id_type=MESH)

    pl.semaphore_wait(barrier, n + 4 - 2 * stays.astype(jnp.int32))

    own = [
        copies.local(packed_ref, packed_all.at[b, c]),
        copies.local(up_ref.at[c], up_all.at[b, c]),
        copies.local(gu_ref.at[b], gu_all.at[:, b, c]),
        copies.local(down_ref, down_all.at[c]),
    ]
    out_copy = pltpu.make_async_remote_copy(
        src_ref=out_ref,
        dst_ref=out_all.at[target[0]],
        send_sem=out_sems.at[0],
        recv_sem=out_sems.at[1],
        device_id=target,
        device_id_type=MESH,
    )
    out_stay = pltpu.make_async_copy(out_ref, out_all.at[b], out_sems.at[0])

    @pl.when(jnp.logical_not(stays))
    def _():
        out_copy.start()

    @pl.when(stays)
    def _():
        out_stay.start()

    up_copies = [
        copies.remote(up_ref.at[peer[1]], up_all.at[b, c], peer) for peer in ctx_peers
    ]
    far_device, near_device = ctx_peers[0], ctx_peers[1]
    down_far = copies.remote(down_ref, down_all.at[c], far_device)

    copies.arrive(own[0])
    packed_ring = RingGather(
        place, copies, own_rows, lambda rank, rows: packed_all.at[rank, c, rows]
    )
    up_ring = RingGather(
        place, copies, up_ref.shape[1], lambda rank, rows: up_all.at[rank, :, rows]
    )
    out_ring = RingGather(place, copies, out_rows, lambda rank, rows: out_all.at[rank, rows])

    packed_far = []

    def packed_step():
        packed_ring.advance()
        ranks = packed_ring.arrived() if packed_ring.step > 1 else [b]
        for rank in ranks:
            block = packed_all.at[rank, c]
            packed_far.append((rank, copies.remote(block, block, far_device)))

    packed_step()
    gu_copies = [
        (
            lax.rem(b - k + n, n),
            copies.remote(gu_ref.at[peer[0]], gu_all.at[:, b, c], peer),
        )
        for k, peer in zip(range(1, n), peers)
    ]
    for copy in own[1:2] + up_copies:
        copies.arrive(copy)
    up_ring.advance()
    packed_step()

    @pl.when(jnp.logical_not(stays))
    def _():
        out_copy.wait()

    @pl.when(stays)
    def _():
        out_stay.wait()

    out_ring.advance()
    gu_far = []
    copies.arrive(own[2])
    own_gu = gu_all.at[:, b, c]
    gu_far.append(copies.remote(own_gu, own_gu, far_device))
    waiting = list(gu_copies)
    copies.arrive(own[3])
    down_near = [copies.remote(down_all.at[c], down_all.at[c], near_device)]

    def forward_gu(count):
        for _ in range(min(count, len(waiting))):
            rank, copy = waiting.pop(0)
            copies.arrive(copy)
            block = gu_all.at[:, rank, c]
            gu_far.append(copies.remote(block, block, far_device))

    for _ in range(place.h):
        up_ring.advance()
        if packed_ring.step <= place.h:
            packed_step()
        forward_gu(2)
        out_ring.advance()
    copies.arrive(down_far)
    far = place.far
    down_near.append(copies.remote(down_all.at[far], down_all.at[far], near_device))
    forward_gu(n)
    own_packed = packed_all.at[:, c]
    copies.remote(own_packed, own_packed, near_device)
    own_gu = gu_all.at[:, :, c]
    copies.remote(own_gu, own_gu, near_device)
    for _, copy in packed_far:
        copies.arrive(copy)
    far_packed = packed_all.at[:, far]
    copies.remote(far_packed, far_packed, near_device)
    for copy in gu_far:
        copies.arrive(copy)
    far_gu = gu_all.at[:, :, far]
    copies.remote(far_gu, far_gu, near_device)
    copies.drain()


def spread_weights(n_batch, packed, up_parts, out_rows, gu_parts, down_rows):
    own_rows, packed_cols = packed.shape
    _, gain_rows, up_cols = up_parts.shape
    ff = gu_parts.shape[-1]
    shapes = (
        jax.ShapeDtypeStruct((n_batch, 4, own_rows, packed_cols), BF),
        jax.ShapeDtypeStruct((n_batch, 4, gain_rows, up_cols), BF),
        jax.ShapeDtypeStruct((n_batch,) + out_rows.shape, BF),
        jax.ShapeDtypeStruct((2, n_batch, 4, own_rows, ff), BF),
        jax.ShapeDtypeStruct((4,) + down_rows.shape, BF),
    )
    sems = 6 * n_batch + 3 * n_batch + 32
    return pl.pallas_call(
        functools.partial(weights_kernel, n_batch),
        out_shape=shapes,
        in_specs=[pl.BlockSpec(memory_space=pl.ANY)] * 5,
        out_specs=[pl.BlockSpec(memory_space=pl.ANY)] * 5,
        scratch_shapes=[
            pltpu.SemaphoreType.DMA((sems,)),
            pltpu.SemaphoreType.DMA((sems,)),
            pltpu.SemaphoreType.DMA((2,)),
        ],
        compiler_params=pltpu.CompilerParams(collective_id=0, has_side_effects=True),
        name="spread_weights",
    )(packed, up_parts, out_rows, gu_parts, down_rows)


def mlp_kernel(
    n_batch,
    rows_ref,
    gate_ref,
    up_ref,
    down_ref,
    cot_ref,
    *refs,
):
    (
        sum_ref,
        down_grad,
        term_out,
        gu_out,
        rows_v,
        cot_v,
        gate_v,
        up_v,
        down_v,
        act_v,
        ggate_v,
        gup_v,
        in_v,
        term_v,
        got_v,
        gu_got,
        gu_last,
        down_got,
        down_last,
        send_sems,
        recv_sems,
        back_send,
        back_recv,
        load_sems,
        store_sems,
        part_send,
        part_recv,
    ) = refs
    place = Place(n_batch)
    far = place.h
    n_tok = rows_ref.shape[0]
    cut = n_tok // 2
    width = rows_ref.shape[1]
    ff = gate_ref.shape[-1]
    up_device, down_device = place.up(), place.down()
    far_device, near_device = (place.b, place.far), (place.b, place.near)
    barrier = greet(place, [up_device, down_device, far_device, near_device])
    parts = Copies(part_send, part_recv)
    own_rows = gate_v.shape[2]
    block = 4 * own_rows

    load_rows = pltpu.make_async_copy(rows_ref, rows_v.at[0, pl.ds(0, n_tok)], load_sems.at[0])
    load_rows.start()
    loads = [
        pltpu.make_async_copy(source, target, load_sems.at[1 + i])
        for i, (source, target) in enumerate(
            [(gate_ref, gate_v), (up_ref, up_v), (down_ref, down_v)]
        )
    ]
    spots = [(0, 0, 0), (far, 0, 1)]
    spots += [(side * step, step, (side + 1) // 2) for step in range(1, far) for side in (-1, 1)]
    for i, (distance, group, side) in enumerate(spots):
        loads.append(
            pltpu.make_async_copy(
                cot_ref.at[place.rank_of(distance)], cot_v.at[group, pl.ds(side * n_tok, n_tok)], load_sems.at[4 + i]
            )
        )
    for copy in loads:
        copy.start()
    load_rows.wait()
    pl.semaphore_wait(barrier, 4)

    def piece(side, half):
        return pl.ds(side * n_tok + half * cut, cut)

    def hop(step, side, half):
        source_group, source_side = step - 1, side
        target_group, target_side = step, side
        if isinstance(step, int) and step == 1:
            source_side = 0
        if isinstance(step, int) and step == far:
            target_group, target_side = 0, 1
        return pltpu.make_async_remote_copy(
            src_ref=rows_v.at[source_group, piece(source_side, half)],
            dst_ref=rows_v.at[target_group, piece(target_side, half)],
            send_sem=send_sems.at[step, side, half],
            recv_sem=recv_sems.at[step, side, half],
            device_id=down_device if side else up_device,
            device_id_type=MESH,
        )

    both = [(side, half) for half in (0, 1) for side in (0, 1)]
    ends = [(0, 0), (1, 1)]
    for side, half in both:
        hop(1, side, half).start()
    for copy in loads:
        copy.wait()

    def stores(group):
        return [
            pltpu.make_async_copy(term_v.at[group], term_out.at[group], store_sems.at[0, group])
        ]

    def compute(group):
        rows = rows_v[group]
        cots = cot_v[group]
        down_all = down_v[...].reshape(ff, width)
        start = 0
        while start < ff:
            size = min(256, ff - start)
            tile = slice(start, start + size)
            gate = dot(rows, gate_v[..., tile].reshape(width, size))
            up = dot(rows, up_v[..., tile].reshape(width, size))
            grad_act = dot_right_t(cots, down_all[tile])
            sigmoid = 1.0 / (1.0 + jnp.exp(-gate))
            silu = gate * sigmoid
            act_v[group, :, tile] = (silu * up).astype(BF)
            slope = sigmoid * (1.0 + gate * (1.0 - sigmoid))
            ggate_v[group, :, tile] = (grad_act * up * slope).astype(BF)
            gup_v[group, :, tile] = (grad_act * silu).astype(BF)
            start += size
        ggate = ggate_v[group]
        gup = gup_v[group]
        act = act_v[group]
        tile_cols = 2 * block

        @pl.loop(0, width // tile_cols)
        def _(t):
            cols = pl.ds(pl.multiple_of(t * tile_cols, tile_cols), tile_cols)
            back = dot_right_t(ggate, gate_v[pl.ds(2 * t, 2)].reshape(tile_cols, ff))
            back += dot_right_t(gup, up_v[pl.ds(2 * t, 2)].reshape(tile_cols, ff))
            in_v[group, :, cols] = back.astype(BF)
            down = down_v[:, :, cols].reshape(ff, tile_cols)
            term_v[group, :, cols] = dot(act, down).astype(BF)

        for copy in stores(group):
            copy.start()

    @pl.loop(1, far)
    def _(step):
        for side, half in both:
            hop(step, side, half).wait_recv()

        @pl.when(step < far - 1)
        def _():
            for side, half in both:
                hop(step + 1, side, half).start()

        @pl.when(step == far - 1)
        def _():
            for side, half in ends:
                hop(far, side, half).start()

        compute(step)

    for side, half in ends:
        hop(far, side, half).wait_recv()
    compute(0)

    def back_hop(step, side, half, source):
        return pltpu.make_async_remote_copy(
            src_ref=source,
            dst_ref=got_v.at[step, side, half],
            send_sem=back_send.at[step, side, half],
            recv_sem=back_recv.at[step, side, half],
            device_id=up_device if side else down_device,
            device_id_type=MESH,
        )

    def held(step, side, half):
        return in_v.at[step, piece(side, half)]

    for side, half in ends:
        back_hop(far - 1, side, half, held(0, 1, half)).start()

    def pass_on(step, side, half, added):
        own = held(step, side, half)
        if added:
            back_hop(step, side, half, own).wait_recv()
            own[...] = (own[...].astype(F32) + got_v[step, side, half].astype(F32)).astype(BF)
        back_hop(step - 1, side, half, own).start()

    for side, half in both:
        if (side, half) not in ends:
            pass_on(far - 1, side, half, False)

    def gate_up_terms(first, last):
        @pl.loop(first, last)
        def _(t):
            cols = pl.ds(pl.multiple_of(t * 2 * block, 2 * block), 2 * block)
            rows = rows_v[:, :, cols].reshape(n_batch * n_tok, 2 * block)
            for target, grads in ((gate_v, ggate_v), (up_v, gup_v)):
                term = dot_left_t(rows, grads[...].reshape(n_batch * n_tok, ff))
                target[pl.ds(2 * t, 2)] = term.astype(BF).reshape(2, 4, own_rows, ff)

    def down_terms():
        @pl.loop(0, width // (2 * block))
        def _(t):
            cols = pl.ds(pl.multiple_of(t * 2 * block, 2 * block), 2 * block)
            grads = cot_v[:, :, cols].reshape(n_batch * n_tok, 2 * block)
            term = dot_left_t(act_v[...].reshape(n_batch * n_tok, ff), grads)
            down_v[:, :, cols] = term.astype(BF).reshape(4, ff // 4, 2 * block)

    def pass_all(step):
        for side, half in [(1, 0), (0, 1), (0, 0), (1, 1)]:
            if step < far - 1 or (side, half) in ends:
                pass_on(step, side, half, True)

    steps = iter(range(far - 1, 0, -1))
    tiles = width // (2 * block)
    outer, inner = place.outer, place.inner

    gate_up_terms(0, tiles // 2)
    pass_all(next(steps))
    gate_up_terms(tiles // 2, tiles)
    near_copies = [
        parts.remote(
            target.at[:, 2 * side + 1 - inner], gu_got.at[kind, side], near_device
        )
        for side in (0, 1)
        for kind, target in enumerate((gate_v, up_v))
    ]
    for step in steps:
        pass_all(step)
        if step > 1:
            down_terms()
    down_copies = [
        parts.remote(down_v.at[2 * side + 1 - inner], down_got.at[side], near_device)
        for side in (0, 1)
    ]
    for copy in near_copies:
        parts.arrive(copy)
    far_copies = []
    for kind, target in enumerate((gate_v, up_v)):
        for side in (1 - outer, outer):
            kept = target.at[:, 2 * side + inner]
            kept[...] = (kept[...].astype(F32) + gu_got[kind, side].astype(F32)).astype(BF)
            if side is not outer:
                far_copies.append(parts.remote(kept, gu_last.at[kind], far_device))
    for copy in down_copies:
        parts.arrive(copy)
    other = down_v.at[2 * (1 - outer) + inner]
    other[...] = (other[...].astype(F32) + down_got[1 - outer].astype(F32)).astype(BF)
    down_far = parts.remote(other, down_last, far_device)
    for half in (0, 1):
        for side in (0, 1):
            back_hop(0, side, half, held(0, 0, half)).wait_recv()
        rows = slice(half * cut, (half + 1) * cut)
        sum_ref[rows, :] = (
            in_v[0, rows, :].astype(F32)
            + got_v[0, 0, half].astype(F32)
            + got_v[0, 1, half].astype(F32)
        )
    for kind, target in enumerate((gate_v, up_v)):
        parts.arrive(far_copies[kind])
        kept = target.at[:, 2 * outer + inner]
        kept[...] = (kept[...].astype(F32) + gu_last[kind].astype(F32)).astype(BF)
        parts.local(kept, gu_out.at[:, kind])
    parts.arrive(down_far)
    down_grad[...] = (
        down_v[2 * outer + inner].astype(F32)
        + down_got[outer].astype(F32)
        + down_last[...].astype(F32)
    )
    parts.drain()

    for step in range(1, far + 1):
        for side, half in both if step < far else ends:
            hop(step, side, half).wait_send()
    for side, half in ends:
        back_hop(far - 1, side, half, held(0, 1, half)).wait_send()
    for step in range(far - 1, 0, -1):
        for side, half in both:
            back_hop(step - 1, side, half, held(step, side, half)).wait_send()
    for group in range(far):
        for copy in stores(group):
            copy.wait()


def fused_mlp(n_batch, rows, cots, own_gate, own_up, own_down):
    n_tok, width = rows.shape
    ff = own_gate.shape[-1]
    own_rows = own_gate.shape[2]
    far = n_batch // 2
    pair = 2 * n_tok
    flops = 18 * n_batch * n_tok * width * ff
    return pl.pallas_call(
        functools.partial(mlp_kernel, n_batch),
        out_shape=(
            jax.ShapeDtypeStruct((n_tok, width), F32),
            jax.ShapeDtypeStruct((ff // 4, width), F32),
            jax.ShapeDtypeStruct((far, pair, width), BF),
            jax.ShapeDtypeStruct((n_batch, 2, own_rows, ff), BF),
        ),
        in_specs=[pl.BlockSpec(memory_space=pl.ANY)] * 5,
        out_specs=[pl.BlockSpec(memory_space=pltpu.VMEM)] * 2
        + [pl.BlockSpec(memory_space=pl.ANY)] * 2,
        scratch_shapes=[
            pltpu.VMEM((far, pair, width), BF),
            pltpu.VMEM((far, pair, width), BF),
            pltpu.VMEM((n_batch, 4, own_rows, ff), BF),
            pltpu.VMEM((n_batch, 4, own_rows, ff), BF),
            pltpu.VMEM((4, ff // 4, width), BF),
            pltpu.VMEM((far, pair, ff), BF),
            pltpu.VMEM((far, pair, ff), BF),
            pltpu.VMEM((far, pair, ff), BF),
            pltpu.VMEM((far, pair, width), BF),
            pltpu.VMEM((far, pair, width), BF),
            pltpu.VMEM((far, 2, 2, n_tok // 2, width), BF),
            pltpu.VMEM((2, 2, n_batch, own_rows, ff), BF),
            pltpu.VMEM((2, n_batch, own_rows, ff), BF),
            pltpu.VMEM((2, ff // 4, width), BF),
            pltpu.VMEM((ff // 4, width), BF),
            pltpu.SemaphoreType.DMA((far + 1, 2, 2)),
            pltpu.SemaphoreType.DMA((far + 1, 2, 2)),
            pltpu.SemaphoreType.DMA((far, 2, 2)),
            pltpu.SemaphoreType.DMA((far, 2, 2)),
            pltpu.SemaphoreType.DMA((4 + n_batch,)),
            pltpu.SemaphoreType.DMA((1, far)),
            pltpu.SemaphoreType.DMA((16,)),
            pltpu.SemaphoreType.DMA((16,)),
        ],
        compiler_params=pltpu.CompilerParams(
            collective_id=1, has_side_effects=True, vmem_limit_bytes=60 * 1024 * 1024
        ),
        cost_estimate=pl.CostEstimate(
            flops=flops, bytes_accessed=24 * 1024 * 1024, transcendentals=n_batch * n_tok * ff
        ),
        name="fused_mlp",
    )(rows, own_gate, own_up, own_down, cots)


class RingCollect:
    def __init__(self, place, block, got, send_sems, recv_sems):
        self.place, self.block, self.got = place, block, got
        self.send_sems, self.recv_sems = send_sems, recv_sems
        self.cut = got.shape[3]
        self.step = place.h
        self.sent = []

    def held(self, step, half):
        return self.block(step).at[pl.ds(half * self.cut, self.cut)]

    def hop(self, step, side, half, source):
        place = self.place
        return pltpu.make_async_remote_copy(
            src_ref=source,
            dst_ref=self.got.at[step, side, half],
            send_sem=self.send_sems.at[step, side, half],
            recv_sem=self.recv_sems.at[step, side, half],
            device_id=place.up() if side else place.down(),
            device_id_type=MESH,
        )

    def send(self, step, side, half, source):
        copy = self.hop(step, side, half, source)
        copy.start()
        self.sent.append(copy)

    def advance(self):
        far = self.place.h
        step = self.step
        self.step -= 1
        if step == far:
            for side in (0, 1):
                self.send(far - 1, side, side, self.held(far, side))
            for side in (0, 1):
                half = 1 - side
                self.send(far - 2, side, half, self.held((2 * side - 1) * (far - 1), half))
            return
        pieces = [(0, 0), (1, 1)] if step == far - 1 else [(1, 0), (0, 1), (0, 0), (1, 1)]
        for side, half in pieces:
            own = self.held((2 * side - 1) * step, half)
            self.hop(step, side, half, own).wait_recv()
            own[...] = (own[...].astype(F32) + self.got[step, side, half].astype(F32)).astype(BF)
            self.send(step - 1, side, half, own)

    def finish(self, half):
        own = self.held(0, half)
        for side in (0, 1):
            self.hop(0, side, half, own).wait_recv()
        return (
            own[...].astype(F32)
            + self.got[0, 0, half].astype(F32)
            + self.got[0, 1, half].astype(F32)
        )

    def drain(self):
        for copy in self.sent:
            copy.wait_send()


def tail_kernel(
    n_batch,
    gain_rows,
    out_ref,
    up_ref,
    project_ref,
    rows_ref,
    gain_ref,
    out_grad,
    up_grad,
    in_grad,
    gain_grad,
    out_v,
    up_v,
    in_v,
    out_got,
    up_got,
    in_got,
    out_sum,
    out_all,
    up_sum,
    up_all,
    in_sum,
    in_all,
    ring_send,
    ring_recv,
    send_sems,
    recv_sems,
    project_v,
    rows_v,
    load_sems,
    out_sems,
):
    place = Place(n_batch)
    copies = Copies(send_sems, recv_sems)
    b, c, n = place.b, place.c, n_batch
    own_rows = in_grad.shape[0]
    index = b * 4 + c
    slab = c * n + b
    target = (lax.div(slab, 4), lax.rem(slab, 4))
    source = (lax.rem(index, n), lax.div(index, n))
    stays = slab == index
    ctx_peers = [(b, place.far), (b, place.near), (b, lax.rem(place.near + 2, 4))]

    loads = [
        pltpu.make_async_copy(held, kept, load_sems.at[i])
        for i, (held, kept) in enumerate([(out_ref, out_v), (up_ref, up_v), (rows_ref, rows_v)])
    ]
    for copy in loads:
        copy.start()
    barrier = greet(place, [place.up(), place.down()] + ctx_peers)

    @pl.when(jnp.logical_not(stays))
    def _():
        for device in (target, source):
            pl.semaphore_signal(barrier, inc=1, device_id=device, device_id_type=MESH)

    pl.semaphore_wait(barrier, 7 - 2 * stays.astype(jnp.int32))

    rings = []
    for i, (kept, got) in enumerate([(out_v, out_got), (up_v, up_got), (in_v, in_got)]):
        rings.append(
            RingCollect(
                place,
                lambda step, kept=kept: kept.at[place.rank_of(step)],
                got,
                ring_send.at[i],
                ring_recv.at[i],
            )
        )
    part_cols = project_ref.shape[2]
    project_copies = [
        copies.remote(project_ref.at[peer[1]], project_v.at[c], peer) for peer in ctx_peers
    ]
    project_copies.append(copies.local(project_ref.at[c], project_v.at[c]))
    for copy, ring in zip(loads[:2], rings):
        copy.wait()
        ring.advance()
    for copy in project_copies:
        copies.arrive(copy)
    loads[2].wait()
    project = project_v[...].reshape(-1, part_cols)
    part_rows = own_rows + 16
    n_all = project.shape[0]
    width = rows_ref.shape[3]
    ahead = max(1, 256 // (4 * own_rows))
    chunk = ahead * 4 * own_rows

    @pl.loop(0, width // chunk)
    def _(t):
        cols = pl.ds(pl.multiple_of(t * chunk, chunk), chunk)
        term = dot_left_t(rows_v[:, :, :, cols].reshape(n_all, chunk), project).astype(BF)
        term = term.reshape(ahead, 4, own_rows, part_cols)
        for part in range(4):
            in_v[pl.ds(t * ahead, ahead), pl.ds(part * part_rows, own_rows), :] = term[:, part]

    for part in range(4):
        in_v[:, part * part_rows + own_rows : (part + 1) * part_rows, :] = gain_ref[:, part]
    rings[2].advance()
    for _ in range(place.h - 1):
        for ring in rings:
            ring.advance()

    in_ring, up_ring, out_ring = rings[2], rings[1], rings[0]
    out_cut, up_cut, in_cut = out_ring.cut, up_ring.cut, in_ring.cut
    for half in (0, 1):
        out_sum[pl.ds(half * out_cut, out_cut), :] = out_ring.finish(half).astype(BF)
    out_copy = pltpu.make_async_remote_copy(
        src_ref=out_sum,
        dst_ref=out_all,
        send_sem=out_sems.at[0],
        recv_sem=out_sems.at[1],
        device_id=target,
        device_id_type=MESH,
    )
    out_stay = pltpu.make_async_copy(out_sum, out_all, out_sems.at[0])

    @pl.when(jnp.logical_not(stays))
    def _():
        out_copy.start()

    @pl.when(stays)
    def _():
        out_stay.start()

    for half in (0, 1):
        up_sum[pl.ds(half * up_cut, up_cut), :] = up_ring.finish(half).astype(BF)
    up_copies = [
        copies.remote(
            up_sum.at[pl.ds(peer[1] * gain_rows, gain_rows)], up_all.at[c], peer
        )
        for peer in ctx_peers
    ]
    up_copies.append(
        copies.local(up_sum.at[pl.ds(c * gain_rows, gain_rows)], up_all.at[c])
    )
    for half in (0, 1):
        in_sum[pl.ds(half * in_cut, in_cut), :] = in_ring.finish(half).astype(BF)
    in_copies = [
        copies.remote(in_sum.at[pl.ds(peer[1] * part_rows, part_rows)], in_all.at[c], peer)
        for peer in ctx_peers
    ]
    in_copies.append(copies.local(in_sum.at[pl.ds(c * part_rows, part_rows)], in_all.at[c]))

    @pl.when(jnp.logical_not(stays))
    def _():
        out_copy.wait()

    @pl.when(stays)
    def _():
        out_stay.wait()

    out_grad[...] = out_all[...].astype(F32)
    for copy in up_copies:
        copies.arrive(copy)
    cols = up_all.shape[2]
    for part in range(4):
        up_grad[:, part * cols : (part + 1) * cols] = up_all[part].astype(F32)
    for copy in in_copies:
        copies.arrive(copy)
    cols = in_all.shape[2]
    gains = jnp.zeros(gain_grad.shape, F32)
    for part in range(4):
        in_grad[:, part * cols : (part + 1) * cols] = in_all[part, :own_rows, :].astype(F32)
        gains = gains + in_all[part, own_rows:, :].astype(F32)
    gain_grad[...] = gains
    copies.drain()
    for ring in rings:
        ring.drain()


def collect_weights(n_batch, gain_rows, out_terms, up_terms, project, attn_in_all, gain_terms):
    far = n_batch // 2
    out_rows, width = out_terms.shape[1:]
    up_rows, up_cols = up_terms.shape[1:]
    in_cols = project.shape[2]
    own_rows = width // (4 * n_batch)
    in_rows = 4 * (own_rows + 16)
    shapes = [out_terms.shape[1:], up_terms.shape[1:], (in_rows, in_cols)]
    sems = 2 * n_batch + 16
    return pl.pallas_call(
        functools.partial(tail_kernel, n_batch, gain_rows),
        out_shape=(
            jax.ShapeDtypeStruct((out_rows, width), F32),
            jax.ShapeDtypeStruct((gain_rows, 4 * up_cols), F32),
            jax.ShapeDtypeStruct((own_rows, 4 * in_cols), F32),
            jax.ShapeDtypeStruct((16, in_cols), F32),
        ),
        in_specs=[pl.BlockSpec(memory_space=pl.ANY)] * 4 + [pl.BlockSpec(memory_space=pltpu.VMEM)],
        out_specs=[pl.BlockSpec(memory_space=pltpu.VMEM)] * 4,
        scratch_shapes=[pltpu.VMEM((n_batch,) + shape, BF) for shape in shapes]
        + [pltpu.VMEM((far, 2, 2, rows // 2, cols), BF) for rows, cols in shapes]
        + [
            pltpu.VMEM((out_rows, width), BF),
            pltpu.VMEM((out_rows, width), BF),
            pltpu.VMEM((up_rows, up_cols), BF),
            pltpu.VMEM((4, gain_rows, up_cols), BF),
            pltpu.VMEM((in_rows, in_cols), BF),
            pltpu.VMEM((4, own_rows + 16, in_cols), BF),
            pltpu.SemaphoreType.DMA((3, far, 2, 2)),
            pltpu.SemaphoreType.DMA((3, far, 2, 2)),
            pltpu.SemaphoreType.DMA((sems,)),
            pltpu.SemaphoreType.DMA((sems,)),
            pltpu.VMEM(project.shape, BF),
            pltpu.VMEM(attn_in_all.shape, BF),
            pltpu.SemaphoreType.DMA((3,)),
            pltpu.SemaphoreType.DMA((2,)),
        ],
        compiler_params=pltpu.CompilerParams(
            collective_id=2, has_side_effects=True, vmem_limit_bytes=48 * 1024 * 1024
        ),
        name="collect_weights",
    )(out_terms, up_terms, project, attn_in_all, gain_terms)


class CtxCollect:
    def __init__(self, place, copies, part, near_got, far_got):
        self.place, self.copies, self.part = place, copies, part
        self.near_got, self.far_got = near_got, far_got
        self.near = {}
        self.far = {}

    def start(self, item):
        place = self.place
        self.near[item] = [
            self.copies.remote(
                self.part.at[2 * side + 1 - place.inner, item],
                self.near_got.at[side, item],
                (place.b, place.near),
            )
            for side in (0, 1)
        ]

    def cross(self, item):
        place = self.place
        for copy in self.near[item]:
            self.copies.arrive(copy)
        other = self.part.at[2 * (1 - place.outer) + place.inner, item]
        added = other[...].astype(F32) + self.near_got[1 - place.outer, item].astype(F32)
        other[...] = added.astype(BF)
        self.far[item] = self.copies.remote(
            other, self.far_got.at[item], (place.b, place.far)
        )

    def finish(self, item):
        place = self.place
        self.copies.arrive(self.far[item])
        return (
            self.part[2 * place.outer + place.inner, item].astype(F32)
            + self.near_got[place.outer, item].astype(F32)
            + self.far_got[item].astype(F32)
        )


class CtxGather:
    def __init__(self, place, copies, everyone):
        self.place, self.copies, self.everyone = place, copies, everyone
        self.far = {}
        self.near = {}

    def start(self, item):
        place = self.place
        own = self.everyone.at[place.c, item]
        self.far[item] = self.copies.remote(own, own, (place.b, place.far))
        self.near[item] = [self.copies.remote(own, own, (place.b, place.near))]

    def cross(self, item):
        place = self.place
        self.copies.arrive(self.far[item])
        other = self.everyone.at[place.far, item]
        self.near[item].append(self.copies.remote(other, other, (place.b, place.near)))

    def finish(self, item):
        for copy in self.near[item]:
            self.copies.arrive(copy)


def greet_lines(place):
    devices = [place.up(), place.down(), (place.b, place.far), (place.b, place.near)]
    pl.semaphore_wait(greet(place, devices), 4)


def turn(values, cosine, sine):
    half_size = HD // 2
    front, back = values[:, :half_size], values[:, half_size:]
    return front * cosine - back * sine, back * cosine + front * sine


def softmax_rows(queries, keys, keep, score_scale):
    scores = dot_right_t(queries, keys) * score_scale
    rows = lax.broadcasted_iota(jnp.int32, scores.shape, 0)
    cols = lax.broadcasted_iota(jnp.int32, scores.shape, 1)
    masked = jnp.where((cols <= rows) & (keep > 0.5), scores, -1e30)
    raised = jnp.exp(masked - jnp.max(masked, axis=-1, keepdims=True))
    return raised / jnp.sum(raised, axis=-1, keepdims=True)


def attention_kernel(
    n_batch,
    heads,
    qkv_ref,
    rows_ref,
    cot_ref,
    up_ref,
    out_ref,
    cos_ref,
    sin_ref,
    keep_ref,
    attended,
    qkv_out,
    turned_out,
    mixed_out,
    rows_all,
    cot_all,
    qkv_v,
    up_v,
    out_v,
    turned_v,
    mixed_v,
    part_v,
    near_got,
    far_got,
    send_sems,
    recv_sems,
    load_sems,
):
    place = Place(n_batch)
    copies = Copies(send_sems, recv_sems)
    b, c = place.b, place.c
    micro, pos_dev = qkv_ref.shape[:2]
    n_tok = micro * pos_dev
    length = 4 * pos_dev
    score_scale = 1.0 / math.sqrt(HD)
    loads = [
        pltpu.make_async_copy(source, target, load_sems.at[i])
        for i, (source, target) in enumerate(
            [(qkv_ref, qkv_v.at[c]), (up_ref, up_v), (out_ref, out_v)]
        )
    ]
    for copy in loads:
        copy.start()
    greet_lines(place)
    loads[0].wait()
    qkv = CtxGather(place, copies, qkv_v)
    for item in range(micro):
        qkv.start(item)
    cot_own = copies.local(cot_ref, cot_all.at[b])
    rows_own = copies.local(rows_ref, rows_all.at[c, 0])
    copies.arrive(cot_own)
    cots = RingGather(place, copies, n_tok, lambda rank, rows: cot_all.at[rank, rows])
    cots.advance()
    copies.arrive(rows_own)
    rows = CtxGather(place, copies, rows_all)
    for item in range(micro):
        qkv.cross(item)
    rows.start(0)
    for copy in loads[1:]:
        copy.wait()
    attended_sum = CtxCollect(place, copies, part_v, near_got, far_got)
    cosine, sine = cos_ref[...], sin_ref[...]
    latent = qkv_v.shape[3] - 2 * HD
    for item in range(micro):
        qkv.finish(item)
        q_normed = qkv_v[:, item, :, :latent].reshape(length, latent)
        keys = qkv_v[:, item, :, latent : latent + HD].reshape(length, HD)
        values = qkv_v[:, item, :, latent + HD :].reshape(length, HD)
        keep = keep_ref[item]

        @pl.loop(0, heads)
        def _(head):
            cols = pl.ds(pl.multiple_of(head * HD, HD), HD)
            front, back = turn(dot(q_normed, up_v[:, cols]), cosine, sine)
            turned_v[item, :, pl.ds(pl.multiple_of(head * HD, HD), HD // 2)] = front.astype(BF)
            turned_v[item, :, pl.ds(pl.multiple_of(head * HD + HD // 2, HD // 2), HD // 2)] = (
                back.astype(BF)
            )
            weights = softmax_rows(turned_v[item, :, cols], keys, keep, score_scale)
            mixed = dot(weights.astype(BF), values).astype(BF)
            mixed_v[:, item, :, cols] = mixed.reshape(4, pos_dev, HD)

        if cots.step <= place.h:
            cots.advance()
        mixed = mixed_v[:, item].reshape(length, heads * HD)
        width = out_v.shape[1]

        @pl.loop(0, width // 512)
        def _(t):
            cols = pl.ds(pl.multiple_of(t * 512, 512), 512)
            part = dot(mixed, out_v[:, cols]).astype(BF)
            part_v[:, item, :, cols] = part.reshape(4, pos_dev, 512)

        attended_sum.start(item)
        if item > 0:
            attended_sum.cross(item - 1)
    copies.local(qkv_v, qkv_out)
    copies.local(turned_v, turned_out)
    copies.local(mixed_v, mixed_out)
    if cots.step <= place.h:
        cots.advance()
    attended_sum.cross(micro - 1)
    rows.cross(0)
    for item in range(micro):
        attended[item] = attended_sum.finish(item)
    while cots.step <= place.h:
        cots.advance()
    copies.drain()


def attention(n_batch, qkv, attn_in, grad_mo, own_qup, own_out, cos_all, sin_all, keep):
    micro, pos_dev, qkv_cols = qkv.shape
    n_tok, width = attn_in.shape
    latent, head_cols = own_qup.shape
    length = 4 * pos_dev
    sems = 2 * n_batch + 48
    anywhere = pl.BlockSpec(memory_space=pl.ANY)
    near = pl.BlockSpec(memory_space=pltpu.VMEM)
    return pl.pallas_call(
        functools.partial(attention_kernel, n_batch, head_cols // HD),
        out_shape=(
            jax.ShapeDtypeStruct((micro, pos_dev, width), F32),
            jax.ShapeDtypeStruct((4, micro, pos_dev, qkv_cols), BF),
            jax.ShapeDtypeStruct((micro, length, head_cols), BF),
            jax.ShapeDtypeStruct((4, micro, pos_dev, head_cols), BF),
            jax.ShapeDtypeStruct((4, 1, n_tok, width), BF),
            jax.ShapeDtypeStruct((n_batch, n_tok, width), BF),
        ),
        in_specs=[anywhere] * 5 + [near] * 3,
        out_specs=[near] + [anywhere] * 5,
        scratch_shapes=[
            pltpu.VMEM((4, micro, pos_dev, qkv_cols), BF),
            pltpu.VMEM((latent, head_cols), BF),
            pltpu.VMEM((head_cols, width), BF),
            pltpu.VMEM((micro, length, head_cols), BF),
            pltpu.VMEM((4, micro, pos_dev, head_cols), BF),
            pltpu.VMEM((4, micro, pos_dev, width), BF),
            pltpu.VMEM((2, micro, pos_dev, width), BF),
            pltpu.VMEM((micro, pos_dev, width), BF),
            pltpu.SemaphoreType.DMA((sems,)),
            pltpu.SemaphoreType.DMA((sems,)),
            pltpu.SemaphoreType.DMA((3,)),
        ],
        compiler_params=pltpu.CompilerParams(
            collective_id=3, has_side_effects=True, vmem_limit_bytes=40 * 1024 * 1024
        ),
        name="attention",
    )(qkv, attn_in, grad_mo, own_qup, own_out, cos_all, sin_all, keep)


def attention_back_kernel(
    n_batch,
    heads,
    has_terms,
    grad_ref,
    qkv_ref,
    turned_ref,
    mixed_ref,
    up_ref,
    out_ref,
    gu_ref,
    *refs,
):
    terms_ref, refs = (refs[0], refs[1:]) if has_terms else (None, refs)
    (
        cos_ref,
        sin_ref,
        keep_ref,
        back_out,
        out_terms,
        up_terms,
        gu_grad,
    ) = refs[:7]
    terms_sum, refs = (refs[7], refs[8:]) if has_terms else (None, refs[7:])
    (
        grad_v,
        qkv_v,
        turned_v,
        mixed_v,
        up_v,
        out_v,
        mixgrad_v,
        qgrad_v,
        kgrad_v,
        vgrad_v,
        part_v,
        near_got,
        far_got,
        outgrad_v,
        upgrad_v,
        send_sems,
        recv_sems,
        load_sems,
    ) = refs[:18]
    place = Place(n_batch)
    copies = Copies(send_sems, recv_sems)
    b, c, n = place.b, place.c, n_batch
    micro, pos_dev, width = grad_ref.shape
    length = 4 * pos_dev
    head_cols = heads * HD
    latent = qkv_ref.shape[3] - 2 * HD
    score_scale = 1.0 / math.sqrt(HD)
    pairs = [
        (grad_ref, grad_v.at[c]),
        (out_ref, out_v),
        (qkv_ref, qkv_v),
        (turned_ref, turned_v),
        (up_ref, up_v),
        (mixed_ref, mixed_v),
    ]
    if has_terms:
        terms_v, terms_got, ring_send, ring_recv = refs[18:]
        pairs.append((terms_ref, terms_v))
    loads = [
        pltpu.make_async_copy(source, target, load_sems.at[i])
        for i, (source, target) in enumerate(pairs)
    ]
    for copy in loads:
        copy.start()
    peers = [(lax.rem(b + k, n), c) for k in range(1, n)]
    others = peers + [(b, place.far), (b, place.near)]
    pl.semaphore_wait(greet(place, others), n + 1)
    loads[0].wait()
    grads = CtxGather(place, copies, grad_v)
    for item in range(micro):
        grads.start(item)
    steps = []
    if has_terms:

        def spot(step):
            return 0 if step == 0 else 1 if step == place.h else 2 * abs(step) + (step > 0)

        terms = RingCollect(
            place, lambda step: terms_v.at[spot(step)], terms_got, ring_send, ring_recv
        )
        loads[6].wait()
        steps = [terms.advance] * place.h

    def ring_step():
        if steps:
            steps.pop()()

    ring_step()
    copies.local(gu_ref.at[b], gu_grad.at[b])
    for peer in peers:
        copies.remote(gu_ref.at[peer[0]], gu_grad.at[b], peer)
    for item in range(micro):
        grads.cross(item)
    for copy in loads[1:6]:
        copy.wait()
    back_sum = CtxCollect(place, copies, part_v, near_got, far_got)
    cosine, sine = cos_ref[...], sin_ref[...]
    for item in range(micro):
        grads.finish(item)
        incoming = grad_v[:, item].reshape(length, width)
        keys = qkv_v[:, item, :, latent : latent + HD].reshape(length, HD)
        values = qkv_v[:, item, :, latent + HD :].reshape(length, HD)
        keep = keep_ref[item]
        kgrad_v[...] = jnp.zeros_like(kgrad_v)
        vgrad_v[...] = jnp.zeros_like(vgrad_v)

        @pl.loop(0, heads)
        def _(head):
            cols = pl.ds(pl.multiple_of(head * HD, HD), HD)
            grad_mixed = dot_right_t(incoming, out_v[cols, :]).astype(BF)
            queries = turned_v[item, :, cols]
            weights = softmax_rows(queries, keys, keep, score_scale)
            grad_probs = dot_right_t(grad_mixed, values)
            row_dot = jnp.sum(weights * grad_probs, axis=-1, keepdims=True)
            grad_scores = (weights * (grad_probs - row_dot)).astype(BF)
            front, back = turn(dot(grad_scores, keys) * score_scale, cosine, -sine)
            front, back = front.astype(BF), back.astype(BF)
            base = pl.multiple_of(head * HD, HD)
            qgrad_v[:, item, :, pl.ds(base, HD // 2)] = front.reshape(4, pos_dev, HD // 2)
            base = pl.multiple_of(head * HD + HD // 2, HD // 2)
            qgrad_v[:, item, :, pl.ds(base, HD // 2)] = back.reshape(4, pos_dev, HD // 2)
            kgrad_v[...] += dot_left_t(grad_scores, queries) * score_scale
            vgrad_v[...] += dot_left_t(weights.astype(BF), grad_mixed)

        ring_step()
        qgrad = qgrad_v[:, item].reshape(length, head_cols)
        part_v[:, item, :, :latent] = (
            dot_right_t(qgrad, up_v[...]).astype(BF).reshape(4, pos_dev, latent)
        )
        part_v[:, item, :, latent : latent + HD] = (
            kgrad_v[...].astype(BF).reshape(4, pos_dev, HD)
        )
        part_v[:, item, :, latent + HD :] = vgrad_v[...].astype(BF).reshape(4, pos_dev, HD)
        back_sum.start(item)
        if item > 0:
            back_sum.cross(item - 1)
    n_all = 4 * micro * pos_dev
    out_rows = head_cols // n

    back_sum.cross(micro - 1)
    ring_step()

    @pl.loop(0, width // 512)
    def _(t):
        cols = pl.ds(pl.multiple_of(t * 512, 512), 512)
        term = dot_left_t(
            mixed_v[...].reshape(n_all, head_cols), grad_v[:, :, :, cols].reshape(n_all, 512)
        )
        outgrad_v[:, :, cols] = term.astype(BF).reshape(n, out_rows, 512)

    copies.local(outgrad_v, out_terms)
    for item in range(micro):
        back_out[item] = back_sum.finish(item)
    ring_step()

    @pl.loop(0, head_cols // HD)
    def _(t):
        cols = pl.ds(pl.multiple_of(t * HD, HD), HD)
        term = dot_left_t(
            qkv_v[:, :, :, :latent].reshape(n_all, latent),
            qgrad_v[:, :, :, cols].reshape(n_all, HD),
        )
        upgrad_v[:, :, cols] = term.astype(BF).reshape(n, latent // n, HD)

    copies.local(upgrad_v, up_terms)
    if has_terms:
        while steps:
            ring_step()
        cut = terms.cut
        for half in (0, 1):
            terms_sum[half * cut : (half + 1) * cut, :] = terms.finish(half)
        terms.drain()
    copies.drain()


def attention_back(
    n_batch, grad_att, qkv_all, turned, mixed, own_qup, own_out, grad_gu, terms, tables
):
    micro, pos_dev, width = grad_att.shape
    n_tok = micro * pos_dev
    qkv_cols = qkv_all.shape[3]
    latent, head_cols = own_qup.shape
    length = 4 * pos_dev
    far = n_batch // 2
    has_terms = terms is not None
    sems = 2 * n_batch + 48
    anywhere = pl.BlockSpec(memory_space=pl.ANY)
    near = pl.BlockSpec(memory_space=pltpu.VMEM)
    out_shape = [
        jax.ShapeDtypeStruct((micro, pos_dev, qkv_cols), F32),
        jax.ShapeDtypeStruct((n_batch, head_cols // n_batch, width), BF),
        jax.ShapeDtypeStruct((n_batch, latent // n_batch, head_cols), BF),
        jax.ShapeDtypeStruct(grad_gu.shape, BF),
    ]
    out_specs = [near] + [anywhere] * 3
    scratch = [
        pltpu.VMEM((4, micro, pos_dev, width), BF),
        pltpu.VMEM((4, micro, pos_dev, qkv_cols), BF),
        pltpu.VMEM((micro, length, head_cols), BF),
        pltpu.VMEM((4, micro, pos_dev, head_cols), BF),
        pltpu.VMEM((latent, head_cols), BF),
        pltpu.VMEM((head_cols, width), BF),
        pltpu.VMEM((8, 128), BF),
        pltpu.VMEM((4, micro, pos_dev, head_cols), BF),
        pltpu.VMEM((length, HD), F32),
        pltpu.VMEM((length, HD), F32),
        pltpu.VMEM((4, micro, pos_dev, qkv_cols), BF),
        pltpu.VMEM((2, micro, pos_dev, qkv_cols), BF),
        pltpu.VMEM((micro, pos_dev, qkv_cols), BF),
        pltpu.VMEM((n_batch, head_cols // n_batch, width), BF),
        pltpu.VMEM((n_batch, latent // n_batch, head_cols), BF),
        pltpu.SemaphoreType.DMA((sems,)),
        pltpu.SemaphoreType.DMA((sems,)),
        pltpu.SemaphoreType.DMA((7,)),
    ]
    args = [grad_att, qkv_all, turned, mixed, own_qup, own_out, grad_gu]
    if has_terms:
        args.append(terms)
        out_shape.append(jax.ShapeDtypeStruct((n_tok, width), F32))
        out_specs.append(near)
        scratch += [
            pltpu.VMEM(terms.shape, BF),
            pltpu.VMEM((far, 2, 2, n_tok // 2, width), BF),
            pltpu.SemaphoreType.DMA((far, 2, 2)),
            pltpu.SemaphoreType.DMA((far, 2, 2)),
        ]
    return pl.pallas_call(
        functools.partial(attention_back_kernel, n_batch, head_cols // HD, has_terms),
        out_shape=tuple(out_shape),
        in_specs=[anywhere] * len(args) + [near] * 3,
        out_specs=out_specs,
        scratch_shapes=scratch,
        compiler_params=pltpu.CompilerParams(
            collective_id=4, has_side_effects=True, vmem_limit_bytes=56 * 1024 * 1024
        ),
        name="attention_back",
    )(*args, *tables)


def permuted_mlp(ring, rows_own, cots, gu_rows, own_down):
    mlp_in = ring.spread(rows_own)
    n_tok, width = rows_own.shape
    _, n_batch, n_ctx, own_rows, ff = gu_rows.shape
    own_gate, own_up = gu_rows.reshape(2, width, ff)
    own_down = own_down.reshape(ff, width)
    far = ring.h
    groups = [[0]] + [[-step, step] for step in range(1, far)] + [[far]]
    out_terms = {}
    in_terms = {}
    kept = []
    for group in groups:
        rows = jnp.concatenate([mlp_in[step] for step in group], axis=0)
        grad_rows = jnp.concatenate([pick(cots, ring.rank_of(step)) for step in group], axis=0)
        gate_part = dot(rows, own_gate)
        up_part = dot(rows, own_up)
        sigmoid_gate = jax.nn.sigmoid(gate_part)
        silu_gate = gate_part * sigmoid_gate
        activated = (silu_gate * up_part).astype(BF)
        grad_act = dot_right_t(grad_rows, own_down)
        grad_gate = (
            grad_act * up_part * (sigmoid_gate * (1.0 + gate_part * (1.0 - sigmoid_gate)))
        ).astype(BF)
        grad_up = (grad_act * silu_gate).astype(BF)
        in_term = dot_right_t(grad_gate, own_gate) + dot_right_t(grad_up, own_up)
        out_term = dot(activated, own_down)
        for place_in, step in enumerate(group):
            cut = slice(place_in * n_tok, (place_in + 1) * n_tok)
            in_terms[step] = in_term[cut]
            out_terms[step] = out_term[cut]
        kept.append((rows, grad_rows, activated, grad_gate, grad_up))
    rows, grad_rows, activated, grad_gate, grad_up = (
        jnp.concatenate(items, axis=0) for items in zip(*kept)
    )
    grad_gu = jnp.stack([dot_left_t(rows, grad_gate), dot_left_t(rows, grad_up)])
    grad_gu = grad_gu.reshape(2, n_batch, n_ctx, own_rows, ff).transpose(2, 1, 0, 3, 4)
    grad_down = dot_left_t(activated, grad_rows)
    return (
        ring.collect(lambda step: in_terms[step]),
        ctx_collect(grad_down.reshape(n_ctx, ff // n_ctx, width)),
        out_terms,
        ctx_collect(grad_gu).astype(BF),
    )


def shards(
    tokens,
    cotangent,
    lengths,
    slot_sequence,
    proj_in,
    query_up,
    proj_out,
    attn_gain,
    query_gain,
    mlp_gain,
    gate_up,
    down_proj,
):
    n_ctx = lax.axis_size("ctx")
    n_batch = lax.axis_size("batch")
    ctx_rank = lax.axis_index("ctx")
    batch_rank = lax.axis_index("batch")
    ring = Ring()
    micro, pos_dev, width = tokens.shape
    n_tok = micro * pos_dev
    full_length = pos_dev * n_ctx
    heads = H // n_ctx
    score_scale = 1.0 / math.sqrt(HD)
    in_cols = proj_in.shape[1]

    slot_total = lengths.shape[0]
    slot_ids = jnp.arange(slot_total, dtype=jnp.int32)
    seq_lengths = jnp.sum(
        jnp.where(slot_sequence[:, None] == slot_ids[None, :], lengths[None, :], 0), axis=1
    )
    own_lengths = lax.dynamic_slice_in_dim(seq_lengths, batch_rank * micro, micro)
    query_pos = ctx_rank * pos_dev + jnp.arange(pos_dev, dtype=jnp.int32)
    key_pos = jnp.arange(full_length, dtype=jnp.int32)
    cos_all, sin_all = rope_tables(key_pos)
    cos_own, sin_own = rope_tables(query_pos)

    own_rows = proj_in.shape[0]
    gain_rows = query_gain.shape[0]
    gains = jnp.stack(
        [attn_gain, mlp_gain, jnp.pad(query_gain, (0, own_rows - gain_rows))], axis=1
    )
    packed = jnp.concatenate([proj_in, jnp.pad(gains, ((0, 0), (0, 125)))], axis=1)
    up_parts = query_up.reshape(gain_rows, n_ctx, heads * HD).swapaxes(0, 1)
    ff_all = gate_up.shape[1] // 2
    ff = ff_all // n_batch
    gu_parts = gate_up.reshape(own_rows, 2, n_batch, ff).transpose(2, 1, 0, 3)
    packed, own_qup, own_out, gu_rows, own_down = spread_weights(
        n_batch, packed, up_parts, proj_out, gu_parts, down_proj
    )
    packed = packed.reshape(width, in_cols + 128)
    own_qup = own_qup.reshape(QR, heads * HD)
    own_out = own_out.reshape(heads * HD, width)
    full_in = packed[:, :in_cols]
    gains = packed[:, in_cols : in_cols + 3].T.astype(F32)
    gain_norm = gains[0]
    gain_mlp = gains[1]
    gain_query = gains[2].reshape(n_batch * n_ctx, own_rows)[:, :gain_rows].reshape(QR)

    residual = tokens.reshape(n_tok, width).astype(F32)
    valid_rows = (query_pos[None, :] < own_lengths[:, None]).astype(F32).reshape(n_tok, 1)
    grad_out = cotangent.reshape(n_tok, width).astype(F32) * valid_rows
    scale_one = rms_scale(residual)
    normed_one = residual * scale_one
    attn_in = (normed_one * gain_norm).astype(BF)
    projected = dot(attn_in, full_in)
    q_latent = projected[:, :QR]
    scale_query = rms_scale(q_latent)
    normed_query = q_latent * scale_query
    q_normed = (normed_query * gain_query).astype(BF)
    k_rot = rotate(
        projected[:, QR : QR + HD].reshape(micro, pos_dev, HD), cos_own, sin_own
    ).astype(BF)
    v_low = projected[:, QR + HD :].astype(BF)
    qkv = jnp.concatenate([q_normed, k_rot.reshape(n_tok, HD), v_low], axis=1)
    keep = (key_pos[None, None, :] < own_lengths[:, None, None]).astype(F32)
    attended, qkv_all, turned, mixed, attn_in_all, cots = attention(
        n_batch,
        qkv.reshape(micro, pos_dev, in_cols),
        attn_in,
        grad_out.astype(BF),
        own_qup,
        own_out,
        cos_all,
        sin_all,
        keep,
    )
    hidden_res = residual + attended.reshape(n_tok, width)

    scale_two = rms_scale(hidden_res)
    normed_two = hidden_res * scale_two
    mlp_in = (normed_two * gain_mlp).astype(BF)
    resident = 10 * n_batch * n_tok * width <= 24 * 1024 * 1024
    if resident:
        grad_mlp_in, grad_down, terms, grad_gu_own = fused_mlp(
            n_batch, mlp_in, cots, gu_rows[0], gu_rows[1], own_down
        )
        terms = terms.reshape(n_batch, n_tok, width)
    else:
        terms = None
        grad_mlp_in, grad_down, out_terms, grad_gu_own = permuted_mlp(
            ring, mlp_in, cots, gu_rows, own_down
        )
    gain_mlp_term = jnp.sum(grad_mlp_in * normed_two, axis=0)
    grad_hidden = grad_out + norm_back(grad_mlp_in * gain_mlp, normed_two, scale_two)
    back_own, out_grads, up_grads, grad_gu_own, *sums = attention_back(
        n_batch,
        grad_hidden.astype(BF).reshape(micro, pos_dev, width),
        qkv_all,
        turned,
        mixed,
        own_qup,
        own_out,
        grad_gu_own,
        terms,
        (cos_all, sin_all, keep),
    )
    out_sum = sums[0] if resident else ring.collect(lambda step: out_terms[step])
    layer_out = hidden_res + out_sum
    back_own = back_own.reshape(n_tok, in_cols)
    grad_qn = back_own[:, :QR]
    gain_query_term = jnp.sum(grad_qn * normed_query, axis=0)
    grad_latent = norm_back(grad_qn * gain_query, normed_query, scale_query)
    grad_key_raw = rotate_back(
        back_own[:, QR : QR + HD].reshape(micro, pos_dev, HD), cos_own, sin_own
    ).reshape(n_tok, HD)
    grad_project = jnp.concatenate(
        [grad_latent, grad_key_raw, back_own[:, QR + HD :]], axis=1
    ).astype(BF)
    grad_attn_in = dot_right_t(grad_project, full_in)
    gain_norm_term = jnp.sum(grad_attn_in * normed_one, axis=0)
    grad_tokens = grad_hidden + norm_back(grad_attn_in * gain_norm, normed_one, scale_one)

    part_cols = in_cols // n_ctx
    project_parts = grad_project.reshape(n_tok, n_ctx, part_cols).swapaxes(0, 1)
    gain_terms = jnp.stack(
        [
            gain_norm_term.reshape(n_batch, n_ctx, own_rows),
            gain_mlp_term.reshape(n_batch, n_ctx, own_rows),
            jnp.pad(
                gain_query_term.reshape(n_batch, n_ctx, gain_rows),
                ((0, 0), (0, 0), (0, own_rows - gain_rows)),
            ),
        ],
        axis=2,
    )
    gain_terms = jnp.pad(gain_terms, ((0, 0), (0, 0), (0, 13), (0, part_cols - own_rows)))
    grad_proj_out, grad_query_up, grad_proj_in, gain_sums = collect_weights(
        n_batch, gain_rows, out_grads, up_grads, project_parts, attn_in_all, gain_terms.astype(BF)
    )
    grad_gate_up = grad_gu_own.transpose(2, 1, 0, 3).reshape(own_rows, 2 * ff_all).astype(F32)
    gain_sums = gain_sums[:, :own_rows]

    return (
        layer_out.reshape(tokens.shape).astype(BF),
        grad_tokens.reshape(tokens.shape).astype(BF),
        grad_proj_in,
        grad_query_up,
        grad_proj_out,
        gain_sums[0],
        gain_sums[2, :gain_rows],
        gain_sums[1],
        grad_gate_up,
        grad_down,
    )


def solution(mesh):
    rows = P(("batch", "ctx"), None)
    vector = P(("batch", "ctx"))
    acts = P("batch", "ctx", None)
    return jax.shard_map(
        shards,
        mesh=mesh,
        in_specs=(acts, acts, P(), P(), rows, rows, rows, vector, vector, vector, rows, rows),
        out_specs=(acts, acts, rows, rows, rows, vector, vector, vector, rows, rows),
        check_vma=False,
    )
```

```python
import functools
import math

import jax
import jax.numpy as jnp
from jax import lax
from jax.experimental import pallas as pl
from jax.experimental.pallas import tpu as pltpu
from jax.sharding import PartitionSpec as P

H = 16
HD = 256
QR = 1024
EPSILON = 1e-06
BF = jnp.bfloat16
F32 = jnp.float32


def rms_scale(values):
    return lax.rsqrt(jnp.mean(values * values, axis=-1, keepdims=True) + EPSILON)


def rope_tables(positions):
    half_size = HD // 2
    frequency = 10000.0 ** (-(jnp.arange(half_size, dtype=F32) * 2.0 / HD))
    angles = positions.astype(F32)[:, None] * frequency[None, :]
    return (jnp.cos(angles), jnp.sin(angles))


def rotate(values, cosine_table, sine_table):
    half_size = values.shape[-1] // 2
    front_half = values[..., :half_size]
    back_half = values[..., half_size:]
    return jnp.concatenate(
        [
            front_half * cosine_table - back_half * sine_table,
            back_half * cosine_table + front_half * sine_table,
        ],
        axis=-1,
    )


def rotate_back(values, cosine_table, sine_table):
    return rotate(values, cosine_table, -sine_table)


def dot(left_side, right_side):
    return jnp.dot(left_side, right_side, preferred_element_type=F32)


def dot_right_t(left_side, right_side):
    return lax.dot_general(
        left_side, right_side, (((1,), (1,)), ((), ())), preferred_element_type=F32
    )


def dot_left_t(left_side, right_side):
    return lax.dot_general(
        left_side, right_side, (((0,), (0,)), ((), ())), preferred_element_type=F32
    )


def norm_back(grad_normed, normed, inv_rms):
    return inv_rms * (grad_normed - normed * jnp.mean(grad_normed * normed, axis=-1, keepdims=True))


def pick(array, index, axis=0):
    return lax.dynamic_index_in_dim(array, index, axis, keepdims=False)


def place(array, block, index, axis=0):
    return lax.dynamic_update_index_in_dim(array, block, index, axis)


class Ring:
    def __init__(self):
        self.n = lax.axis_size("batch")
        self.h = self.n // 2
        rank = lax.axis_index("batch")
        self.at = jnp.where(rank % 2 == 0, rank // 2, self.n - 1 - rank // 2)
        order = [2 * i for i in range(self.h)] + [2 * i + 1 for i in reversed(range(self.h))]
        self.up = [(order[i], order[(i + 1) % self.n]) for i in range(self.n)]
        self.down = [(there, here) for here, there in self.up]

    def rank_of(self, step):
        spot = (self.at + step) % self.n
        return jnp.where(spot < self.h, 2 * spot, 2 * (self.n - 1 - spot) + 1)

    def spread(self, block):
        found = {0: block}
        upward = downward = block
        for step in range(1, self.h):
            upward = lax.ppermute(upward, "batch", self.up)
            downward = lax.ppermute(downward, "batch", self.down)
            found[-step] = upward
            found[step] = downward
        cut = block.shape[0] // 2
        found[self.h] = jnp.concatenate(
            [
                lax.ppermute(upward[:cut], "batch", self.up),
                lax.ppermute(downward[cut:], "batch", self.down),
            ],
            axis=0,
        )
        return found

    def gather(self, block):
        found = self.spread(block)
        whole = jnp.zeros((self.n,) + block.shape, block.dtype)
        for step, part in found.items():
            whole = place(whole, part, self.rank_of(step))
        return whole

    def collect(self, term):
        far = term(self.h)
        cut = far.shape[0] // 2
        downward = lax.ppermute(far[:cut].astype(BF), "batch", self.down)
        upward = lax.ppermute(far[cut:].astype(BF), "batch", self.up)
        for step in range(self.h - 1, 0, -1):
            for_lower = term(-step).astype(F32)
            for_upper = term(step).astype(F32)
            if step == self.h - 1:
                for_lower = jnp.concatenate(
                    [for_lower[:cut] + downward.astype(F32), for_lower[cut:]], axis=0
                )
                for_upper = jnp.concatenate(
                    [for_upper[:cut], for_upper[cut:] + upward.astype(F32)], axis=0
                )
            else:
                for_lower = for_lower + downward.astype(F32)
                for_upper = for_upper + upward.astype(F32)
            downward = lax.ppermute(for_lower.astype(BF), "batch", self.down)
            upward = lax.ppermute(for_upper.astype(BF), "batch", self.up)
        own = term(0).astype(F32)
        return own + downward.astype(F32) + upward.astype(F32)

    def collect_rows(self, stacked):
        return self.collect(lambda step: pick(stacked, self.rank_of(step)))


FAR = [(0, 2), (1, 3), (2, 0), (3, 1)]
NEAR = [(0, 1), (1, 0), (2, 3), (3, 2)]


def ctx_place():
    rank = lax.axis_index("ctx")
    return rank // 2, rank % 2


def in_order(mine, theirs, at):
    return jnp.where(at == 0, jnp.stack([mine, theirs]), jnp.stack([theirs, mine]))


def ctx_gather(block):
    outer, inner = ctx_place()
    pair = in_order(block, lax.ppermute(block, "ctx", FAR), outer)
    whole = in_order(pair, lax.ppermute(pair, "ctx", NEAR), inner)
    whole = jnp.swapaxes(whole, 0, 1)
    return whole.reshape((4,) + block.shape)


def near_collect(stacked):
    _, inner = ctx_place()
    parts = stacked.reshape((2, 2) + stacked.shape[1:])
    got = lax.ppermute(pick(parts, 1 - inner, 1).astype(BF), "ctx", NEAR)
    return pick(parts, inner, 1).astype(F32) + got.astype(F32)


def ctx_collect(stacked):
    outer, _ = ctx_place()
    half = near_collect(stacked)
    got = lax.ppermute(pick(half, 1 - outer).astype(BF), "ctx", FAR)
    return pick(half, outer) + got.astype(F32)


def ctx_exchange(stacked):
    outer, inner = ctx_place()
    parts = stacked.reshape((2, 2) + stacked.shape[1:])
    got = lax.ppermute(pick(parts, 1 - outer), "ctx", FAR)
    parts = in_order(pick(parts, outer), got, outer)
    got = lax.ppermute(pick(parts, 1 - inner, 1), "ctx", NEAR)
    whole = in_order(pick(parts, inner, 1), got, inner)
    return jnp.swapaxes(whole, 0, 1).reshape(stacked.shape)


MESH = pl.DeviceIdType.MESH


class Place:
    def __init__(self, n_batch):
        self.n = n_batch
        self.h = n_batch // 2
        self.b = lax.axis_index("batch")
        self.c = lax.axis_index("ctx")
        self.outer = lax.div(self.c, 2)
        self.inner = lax.rem(self.c, 2)
        self.far = lax.rem(self.c + 2, 4)
        self.near = self.c + 1 - 2 * self.inner
        odd = lax.rem(self.b, 2)
        half = lax.div(self.b, 2)
        self.at = half + odd * (self.n - 1 - 2 * half)

    def rank_of(self, step):
        spot = lax.rem(self.at + step + 2 * self.n, self.n)
        back = lax.div(spot, self.h)
        return (1 - back) * 2 * spot + back * (2 * (self.n - 1 - spot) + 1)

    def up(self):
        return (self.rank_of(1), self.c)

    def down(self):
        return (self.rank_of(-1), self.c)


class Copies:
    def __init__(self, send_sems, recv_sems):
        self.send_sems = send_sems
        self.recv_sems = recv_sems
        self.count = 0
        self.open_sends = []
        self.open_recvs = []

    def remote(self, source, target, device):
        index = self.count
        self.count += 1
        copy = pltpu.make_async_remote_copy(
            src_ref=source,
            dst_ref=target,
            send_sem=self.send_sems.at[index],
            recv_sem=self.recv_sems.at[index],
            device_id=device,
            device_id_type=MESH,
        )
        copy.start()
        self.open_sends.append(copy)
        self.open_recvs.append(copy)
        return copy

    def local(self, source, target):
        index = self.count
        self.count += 1
        copy = pltpu.make_async_copy(source, target, self.recv_sems.at[index])
        copy.start()
        self.open_recvs.append(copy)
        return copy

    def arrive(self, copy):
        if any(copy is other for other in self.open_recvs):
            self.open_recvs = [other for other in self.open_recvs if other is not copy]
            if any(copy is other for other in self.open_sends):
                copy.wait_recv()
            else:
                copy.wait()

    def drain(self):
        for copy in list(self.open_recvs):
            self.arrive(copy)
        for copy in self.open_sends:
            copy.wait_send()


def greet(place, others):
    barrier = pltpu.get_barrier_semaphore()
    for device in others:
        pl.semaphore_signal(barrier, inc=1, device_id=device, device_id_type=MESH)
    return barrier


class RingGather:
    def __init__(self, place, copies, rows, slot):
        self.place, self.copies, self.rows, self.slot = place, copies, rows, slot
        self.step = 0
        self.moving = ()

    def advance(self):
        place, copies = self.place, self.copies
        for copy in self.moving:
            copies.arrive(copy)
        self.moving = ()
        self.step += 1
        cut = self.rows // 2
        if self.step > place.h:
            return
        lower = place.rank_of(1 - self.step)
        upper = place.rank_of(self.step - 1)
        if self.step < place.h:
            whole = pl.ds(0, self.rows)
            pieces = (whole, whole)
        else:
            pieces = (pl.ds(0, cut), pl.ds(cut, self.rows - cut))
        upward, downward = self.slot(lower, pieces[0]), self.slot(upper, pieces[1])
        self.moving = (
            copies.remote(upward, upward, place.up()),
            copies.remote(downward, downward, place.down()),
        )

    def arrived(self):
        step = self.step - 1
        if step == 0:
            return []
        if step == self.place.h:
            return [self.place.rank_of(step)]
        return [self.place.rank_of(-step), self.place.rank_of(step)]


def weights_kernel(
    n_batch,
    packed_ref,
    up_ref,
    out_ref,
    gu_ref,
    down_ref,
    packed_all,
    up_all,
    out_all,
    gu_all,
    down_all,
    send_sems,
    recv_sems,
    out_sems,
    flat_v,
    gu_v,
):
    place = Place(n_batch)
    copies = Copies(send_sems, recv_sems)
    b, c, n = place.b, place.c, n_batch
    own_rows = packed_ref.shape[0]
    out_rows = out_ref.shape[0]
    index = b * 4 + c
    target = (lax.rem(index, n), lax.div(index, n))
    slab = c * n + b
    source = (lax.div(slab, 4), lax.rem(slab, 4))
    stays = slab == index
    peers = [(lax.rem(b + k, n), c) for k in range(1, n)]
    ctx_peers = [(b, place.far), (b, place.near), (b, lax.rem(place.near + 2, 4))]

    barrier = greet(place, peers + ctx_peers)

    @pl.when(jnp.logical_not(stays))
    def _():
        for device in (target, source):
            pl.semaphore_signal(barrier, inc=1, device_id=device, device_id_type=MESH)

    pl.semaphore_wait(barrier, n + 4 - 2 * stays.astype(jnp.int32))

    head_cols = up_ref.shape[1] // 4

    def up_cols(rank):
        return up_ref.at[:, pl.ds(pl.multiple_of(rank * head_cols, head_cols), head_cols)]

    own = [
        copies.local(packed_ref, packed_all.at[b, c]),
        copies.local(up_cols(c), up_all.at[b, c]),
        copies.local(gu_ref, flat_v),
        copies.local(down_ref, down_all.at[c]),
    ]
    out_copy = pltpu.make_async_remote_copy(
        src_ref=out_ref,
        dst_ref=out_all.at[target[0]],
        send_sem=out_sems.at[0],
        recv_sem=out_sems.at[1],
        device_id=target,
        device_id_type=MESH,
    )
    out_stay = pltpu.make_async_copy(out_ref, out_all.at[b], out_sems.at[0])

    @pl.when(jnp.logical_not(stays))
    def _():
        out_copy.start()

    @pl.when(stays)
    def _():
        out_stay.start()

    up_copies = [
        copies.remote(up_cols(peer[1]), up_all.at[b, c], peer) for peer in ctx_peers
    ]
    far_device, near_device = ctx_peers[0], ctx_peers[1]
    down_far = copies.remote(down_ref, down_all.at[c], far_device)

    copies.arrive(own[0])
    packed_ring = RingGather(
        place, copies, own_rows, lambda rank, rows: packed_all.at[rank, c, rows]
    )
    up_ring = RingGather(
        place, copies, up_ref.shape[0], lambda rank, rows: up_all.at[rank, :, rows]
    )
    out_ring = RingGather(place, copies, out_rows, lambda rank, rows: out_all.at[rank, rows])

    packed_far = []

    def packed_step():
        packed_ring.advance()
        ranks = packed_ring.arrived() if packed_ring.step > 1 else [b]
        for rank in ranks:
            block = packed_all.at[rank, c]
            packed_far.append((rank, copies.remote(block, block, far_device)))

    packed_step()
    copies.arrive(own[2])
    ff = gu_v.shape[3]
    for slab_at in range(n):
        for kind in (0, 1):
            start = (kind * n + slab_at) * ff
            gu_v[slab_at, kind] = flat_v[:, start : start + ff]
    own.append(copies.local(gu_v.at[b], gu_all.at[:, b, c]))
    gu_copies = [
        (
            lax.rem(b - k + n, n),
            copies.remote(gu_v.at[peer[0]], gu_all.at[:, b, c], peer),
        )
        for k, peer in zip(range(1, n), peers)
    ]
    for copy in own[1:2] + up_copies:
        copies.arrive(copy)
    up_ring.advance()
    packed_step()

    @pl.when(jnp.logical_not(stays))
    def _():
        out_copy.wait()

    @pl.when(stays)
    def _():
        out_stay.wait()

    out_ring.advance()
    gu_far = []
    copies.arrive(own[4])
    own_gu = gu_all.at[:, b, c]
    gu_far.append(copies.remote(own_gu, own_gu, far_device))
    waiting = list(gu_copies)
    copies.arrive(own[3])
    down_near = [copies.remote(down_all.at[c], down_all.at[c], near_device)]

    def forward_gu(count):
        for _ in range(min(count, len(waiting))):
            rank, copy = waiting.pop(0)
            copies.arrive(copy)
            block = gu_all.at[:, rank, c]
            gu_far.append(copies.remote(block, block, far_device))

    for _ in range(place.h):
        up_ring.advance()
        if packed_ring.step <= place.h:
            packed_step()
        forward_gu(2)
        out_ring.advance()
    copies.arrive(down_far)
    far = place.far
    down_near.append(copies.remote(down_all.at[far], down_all.at[far], near_device))
    forward_gu(n)
    own_packed = packed_all.at[:, c]
    copies.remote(own_packed, own_packed, near_device)
    own_gu = gu_all.at[:, :, c]
    copies.remote(own_gu, own_gu, near_device)
    for _, copy in packed_far:
        copies.arrive(copy)
    far_packed = packed_all.at[:, far]
    copies.remote(far_packed, far_packed, near_device)
    for copy in gu_far:
        copies.arrive(copy)
    far_gu = gu_all.at[:, :, far]
    copies.remote(far_gu, far_gu, near_device)
    copies.drain()


def spread_weights(n_batch, packed, up_rows, out_rows, gu_rows, down_rows):
    own_rows, packed_cols = packed.shape
    gain_rows, up_cols = up_rows.shape
    ff = gu_rows.shape[1] // (2 * n_batch)
    shapes = (
        jax.ShapeDtypeStruct((n_batch, 4, own_rows, packed_cols), BF),
        jax.ShapeDtypeStruct((n_batch, 4, gain_rows, up_cols // 4), BF),
        jax.ShapeDtypeStruct((n_batch,) + out_rows.shape, BF),
        jax.ShapeDtypeStruct((2, n_batch, 4, own_rows, ff), BF),
        jax.ShapeDtypeStruct((4,) + down_rows.shape, BF),
    )
    sems = 6 * n_batch + 3 * n_batch + 32
    return pl.pallas_call(
        functools.partial(weights_kernel, n_batch),
        out_shape=shapes,
        in_specs=[pl.BlockSpec(memory_space=pl.ANY)] * 5,
        out_specs=[pl.BlockSpec(memory_space=pl.ANY)] * 5,
        scratch_shapes=[
            pltpu.SemaphoreType.DMA((sems,)),
            pltpu.SemaphoreType.DMA((sems,)),
            pltpu.SemaphoreType.DMA((2,)),
            pltpu.VMEM(gu_rows.shape, BF),
            pltpu.VMEM((n_batch, 2, own_rows, ff), BF),
        ],
        compiler_params=pltpu.CompilerParams(collective_id=0, has_side_effects=True),
        name="spread_weights",
    )(packed, up_rows, out_rows, gu_rows, down_rows)


def mlp_kernel(
    n_batch,
    rows_ref,
    gate_ref,
    up_ref,
    down_ref,
    cot_ref,
    *refs,
):
    (
        sum_ref,
        down_part,
        term_out,
        gu_out,
        rows_v,
        cot_v,
        gate_v,
        up_v,
        down_v,
        act_v,
        ggate_v,
        gup_v,
        in_v,
        term_v,
        got_v,
        gu_got,
        gu_last,
        down_got,
        send_sems,
        recv_sems,
        back_send,
        back_recv,
        load_sems,
        store_sems,
        part_send,
        part_recv,
    ) = refs
    place = Place(n_batch)
    far = place.h
    n_tok = rows_ref.shape[0]
    cut = n_tok // 2
    width = rows_ref.shape[1]
    ff = gate_ref.shape[-1]
    up_device, down_device = place.up(), place.down()
    far_device, near_device = (place.b, place.far), (place.b, place.near)
    barrier = greet(place, [up_device, down_device, far_device, near_device])
    parts = Copies(part_send, part_recv)
    own_rows = gate_v.shape[2]
    block = 4 * own_rows

    load_rows = pltpu.make_async_copy(rows_ref, rows_v.at[0, pl.ds(0, n_tok)], load_sems.at[0])
    load_rows.start()
    loads = [
        pltpu.make_async_copy(source, target, load_sems.at[1 + i])
        for i, (source, target) in enumerate(
            [(gate_ref, gate_v), (up_ref, up_v), (down_ref, down_v)]
        )
    ]
    spots = [(0, 0, 0), (far, 0, 1)]
    spots += [(side * step, step, (side + 1) // 2) for step in range(1, far) for side in (-1, 1)]
    for i, (distance, group, side) in enumerate(spots):
        loads.append(
            pltpu.make_async_copy(
                cot_ref.at[place.rank_of(distance)], cot_v.at[group, pl.ds(side * n_tok, n_tok)], load_sems.at[4 + i]
            )
        )
    for copy in loads:
        copy.start()
    load_rows.wait()
    pl.semaphore_wait(barrier, 4)

    def piece(side, half):
        return pl.ds(side * n_tok + half * cut, cut)

    def hop(step, side, half):
        source_group, source_side = step - 1, side
        target_group, target_side = step, side
        if isinstance(step, int) and step == 1:
            source_side = 0
        if isinstance(step, int) and step == far:
            target_group, target_side = 0, 1
        return pltpu.make_async_remote_copy(
            src_ref=rows_v.at[source_group, piece(source_side, half)],
            dst_ref=rows_v.at[target_group, piece(target_side, half)],
            send_sem=send_sems.at[step, side, half],
            recv_sem=recv_sems.at[step, side, half],
            device_id=down_device if side else up_device,
            device_id_type=MESH,
        )

    both = [(side, half) for half in (0, 1) for side in (0, 1)]
    ends = [(0, 0), (1, 1)]
    for side, half in both:
        hop(1, side, half).start()
    for copy in loads:
        copy.wait()

    def stores(group):
        return [
            pltpu.make_async_copy(term_v.at[group], term_out.at[group], store_sems.at[0, group])
        ]

    def compute(group):
        rows = rows_v[group]
        cots = cot_v[group]
        down_all = down_v[...].reshape(ff, width)
        start = 0
        while start < ff:
            size = min(256, ff - start)
            tile = slice(start, start + size)
            gate = dot(rows, gate_v[..., tile].reshape(width, size))
            up = dot(rows, up_v[..., tile].reshape(width, size))
            grad_act = dot_right_t(cots, down_all[tile])
            sigmoid = 1.0 / (1.0 + jnp.exp(-gate))
            silu = gate * sigmoid
            act_v[group, :, tile] = (silu * up).astype(BF)
            slope = sigmoid * (1.0 + gate * (1.0 - sigmoid))
            ggate_v[group, :, tile] = (grad_act * up * slope).astype(BF)
            gup_v[group, :, tile] = (grad_act * silu).astype(BF)
            start += size
        ggate = ggate_v[group]
        gup = gup_v[group]
        act = act_v[group]
        tile_cols = 2 * block

        @pl.loop(0, width // tile_cols)
        def _(t):
            cols = pl.ds(pl.multiple_of(t * tile_cols, tile_cols), tile_cols)
            back = dot_right_t(ggate, gate_v[pl.ds(2 * t, 2)].reshape(tile_cols, ff))
            back += dot_right_t(gup, up_v[pl.ds(2 * t, 2)].reshape(tile_cols, ff))
            in_v[group, :, cols] = back.astype(BF)
            down = down_v[:, :, cols].reshape(ff, tile_cols)
            term_v[group, :, cols] = dot(act, down).astype(BF)

        for copy in stores(group):
            copy.start()

    @pl.loop(1, far)
    def _(step):
        for side, half in both:
            hop(step, side, half).wait_recv()

        @pl.when(step < far - 1)
        def _():
            for side, half in both:
                hop(step + 1, side, half).start()

        @pl.when(step == far - 1)
        def _():
            for side, half in ends:
                hop(far, side, half).start()

        compute(step)

    for side, half in ends:
        hop(far, side, half).wait_recv()
    compute(0)

    def back_hop(step, side, half, source):
        return pltpu.make_async_remote_copy(
            src_ref=source,
            dst_ref=got_v.at[step, side, half],
            send_sem=back_send.at[step, side, half],
            recv_sem=back_recv.at[step, side, half],
            device_id=up_device if side else down_device,
            device_id_type=MESH,
        )

    def held(step, side, half):
        return in_v.at[step, piece(side, half)]

    for side, half in ends:
        back_hop(far - 1, side, half, held(0, 1, half)).start()

    def pass_on(step, side, half, added):
        own = held(step, side, half)
        if added:
            back_hop(step, side, half, own).wait_recv()
            own[...] = (own[...].astype(F32) + got_v[step, side, half].astype(F32)).astype(BF)
        back_hop(step - 1, side, half, own).start()

    for side, half in both:
        if (side, half) not in ends:
            pass_on(far - 1, side, half, False)

    def gate_up_terms(t):
        cols = slice(t * 2 * block, (t + 1) * 2 * block)
        rows = rows_v[:, :, cols].reshape(n_batch * n_tok, 2 * block)
        for target, grads in ((gate_v, ggate_v), (up_v, gup_v)):
            term = dot_left_t(rows, grads[...].reshape(n_batch * n_tok, ff))
            target[2 * t : 2 * t + 2] = term.astype(BF).reshape(2, 4, own_rows, ff)

    def down_terms():
        @pl.loop(0, width // (2 * block))
        def _(t):
            cols = pl.ds(pl.multiple_of(t * 2 * block, 2 * block), 2 * block)
            grads = cot_v[:, :, cols].reshape(n_batch * n_tok, 2 * block)
            term = dot_left_t(act_v[...].reshape(n_batch * n_tok, ff), grads)
            down_v[:, :, cols] = term.astype(BF).reshape(4, ff // 4, 2 * block)

    def pass_all(step):
        for side, half in [(1, 0), (0, 1), (0, 0), (1, 1)]:
            if step < far - 1 or (side, half) in ends:
                pass_on(step, side, half, True)

    steps = list(range(1, far))
    outer, inner = place.outer, place.inner
    kinds = list(enumerate((gate_v, up_v)))
    near_copies, far_copies = {}, {}

    def send_near(t):
        pair = pl.ds(2 * t, 2)
        near_copies[t] = [
            parts.remote(
                target.at[pair, 2 * side + 1 - inner], gu_got.at[kind, side, pair], near_device
            )
            for side in (0, 1)
            for kind, target in kinds
        ]

    def send_far(t):
        pair = pl.ds(2 * t, 2)
        for copy in near_copies[t]:
            parts.arrive(copy)
        far_copies[t] = []
        for kind, target in kinds:
            other = target.at[pair, 2 * (1 - outer) + inner]
            added = other[...].astype(F32) + gu_got[kind, 1 - outer, pair].astype(F32)
            other[...] = added.astype(BF)
            far_copies[t].append(parts.remote(other, gu_last.at[kind, pair], far_device))

    def take_far(t):
        pair = pl.ds(2 * t, 2)
        for copy in far_copies[t]:
            parts.arrive(copy)
        for kind, target in kinds:
            kept = target.at[pair, 2 * outer + inner]
            added = kept[...].astype(F32) + gu_got[kind, outer, pair].astype(F32)
            kept[...] = (added + gu_last[kind, pair].astype(F32)).astype(BF)
            parts.local(kept, gu_out.at[pair, kind])

    def ring_step():
        if steps:
            pass_all(steps.pop())

    tiles = width // (2 * block)
    for t in range(tiles):
        gate_up_terms(t)
        send_near(t)
        if t > 0:
            send_far(t - 1)
        ring_step()
    while steps:
        ring_step()
    send_far(tiles - 1)
    down_terms()
    down_copies = [
        parts.remote(down_v.at[2 * side + 1 - inner], down_got.at[side], near_device)
        for side in (0, 1)
    ]
    for half in (0, 1):
        for side in (0, 1):
            back_hop(0, side, half, held(0, 0, half)).wait_recv()
        rows = slice(half * cut, (half + 1) * cut)
        sum_ref[rows, :] = (
            in_v[0, rows, :].astype(F32)
            + got_v[0, 0, half].astype(F32)
            + got_v[0, 1, half].astype(F32)
        )
    for side in (0, 1):
        parts.arrive(down_copies[side])
        added = down_v[2 * side + inner].astype(F32) + down_got[side].astype(F32)
        down_got[side] = added.astype(BF)
    parts.local(down_got, down_part)
    for t in range(tiles):
        take_far(t)
    parts.drain()

    for step in range(1, far + 1):
        for side, half in both if step < far else ends:
            hop(step, side, half).wait_send()
    for side, half in ends:
        back_hop(far - 1, side, half, held(0, 1, half)).wait_send()
    for step in range(far - 1, 0, -1):
        for side, half in both:
            back_hop(step - 1, side, half, held(step, side, half)).wait_send()
    for group in range(far):
        for copy in stores(group):
            copy.wait()


def fused_mlp(n_batch, rows, cots, own_gate, own_up, own_down):
    n_tok, width = rows.shape
    ff = own_gate.shape[-1]
    own_rows = own_gate.shape[2]
    far = n_batch // 2
    pair = 2 * n_tok
    flops = 18 * n_batch * n_tok * width * ff
    return pl.pallas_call(
        functools.partial(mlp_kernel, n_batch),
        out_shape=(
            jax.ShapeDtypeStruct((n_tok, width), F32),
            jax.ShapeDtypeStruct((2, ff // 4, width), BF),
            jax.ShapeDtypeStruct((far, pair, width), BF),
            jax.ShapeDtypeStruct((n_batch, 2, own_rows, ff), BF),
        ),
        in_specs=[pl.BlockSpec(memory_space=pl.ANY)] * 5,
        out_specs=[pl.BlockSpec(memory_space=pltpu.VMEM)]
        + [pl.BlockSpec(memory_space=pl.ANY)] * 3,
        scratch_shapes=[
            pltpu.VMEM((far, pair, width), BF),
            pltpu.VMEM((far, pair, width), BF),
            pltpu.VMEM((n_batch, 4, own_rows, ff), BF),
            pltpu.VMEM((n_batch, 4, own_rows, ff), BF),
            pltpu.VMEM((4, ff // 4, width), BF),
            pltpu.VMEM((far, pair, ff), BF),
            pltpu.VMEM((far, pair, ff), BF),
            pltpu.VMEM((far, pair, ff), BF),
            pltpu.VMEM((far, pair, width), BF),
            pltpu.VMEM((far, pair, width), BF),
            pltpu.VMEM((far, 2, 2, n_tok // 2, width), BF),
            pltpu.VMEM((2, 2, n_batch, own_rows, ff), BF),
            pltpu.VMEM((2, n_batch, own_rows, ff), BF),
            pltpu.VMEM((2, ff // 4, width), BF),
            pltpu.SemaphoreType.DMA((far + 1, 2, 2)),
            pltpu.SemaphoreType.DMA((far + 1, 2, 2)),
            pltpu.SemaphoreType.DMA((far, 2, 2)),
            pltpu.SemaphoreType.DMA((far, 2, 2)),
            pltpu.SemaphoreType.DMA((4 + n_batch,)),
            pltpu.SemaphoreType.DMA((1, far)),
            pltpu.SemaphoreType.DMA((72,)),
            pltpu.SemaphoreType.DMA((72,)),
        ],
        compiler_params=pltpu.CompilerParams(
            collective_id=1, has_side_effects=True, vmem_limit_bytes=60 * 1024 * 1024
        ),
        cost_estimate=pl.CostEstimate(
            flops=flops, bytes_accessed=24 * 1024 * 1024, transcendentals=n_batch * n_tok * ff
        ),
        name="fused_mlp",
    )(rows, own_gate, own_up, own_down, cots)


class RingCollect:
    def __init__(self, place, block, got, send_sems, recv_sems):
        self.place, self.block, self.got = place, block, got
        self.send_sems, self.recv_sems = send_sems, recv_sems
        self.cut = got.shape[3]
        self.step = place.h
        self.sent = []

    def held(self, step, half):
        return self.block(step).at[pl.ds(half * self.cut, self.cut)]

    def hop(self, step, side, half, source):
        place = self.place
        return pltpu.make_async_remote_copy(
            src_ref=source,
            dst_ref=self.got.at[step, side, half],
            send_sem=self.send_sems.at[step, side, half],
            recv_sem=self.recv_sems.at[step, side, half],
            device_id=place.up() if side else place.down(),
            device_id_type=MESH,
        )

    def send(self, step, side, half, source):
        copy = self.hop(step, side, half, source)
        copy.start()
        self.sent.append(copy)

    def advance(self):
        far = self.place.h
        step = self.step
        self.step -= 1
        if step == far:
            for side in (0, 1):
                self.send(far - 1, side, side, self.held(far, side))
            for side in (0, 1):
                half = 1 - side
                self.send(far - 2, side, half, self.held((2 * side - 1) * (far - 1), half))
            return
        pieces = [(0, 0), (1, 1)] if step == far - 1 else [(1, 0), (0, 1), (0, 0), (1, 1)]
        for side, half in pieces:
            own = self.held((2 * side - 1) * step, half)
            self.hop(step, side, half, own).wait_recv()
            own[...] = (own[...].astype(F32) + self.got[step, side, half].astype(F32)).astype(BF)
            self.send(step - 1, side, half, own)

    def finish(self, half):
        own = self.held(0, half)
        for side in (0, 1):
            self.hop(0, side, half, own).wait_recv()
        return (
            own[...].astype(F32)
            + self.got[0, 0, half].astype(F32)
            + self.got[0, 1, half].astype(F32)
        )

    def drain(self):
        for copy in self.sent:
            copy.wait_send()


def tail_kernel(
    n_batch,
    gain_rows,
    out_ref,
    up_ref,
    project_ref,
    rows_ref,
    gu_ref,
    gain_ref,
    out_grad,
    up_grad,
    in_grad,
    gain_grad,
    gu_grad,
    out_v,
    up_v,
    in_v,
    out_got,
    up_got,
    in_got,
    out_sum,
    out_all,
    up_sum,
    up_all,
    in_sum,
    in_all,
    ring_send,
    ring_recv,
    send_sems,
    recv_sems,
    project_v,
    rows_v,
    gu_v,
    load_sems,
    out_sems,
):
    place = Place(n_batch)
    copies = Copies(send_sems, recv_sems)
    b, c, n = place.b, place.c, n_batch
    own_rows = in_grad.shape[0]
    index = b * 4 + c
    slab = c * n + b
    target = (lax.div(slab, 4), lax.rem(slab, 4))
    source = (lax.rem(index, n), lax.div(index, n))
    stays = slab == index
    ctx_peers = [(b, place.far), (b, place.near), (b, lax.rem(place.near + 2, 4))]

    loads = [
        pltpu.make_async_copy(held, kept, load_sems.at[i])
        for i, (held, kept) in enumerate([(out_ref, out_v), (up_ref, up_v), (rows_ref, rows_v), (gu_ref, gu_v)])
    ]
    for copy in loads:
        copy.start()
    barrier = greet(place, [place.up(), place.down()] + ctx_peers)

    @pl.when(jnp.logical_not(stays))
    def _():
        for device in (target, source):
            pl.semaphore_signal(barrier, inc=1, device_id=device, device_id_type=MESH)

    pl.semaphore_wait(barrier, 7 - 2 * stays.astype(jnp.int32))

    rings = []
    for i, (kept, got) in enumerate([(out_v, out_got), (up_v, up_got), (in_v, in_got)]):
        rings.append(
            RingCollect(
                place,
                lambda step, kept=kept: kept.at[place.rank_of(step)],
                got,
                ring_send.at[i],
                ring_recv.at[i],
            )
        )
    part_cols = project_ref.shape[2]
    project_copies = [
        copies.remote(project_ref.at[peer[1]], project_v.at[c], peer) for peer in ctx_peers
    ]
    project_copies.append(copies.local(project_ref.at[c], project_v.at[c]))
    for copy, ring in zip(loads[:2], rings):
        copy.wait()
        ring.advance()
    for copy in project_copies:
        copies.arrive(copy)
    loads[2].wait()
    project = project_v[...].reshape(-1, part_cols)
    part_rows = own_rows + 16
    n_all = project.shape[0]
    width = rows_ref.shape[3]
    ahead = max(1, 256 // (4 * own_rows))
    chunk = ahead * 4 * own_rows

    @pl.loop(0, width // chunk)
    def _(t):
        cols = pl.ds(pl.multiple_of(t * chunk, chunk), chunk)
        term = dot_left_t(rows_v[:, :, :, cols].reshape(n_all, chunk), project).astype(BF)
        term = term.reshape(ahead, 4, own_rows, part_cols)
        for part in range(4):
            in_v[pl.ds(t * ahead, ahead), pl.ds(part * part_rows, own_rows), :] = term[:, part]

    for part in range(4):
        in_v[:, part * part_rows + own_rows : (part + 1) * part_rows, :] = gain_ref[:, part]
    rings[2].advance()
    for _ in range(place.h - 1):
        for ring in rings:
            ring.advance()

    loads[3].wait()
    ff = gu_v.shape[3]
    for slab_at in range(n):
        for kind in (0, 1):
            start = (kind * n + slab_at) * ff
            gu_grad[:, start : start + ff] = gu_v[slab_at, kind].astype(F32)

    in_ring, up_ring, out_ring = rings[2], rings[1], rings[0]
    out_cut, up_cut, in_cut = out_ring.cut, up_ring.cut, in_ring.cut
    for half in (0, 1):
        out_sum[pl.ds(half * out_cut, out_cut), :] = out_ring.finish(half).astype(BF)
    out_copy = pltpu.make_async_remote_copy(
        src_ref=out_sum,
        dst_ref=out_all,
        send_sem=out_sems.at[0],
        recv_sem=out_sems.at[1],
        device_id=target,
        device_id_type=MESH,
    )
    out_stay = pltpu.make_async_copy(out_sum, out_all, out_sems.at[0])

    @pl.when(jnp.logical_not(stays))
    def _():
        out_copy.start()

    @pl.when(stays)
    def _():
        out_stay.start()

    for half in (0, 1):
        up_sum[pl.ds(half * up_cut, up_cut), :] = up_ring.finish(half).astype(BF)
    up_copies = [
        copies.remote(
            up_sum.at[pl.ds(peer[1] * gain_rows, gain_rows)], up_all.at[c], peer
        )
        for peer in ctx_peers
    ]
    up_copies.append(
        copies.local(up_sum.at[pl.ds(c * gain_rows, gain_rows)], up_all.at[c])
    )
    for half in (0, 1):
        in_sum[pl.ds(half * in_cut, in_cut), :] = in_ring.finish(half).astype(BF)
    in_copies = [
        copies.remote(in_sum.at[pl.ds(peer[1] * part_rows, part_rows)], in_all.at[c], peer)
        for peer in ctx_peers
    ]
    in_copies.append(copies.local(in_sum.at[pl.ds(c * part_rows, part_rows)], in_all.at[c]))

    @pl.when(jnp.logical_not(stays))
    def _():
        out_copy.wait()

    @pl.when(stays)
    def _():
        out_stay.wait()

    out_grad[...] = out_all[...].astype(F32)
    for copy in up_copies:
        copies.arrive(copy)
    cols = up_all.shape[2]
    for part in range(4):
        up_grad[:, part * cols : (part + 1) * cols] = up_all[part].astype(F32)
    for copy in in_copies:
        copies.arrive(copy)
    cols = in_all.shape[2]
    gains = jnp.zeros(gain_grad.shape, F32)
    for part in range(4):
        in_grad[:, part * cols : (part + 1) * cols] = in_all[part, :own_rows, :].astype(F32)
        gains = gains + in_all[part, own_rows:, :].astype(F32)
    gain_grad[...] = gains
    copies.drain()
    for ring in rings:
        ring.drain()


def collect_weights(n_batch, gain_rows, out_terms, up_terms, project, attn_in_all, grad_gu, gain_terms):
    far = n_batch // 2
    out_rows, width = out_terms.shape[1:]
    up_rows, up_cols = up_terms.shape[1:]
    in_cols = project.shape[2]
    own_rows = width // (4 * n_batch)
    in_rows = 4 * (own_rows + 16)
    shapes = [out_terms.shape[1:], up_terms.shape[1:], (in_rows, in_cols)]
    sems = 2 * n_batch + 16
    return pl.pallas_call(
        functools.partial(tail_kernel, n_batch, gain_rows),
        out_shape=(
            jax.ShapeDtypeStruct((out_rows, width), F32),
            jax.ShapeDtypeStruct((gain_rows, 4 * up_cols), F32),
            jax.ShapeDtypeStruct((own_rows, 4 * in_cols), F32),
            jax.ShapeDtypeStruct((16, in_cols), F32),
            jax.ShapeDtypeStruct((own_rows, 2 * n_batch * grad_gu.shape[3]), F32),
        ),
        in_specs=[pl.BlockSpec(memory_space=pl.ANY)] * 5 + [pl.BlockSpec(memory_space=pltpu.VMEM)],
        out_specs=[pl.BlockSpec(memory_space=pltpu.VMEM)] * 5,
        scratch_shapes=[pltpu.VMEM((n_batch,) + shape, BF) for shape in shapes]
        + [pltpu.VMEM((far, 2, 2, rows // 2, cols), BF) for rows, cols in shapes]
        + [
            pltpu.VMEM((out_rows, width), BF),
            pltpu.VMEM((out_rows, width), BF),
            pltpu.VMEM((up_rows, up_cols), BF),
            pltpu.VMEM((4, gain_rows, up_cols), BF),
            pltpu.VMEM((in_rows, in_cols), BF),
            pltpu.VMEM((4, own_rows + 16, in_cols), BF),
            pltpu.SemaphoreType.DMA((3, far, 2, 2)),
            pltpu.SemaphoreType.DMA((3, far, 2, 2)),
            pltpu.SemaphoreType.DMA((sems,)),
            pltpu.SemaphoreType.DMA((sems,)),
            pltpu.VMEM(project.shape, BF),
            pltpu.VMEM(attn_in_all.shape, BF),
            pltpu.VMEM(grad_gu.shape, BF),
            pltpu.SemaphoreType.DMA((4,)),
            pltpu.SemaphoreType.DMA((2,)),
        ],
        compiler_params=pltpu.CompilerParams(
            collective_id=2, has_side_effects=True, vmem_limit_bytes=48 * 1024 * 1024
        ),
        name="collect_weights",
    )(out_terms, up_terms, project, attn_in_all, grad_gu, gain_terms)


class CtxCollect:
    def __init__(self, place, copies, part, near_got, far_got):
        self.place, self.copies, self.part = place, copies, part
        self.near_got, self.far_got = near_got, far_got
        self.near = {}
        self.far = {}

    def start(self, item):
        place = self.place
        self.near[item] = [
            self.copies.remote(
                self.part.at[2 * side + 1 - place.inner, item],
                self.near_got.at[side, item],
                (place.b, place.near),
            )
            for side in (0, 1)
        ]

    def cross(self, item):
        place = self.place
        for copy in self.near[item]:
            self.copies.arrive(copy)
        other = self.part.at[2 * (1 - place.outer) + place.inner, item]
        added = other[...].astype(F32) + self.near_got[1 - place.outer, item].astype(F32)
        other[...] = added.astype(BF)
        self.far[item] = self.copies.remote(
            other, self.far_got.at[item], (place.b, place.far)
        )

    def finish(self, item):
        place = self.place
        self.copies.arrive(self.far[item])
        return (
            self.part[2 * place.outer + place.inner, item].astype(F32)
            + self.near_got[place.outer, item].astype(F32)
            + self.far_got[item].astype(F32)
        )


class CtxGather:
    def __init__(self, place, copies, everyone):
        self.place, self.copies, self.everyone = place, copies, everyone
        self.far = {}
        self.near = {}

    def start(self, item):
        place = self.place
        own = self.everyone.at[place.c, item]
        self.far[item] = self.copies.remote(own, own, (place.b, place.far))
        self.near[item] = [self.copies.remote(own, own, (place.b, place.near))]

    def cross(self, item):
        place = self.place
        self.copies.arrive(self.far[item])
        other = self.everyone.at[place.far, item]
        self.near[item].append(self.copies.remote(other, other, (place.b, place.near)))

    def finish(self, item):
        for copy in self.near[item]:
            self.copies.arrive(copy)


def greet_lines(place):
    devices = [place.up(), place.down(), (place.b, place.far), (place.b, place.near)]
    pl.semaphore_wait(greet(place, devices), 4)


def turn(values, cosine, sine):
    half_size = HD // 2
    front, back = values[:, :half_size], values[:, half_size:]
    return front * cosine - back * sine, back * cosine + front * sine


def softmax_rows(queries, keys, keep, score_scale):
    scores = dot_right_t(queries, keys) * score_scale
    rows = lax.broadcasted_iota(jnp.int32, scores.shape, 0)
    cols = lax.broadcasted_iota(jnp.int32, scores.shape, 1)
    masked = jnp.where((cols <= rows) & (keep > 0.5), scores, -1e30)
    raised = jnp.exp(masked - jnp.max(masked, axis=-1, keepdims=True))
    return raised / jnp.sum(raised, axis=-1, keepdims=True)


def attention_kernel(
    n_batch,
    heads,
    qkv_ref,
    rows_ref,
    cot_ref,
    up_ref,
    out_ref,
    cos_ref,
    sin_ref,
    keep_ref,
    attended,
    qkv_out,
    turned_out,
    mixed_out,
    rows_all,
    cot_all,
    qkv_v,
    up_v,
    out_v,
    turned_v,
    mixed_v,
    part_v,
    near_got,
    far_got,
    send_sems,
    recv_sems,
    load_sems,
):
    place = Place(n_batch)
    copies = Copies(send_sems, recv_sems)
    b, c = place.b, place.c
    micro, pos_dev = qkv_ref.shape[:2]
    n_tok = micro * pos_dev
    length = 4 * pos_dev
    score_scale = 1.0 / math.sqrt(HD)
    loads = [
        pltpu.make_async_copy(source, target, load_sems.at[i])
        for i, (source, target) in enumerate(
            [(qkv_ref, qkv_v.at[c]), (up_ref, up_v), (out_ref, out_v)]
        )
    ]
    for copy in loads:
        copy.start()
    greet_lines(place)
    loads[0].wait()
    qkv = CtxGather(place, copies, qkv_v)
    for item in range(micro):
        qkv.start(item)
    cot_own = copies.local(cot_ref, cot_all.at[b])
    rows_own = copies.local(rows_ref, rows_all.at[c, 0])
    copies.arrive(cot_own)
    cots = RingGather(place, copies, n_tok, lambda rank, rows: cot_all.at[rank, rows])
    cots.advance()
    copies.arrive(rows_own)
    rows = CtxGather(place, copies, rows_all)
    for item in range(micro):
        qkv.cross(item)
    rows.start(0)
    for copy in loads[1:]:
        copy.wait()
    attended_sum = CtxCollect(place, copies, part_v, near_got, far_got)
    cosine, sine = cos_ref[...], sin_ref[...]
    latent = qkv_v.shape[3] - 2 * HD
    for item in range(micro):
        qkv.finish(item)
        q_normed = qkv_v[:, item, :, :latent].reshape(length, latent)
        keys = qkv_v[:, item, :, latent : latent + HD].reshape(length, HD)
        values = qkv_v[:, item, :, latent + HD :].reshape(length, HD)
        keep = keep_ref[item]

        @pl.loop(0, heads)
        def _(head):
            cols = pl.ds(pl.multiple_of(head * HD, HD), HD)
            front, back = turn(dot(q_normed, up_v[:, cols]), cosine, sine)
            turned_v[item, :, pl.ds(pl.multiple_of(head * HD, HD), HD // 2)] = front.astype(BF)
            turned_v[item, :, pl.ds(pl.multiple_of(head * HD + HD // 2, HD // 2), HD // 2)] = (
                back.astype(BF)
            )
            weights = softmax_rows(turned_v[item, :, cols], keys, keep, score_scale)
            mixed = dot(weights.astype(BF), values).astype(BF)
            mixed_v[:, item, :, cols] = mixed.reshape(4, pos_dev, HD)

        if cots.step <= place.h:
            cots.advance()
        mixed = mixed_v[:, item].reshape(length, heads * HD)
        width = out_v.shape[1]

        @pl.loop(0, width // 512)
        def _(t):
            cols = pl.ds(pl.multiple_of(t * 512, 512), 512)
            part = dot(mixed, out_v[:, cols]).astype(BF)
            part_v[:, item, :, cols] = part.reshape(4, pos_dev, 512)

        attended_sum.start(item)
        if item > 0:
            attended_sum.cross(item - 1)
    copies.local(qkv_v, qkv_out)
    copies.local(turned_v, turned_out)
    copies.local(mixed_v, mixed_out)
    if cots.step <= place.h:
        cots.advance()
    attended_sum.cross(micro - 1)
    rows.cross(0)
    for item in range(micro):
        attended[item] = attended_sum.finish(item)
    while cots.step <= place.h:
        cots.advance()
    copies.drain()


def attention(n_batch, qkv, attn_in, grad_mo, own_qup, own_out, cos_all, sin_all, keep):
    micro, pos_dev, qkv_cols = qkv.shape
    n_tok, width = attn_in.shape
    latent, head_cols = own_qup.shape
    length = 4 * pos_dev
    sems = 2 * n_batch + 48
    anywhere = pl.BlockSpec(memory_space=pl.ANY)
    near = pl.BlockSpec(memory_space=pltpu.VMEM)
    return pl.pallas_call(
        functools.partial(attention_kernel, n_batch, head_cols // HD),
        out_shape=(
            jax.ShapeDtypeStruct((micro, pos_dev, width), F32),
            jax.ShapeDtypeStruct((4, micro, pos_dev, qkv_cols), BF),
            jax.ShapeDtypeStruct((micro, length, head_cols), BF),
            jax.ShapeDtypeStruct((4, micro, pos_dev, head_cols), BF),
            jax.ShapeDtypeStruct((4, 1, n_tok, width), BF),
            jax.ShapeDtypeStruct((n_batch, n_tok, width), BF),
        ),
        in_specs=[anywhere] * 5 + [near] * 3,
        out_specs=[near] + [anywhere] * 5,
        scratch_shapes=[
            pltpu.VMEM((4, micro, pos_dev, qkv_cols), BF),
            pltpu.VMEM((latent, head_cols), BF),
            pltpu.VMEM((head_cols, width), BF),
            pltpu.VMEM((micro, length, head_cols), BF),
            pltpu.VMEM((4, micro, pos_dev, head_cols), BF),
            pltpu.VMEM((4, micro, pos_dev, width), BF),
            pltpu.VMEM((2, micro, pos_dev, width), BF),
            pltpu.VMEM((micro, pos_dev, width), BF),
            pltpu.SemaphoreType.DMA((sems,)),
            pltpu.SemaphoreType.DMA((sems,)),
            pltpu.SemaphoreType.DMA((3,)),
        ],
        compiler_params=pltpu.CompilerParams(
            collective_id=3, has_side_effects=True, vmem_limit_bytes=40 * 1024 * 1024
        ),
        name="attention",
    )(qkv, attn_in, grad_mo, own_qup, own_out, cos_all, sin_all, keep)


def attention_back_kernel(
    n_batch,
    heads,
    has_terms,
    grad_ref,
    qkv_ref,
    turned_ref,
    mixed_ref,
    up_ref,
    out_ref,
    gu_ref,
    down_ref,
    *refs,
):
    terms_ref, refs = (refs[0], refs[1:]) if has_terms else (None, refs)
    (
        cos_ref,
        sin_ref,
        keep_ref,
        back_out,
        out_terms,
        up_terms,
        gu_grad,
        down_grad,
    ) = refs[:8]
    terms_sum, refs = (refs[8], refs[9:]) if has_terms else (None, refs[8:])
    (
        grad_v,
        qkv_v,
        turned_v,
        mixed_v,
        up_v,
        out_v,
        qgrad_v,
        kgrad_v,
        vgrad_v,
        part_v,
        near_got,
        far_got,
        outgrad_v,
        upgrad_v,
        down_v,
        send_sems,
        recv_sems,
        load_sems,
    ) = refs[:18]
    place = Place(n_batch)
    copies = Copies(send_sems, recv_sems)
    b, c, n = place.b, place.c, n_batch
    micro, pos_dev, width = grad_ref.shape
    length = 4 * pos_dev
    head_cols = heads * HD
    latent = qkv_ref.shape[3] - 2 * HD
    score_scale = 1.0 / math.sqrt(HD)
    pairs = [
        (grad_ref, grad_v.at[c]),
        (out_ref, out_v),
        (qkv_ref, qkv_v),
        (turned_ref, turned_v),
        (up_ref, up_v),
        (mixed_ref, mixed_v),
    ]
    if has_terms:
        terms_v, terms_got, ring_send, ring_recv = refs[18:]
        pairs.append((terms_ref, terms_v))
    loads = [
        pltpu.make_async_copy(source, target, load_sems.at[i])
        for i, (source, target) in enumerate(pairs)
    ]
    for copy in loads:
        copy.start()
    peers = [(lax.rem(b + k, n), c) for k in range(1, n)]
    others = peers + [(b, place.far), (b, place.near)]
    pl.semaphore_wait(greet(place, others), n + 1)
    loads[0].wait()
    grads = CtxGather(place, copies, grad_v)
    for item in range(micro):
        grads.start(item)
    steps = []
    if has_terms:

        def spot(step):
            return 0 if step == 0 else 1 if step == place.h else 2 * abs(step) + (step > 0)

        terms = RingCollect(
            place, lambda step: terms_v.at[spot(step)], terms_got, ring_send, ring_recv
        )
        loads[6].wait()
        steps = [terms.advance] * place.h

    def ring_step():
        if steps:
            steps.pop()()

    ring_step()
    copies.local(gu_ref.at[b], gu_grad.at[b])
    for peer in peers:
        copies.remote(gu_ref.at[peer[0]], gu_grad.at[b], peer)
    for item in range(micro):
        grads.cross(item)
    down_own = copies.local(down_ref.at[place.outer], down_v.at[0])
    down_far = copies.remote(down_ref.at[1 - place.outer], down_v.at[1], (b, place.far))
    for copy in loads[1:6]:
        copy.wait()
    back_sum = CtxCollect(place, copies, part_v, near_got, far_got)
    cosine, sine = cos_ref[...], sin_ref[...]
    for item in range(micro):
        grads.finish(item)
        incoming = grad_v[:, item].reshape(length, width)
        keys = qkv_v[:, item, :, latent : latent + HD].reshape(length, HD)
        values = qkv_v[:, item, :, latent + HD :].reshape(length, HD)
        keep = keep_ref[item]
        kgrad_v[...] = jnp.zeros_like(kgrad_v)
        vgrad_v[...] = jnp.zeros_like(vgrad_v)

        @pl.loop(0, heads)
        def _(head):
            cols = pl.ds(pl.multiple_of(head * HD, HD), HD)
            grad_mixed = dot_right_t(incoming, out_v[cols, :]).astype(BF)
            queries = turned_v[item, :, cols]
            weights = softmax_rows(queries, keys, keep, score_scale)
            grad_probs = dot_right_t(grad_mixed, values)
            row_dot = jnp.sum(weights * grad_probs, axis=-1, keepdims=True)
            grad_scores = (weights * (grad_probs - row_dot)).astype(BF)
            front, back = turn(dot(grad_scores, keys) * score_scale, cosine, -sine)
            front, back = front.astype(BF), back.astype(BF)
            base = pl.multiple_of(head * HD, HD)
            qgrad_v[:, item, :, pl.ds(base, HD // 2)] = front.reshape(4, pos_dev, HD // 2)
            base = pl.multiple_of(head * HD + HD // 2, HD // 2)
            qgrad_v[:, item, :, pl.ds(base, HD // 2)] = back.reshape(4, pos_dev, HD // 2)
            kgrad_v[...] += dot_left_t(grad_scores, queries) * score_scale
            vgrad_v[...] += dot_left_t(weights.astype(BF), grad_mixed)

        ring_step()
        qgrad = qgrad_v[:, item].reshape(length, head_cols)
        part_v[:, item, :, :latent] = (
            dot_right_t(qgrad, up_v[...]).astype(BF).reshape(4, pos_dev, latent)
        )
        part_v[:, item, :, latent : latent + HD] = (
            kgrad_v[...].astype(BF).reshape(4, pos_dev, HD)
        )
        part_v[:, item, :, latent + HD :] = vgrad_v[...].astype(BF).reshape(4, pos_dev, HD)
        back_sum.start(item)
        if item > 0:
            back_sum.cross(item - 1)
    n_all = 4 * micro * pos_dev
    out_rows = head_cols // n

    back_sum.cross(micro - 1)
    ring_step()

    @pl.loop(0, width // 512)
    def _(t):
        cols = pl.ds(pl.multiple_of(t * 512, 512), 512)
        term = dot_left_t(
            mixed_v[...].reshape(n_all, head_cols), grad_v[:, :, :, cols].reshape(n_all, 512)
        )
        outgrad_v[:, :, cols] = term.astype(BF).reshape(n, out_rows, 512)

    copies.local(outgrad_v, out_terms)
    for item in range(micro):
        back_out[item] = back_sum.finish(item)
    ring_step()

    @pl.loop(0, head_cols // HD)
    def _(t):
        cols = pl.ds(pl.multiple_of(t * HD, HD), HD)
        term = dot_left_t(
            qkv_v[:, :, :, :latent].reshape(n_all, latent),
            qgrad_v[:, :, :, cols].reshape(n_all, HD),
        )
        upgrad_v[:, :, cols] = term.astype(BF).reshape(n, latent // n, HD)

    copies.local(upgrad_v, up_terms)
    copies.arrive(down_own)
    copies.arrive(down_far)
    down_grad[...] = down_v[0].astype(F32) + down_v[1].astype(F32)
    if has_terms:
        while steps:
            ring_step()
        cut = terms.cut
        for half in (0, 1):
            terms_sum[half * cut : (half + 1) * cut, :] = terms.finish(half)
        terms.drain()
    copies.drain()


def attention_back(
    n_batch, grad_att, qkv_all, turned, mixed, own_qup, own_out, grad_gu, down_part, terms, tables
):
    micro, pos_dev, width = grad_att.shape
    n_tok = micro * pos_dev
    qkv_cols = qkv_all.shape[3]
    latent, head_cols = own_qup.shape
    length = 4 * pos_dev
    far = n_batch // 2
    has_terms = terms is not None
    sems = 2 * n_batch + 48
    anywhere = pl.BlockSpec(memory_space=pl.ANY)
    near = pl.BlockSpec(memory_space=pltpu.VMEM)
    out_shape = [
        jax.ShapeDtypeStruct((micro, pos_dev, qkv_cols), F32),
        jax.ShapeDtypeStruct((n_batch, head_cols // n_batch, width), BF),
        jax.ShapeDtypeStruct((n_batch, latent // n_batch, head_cols), BF),
        jax.ShapeDtypeStruct(grad_gu.shape, BF),
        jax.ShapeDtypeStruct(down_part.shape[1:], F32),
    ]
    out_specs = [near] + [anywhere] * 3 + [near]
    scratch = [
        pltpu.VMEM((4, micro, pos_dev, width), BF),
        pltpu.VMEM((4, micro, pos_dev, qkv_cols), BF),
        pltpu.VMEM((micro, length, head_cols), BF),
        pltpu.VMEM((4, micro, pos_dev, head_cols), BF),
        pltpu.VMEM((latent, head_cols), BF),
        pltpu.VMEM((head_cols, width), BF),
        pltpu.VMEM((4, micro, pos_dev, head_cols), BF),
        pltpu.VMEM((length, HD), F32),
        pltpu.VMEM((length, HD), F32),
        pltpu.VMEM((4, micro, pos_dev, qkv_cols), BF),
        pltpu.VMEM((2, micro, pos_dev, qkv_cols), BF),
        pltpu.VMEM((micro, pos_dev, qkv_cols), BF),
        pltpu.VMEM((n_batch, head_cols // n_batch, width), BF),
        pltpu.VMEM((n_batch, latent // n_batch, head_cols), BF),
        pltpu.VMEM(down_part.shape, BF),
        pltpu.SemaphoreType.DMA((sems,)),
        pltpu.SemaphoreType.DMA((sems,)),
        pltpu.SemaphoreType.DMA((7,)),
    ]
    args = [grad_att, qkv_all, turned, mixed, own_qup, own_out, grad_gu, down_part]
    if has_terms:
        args.append(terms)
        out_shape.append(jax.ShapeDtypeStruct((n_tok, width), F32))
        out_specs.append(near)
        scratch += [
            pltpu.VMEM(terms.shape, BF),
            pltpu.VMEM((far, 2, 2, n_tok // 2, width), BF),
            pltpu.SemaphoreType.DMA((far, 2, 2)),
            pltpu.SemaphoreType.DMA((far, 2, 2)),
        ]
    return pl.pallas_call(
        functools.partial(attention_back_kernel, n_batch, head_cols // HD, has_terms),
        out_shape=tuple(out_shape),
        in_specs=[anywhere] * len(args) + [near] * 3,
        out_specs=out_specs,
        scratch_shapes=scratch,
        compiler_params=pltpu.CompilerParams(
            collective_id=4, has_side_effects=True, vmem_limit_bytes=56 * 1024 * 1024
        ),
        name="attention_back",
    )(*args, *tables)


def permuted_mlp(ring, rows_own, cots, gu_rows, own_down):
    mlp_in = ring.spread(rows_own)
    n_tok, width = rows_own.shape
    _, n_batch, n_ctx, own_rows, ff = gu_rows.shape
    own_gate, own_up = gu_rows.reshape(2, width, ff)
    own_down = own_down.reshape(ff, width)
    far = ring.h
    groups = [[0]] + [[-step, step] for step in range(1, far)] + [[far]]
    out_terms = {}
    in_terms = {}
    kept = []
    for group in groups:
        rows = jnp.concatenate([mlp_in[step] for step in group], axis=0)
        grad_rows = jnp.concatenate([pick(cots, ring.rank_of(step)) for step in group], axis=0)
        gate_part = dot(rows, own_gate)
        up_part = dot(rows, own_up)
        sigmoid_gate = jax.nn.sigmoid(gate_part)
        silu_gate = gate_part * sigmoid_gate
        activated = (silu_gate * up_part).astype(BF)
        grad_act = dot_right_t(grad_rows, own_down)
        grad_gate = (
            grad_act * up_part * (sigmoid_gate * (1.0 + gate_part * (1.0 - sigmoid_gate)))
        ).astype(BF)
        grad_up = (grad_act * silu_gate).astype(BF)
        in_term = dot_right_t(grad_gate, own_gate) + dot_right_t(grad_up, own_up)
        out_term = dot(activated, own_down)
        for place_in, step in enumerate(group):
            cut = slice(place_in * n_tok, (place_in + 1) * n_tok)
            in_terms[step] = in_term[cut]
            out_terms[step] = out_term[cut]
        kept.append((rows, grad_rows, activated, grad_gate, grad_up))
    rows, grad_rows, activated, grad_gate, grad_up = (
        jnp.concatenate(items, axis=0) for items in zip(*kept)
    )
    grad_gu = jnp.stack([dot_left_t(rows, grad_gate), dot_left_t(rows, grad_up)])
    grad_gu = grad_gu.reshape(2, n_batch, n_ctx, own_rows, ff).transpose(2, 1, 0, 3, 4)
    grad_down = dot_left_t(activated, grad_rows)
    return (
        ring.collect(lambda step: in_terms[step]),
        near_collect(grad_down.reshape(n_ctx, ff // n_ctx, width)).astype(BF),
        out_terms,
        ctx_collect(grad_gu).astype(BF),
    )


def shards(
    tokens,
    cotangent,
    lengths,
    slot_sequence,
    proj_in,
    query_up,
    proj_out,
    attn_gain,
    query_gain,
    mlp_gain,
    gate_up,
    down_proj,
):
    n_ctx = lax.axis_size("ctx")
    n_batch = lax.axis_size("batch")
    ctx_rank = lax.axis_index("ctx")
    batch_rank = lax.axis_index("batch")
    ring = Ring()
    micro, pos_dev, width = tokens.shape
    n_tok = micro * pos_dev
    full_length = pos_dev * n_ctx
    heads = H // n_ctx
    score_scale = 1.0 / math.sqrt(HD)
    in_cols = proj_in.shape[1]

    slot_total = lengths.shape[0]
    slot_ids = jnp.arange(slot_total, dtype=jnp.int32)
    seq_lengths = jnp.sum(
        jnp.where(slot_sequence[:, None] == slot_ids[None, :], lengths[None, :], 0), axis=1
    )
    own_lengths = lax.dynamic_slice_in_dim(seq_lengths, batch_rank * micro, micro)
    query_pos = ctx_rank * pos_dev + jnp.arange(pos_dev, dtype=jnp.int32)
    key_pos = jnp.arange(full_length, dtype=jnp.int32)
    cos_all, sin_all = rope_tables(key_pos)
    cos_own, sin_own = rope_tables(query_pos)

    own_rows = proj_in.shape[0]
    gain_rows = query_gain.shape[0]
    gains = jnp.stack(
        [attn_gain, mlp_gain, jnp.pad(query_gain, (0, own_rows - gain_rows))], axis=1
    )
    packed = jnp.concatenate([proj_in, jnp.pad(gains, ((0, 0), (0, 125)))], axis=1)
    ff_all = gate_up.shape[1] // 2
    ff = ff_all // n_batch
    packed, own_qup, own_out, gu_rows, own_down = spread_weights(
        n_batch, packed, query_up, proj_out, gate_up, down_proj
    )
    packed = packed.reshape(width, in_cols + 128)
    own_qup = own_qup.reshape(QR, heads * HD)
    own_out = own_out.reshape(heads * HD, width)
    full_in = packed[:, :in_cols]
    gains = packed[:, in_cols : in_cols + 3].T.astype(F32)
    gain_norm = gains[0]
    gain_mlp = gains[1]
    gain_query = gains[2].reshape(n_batch * n_ctx, own_rows)[:, :gain_rows].reshape(QR)

    residual = tokens.reshape(n_tok, width).astype(F32)
    valid_rows = (query_pos[None, :] < own_lengths[:, None]).astype(F32).reshape(n_tok, 1)
    grad_out = cotangent.reshape(n_tok, width).astype(F32) * valid_rows
    scale_one = rms_scale(residual)
    normed_one = residual * scale_one
    attn_in = (normed_one * gain_norm).astype(BF)
    projected = dot(attn_in, full_in)
    q_latent = projected[:, :QR]
    scale_query = rms_scale(q_latent)
    normed_query = q_latent * scale_query
    q_normed = (normed_query * gain_query).astype(BF)
    k_rot = rotate(
        projected[:, QR : QR + HD].reshape(micro, pos_dev, HD), cos_own, sin_own
    ).astype(BF)
    v_low = projected[:, QR + HD :].astype(BF)
    qkv = jnp.concatenate([q_normed, k_rot.reshape(n_tok, HD), v_low], axis=1)
    keep = (key_pos[None, None, :] < own_lengths[:, None, None]).astype(F32)
    attended, qkv_all, turned, mixed, attn_in_all, cots = attention(
        n_batch,
        qkv.reshape(micro, pos_dev, in_cols),
        attn_in,
        grad_out.astype(BF),
        own_qup,
        own_out,
        cos_all,
        sin_all,
        keep,
    )
    hidden_res = residual + attended.reshape(n_tok, width)

    scale_two = rms_scale(hidden_res)
    normed_two = hidden_res * scale_two
    mlp_in = (normed_two * gain_mlp).astype(BF)
    resident = 10 * n_batch * n_tok * width <= 24 * 1024 * 1024
    if resident:
        grad_mlp_in, down_part, terms, grad_gu_own = fused_mlp(
            n_batch, mlp_in, cots, gu_rows[0], gu_rows[1], own_down
        )
        terms = terms.reshape(n_batch, n_tok, width)
    else:
        terms = None
        grad_mlp_in, down_part, out_terms, grad_gu_own = permuted_mlp(
            ring, mlp_in, cots, gu_rows, own_down
        )
    gain_mlp_term = jnp.sum(grad_mlp_in * normed_two, axis=0)
    grad_hidden = grad_out + norm_back(grad_mlp_in * gain_mlp, normed_two, scale_two)
    back_own, out_grads, up_grads, grad_gu_own, grad_down, *sums = attention_back(
        n_batch,
        grad_hidden.astype(BF).reshape(micro, pos_dev, width),
        qkv_all,
        turned,
        mixed,
        own_qup,
        own_out,
        grad_gu_own,
        down_part,
        terms,
        (cos_all, sin_all, keep),
    )
    out_sum = sums[0] if resident else ring.collect(lambda step: out_terms[step])
    layer_out = hidden_res + out_sum
    back_own = back_own.reshape(n_tok, in_cols)
    grad_qn = back_own[:, :QR]
    gain_query_term = jnp.sum(grad_qn * normed_query, axis=0)
    grad_latent = norm_back(grad_qn * gain_query, normed_query, scale_query)
    grad_key_raw = rotate_back(
        back_own[:, QR : QR + HD].reshape(micro, pos_dev, HD), cos_own, sin_own
    ).reshape(n_tok, HD)
    grad_project = jnp.concatenate(
        [grad_latent, grad_key_raw, back_own[:, QR + HD :]], axis=1
    ).astype(BF)
    grad_attn_in = dot_right_t(grad_project, full_in)
    gain_norm_term = jnp.sum(grad_attn_in * normed_one, axis=0)
    grad_tokens = grad_hidden + norm_back(grad_attn_in * gain_norm, normed_one, scale_one)

    part_cols = in_cols // n_ctx
    project_parts = grad_project.reshape(n_tok, n_ctx, part_cols).swapaxes(0, 1)
    gain_terms = jnp.stack(
        [
            gain_norm_term.reshape(n_batch, n_ctx, own_rows),
            gain_mlp_term.reshape(n_batch, n_ctx, own_rows),
            jnp.pad(
                gain_query_term.reshape(n_batch, n_ctx, gain_rows),
                ((0, 0), (0, 0), (0, own_rows - gain_rows)),
            ),
        ],
        axis=2,
    )
    gain_terms = jnp.pad(gain_terms, ((0, 0), (0, 0), (0, 13), (0, part_cols - own_rows)))
    grad_proj_out, grad_query_up, grad_proj_in, gain_sums, grad_gate_up = collect_weights(
        n_batch,
        gain_rows,
        out_grads,
        up_grads,
        project_parts,
        attn_in_all,
        grad_gu_own,
        gain_terms.astype(BF),
    )
    gain_sums = gain_sums[:, :own_rows]

    return (
        layer_out.reshape(tokens.shape).astype(BF),
        grad_tokens.reshape(tokens.shape).astype(BF),
        grad_proj_in,
        grad_query_up,
        grad_proj_out,
        gain_sums[0],
        gain_sums[2, :gain_rows],
        gain_sums[1],
        grad_gate_up,
        grad_down,
    )


def solution(mesh):
    rows = P(("batch", "ctx"), None)
    vector = P(("batch", "ctx"))
    acts = P("batch", "ctx", None)
    return jax.shard_map(
        shards,
        mesh=mesh,
        in_specs=(acts, acts, P(), P(), rows, rows, rows, vector, vector, vector, rows, rows),
        out_specs=(acts, acts, rows, rows, rows, vector, vector, vector, rows, rows),
        check_vma=False,
    )
```

```python
import functools
import math

import jax
import jax.numpy as jnp
from jax import lax
from jax.experimental import pallas as pl
from jax.experimental.pallas import tpu as pltpu
from jax.sharding import PartitionSpec as P

H = 16
HD = 256
QR = 1024
EPSILON = 1e-06
BF = jnp.bfloat16
F32 = jnp.float32


def rms_scale(values):
    return lax.rsqrt(jnp.mean(values * values, axis=-1, keepdims=True) + EPSILON)


def rope_tables(positions):
    half_size = HD // 2
    frequency = 10000.0 ** (-(jnp.arange(half_size, dtype=F32) * 2.0 / HD))
    angles = positions.astype(F32)[:, None] * frequency[None, :]
    return (jnp.cos(angles), jnp.sin(angles))


def rotate(values, cosine_table, sine_table):
    half_size = values.shape[-1] // 2
    front_half = values[..., :half_size]
    back_half = values[..., half_size:]
    return jnp.concatenate(
        [
            front_half * cosine_table - back_half * sine_table,
            back_half * cosine_table + front_half * sine_table,
        ],
        axis=-1,
    )


def rotate_back(values, cosine_table, sine_table):
    return rotate(values, cosine_table, -sine_table)


def dot(left_side, right_side):
    return jnp.dot(left_side, right_side, preferred_element_type=F32)


def dot_right_t(left_side, right_side):
    return lax.dot_general(
        left_side, right_side, (((1,), (1,)), ((), ())), preferred_element_type=F32
    )


def dot_left_t(left_side, right_side):
    return lax.dot_general(
        left_side, right_side, (((0,), (0,)), ((), ())), preferred_element_type=F32
    )


def norm_back(grad_normed, normed, inv_rms):
    return inv_rms * (grad_normed - normed * jnp.mean(grad_normed * normed, axis=-1, keepdims=True))


def pick(array, index, axis=0):
    return lax.dynamic_index_in_dim(array, index, axis, keepdims=False)


def place(array, block, index, axis=0):
    return lax.dynamic_update_index_in_dim(array, block, index, axis)


class Ring:
    def __init__(self):
        self.n = lax.axis_size("batch")
        self.h = self.n // 2
        rank = lax.axis_index("batch")
        self.at = jnp.where(rank % 2 == 0, rank // 2, self.n - 1 - rank // 2)
        order = [2 * i for i in range(self.h)] + [2 * i + 1 for i in reversed(range(self.h))]
        self.up = [(order[i], order[(i + 1) % self.n]) for i in range(self.n)]
        self.down = [(there, here) for here, there in self.up]

    def rank_of(self, step):
        spot = (self.at + step) % self.n
        return jnp.where(spot < self.h, 2 * spot, 2 * (self.n - 1 - spot) + 1)

    def spread(self, block):
        found = {0: block}
        upward = downward = block
        for step in range(1, self.h):
            upward = lax.ppermute(upward, "batch", self.up)
            downward = lax.ppermute(downward, "batch", self.down)
            found[-step] = upward
            found[step] = downward
        cut = block.shape[0] // 2
        found[self.h] = jnp.concatenate(
            [
                lax.ppermute(upward[:cut], "batch", self.up),
                lax.ppermute(downward[cut:], "batch", self.down),
            ],
            axis=0,
        )
        return found

    def gather(self, block):
        found = self.spread(block)
        whole = jnp.zeros((self.n,) + block.shape, block.dtype)
        for step, part in found.items():
            whole = place(whole, part, self.rank_of(step))
        return whole

    def collect(self, term):
        far = term(self.h)
        cut = far.shape[0] // 2
        downward = lax.ppermute(far[:cut].astype(BF), "batch", self.down)
        upward = lax.ppermute(far[cut:].astype(BF), "batch", self.up)
        for step in range(self.h - 1, 0, -1):
            for_lower = term(-step).astype(F32)
            for_upper = term(step).astype(F32)
            if step == self.h - 1:
                for_lower = jnp.concatenate(
                    [for_lower[:cut] + downward.astype(F32), for_lower[cut:]], axis=0
                )
                for_upper = jnp.concatenate(
                    [for_upper[:cut], for_upper[cut:] + upward.astype(F32)], axis=0
                )
            else:
                for_lower = for_lower + downward.astype(F32)
                for_upper = for_upper + upward.astype(F32)
            downward = lax.ppermute(for_lower.astype(BF), "batch", self.down)
            upward = lax.ppermute(for_upper.astype(BF), "batch", self.up)
        own = term(0).astype(F32)
        return own + downward.astype(F32) + upward.astype(F32)

    def collect_rows(self, stacked):
        return self.collect(lambda step: pick(stacked, self.rank_of(step)))


FAR = [(0, 2), (1, 3), (2, 0), (3, 1)]
NEAR = [(0, 1), (1, 0), (2, 3), (3, 2)]


def ctx_place():
    rank = lax.axis_index("ctx")
    return rank // 2, rank % 2


def in_order(mine, theirs, at):
    return jnp.where(at == 0, jnp.stack([mine, theirs]), jnp.stack([theirs, mine]))


def ctx_gather(block):
    outer, inner = ctx_place()
    pair = in_order(block, lax.ppermute(block, "ctx", FAR), outer)
    whole = in_order(pair, lax.ppermute(pair, "ctx", NEAR), inner)
    whole = jnp.swapaxes(whole, 0, 1)
    return whole.reshape((4,) + block.shape)


def near_collect(stacked):
    _, inner = ctx_place()
    parts = stacked.reshape((2, 2) + stacked.shape[1:])
    got = lax.ppermute(pick(parts, 1 - inner, 1).astype(BF), "ctx", NEAR)
    return pick(parts, inner, 1).astype(F32) + got.astype(F32)


def ctx_collect(stacked):
    outer, _ = ctx_place()
    half = near_collect(stacked)
    got = lax.ppermute(pick(half, 1 - outer).astype(BF), "ctx", FAR)
    return pick(half, outer) + got.astype(F32)


def ctx_exchange(stacked):
    outer, inner = ctx_place()
    parts = stacked.reshape((2, 2) + stacked.shape[1:])
    got = lax.ppermute(pick(parts, 1 - outer), "ctx", FAR)
    parts = in_order(pick(parts, outer), got, outer)
    got = lax.ppermute(pick(parts, 1 - inner, 1), "ctx", NEAR)
    whole = in_order(pick(parts, inner, 1), got, inner)
    return jnp.swapaxes(whole, 0, 1).reshape(stacked.shape)


MESH = pl.DeviceIdType.MESH


class Place:
    def __init__(self, n_batch):
        self.n = n_batch
        self.h = n_batch // 2
        self.b = lax.axis_index("batch")
        self.c = lax.axis_index("ctx")
        self.outer = lax.div(self.c, 2)
        self.inner = lax.rem(self.c, 2)
        self.far = lax.rem(self.c + 2, 4)
        self.near = self.c + 1 - 2 * self.inner
        odd = lax.rem(self.b, 2)
        half = lax.div(self.b, 2)
        self.at = half + odd * (self.n - 1 - 2 * half)

    def rank_of(self, step):
        spot = lax.rem(self.at + step + 2 * self.n, self.n)
        back = lax.div(spot, self.h)
        return (1 - back) * 2 * spot + back * (2 * (self.n - 1 - spot) + 1)

    def up(self):
        return (self.rank_of(1), self.c)

    def down(self):
        return (self.rank_of(-1), self.c)


class Copies:
    def __init__(self, send_sems, recv_sems):
        self.send_sems = send_sems
        self.recv_sems = recv_sems
        self.count = 0
        self.open_sends = []
        self.open_recvs = []

    def remote(self, source, target, device):
        index = self.count
        self.count += 1
        copy = pltpu.make_async_remote_copy(
            src_ref=source,
            dst_ref=target,
            send_sem=self.send_sems.at[index],
            recv_sem=self.recv_sems.at[index],
            device_id=device,
            device_id_type=MESH,
        )
        copy.start()
        self.open_sends.append(copy)
        self.open_recvs.append(copy)
        return copy

    def local(self, source, target):
        index = self.count
        self.count += 1
        copy = pltpu.make_async_copy(source, target, self.recv_sems.at[index])
        copy.start()
        self.open_recvs.append(copy)
        return copy

    def arrive(self, copy):
        if any(copy is other for other in self.open_recvs):
            self.open_recvs = [other for other in self.open_recvs if other is not copy]
            if any(copy is other for other in self.open_sends):
                copy.wait_recv()
            else:
                copy.wait()

    def drain(self):
        for copy in list(self.open_recvs):
            self.arrive(copy)
        for copy in self.open_sends:
            copy.wait_send()


def greet(place, others):
    barrier = pltpu.get_barrier_semaphore()
    for device in others:
        pl.semaphore_signal(barrier, inc=1, device_id=device, device_id_type=MESH)
    return barrier


class RingGather:
    def __init__(self, place, copies, rows, slot):
        self.place, self.copies, self.rows, self.slot = place, copies, rows, slot
        self.step = 0
        self.moving = ()

    def advance(self):
        place, copies = self.place, self.copies
        for copy in self.moving:
            copies.arrive(copy)
        self.moving = ()
        self.step += 1
        cut = self.rows // 2
        if self.step > place.h:
            return
        lower = place.rank_of(1 - self.step)
        upper = place.rank_of(self.step - 1)
        if self.step < place.h:
            whole = pl.ds(0, self.rows)
            pieces = (whole, whole)
        else:
            pieces = (pl.ds(0, cut), pl.ds(cut, self.rows - cut))
        upward, downward = self.slot(lower, pieces[0]), self.slot(upper, pieces[1])
        self.moving = (
            copies.remote(upward, upward, place.up()),
            copies.remote(downward, downward, place.down()),
        )

    def arrived(self):
        step = self.step - 1
        if step == 0:
            return []
        if step == self.place.h:
            return [self.place.rank_of(step)]
        return [self.place.rank_of(-step), self.place.rank_of(step)]


def mlp_kernel(
    n_batch,
    rows_ref,
    gu_ref,
    down_ref,
    cot_ref,
    *refs,
):
    (
        sum_ref,
        down_part,
        term_out,
        gu_out,
        rows_v,
        cot_v,
        gate_v,
        up_v,
        down_v,
        act_v,
        ggate_v,
        gup_v,
        in_v,
        term_v,
        got_v,
        gu_got,
        gu_last,
        down_got,
        send_sems,
        recv_sems,
        back_send,
        back_recv,
        load_sems,
        store_sems,
        part_send,
        part_recv,
    ) = refs
    place = Place(n_batch)
    far = place.h
    n_tok = rows_ref.shape[0]
    cut = n_tok // 2
    width = rows_ref.shape[1]
    ff = gu_ref.shape[-1]
    up_device, down_device = place.up(), place.down()
    far_device, near_device = (place.b, place.far), (place.b, place.near)
    barrier = greet(place, [up_device, down_device, far_device, near_device])
    parts = Copies(part_send, part_recv)
    own_rows = gate_v.shape[2]
    block = 4 * own_rows

    load_rows = pltpu.make_async_copy(rows_ref, rows_v.at[0, pl.ds(0, n_tok)], load_sems.at[0])
    load_rows.start()
    loads = [
        pltpu.make_async_copy(source, target, load_sems.at[1 + i])
        for i, (source, target) in enumerate(
            [(gu_ref.at[0], gate_v), (gu_ref.at[1], up_v), (down_ref, down_v)]
        )
    ]
    spots = [(0, 0, 0), (far, 0, 1)]
    spots += [(side * step, step, (side + 1) // 2) for step in range(1, far) for side in (-1, 1)]
    for i, (distance, group, side) in enumerate(spots):
        loads.append(
            pltpu.make_async_copy(
                cot_ref.at[place.rank_of(distance)], cot_v.at[group, pl.ds(side * n_tok, n_tok)], load_sems.at[4 + i]
            )
        )
    for copy in loads:
        copy.start()
    load_rows.wait()
    pl.semaphore_wait(barrier, 4)

    def piece(side, half):
        return pl.ds(side * n_tok + half * cut, cut)

    def hop(step, side, half):
        source_group, source_side = step - 1, side
        target_group, target_side = step, side
        if isinstance(step, int) and step == 1:
            source_side = 0
        if isinstance(step, int) and step == far:
            target_group, target_side = 0, 1
        return pltpu.make_async_remote_copy(
            src_ref=rows_v.at[source_group, piece(source_side, half)],
            dst_ref=rows_v.at[target_group, piece(target_side, half)],
            send_sem=send_sems.at[step, side, half],
            recv_sem=recv_sems.at[step, side, half],
            device_id=down_device if side else up_device,
            device_id_type=MESH,
        )

    both = [(side, half) for half in (0, 1) for side in (0, 1)]
    ends = [(0, 0), (1, 1)]
    for side, half in both:
        hop(1, side, half).start()
    for copy in loads:
        copy.wait()

    def stores(group):
        return [
            pltpu.make_async_copy(term_v.at[group], term_out.at[group], store_sems.at[0, group])
        ]

    def compute(group):
        rows = rows_v[group]
        cots = cot_v[group]
        down_all = down_v[...].reshape(ff, width)
        start = 0
        while start < ff:
            size = min(256, ff - start)
            tile = slice(start, start + size)
            gate = dot(rows, gate_v[..., tile].reshape(width, size))
            up = dot(rows, up_v[..., tile].reshape(width, size))
            grad_act = dot_right_t(cots, down_all[tile])
            sigmoid = 1.0 / (1.0 + jnp.exp(-gate))
            silu = gate * sigmoid
            act_v[group, :, tile] = (silu * up).astype(BF)
            slope = sigmoid * (1.0 + gate * (1.0 - sigmoid))
            ggate_v[group, :, tile] = (grad_act * up * slope).astype(BF)
            gup_v[group, :, tile] = (grad_act * silu).astype(BF)
            start += size
        ggate = ggate_v[group]
        gup = gup_v[group]
        act = act_v[group]
        tile_cols = 2 * block

        @pl.loop(0, width // tile_cols)
        def _(t):
            cols = pl.ds(pl.multiple_of(t * tile_cols, tile_cols), tile_cols)
            back = dot_right_t(ggate, gate_v[pl.ds(2 * t, 2)].reshape(tile_cols, ff))
            back += dot_right_t(gup, up_v[pl.ds(2 * t, 2)].reshape(tile_cols, ff))
            in_v[group, :, cols] = back.astype(BF)
            down = down_v[:, :, cols].reshape(ff, tile_cols)
            term_v[group, :, cols] = dot(act, down).astype(BF)

        for copy in stores(group):
            copy.start()

    @pl.loop(1, far)
    def _(step):
        for side, half in both:
            hop(step, side, half).wait_recv()

        @pl.when(step < far - 1)
        def _():
            for side, half in both:
                hop(step + 1, side, half).start()

        @pl.when(step == far - 1)
        def _():
            for side, half in ends:
                hop(far, side, half).start()

        compute(step)

    for side, half in ends:
        hop(far, side, half).wait_recv()
    compute(0)

    def back_hop(step, side, half, source):
        return pltpu.make_async_remote_copy(
            src_ref=source,
            dst_ref=got_v.at[step, side, half],
            send_sem=back_send.at[step, side, half],
            recv_sem=back_recv.at[step, side, half],
            device_id=up_device if side else down_device,
            device_id_type=MESH,
        )

    def held(step, side, half):
        return in_v.at[step, piece(side, half)]

    for side, half in ends:
        back_hop(far - 1, side, half, held(0, 1, half)).start()

    def pass_on(step, side, half, added):
        own = held(step, side, half)
        if added:
            back_hop(step, side, half, own).wait_recv()
            own[...] = (own[...].astype(F32) + got_v[step, side, half].astype(F32)).astype(BF)
        back_hop(step - 1, side, half, own).start()

    for side, half in both:
        if (side, half) not in ends:
            pass_on(far - 1, side, half, False)

    def gate_up_terms(t):
        cols = slice(t * 2 * block, (t + 1) * 2 * block)
        rows = rows_v[:, :, cols].reshape(n_batch * n_tok, 2 * block)
        for target, grads in ((gate_v, ggate_v), (up_v, gup_v)):
            term = dot_left_t(rows, grads[...].reshape(n_batch * n_tok, ff))
            target[2 * t : 2 * t + 2] = term.astype(BF).reshape(2, 4, own_rows, ff)

    def down_terms():
        @pl.loop(0, width // (2 * block))
        def _(t):
            cols = pl.ds(pl.multiple_of(t * 2 * block, 2 * block), 2 * block)
            grads = cot_v[:, :, cols].reshape(n_batch * n_tok, 2 * block)
            term = dot_left_t(act_v[...].reshape(n_batch * n_tok, ff), grads)
            down_v[:, :, cols] = term.astype(BF).reshape(4, ff // 4, 2 * block)

    def pass_all(step):
        for side, half in [(1, 0), (0, 1), (0, 0), (1, 1)]:
            if step < far - 1 or (side, half) in ends:
                pass_on(step, side, half, True)

    steps = list(range(1, far))
    outer, inner = place.outer, place.inner
    kinds = list(enumerate((gate_v, up_v)))
    near_copies, far_copies = {}, {}

    def send_near(t):
        pair = pl.ds(2 * t, 2)
        near_copies[t] = [
            parts.remote(
                target.at[pair, 2 * side + 1 - inner], gu_got.at[kind, side, pair], near_device
            )
            for side in (0, 1)
            for kind, target in kinds
        ]

    def send_far(t):
        pair = pl.ds(2 * t, 2)
        for copy in near_copies[t]:
            parts.arrive(copy)
        far_copies[t] = []
        for kind, target in kinds:
            other = target.at[pair, 2 * (1 - outer) + inner]
            added = other[...].astype(F32) + gu_got[kind, 1 - outer, pair].astype(F32)
            other[...] = added.astype(BF)
            far_copies[t].append(parts.remote(other, gu_last.at[kind, pair], far_device))

    def take_far(t):
        pair = pl.ds(2 * t, 2)
        for copy in far_copies[t]:
            parts.arrive(copy)
        for kind, target in kinds:
            kept = target.at[pair, 2 * outer + inner]
            added = kept[...].astype(F32) + gu_got[kind, outer, pair].astype(F32)
            kept[...] = (added + gu_last[kind, pair].astype(F32)).astype(BF)
            parts.local(kept, gu_out.at[pair, kind])

    def ring_step():
        if steps:
            pass_all(steps.pop())

    tiles = width // (2 * block)
    for t in range(tiles):
        gate_up_terms(t)
        send_near(t)
        if t > 0:
            send_far(t - 1)
        ring_step()
    while steps:
        ring_step()
    send_far(tiles - 1)
    down_terms()
    down_copies = [
        parts.remote(down_v.at[2 * side + 1 - inner], down_got.at[side], near_device)
        for side in (0, 1)
    ]
    for half in (0, 1):
        for side in (0, 1):
            back_hop(0, side, half, held(0, 0, half)).wait_recv()
        rows = slice(half * cut, (half + 1) * cut)
        sum_ref[rows, :] = (
            in_v[0, rows, :].astype(F32)
            + got_v[0, 0, half].astype(F32)
            + got_v[0, 1, half].astype(F32)
        )
    for side in (0, 1):
        parts.arrive(down_copies[side])
        added = down_v[2 * side + inner].astype(F32) + down_got[side].astype(F32)
        down_got[side] = added.astype(BF)
    parts.local(down_got, down_part)
    for t in range(tiles):
        take_far(t)
    parts.drain()

    for step in range(1, far + 1):
        for side, half in both if step < far else ends:
            hop(step, side, half).wait_send()
    for side, half in ends:
        back_hop(far - 1, side, half, held(0, 1, half)).wait_send()
    for step in range(far - 1, 0, -1):
        for side, half in both:
            back_hop(step - 1, side, half, held(step, side, half)).wait_send()
    for group in range(far):
        for copy in stores(group):
            copy.wait()


def fused_mlp(n_batch, rows, cots, gu_rows, own_down):
    n_tok, width = rows.shape
    ff = gu_rows.shape[-1]
    own_rows = gu_rows.shape[3]
    far = n_batch // 2
    pair = 2 * n_tok
    flops = 18 * n_batch * n_tok * width * ff
    return pl.pallas_call(
        functools.partial(mlp_kernel, n_batch),
        out_shape=(
            jax.ShapeDtypeStruct((n_tok, width), F32),
            jax.ShapeDtypeStruct((2, ff // 4, width), BF),
            jax.ShapeDtypeStruct((far, pair, width), BF),
            jax.ShapeDtypeStruct((n_batch, 2, own_rows, ff), BF),
        ),
        in_specs=[pl.BlockSpec(memory_space=pl.ANY)] * 4,
        out_specs=[pl.BlockSpec(memory_space=pltpu.VMEM)]
        + [pl.BlockSpec(memory_space=pl.ANY)] * 3,
        scratch_shapes=[
            pltpu.VMEM((far, pair, width), BF),
            pltpu.VMEM((far, pair, width), BF),
            pltpu.VMEM((n_batch, 4, own_rows, ff), BF),
            pltpu.VMEM((n_batch, 4, own_rows, ff), BF),
            pltpu.VMEM((4, ff // 4, width), BF),
            pltpu.VMEM((far, pair, ff), BF),
            pltpu.VMEM((far, pair, ff), BF),
            pltpu.VMEM((far, pair, ff), BF),
            pltpu.VMEM((far, pair, width), BF),
            pltpu.VMEM((far, pair, width), BF),
            pltpu.VMEM((far, 2, 2, n_tok // 2, width), BF),
            pltpu.VMEM((2, 2, n_batch, own_rows, ff), BF),
            pltpu.VMEM((2, n_batch, own_rows, ff), BF),
            pltpu.VMEM((2, ff // 4, width), BF),
            pltpu.SemaphoreType.DMA((far + 1, 2, 2)),
            pltpu.SemaphoreType.DMA((far + 1, 2, 2)),
            pltpu.SemaphoreType.DMA((far, 2, 2)),
            pltpu.SemaphoreType.DMA((far, 2, 2)),
            pltpu.SemaphoreType.DMA((4 + n_batch,)),
            pltpu.SemaphoreType.DMA((1, far)),
            pltpu.SemaphoreType.DMA((72,)),
            pltpu.SemaphoreType.DMA((72,)),
        ],
        compiler_params=pltpu.CompilerParams(
            collective_id=1, has_side_effects=True, vmem_limit_bytes=60 * 1024 * 1024
        ),
        cost_estimate=pl.CostEstimate(
            flops=flops, bytes_accessed=24 * 1024 * 1024, transcendentals=n_batch * n_tok * ff
        ),
        name="fused_mlp",
    )(rows, gu_rows, own_down, cots)


class RingCollect:
    def __init__(self, place, block, got, send_sems, recv_sems):
        self.place, self.block, self.got = place, block, got
        self.send_sems, self.recv_sems = send_sems, recv_sems
        self.cut = got.shape[3]
        self.step = place.h
        self.sent = []

    def held(self, step, half):
        return self.block(step).at[pl.ds(half * self.cut, self.cut)]

    def hop(self, step, side, half, source):
        place = self.place
        return pltpu.make_async_remote_copy(
            src_ref=source,
            dst_ref=self.got.at[step, side, half],
            send_sem=self.send_sems.at[step, side, half],
            recv_sem=self.recv_sems.at[step, side, half],
            device_id=place.up() if side else place.down(),
            device_id_type=MESH,
        )

    def send(self, step, side, half, source):
        copy = self.hop(step, side, half, source)
        copy.start()
        self.sent.append(copy)

    def advance(self):
        far = self.place.h
        step = self.step
        self.step -= 1
        if step == far:
            for side in (0, 1):
                self.send(far - 1, side, side, self.held(far, side))
            for side in (0, 1):
                half = 1 - side
                self.send(far - 2, side, half, self.held((2 * side - 1) * (far - 1), half))
            return
        pieces = [(0, 0), (1, 1)] if step == far - 1 else [(1, 0), (0, 1), (0, 0), (1, 1)]
        for side, half in pieces:
            own = self.held((2 * side - 1) * step, half)
            self.hop(step, side, half, own).wait_recv()
            own[...] = (own[...].astype(F32) + self.got[step, side, half].astype(F32)).astype(BF)
            self.send(step - 1, side, half, own)

    def finish(self, half):
        own = self.held(0, half)
        for side in (0, 1):
            self.hop(0, side, half, own).wait_recv()
        return (
            own[...].astype(F32)
            + self.got[0, 0, half].astype(F32)
            + self.got[0, 1, half].astype(F32)
        )

    def drain(self):
        for copy in self.sent:
            copy.wait_send()


def tail_kernel(
    n_batch,
    gain_rows,
    out_ref,
    up_ref,
    project_ref,
    rows_ref,
    gu_ref,
    gain_ref,
    out_grad,
    up_grad,
    in_grad,
    gain_grad,
    gu_grad,
    out_v,
    up_v,
    in_v,
    out_got,
    up_got,
    in_got,
    up_sum,
    up_all,
    in_sum,
    in_all,
    ring_send,
    ring_recv,
    send_sems,
    recv_sems,
    project_v,
    rows_v,
    gu_v,
    load_sems,
):
    place = Place(n_batch)
    copies = Copies(send_sems, recv_sems)
    b, c, n = place.b, place.c, n_batch
    own_rows = in_grad.shape[0]
    group = HeadGroup(place, out_grad.shape[0])
    ctx_peers = [(b, place.far), (b, place.near), (b, lax.rem(place.near + 2, 4))]

    loads = [
        pltpu.make_async_copy(held, kept, load_sems.at[i])
        for i, (held, kept) in enumerate([(out_ref, out_v), (up_ref, up_v), (rows_ref, rows_v), (gu_ref, gu_v)])
    ]
    for copy in loads:
        copy.start()
    barrier = greet(place, [place.up(), place.down()] + ctx_peers)

    pl.semaphore_wait(barrier, 5)

    rings = []
    for i, (kept, got) in enumerate([(out_v, out_got), (up_v, up_got), (in_v, in_got)]):
        rings.append(
            RingCollect(
                place,
                lambda step, kept=kept: kept.at[place.rank_of(step)],
                got,
                ring_send.at[i],
                ring_recv.at[i],
            )
        )
    part_cols = project_ref.shape[2]
    project_copies = [
        copies.remote(project_ref.at[peer[1]], project_v.at[c], peer) for peer in ctx_peers
    ]
    project_copies.append(copies.local(project_ref.at[c], project_v.at[c]))
    for copy, ring in zip(loads[:2], rings):
        copy.wait()
        ring.advance()
    for copy in project_copies:
        copies.arrive(copy)
    loads[2].wait()
    project = project_v[...].reshape(-1, part_cols)
    part_rows = own_rows + 16
    n_all = project.shape[0]
    width = rows_ref.shape[3]
    ahead = max(1, 256 // (4 * own_rows))
    chunk = ahead * 4 * own_rows

    @pl.loop(0, width // chunk)
    def _(t):
        cols = pl.ds(pl.multiple_of(t * chunk, chunk), chunk)
        term = dot_left_t(rows_v[:, :, :, cols].reshape(n_all, chunk), project).astype(BF)
        term = term.reshape(ahead, 4, own_rows, part_cols)
        for part in range(4):
            in_v[pl.ds(t * ahead, ahead), pl.ds(part * part_rows, own_rows), :] = term[:, part]

    for part in range(4):
        in_v[:, part * part_rows + own_rows : (part + 1) * part_rows, :] = gain_ref[:, part]
    rings[2].advance()
    for _ in range(place.h - 1):
        for ring in rings:
            ring.advance()

    loads[3].wait()
    ff = gu_v.shape[3]
    for slab_at in range(n):
        for kind in (0, 1):
            start = (kind * n + slab_at) * ff
            gu_grad[:, start : start + ff] = gu_v[slab_at, kind].astype(F32)

    in_ring, up_ring, out_ring = rings[2], rings[1], rings[0]
    out_cut, up_cut, in_cut = out_ring.cut, up_ring.cut, in_ring.cut
    for half in (0, 1):
        out_grad[half * out_cut : (half + 1) * out_cut, :] = out_ring.finish(half)
    for half in (0, 1):
        up_sum[pl.ds(half * up_cut, up_cut), :] = up_ring.finish(half).astype(BF)
    up_copies = [
        copies.remote(
            up_sum.at[pl.ds(peer[1] * gain_rows, gain_rows)], up_all.at[c], peer
        )
        for peer in ctx_peers
    ]
    up_copies.append(
        copies.local(up_sum.at[pl.ds(c * gain_rows, gain_rows)], up_all.at[c])
    )
    for half in (0, 1):
        in_sum[pl.ds(half * in_cut, in_cut), :] = in_ring.finish(half).astype(BF)
    in_copies = [
        copies.remote(in_sum.at[pl.ds(peer[1] * part_rows, part_rows)], in_all.at[c], peer)
        for peer in ctx_peers
    ]
    in_copies.append(copies.local(in_sum.at[pl.ds(c * part_rows, part_rows)], in_all.at[c]))

    for copy in up_copies:
        copies.arrive(copy)
    cols = up_all.shape[2]
    heads = cols // HD
    for part in range(4):
        for local in range(heads):
            head = group.head(part, local, heads)
            up_grad[:, head * HD : (head + 1) * HD] = up_all[
                part, :, local * HD : (local + 1) * HD
            ].astype(F32)
    for copy in in_copies:
        copies.arrive(copy)
    cols = in_all.shape[2]
    gains = jnp.zeros(gain_grad.shape, F32)
    for part in range(4):
        in_grad[:, part * cols : (part + 1) * cols] = in_all[part, :own_rows, :].astype(F32)
        gains = gains + in_all[part, own_rows:, :].astype(F32)
    gain_grad[...] = gains
    copies.drain()
    for ring in rings:
        ring.drain()


def collect_weights(n_batch, gain_rows, out_terms, up_terms, project, attn_in_all, grad_gu, gain_terms):
    far = n_batch // 2
    out_rows, width = out_terms.shape[1:]
    up_rows, up_cols = up_terms.shape[1:]
    in_cols = project.shape[2]
    own_rows = width // (4 * n_batch)
    in_rows = 4 * (own_rows + 16)
    shapes = [out_terms.shape[1:], up_terms.shape[1:], (in_rows, in_cols)]
    sems = 2 * n_batch + 16
    return pl.pallas_call(
        functools.partial(tail_kernel, n_batch, gain_rows),
        out_shape=(
            jax.ShapeDtypeStruct((out_rows, width), F32),
            jax.ShapeDtypeStruct((gain_rows, 4 * up_cols), F32),
            jax.ShapeDtypeStruct((own_rows, 4 * in_cols), F32),
            jax.ShapeDtypeStruct((16, in_cols), F32),
            jax.ShapeDtypeStruct((own_rows, 2 * n_batch * grad_gu.shape[3]), F32),
        ),
        in_specs=[pl.BlockSpec(memory_space=pl.ANY)] * 5 + [pl.BlockSpec(memory_space=pltpu.VMEM)],
        out_specs=[pl.BlockSpec(memory_space=pltpu.VMEM)] * 5,
        scratch_shapes=[pltpu.VMEM((n_batch,) + shape, BF) for shape in shapes]
        + [pltpu.VMEM((far, 2, 2, rows // 2, cols), BF) for rows, cols in shapes]
        + [
            pltpu.VMEM((up_rows, up_cols), BF),
            pltpu.VMEM((4, gain_rows, up_cols), BF),
            pltpu.VMEM((in_rows, in_cols), BF),
            pltpu.VMEM((4, own_rows + 16, in_cols), BF),
            pltpu.SemaphoreType.DMA((3, far, 2, 2)),
            pltpu.SemaphoreType.DMA((3, far, 2, 2)),
            pltpu.SemaphoreType.DMA((sems,)),
            pltpu.SemaphoreType.DMA((sems,)),
            pltpu.VMEM(project.shape, BF),
            pltpu.VMEM(attn_in_all.shape, BF),
            pltpu.VMEM(grad_gu.shape, BF),
            pltpu.SemaphoreType.DMA((4,)),
        ],
        compiler_params=pltpu.CompilerParams(
            collective_id=2, has_side_effects=True, vmem_limit_bytes=48 * 1024 * 1024
        ),
        name="collect_weights",
    )(out_terms, up_terms, project, attn_in_all, grad_gu, gain_terms)


class CtxCollect:
    def __init__(self, place, copies, part, near_got, far_got):
        self.place, self.copies, self.part = place, copies, part
        self.near_got, self.far_got = near_got, far_got
        self.near = {}
        self.far = {}

    def start(self, item):
        place = self.place
        self.near[item] = [
            self.copies.remote(
                self.part.at[2 * side + 1 - place.inner, item],
                self.near_got.at[side, item],
                (place.b, place.near),
            )
            for side in (0, 1)
        ]

    def cross(self, item):
        place = self.place
        for copy in self.near[item]:
            self.copies.arrive(copy)
        other = self.part.at[2 * (1 - place.outer) + place.inner, item]
        added = other[...].astype(F32) + self.near_got[1 - place.outer, item].astype(F32)
        other[...] = added.astype(BF)
        self.far[item] = self.copies.remote(
            other, self.far_got.at[item], (place.b, place.far)
        )

    def finish(self, item):
        place = self.place
        self.copies.arrive(self.far[item])
        return (
            self.part[2 * place.outer + place.inner, item].astype(F32)
            + self.near_got[place.outer, item].astype(F32)
            + self.far_got[item].astype(F32)
        )


class CtxGather:
    def __init__(self, place, copies, everyone):
        self.place, self.copies, self.everyone = place, copies, everyone
        self.far = {}
        self.near = {}

    def start(self, item):
        place = self.place
        own = self.everyone.at[place.c, item]
        self.far[item] = self.copies.remote(own, own, (place.b, place.far))
        self.near[item] = [self.copies.remote(own, own, (place.b, place.near))]

    def cross(self, item):
        place = self.place
        self.copies.arrive(self.far[item])
        other = self.everyone.at[place.far, item]
        self.near[item].append(self.copies.remote(other, other, (place.b, place.near)))

    def finish(self, item):
        for copy in self.near[item]:
            self.copies.arrive(copy)


def greet_lines(place):
    devices = [place.up(), place.down(), (place.b, place.far), (place.b, place.near)]
    pl.semaphore_wait(greet(place, devices), 4)


def turn(values, cosine, sine):
    half_size = HD // 2
    front, back = values[:, :half_size], values[:, half_size:]
    return front * cosine - back * sine, back * cosine + front * sine


def softmax_rows(queries, keys, keep, score_scale):
    scores = dot_right_t(queries, keys) * score_scale
    rows = lax.broadcasted_iota(jnp.int32, scores.shape, 0)
    cols = lax.broadcasted_iota(jnp.int32, scores.shape, 1)
    masked = jnp.where((cols <= rows) & (keep > 0.5), scores, -1e30)
    raised = jnp.exp(masked - jnp.max(masked, axis=-1, keepdims=True))
    return raised / jnp.sum(raised, axis=-1, keepdims=True)

def head_group(n_batch, own_rows):
    return min(4, HD // own_rows)


class HeadGroup:
    def __init__(self, place, own_rows):
        self.size = head_group(place.n, own_rows)
        self.count = place.n // self.size
        if self.size == 2:
            self.me = place.inner
            self.others = [(1 - place.inner, (place.b, place.near))]
        else:
            self.me = place.c
            ranks = [place.far, place.near, lax.rem(place.near + 2, 4)]
            self.others = [(rank, (place.b, rank)) for rank in ranks]

    def blocks(self, member):
        return pl.ds(member * self.count, self.count)

    def head(self, rank, local, heads):
        if self.size == 2:
            return 2 * (heads * (rank % 2) + local) + rank // 2
        return heads * rank + local


def front_kernel(
    n_batch,
    heads,
    packed_ref,
    up_ref,
    out_ref,
    gu_ref,
    down_ref,
    tokens_ref,
    cot_ref,
    cos_ref,
    sin_ref,
    cos_own_ref,
    sin_own_ref,
    keep_ref,
    hidden,
    mlp_in,
    gains,
    latents,
    packed_out,
    up_out,
    out_out,
    gu_all,
    down_all,
    qkv_out,
    turned_out,
    mixed_out,
    rows_all,
    cot_all,
    packed_v,
    flat_v,
    gu_v,
    half_v,
    out_v,
    up_v,
    tokens_v,
    rows_v,
    qkv_v,
    turned_v,
    mixed_v,
    part_v,
    near_got,
    far_got,
    send_sems,
    recv_sems,
):
    place = Place(n_batch)
    copies = Copies(send_sems, recv_sems)
    b, c, n = place.b, place.c, n_batch
    own_rows = packed_ref.shape[0]
    gain_rows = up_ref.shape[0]
    out_rows = out_ref.shape[0]
    n_tok, width = tokens_ref.shape
    micro, pos_dev = qkv_v.shape[1:3]
    length = 4 * pos_dev
    in_cols = qkv_v.shape[3]
    latent = in_cols - 2 * HD
    ff = gu_v.shape[3]
    score_scale = 1.0 / math.sqrt(HD)
    group = HeadGroup(place, out_rows)
    peers = [(lax.rem(b + k, n), c) for k in range(1, n)]
    ctx_peers = [(b, place.far), (b, place.near), (b, lax.rem(place.near + 2, 4))]
    far_device, near_device = ctx_peers[0], ctx_peers[1]

    barrier = greet(place, peers + ctx_peers)
    own_packed = copies.local(packed_ref, packed_v.at[b, c])
    own_out = copies.local(out_ref, half_v.at[b])
    own_tokens = copies.local(tokens_ref, tokens_v)
    own_flat = copies.local(gu_ref, flat_v)
    own_down = copies.local(down_ref, down_all.at[c])
    own_cot = copies.local(cot_ref, cot_all.at[b])

    def up_cols(rank, local):
        start = pl.multiple_of(group.head(rank, local, heads) * HD, HD)
        return up_ref.at[:, pl.ds(start, HD)]

    own_up = [
        copies.local(up_cols(c, local), up_v.at[b, c, :, pl.ds(local * HD, HD)])
        for local in range(heads)
    ]
    pl.semaphore_wait(barrier, n + 2)
    up_copies = [
        copies.remote(up_cols(peer[1], local), up_v.at[b, c, :, pl.ds(local * HD, HD)], peer)
        for peer in ctx_peers
        for local in range(heads)
    ]
    copies.arrive(own_packed)
    packed_ring = RingGather(place, copies, own_rows, lambda rank, rows: packed_v.at[rank, c, rows])
    up_ring = RingGather(place, copies, gain_rows, lambda rank, rows: up_v.at[rank, :, rows])
    out_ring = RingGather(place, copies, out_rows, lambda rank, rows: half_v.at[rank, rows])
    cot_ring = RingGather(place, copies, n_tok, lambda rank, rows: cot_all.at[rank, rows])
    packed_far = []

    def packed_step():
        packed_ring.advance()
        ranks = packed_ring.arrived() if packed_ring.step > 1 else [b]
        for rank in ranks:
            block = packed_v.at[rank, c]
            packed_far.append(copies.remote(block, block, far_device))

    packed_step()
    copies.arrive(own_out)
    out_ring.advance()
    for copy in own_up + up_copies:
        copies.arrive(copy)
    up_ring.advance()
    packed_step()
    copies.arrive(own_flat)
    for slab_at in range(n):
        for kind in (0, 1):
            start = (kind * n + slab_at) * ff
            gu_v[slab_at, kind] = flat_v[:, start : start + ff]
    own_gu = copies.local(gu_v.at[b], gu_all.at[:, b, c])
    up_ring.advance()
    while packed_ring.step <= place.h:
        packed_step()
        up_ring.advance()
        if out_ring.step < place.h - 1:
            out_ring.advance()
    gu_copies = []

    def send_gu(count):
        for _ in range(count):
            k = len(gu_copies) + 1
            if k < n:
                peer = peers[k - 1]
                copy = copies.remote(gu_v.at[peer[0]], gu_all.at[:, b, c], peer)
                gu_copies.append((lax.rem(b - k + n, n), copy))

    send_gu(n // 2)
    mine = packed_v.at[:, c]
    packed_near = [copies.remote(mine, mine, near_device)]
    while up_ring.step <= place.h:
        up_ring.advance()
    out_ring.advance()
    for copy in packed_far:
        copies.arrive(copy)
    theirs = packed_v.at[:, place.far]
    packed_near.append(copies.remote(theirs, theirs, near_device))

    copies.arrive(own_tokens)
    residual = tokens_v[...].astype(F32)
    normed = residual * rms_scale(residual)
    for copy in packed_near:
        copies.arrive(copy)
    extra = packed_v[:, :, :, in_cols:].astype(F32)
    gain_wide = jnp.transpose(extra.reshape(width, 128))
    gain_query = jnp.transpose(extra[:, :, :gain_rows].reshape(latent, 128))[2:3]
    gains[0:2, :] = gain_wide[0:2]
    gains[2:3, :latent] = gain_query
    attn_in = (normed * gain_wide[0:1]).astype(BF)
    rows_v[...] = attn_in
    tile = 512
    for start in range(0, in_cols, tile):
        weights = packed_v[:, :, :, start : start + tile].reshape(width, tile)
        part = dot(attn_in, weights)
        if start + tile <= latent:
            latents[:, start : start + tile] = part
        else:
            front, back = turn(part[:, :HD], cos_own_ref[...], sin_own_ref[...])
            half = HD // 2
            qkv_v[c, :, :, latent : latent + half] = (
                front.astype(BF).reshape(micro, pos_dev, half)
            )
            qkv_v[c, :, :, latent + half : latent + HD] = (
                back.astype(BF).reshape(micro, pos_dev, half)
            )
            qkv_v[c, :, :, latent + HD :] = part[:, HD:].astype(BF).reshape(micro, pos_dev, HD)
    q_latent = latents[...]
    q_normed = q_latent * rms_scale(q_latent) * gain_query
    qkv_v[c, :, :, :latent] = q_normed.astype(BF).reshape(micro, pos_dev, latent)
    qkv = CtxGather(place, copies, qkv_v)
    for item in range(micro):
        qkv.start(item)
    while out_ring.step <= place.h:
        out_ring.advance()
    for item in range(micro):
        qkv.cross(item)
    out_swaps = [
        copies.remote(half_v.at[group.blocks(member)], out_v.at[:, group.me], device)
        for member, device in group.others
    ]
    out_swaps.append(copies.local(half_v.at[group.blocks(group.me)], out_v.at[:, group.me]))

    send_gu(n)
    copies.arrive(own_cot)
    cot_ring.advance()
    copies.arrive(own_gu)
    gu_far = [copies.remote(gu_all.at[:, b, c], gu_all.at[:, b, c], far_device)]
    copies.arrive(own_down)
    down_far = copies.remote(down_ref, down_all.at[c], far_device)
    copies.remote(down_ref, down_all.at[c], near_device)
    copies.arrive(copies.local(rows_v, rows_all.at[c, 0]))
    rows = CtxGather(place, copies, rows_all)
    rows.start(0)
    waiting = list(gu_copies)

    def forward_gu(count):
        for _ in range(min(count, len(waiting))):
            rank, copy = waiting.pop(0)
            copies.arrive(copy)
            block = gu_all.at[:, rank, c]
            gu_far.append(copies.remote(block, block, far_device))

    attended_sum = CtxCollect(place, copies, part_v, near_got, far_got)
    cosine, sine = cos_ref[...], sin_ref[...]
    for item in range(micro):
        qkv.finish(item)
        q_all = qkv_v[:, item, :, :latent].reshape(length, latent)
        keys = qkv_v[:, item, :, latent : latent + HD].reshape(length, HD)
        values = qkv_v[:, item, :, latent + HD :].reshape(length, HD)
        keep = keep_ref[item]

        @pl.loop(0, heads)
        def _(head):
            base = pl.multiple_of(head * HD, HD)
            cols = pl.ds(base, HD)
            up = up_v[:, :, :, cols].reshape(latent, HD)
            front, back = turn(dot(q_all, up), cosine, sine)
            turned_v[item, :, pl.ds(base, HD // 2)] = front.astype(BF)
            upper = pl.multiple_of(base + HD // 2, HD // 2)
            turned_v[item, :, pl.ds(upper, HD // 2)] = back.astype(BF)
            weights = softmax_rows(turned_v[item, :, cols], keys, keep, score_scale)
            mixed = dot(weights.astype(BF), values).astype(BF)
            mixed_v[:, item, :, cols] = mixed.reshape(4, pos_dev, HD)

        forward_gu(n // 4)
        if cot_ring.step <= place.h:
            cot_ring.advance()
        mixed = mixed_v[:, item].reshape(length, heads * HD)
        for copy in out_swaps:
            copies.arrive(copy)
        out_swaps = []

        @pl.loop(0, width // 512)
        def _(t):
            cols = pl.ds(pl.multiple_of(t * 512, 512), 512)
            weights = out_v[:, :, :, cols].reshape(heads * HD, 512)
            part = dot(mixed, weights).astype(BF)
            part_v[:, item, :, cols] = part.reshape(4, pos_dev, 512)

        attended_sum.start(item)
        if item > 0:
            attended_sum.cross(item - 1)
    copies.local(packed_v, packed_out)
    copies.local(up_v, up_out)
    copies.local(out_v, out_out)
    copies.local(qkv_v, qkv_out)
    copies.local(turned_v, turned_out)
    copies.local(mixed_v, mixed_out)
    attended_sum.cross(micro - 1)
    rows.cross(0)
    if cot_ring.step <= place.h:
        cot_ring.advance()
    for item in range(micro):
        at = slice(item * pos_dev, (item + 1) * pos_dev)
        total = tokens_v[at, :].astype(F32) + attended_sum.finish(item)
        hidden[at, :] = total
        mlp_in[at, :] = (total * rms_scale(total) * gains[1:2, :]).astype(BF)
    forward_gu(n // 4)
    while cot_ring.step <= place.h:
        cot_ring.advance()
        forward_gu(n // 4)
    forward_gu(n)
    cot_ring.advance()
    mine = gu_all.at[:, :, c]
    copies.remote(mine, mine, near_device)
    copies.arrive(down_far)
    copies.remote(down_all.at[place.far], down_all.at[place.far], near_device)
    for copy in gu_far:
        copies.arrive(copy)
    theirs = gu_all.at[:, :, place.far]
    copies.remote(theirs, theirs, near_device)
    copies.drain()


def front(n_batch, heads, packed, query_up, proj_out, gate_up, down, tokens, cots, tables):
    own_rows, packed_cols = packed.shape
    in_cols = packed_cols - 128
    latent = in_cols - 2 * HD
    gain_rows = query_up.shape[0]
    out_rows, width = proj_out.shape
    n_tok = cots.shape[0]
    pos_dev = tables[0].shape[0] // 4
    micro = n_tok // pos_dev
    ff = gate_up.shape[1] // (2 * n_batch)
    size = head_group(n_batch, out_rows)
    head_cols = heads * HD
    shapes = {
        "packed": (n_batch, 4, own_rows, packed_cols),
        "up": (n_batch, 4, gain_rows, head_cols),
        "out": (n_batch // size, size, out_rows, width),
        "gu": (2, n_batch, 4, own_rows, ff),
        "down": (4,) + down.shape,
        "qkv": (4, micro, pos_dev, in_cols),
        "turned": (micro, 4 * pos_dev, head_cols),
        "mixed": (4, micro, pos_dev, head_cols),
        "rows": (4, 1, n_tok, width),
        "cot": (n_batch, n_tok, width),
    }
    anywhere = pl.BlockSpec(memory_space=pl.ANY)
    near = pl.BlockSpec(memory_space=pltpu.VMEM)
    sems = 13 * n_batch + 100
    return pl.pallas_call(
        functools.partial(front_kernel, n_batch, heads),
        out_shape=(
            jax.ShapeDtypeStruct((n_tok, width), F32),
            jax.ShapeDtypeStruct((n_tok, width), BF),
            jax.ShapeDtypeStruct((8, width), F32),
            jax.ShapeDtypeStruct((n_tok, latent), F32),
        )
        + tuple(jax.ShapeDtypeStruct(shape, BF) for shape in shapes.values()),
        in_specs=[anywhere] * 7 + [near] * 5,
        out_specs=[near] * 4 + [anywhere] * len(shapes),
        scratch_shapes=[
            pltpu.VMEM(shapes["packed"], BF),
            pltpu.VMEM(gate_up.shape, BF),
            pltpu.VMEM((n_batch, 2, own_rows, ff), BF),
            pltpu.VMEM((n_batch, out_rows, width), BF),
            pltpu.VMEM(shapes["out"], BF),
            pltpu.VMEM(shapes["up"], BF),
            pltpu.VMEM((n_tok, width), BF),
            pltpu.VMEM((n_tok, width), BF),
            pltpu.VMEM(shapes["qkv"], BF),
            pltpu.VMEM(shapes["turned"], BF),
            pltpu.VMEM(shapes["mixed"], BF),
            pltpu.VMEM((4, micro, pos_dev, width), BF),
            pltpu.VMEM((2, micro, pos_dev, width), BF),
            pltpu.VMEM((micro, pos_dev, width), BF),
            pltpu.SemaphoreType.DMA((sems,)),
            pltpu.SemaphoreType.DMA((sems,)),
        ],
        compiler_params=pltpu.CompilerParams(
            collective_id=0, has_side_effects=True, vmem_limit_bytes=56 * 1024 * 1024
        ),
        name="front",
    )(packed, query_up, proj_out, gate_up, down, tokens, cots, *tables)


def attention_back_kernel(
    n_batch,
    heads,
    has_terms,
    grad_ref,
    qkv_ref,
    turned_ref,
    mixed_ref,
    up_ref,
    out_ref,
    gu_ref,
    down_ref,
    *refs,
):
    terms_ref, refs = (refs[0], refs[1:]) if has_terms else (None, refs)
    (
        cos_ref,
        sin_ref,
        keep_ref,
        back_out,
        out_terms,
        up_terms,
        gu_grad,
        down_grad,
    ) = refs[:8]
    terms_sum, refs = (refs[8], refs[9:]) if has_terms else (None, refs[8:])
    (
        grad_v,
        qkv_v,
        turned_v,
        mixed_v,
        up_v,
        out_v,
        qgrad_v,
        kgrad_v,
        vgrad_v,
        part_v,
        near_got,
        far_got,
        outgrad_v,
        upgrad_v,
        down_v,
        send_sems,
        recv_sems,
        load_sems,
    ) = refs[:18]
    place = Place(n_batch)
    copies = Copies(send_sems, recv_sems)
    b, c, n = place.b, place.c, n_batch
    micro, pos_dev, width = grad_ref.shape
    length = 4 * pos_dev
    head_cols = heads * HD
    latent = qkv_ref.shape[3] - 2 * HD
    score_scale = 1.0 / math.sqrt(HD)
    pairs = [
        (grad_ref, grad_v.at[c]),
        (out_ref, out_v),
        (qkv_ref, qkv_v),
        (turned_ref, turned_v),
        (up_ref, up_v),
        (mixed_ref, mixed_v),
    ]
    if has_terms:
        terms_v, terms_got, ring_send, ring_recv = refs[18:]
        pairs.append((terms_ref, terms_v))
    loads = [
        pltpu.make_async_copy(source, target, load_sems.at[i])
        for i, (source, target) in enumerate(pairs)
    ]
    for copy in loads:
        copy.start()
    peers = [(lax.rem(b + k, n), c) for k in range(1, n)]
    others = peers + [(b, place.far), (b, place.near), (b, lax.rem(place.near + 2, 4))]
    pl.semaphore_wait(greet(place, others), n + 2)
    out_rows = out_terms.shape[1]
    group = HeadGroup(place, out_rows)
    loads[0].wait()
    grads = CtxGather(place, copies, grad_v)
    for item in range(micro):
        grads.start(item)
    steps = []
    if has_terms:

        def spot(step):
            return 0 if step == 0 else 1 if step == place.h else 2 * abs(step) + (step > 0)

        terms = RingCollect(
            place, lambda step: terms_v.at[spot(step)], terms_got, ring_send, ring_recv
        )
        loads[6].wait()
        steps = [terms.advance] * place.h

    def ring_step():
        if steps:
            steps.pop()()

    ring_step()
    copies.local(gu_ref.at[b], gu_grad.at[b])
    for peer in peers:
        copies.remote(gu_ref.at[peer[0]], gu_grad.at[b], peer)
    for item in range(micro):
        grads.cross(item)
    down_own = copies.local(down_ref.at[place.outer], down_v.at[0])
    down_far = copies.remote(down_ref.at[1 - place.outer], down_v.at[1], (b, place.far))
    for copy in loads[1:6]:
        copy.wait()
    back_sum = CtxCollect(place, copies, part_v, near_got, far_got)
    cosine, sine = cos_ref[...], sin_ref[...]
    for item in range(micro):
        grads.finish(item)
        incoming = grad_v[:, item].reshape(length, width)
        keys = qkv_v[:, item, :, latent : latent + HD].reshape(length, HD)
        values = qkv_v[:, item, :, latent + HD :].reshape(length, HD)
        keep = keep_ref[item]
        kgrad_v[...] = jnp.zeros_like(kgrad_v)
        vgrad_v[...] = jnp.zeros_like(vgrad_v)

        @pl.loop(0, heads)
        def _(head):
            cols = pl.ds(pl.multiple_of(head * HD, HD), HD)
            grad_mixed = dot_right_t(incoming, out_v[head]).astype(BF)
            queries = turned_v[item, :, cols]
            weights = softmax_rows(queries, keys, keep, score_scale)
            grad_probs = dot_right_t(grad_mixed, values)
            row_dot = jnp.sum(weights * grad_probs, axis=-1, keepdims=True)
            grad_scores = (weights * (grad_probs - row_dot)).astype(BF)
            front, back = turn(dot(grad_scores, keys) * score_scale, cosine, -sine)
            front, back = front.astype(BF), back.astype(BF)
            base = pl.multiple_of(head * HD, HD)
            qgrad_v[:, item, :, pl.ds(base, HD // 2)] = front.reshape(4, pos_dev, HD // 2)
            base = pl.multiple_of(head * HD + HD // 2, HD // 2)
            qgrad_v[:, item, :, pl.ds(base, HD // 2)] = back.reshape(4, pos_dev, HD // 2)
            kgrad_v[...] += dot_left_t(grad_scores, queries) * score_scale
            vgrad_v[...] += dot_left_t(weights.astype(BF), grad_mixed)

        ring_step()
        qgrad = qgrad_v[:, item].reshape(length, head_cols)
        part_v[:, item, :, :latent] = (
            dot_right_t(qgrad, up_v[...]).astype(BF).reshape(4, pos_dev, latent)
        )
        part_v[:, item, :, latent : latent + HD] = (
            kgrad_v[...].astype(BF).reshape(4, pos_dev, HD)
        )
        part_v[:, item, :, latent + HD :] = vgrad_v[...].astype(BF).reshape(4, pos_dev, HD)
        back_sum.start(item)
        if item > 0:
            back_sum.cross(item - 1)
    n_all = 4 * micro * pos_dev
    back_sum.cross(micro - 1)
    ring_step()

    @pl.loop(0, width // 512)
    def _(t):
        cols = pl.ds(pl.multiple_of(t * 512, 512), 512)
        term = dot_left_t(
            mixed_v[...].reshape(n_all, head_cols), grad_v[:, :, :, cols].reshape(n_all, 512)
        )
        outgrad_v[:, :, :, cols] = term.astype(BF).reshape(group.count, group.size, out_rows, 512)

    mine = out_terms.at[group.blocks(group.me)]
    copies.local(outgrad_v.at[:, group.me], mine)
    for member, device in group.others:
        copies.remote(outgrad_v.at[:, member], mine, device)
    for item in range(micro):
        back_out[item] = back_sum.finish(item)
    ring_step()

    @pl.loop(0, head_cols // HD)
    def _(t):
        cols = pl.ds(pl.multiple_of(t * HD, HD), HD)
        term = dot_left_t(
            qkv_v[:, :, :, :latent].reshape(n_all, latent),
            qgrad_v[:, :, :, cols].reshape(n_all, HD),
        )
        upgrad_v[:, :, cols] = term.astype(BF).reshape(n, latent // n, HD)

    copies.local(upgrad_v, up_terms)
    copies.arrive(down_own)
    copies.arrive(down_far)
    down_grad[...] = down_v[0].astype(F32) + down_v[1].astype(F32)
    if has_terms:
        while steps:
            ring_step()
        cut = terms.cut
        for half in (0, 1):
            terms_sum[half * cut : (half + 1) * cut, :] = terms.finish(half)
        terms.drain()
    copies.drain()


def attention_back(
    n_batch, grad_att, qkv_all, turned, mixed, own_qup, own_out, grad_gu, down_part, terms, tables
):
    micro, pos_dev, width = grad_att.shape
    n_tok = micro * pos_dev
    qkv_cols = qkv_all.shape[3]
    latent, head_cols = own_qup.shape
    own_out = own_out.reshape(head_cols // HD, HD, width)
    length = 4 * pos_dev
    far = n_batch // 2
    has_terms = terms is not None
    size = head_group(n_batch, head_cols // n_batch)
    sems = 2 * n_batch + 48
    anywhere = pl.BlockSpec(memory_space=pl.ANY)
    near = pl.BlockSpec(memory_space=pltpu.VMEM)
    out_shape = [
        jax.ShapeDtypeStruct((micro, pos_dev, qkv_cols), F32),
        jax.ShapeDtypeStruct((n_batch, head_cols // n_batch, width), BF),
        jax.ShapeDtypeStruct((n_batch, latent // n_batch, head_cols), BF),
        jax.ShapeDtypeStruct(grad_gu.shape, BF),
        jax.ShapeDtypeStruct(down_part.shape[1:], F32),
    ]
    out_specs = [near] + [anywhere] * 3 + [near]
    scratch = [
        pltpu.VMEM((4, micro, pos_dev, width), BF),
        pltpu.VMEM((4, micro, pos_dev, qkv_cols), BF),
        pltpu.VMEM((micro, length, head_cols), BF),
        pltpu.VMEM((4, micro, pos_dev, head_cols), BF),
        pltpu.VMEM((latent, head_cols), BF),
        pltpu.VMEM((head_cols // HD, HD, width), BF),
        pltpu.VMEM((4, micro, pos_dev, head_cols), BF),
        pltpu.VMEM((length, HD), F32),
        pltpu.VMEM((length, HD), F32),
        pltpu.VMEM((4, micro, pos_dev, qkv_cols), BF),
        pltpu.VMEM((2, micro, pos_dev, qkv_cols), BF),
        pltpu.VMEM((micro, pos_dev, qkv_cols), BF),
        pltpu.VMEM((n_batch // size, size, head_cols // n_batch, width), BF),
        pltpu.VMEM((n_batch, latent // n_batch, head_cols), BF),
        pltpu.VMEM(down_part.shape, BF),
        pltpu.SemaphoreType.DMA((sems,)),
        pltpu.SemaphoreType.DMA((sems,)),
        pltpu.SemaphoreType.DMA((7,)),
    ]
    args = [grad_att, qkv_all, turned, mixed, own_qup, own_out, grad_gu, down_part]
    if has_terms:
        args.append(terms)
        out_shape.append(jax.ShapeDtypeStruct((n_tok, width), F32))
        out_specs.append(near)
        scratch += [
            pltpu.VMEM(terms.shape, BF),
            pltpu.VMEM((far, 2, 2, n_tok // 2, width), BF),
            pltpu.SemaphoreType.DMA((far, 2, 2)),
            pltpu.SemaphoreType.DMA((far, 2, 2)),
        ]
    return pl.pallas_call(
        functools.partial(attention_back_kernel, n_batch, head_cols // HD, has_terms),
        out_shape=tuple(out_shape),
        in_specs=[anywhere] * len(args) + [near] * 3,
        out_specs=out_specs,
        scratch_shapes=scratch,
        compiler_params=pltpu.CompilerParams(
            collective_id=4, has_side_effects=True, vmem_limit_bytes=56 * 1024 * 1024
        ),
        name="attention_back",
    )(*args, *tables)


def permuted_mlp(ring, rows_own, cots, gu_rows, own_down):
    mlp_in = ring.spread(rows_own)
    n_tok, width = rows_own.shape
    _, n_batch, n_ctx, own_rows, ff = gu_rows.shape
    own_gate, own_up = gu_rows.reshape(2, width, ff)
    own_down = own_down.reshape(ff, width)
    far = ring.h
    groups = [[0]] + [[-step, step] for step in range(1, far)] + [[far]]
    out_terms = {}
    in_terms = {}
    kept = []
    for group in groups:
        rows = jnp.concatenate([mlp_in[step] for step in group], axis=0)
        grad_rows = jnp.concatenate([pick(cots, ring.rank_of(step)) for step in group], axis=0)
        gate_part = dot(rows, own_gate)
        up_part = dot(rows, own_up)
        sigmoid_gate = jax.nn.sigmoid(gate_part)
        silu_gate = gate_part * sigmoid_gate
        activated = (silu_gate * up_part).astype(BF)
        grad_act = dot_right_t(grad_rows, own_down)
        grad_gate = (
            grad_act * up_part * (sigmoid_gate * (1.0 + gate_part * (1.0 - sigmoid_gate)))
        ).astype(BF)
        grad_up = (grad_act * silu_gate).astype(BF)
        in_term = dot_right_t(grad_gate, own_gate) + dot_right_t(grad_up, own_up)
        out_term = dot(activated, own_down)
        for place_in, step in enumerate(group):
            cut = slice(place_in * n_tok, (place_in + 1) * n_tok)
            in_terms[step] = in_term[cut]
            out_terms[step] = out_term[cut]
        kept.append((rows, grad_rows, activated, grad_gate, grad_up))
    rows, grad_rows, activated, grad_gate, grad_up = (
        jnp.concatenate(items, axis=0) for items in zip(*kept)
    )
    grad_gu = jnp.stack([dot_left_t(rows, grad_gate), dot_left_t(rows, grad_up)])
    grad_gu = grad_gu.reshape(2, n_batch, n_ctx, own_rows, ff).transpose(2, 1, 0, 3, 4)
    grad_down = dot_left_t(activated, grad_rows)
    return (
        ring.collect(lambda step: in_terms[step]),
        near_collect(grad_down.reshape(n_ctx, ff // n_ctx, width)).astype(BF),
        out_terms,
        ctx_collect(grad_gu).astype(BF),
    )


def shards(
    tokens,
    cotangent,
    lengths,
    slot_sequence,
    proj_in,
    query_up,
    proj_out,
    attn_gain,
    query_gain,
    mlp_gain,
    gate_up,
    down_proj,
):
    n_ctx = lax.axis_size("ctx")
    n_batch = lax.axis_size("batch")
    ctx_rank = lax.axis_index("ctx")
    batch_rank = lax.axis_index("batch")
    ring = Ring()
    micro, pos_dev, width = tokens.shape
    n_tok = micro * pos_dev
    full_length = pos_dev * n_ctx
    heads = H // n_ctx
    score_scale = 1.0 / math.sqrt(HD)
    in_cols = proj_in.shape[1]

    slot_total = lengths.shape[0]
    slot_ids = jnp.arange(slot_total, dtype=jnp.int32)
    seq_lengths = jnp.sum(
        jnp.where(slot_sequence[:, None] == slot_ids[None, :], lengths[None, :], 0), axis=1
    )
    own_lengths = lax.dynamic_slice_in_dim(seq_lengths, batch_rank * micro, micro)
    query_pos = ctx_rank * pos_dev + jnp.arange(pos_dev, dtype=jnp.int32)
    key_pos = jnp.arange(full_length, dtype=jnp.int32)
    cos_all, sin_all = rope_tables(key_pos)
    cos_own, sin_own = rope_tables(query_pos)

    own_rows = proj_in.shape[0]
    gain_rows = query_gain.shape[0]
    gains = jnp.stack(
        [attn_gain, mlp_gain, jnp.pad(query_gain, (0, own_rows - gain_rows))], axis=1
    )
    packed = jnp.concatenate([proj_in, jnp.pad(gains, ((0, 0), (0, 125)))], axis=1)
    residual = tokens.reshape(n_tok, width).astype(F32)
    valid_rows = (query_pos[None, :] < own_lengths[:, None]).astype(F32).reshape(n_tok, 1)
    grad_out = cotangent.reshape(n_tok, width).astype(F32) * valid_rows
    keep = (key_pos[None, None, :] < own_lengths[:, None, None]).astype(F32)
    tables = (cos_all, sin_all, jnp.tile(cos_own, (micro, 1)), jnp.tile(sin_own, (micro, 1)), keep)
    (
        hidden_res,
        mlp_in,
        gains,
        q_latent,
        packed,
        own_qup,
        own_out,
        gu_rows,
        own_down,
        qkv_all,
        turned,
        mixed,
        attn_in_all,
        cots,
    ) = front(
        n_batch,
        heads,
        packed,
        query_up,
        proj_out,
        gate_up,
        down_proj,
        tokens.reshape(n_tok, width),
        grad_out.astype(BF),
        tables,
    )
    full_in = packed.reshape(width, in_cols + 128)[:, :in_cols]
    own_qup = own_qup.reshape(QR, heads * HD)
    gain_norm, gain_mlp, gain_query = gains[0], gains[1], gains[2, :QR]
    scale_one = rms_scale(residual)
    normed_one = residual * scale_one
    scale_query = rms_scale(q_latent)
    normed_query = q_latent * scale_query

    scale_two = rms_scale(hidden_res)
    normed_two = hidden_res * scale_two
    resident = 10 * n_batch * n_tok * width <= 24 * 1024 * 1024
    if resident:
        grad_mlp_in, down_part, terms, grad_gu_own = fused_mlp(
            n_batch, mlp_in, cots, gu_rows, own_down
        )
        terms = terms.reshape(n_batch, n_tok, width)
    else:
        terms = None
        grad_mlp_in, down_part, out_terms, grad_gu_own = permuted_mlp(
            ring, mlp_in, cots, gu_rows, own_down
        )
    gain_mlp_term = jnp.sum(grad_mlp_in * normed_two, axis=0)
    grad_hidden = grad_out + norm_back(grad_mlp_in * gain_mlp, normed_two, scale_two)
    back_own, out_grads, up_grads, grad_gu_own, grad_down, *sums = attention_back(
        n_batch,
        grad_hidden.astype(BF).reshape(micro, pos_dev, width),
        qkv_all,
        turned,
        mixed,
        own_qup,
        own_out,
        grad_gu_own,
        down_part,
        terms,
        (cos_all, sin_all, keep),
    )
    out_sum = sums[0] if resident else ring.collect(lambda step: out_terms[step])
    layer_out = hidden_res + out_sum
    back_own = back_own.reshape(n_tok, in_cols)
    grad_qn = back_own[:, :QR]
    gain_query_term = jnp.sum(grad_qn * normed_query, axis=0)
    grad_latent = norm_back(grad_qn * gain_query, normed_query, scale_query)
    grad_key_raw = rotate_back(
        back_own[:, QR : QR + HD].reshape(micro, pos_dev, HD), cos_own, sin_own
    ).reshape(n_tok, HD)
    grad_project = jnp.concatenate(
        [grad_latent, grad_key_raw, back_own[:, QR + HD :]], axis=1
    ).astype(BF)
    grad_attn_in = dot_right_t(grad_project, full_in)
    gain_norm_term = jnp.sum(grad_attn_in * normed_one, axis=0)
    grad_tokens = grad_hidden + norm_back(grad_attn_in * gain_norm, normed_one, scale_one)

    part_cols = in_cols // n_ctx
    project_parts = grad_project.reshape(n_tok, n_ctx, part_cols).swapaxes(0, 1)
    gain_terms = jnp.stack(
        [
            gain_norm_term.reshape(n_batch, n_ctx, own_rows),
            gain_mlp_term.reshape(n_batch, n_ctx, own_rows),
            jnp.pad(
                gain_query_term.reshape(n_batch, n_ctx, gain_rows),
                ((0, 0), (0, 0), (0, own_rows - gain_rows)),
            ),
        ],
        axis=2,
    )
    gain_terms = jnp.pad(gain_terms, ((0, 0), (0, 0), (0, 13), (0, part_cols - own_rows)))
    grad_proj_out, grad_query_up, grad_proj_in, gain_sums, grad_gate_up = collect_weights(
        n_batch,
        gain_rows,
        out_grads,
        up_grads,
        project_parts,
        attn_in_all,
        grad_gu_own,
        gain_terms.astype(BF),
    )
    gain_sums = gain_sums[:, :own_rows]

    return (
        layer_out.reshape(tokens.shape).astype(BF),
        grad_tokens.reshape(tokens.shape).astype(BF),
        grad_proj_in,
        grad_query_up,
        grad_proj_out,
        gain_sums[0],
        gain_sums[2, :gain_rows],
        gain_sums[1],
        grad_gate_up,
        grad_down,
    )


def solution(mesh):
    rows = P(("batch", "ctx"), None)
    vector = P(("batch", "ctx"))
    acts = P("batch", "ctx", None)
    return jax.shard_map(
        shards,
        mesh=mesh,
        in_specs=(acts, acts, P(), P(), rows, rows, rows, vector, vector, vector, rows, rows),
        out_specs=(acts, acts, rows, rows, rows, vector, vector, vector, rows, rows),
        check_vma=False,
    )
```

```python
import functools
import math

import jax
import jax.numpy as jnp
from jax import lax
from jax.experimental import pallas as pl
from jax.experimental.pallas import tpu as pltpu
from jax.sharding import PartitionSpec as P

H = 16
HD = 256
QR = 1024
EPSILON = 1e-06
BF = jnp.bfloat16
F32 = jnp.float32


def rms_scale(values):
    return lax.rsqrt(jnp.mean(values * values, axis=-1, keepdims=True) + EPSILON)


def rope_tables(positions):
    half_size = HD // 2
    frequency = 10000.0 ** (-(jnp.arange(half_size, dtype=F32) * 2.0 / HD))
    angles = positions.astype(F32)[:, None] * frequency[None, :]
    return (jnp.cos(angles), jnp.sin(angles))


def rotate(values, cosine_table, sine_table):
    half_size = values.shape[-1] // 2
    front_half = values[..., :half_size]
    back_half = values[..., half_size:]
    return jnp.concatenate(
        [
            front_half * cosine_table - back_half * sine_table,
            back_half * cosine_table + front_half * sine_table,
        ],
        axis=-1,
    )


def rotate_back(values, cosine_table, sine_table):
    return rotate(values, cosine_table, -sine_table)


def dot(left_side, right_side):
    return jnp.dot(left_side, right_side, preferred_element_type=F32)


def dot_right_t(left_side, right_side):
    return lax.dot_general(
        left_side, right_side, (((1,), (1,)), ((), ())), preferred_element_type=F32
    )


def dot_left_t(left_side, right_side):
    return lax.dot_general(
        left_side, right_side, (((0,), (0,)), ((), ())), preferred_element_type=F32
    )


def norm_back(grad_normed, normed, inv_rms):
    return inv_rms * (grad_normed - normed * jnp.mean(grad_normed * normed, axis=-1, keepdims=True))


def pick(array, index, axis=0):
    return lax.dynamic_index_in_dim(array, index, axis, keepdims=False)


def place(array, block, index, axis=0):
    return lax.dynamic_update_index_in_dim(array, block, index, axis)


class Ring:
    def __init__(self):
        self.n = lax.axis_size("batch")
        self.h = self.n // 2
        rank = lax.axis_index("batch")
        self.at = jnp.where(rank % 2 == 0, rank // 2, self.n - 1 - rank // 2)
        order = [2 * i for i in range(self.h)] + [2 * i + 1 for i in reversed(range(self.h))]
        self.up = [(order[i], order[(i + 1) % self.n]) for i in range(self.n)]
        self.down = [(there, here) for here, there in self.up]

    def rank_of(self, step):
        spot = (self.at + step) % self.n
        return jnp.where(spot < self.h, 2 * spot, 2 * (self.n - 1 - spot) + 1)

    def spread(self, block):
        found = {0: block}
        upward = downward = block
        for step in range(1, self.h):
            upward = lax.ppermute(upward, "batch", self.up)
            downward = lax.ppermute(downward, "batch", self.down)
            found[-step] = upward
            found[step] = downward
        cut = block.shape[0] // 2
        found[self.h] = jnp.concatenate(
            [
                lax.ppermute(upward[:cut], "batch", self.up),
                lax.ppermute(downward[cut:], "batch", self.down),
            ],
            axis=0,
        )
        return found

    def gather(self, block):
        found = self.spread(block)
        whole = jnp.zeros((self.n,) + block.shape, block.dtype)
        for step, part in found.items():
            whole = place(whole, part, self.rank_of(step))
        return whole

    def collect(self, term):
        far = term(self.h)
        cut = far.shape[0] // 2
        downward = lax.ppermute(far[:cut].astype(BF), "batch", self.down)
        upward = lax.ppermute(far[cut:].astype(BF), "batch", self.up)
        for step in range(self.h - 1, 0, -1):
            for_lower = term(-step).astype(F32)
            for_upper = term(step).astype(F32)
            if step == self.h - 1:
                for_lower = jnp.concatenate(
                    [for_lower[:cut] + downward.astype(F32), for_lower[cut:]], axis=0
                )
                for_upper = jnp.concatenate(
                    [for_upper[:cut], for_upper[cut:] + upward.astype(F32)], axis=0
                )
            else:
                for_lower = for_lower + downward.astype(F32)
                for_upper = for_upper + upward.astype(F32)
            downward = lax.ppermute(for_lower.astype(BF), "batch", self.down)
            upward = lax.ppermute(for_upper.astype(BF), "batch", self.up)
        own = term(0).astype(F32)
        return own + downward.astype(F32) + upward.astype(F32)

    def collect_rows(self, stacked):
        return self.collect(lambda step: pick(stacked, self.rank_of(step)))


FAR = [(0, 2), (1, 3), (2, 0), (3, 1)]
NEAR = [(0, 1), (1, 0), (2, 3), (3, 2)]


def ctx_place():
    rank = lax.axis_index("ctx")
    return rank // 2, rank % 2


def in_order(mine, theirs, at):
    return jnp.where(at == 0, jnp.stack([mine, theirs]), jnp.stack([theirs, mine]))


def ctx_gather(block):
    outer, inner = ctx_place()
    pair = in_order(block, lax.ppermute(block, "ctx", FAR), outer)
    whole = in_order(pair, lax.ppermute(pair, "ctx", NEAR), inner)
    whole = jnp.swapaxes(whole, 0, 1)
    return whole.reshape((4,) + block.shape)


def near_collect(stacked):
    _, inner = ctx_place()
    parts = stacked.reshape((2, 2) + stacked.shape[1:])
    got = lax.ppermute(pick(parts, 1 - inner, 1).astype(BF), "ctx", NEAR)
    return pick(parts, inner, 1).astype(F32) + got.astype(F32)


def ctx_collect(stacked):
    outer, _ = ctx_place()
    half = near_collect(stacked)
    got = lax.ppermute(pick(half, 1 - outer).astype(BF), "ctx", FAR)
    return pick(half, outer) + got.astype(F32)


def ctx_exchange(stacked):
    outer, inner = ctx_place()
    parts = stacked.reshape((2, 2) + stacked.shape[1:])
    got = lax.ppermute(pick(parts, 1 - outer), "ctx", FAR)
    parts = in_order(pick(parts, outer), got, outer)
    got = lax.ppermute(pick(parts, 1 - inner, 1), "ctx", NEAR)
    whole = in_order(pick(parts, inner, 1), got, inner)
    return jnp.swapaxes(whole, 0, 1).reshape(stacked.shape)


MESH = pl.DeviceIdType.MESH


class Place:
    def __init__(self, n_batch):
        self.n = n_batch
        self.h = n_batch // 2
        self.b = lax.axis_index("batch")
        self.c = lax.axis_index("ctx")
        self.outer = lax.div(self.c, 2)
        self.inner = lax.rem(self.c, 2)
        self.far = lax.rem(self.c + 2, 4)
        self.near = self.c + 1 - 2 * self.inner
        odd = lax.rem(self.b, 2)
        half = lax.div(self.b, 2)
        self.at = half + odd * (self.n - 1 - 2 * half)

    def rank_of(self, step):
        spot = lax.rem(self.at + step + 2 * self.n, self.n)
        back = lax.div(spot, self.h)
        return (1 - back) * 2 * spot + back * (2 * (self.n - 1 - spot) + 1)

    def up(self):
        return (self.rank_of(1), self.c)

    def down(self):
        return (self.rank_of(-1), self.c)


class Copies:
    def __init__(self, send_sems, recv_sems):
        self.send_sems = send_sems
        self.recv_sems = recv_sems
        self.count = 0
        self.open_sends = []
        self.open_recvs = []

    def remote(self, source, target, device):
        index = self.count
        self.count += 1
        copy = pltpu.make_async_remote_copy(
            src_ref=source,
            dst_ref=target,
            send_sem=self.send_sems.at[index],
            recv_sem=self.recv_sems.at[index],
            device_id=device,
            device_id_type=MESH,
        )
        copy.start()
        self.open_sends.append(copy)
        self.open_recvs.append(copy)
        return copy

    def local(self, source, target):
        index = self.count
        self.count += 1
        copy = pltpu.make_async_copy(source, target, self.recv_sems.at[index])
        copy.start()
        self.open_recvs.append(copy)
        return copy

    def arrive(self, copy):
        if any(copy is other for other in self.open_recvs):
            self.open_recvs = [other for other in self.open_recvs if other is not copy]
            if any(copy is other for other in self.open_sends):
                copy.wait_recv()
            else:
                copy.wait()

    def drain(self):
        for copy in list(self.open_recvs):
            self.arrive(copy)
        for copy in self.open_sends:
            copy.wait_send()


def greet(place, others):
    barrier = pltpu.get_barrier_semaphore()
    for device in others:
        pl.semaphore_signal(barrier, inc=1, device_id=device, device_id_type=MESH)
    return barrier


class RingGather:
    def __init__(self, place, copies, rows, slot):
        self.place, self.copies, self.rows, self.slot = place, copies, rows, slot
        self.step = 0
        self.moving = ()

    def advance(self):
        place, copies = self.place, self.copies
        for copy in self.moving:
            copies.arrive(copy)
        self.moving = ()
        self.step += 1
        cut = self.rows // 2
        if self.step > place.h:
            return
        lower = place.rank_of(1 - self.step)
        upper = place.rank_of(self.step - 1)
        if self.step < place.h:
            whole = pl.ds(0, self.rows)
            pieces = (whole, whole)
        else:
            pieces = (pl.ds(0, cut), pl.ds(cut, self.rows - cut))
        upward, downward = self.slot(lower, pieces[0]), self.slot(upper, pieces[1])
        self.moving = (
            copies.remote(upward, upward, place.up()),
            copies.remote(downward, downward, place.down()),
        )

    def arrived(self):
        step = self.step - 1
        if step == 0:
            return []
        if step == self.place.h:
            return [self.place.rank_of(step)]
        return [self.place.rank_of(-step), self.place.rank_of(step)]


def mlp_kernel(
    n_batch,
    rows_ref,
    gu_ref,
    down_ref,
    cot_ref,
    *refs,
):
    (
        sum_ref,
        act_out,
        term_out,
        gu_out,
        rows_v,
        cot_v,
        gate_v,
        up_v,
        down_v,
        act_v,
        ggate_v,
        gup_v,
        in_v,
        term_v,
        got_v,
        gu_got,
        gu_last,
        send_sems,
        recv_sems,
        back_send,
        back_recv,
        load_sems,
        store_sems,
        part_send,
        part_recv,
    ) = refs
    place = Place(n_batch)
    far = place.h
    n_tok = rows_ref.shape[0]
    cut = n_tok // 2
    width = rows_ref.shape[1]
    ff = gu_ref.shape[-1]
    up_device, down_device = place.up(), place.down()
    far_device, near_device = (place.b, place.far), (place.b, place.near)
    barrier = greet(place, [up_device, down_device, far_device, near_device])
    parts = Copies(part_send, part_recv)
    own_rows = gate_v.shape[2]
    block = 4 * own_rows

    load_rows = pltpu.make_async_copy(rows_ref, rows_v.at[0, pl.ds(0, n_tok)], load_sems.at[0])
    load_rows.start()
    loads = [
        pltpu.make_async_copy(source, target, load_sems.at[1 + i])
        for i, (source, target) in enumerate(
            [(gu_ref.at[0], gate_v), (gu_ref.at[1], up_v), (down_ref, down_v)]
        )
    ]
    spots = [(0, 0, 0), (far, 0, 1)]
    spots += [(side * step, step, (side + 1) // 2) for step in range(1, far) for side in (-1, 1)]
    for i, (distance, group, side) in enumerate(spots):
        loads.append(
            pltpu.make_async_copy(
                cot_ref.at[place.rank_of(distance)], cot_v.at[group, pl.ds(side * n_tok, n_tok)], load_sems.at[4 + i]
            )
        )
    for copy in loads:
        copy.start()
    load_rows.wait()
    pl.semaphore_wait(barrier, 4)

    def piece(side, half):
        return pl.ds(side * n_tok + half * cut, cut)

    def hop(step, side, half):
        source_group, source_side = step - 1, side
        target_group, target_side = step, side
        if isinstance(step, int) and step == 1:
            source_side = 0
        if isinstance(step, int) and step == far:
            target_group, target_side = 0, 1
        return pltpu.make_async_remote_copy(
            src_ref=rows_v.at[source_group, piece(source_side, half)],
            dst_ref=rows_v.at[target_group, piece(target_side, half)],
            send_sem=send_sems.at[step, side, half],
            recv_sem=recv_sems.at[step, side, half],
            device_id=down_device if side else up_device,
            device_id_type=MESH,
        )

    both = [(side, half) for half in (0, 1) for side in (0, 1)]
    ends = [(0, 0), (1, 1)]
    for side, half in both:
        hop(1, side, half).start()
    for copy in loads:
        copy.wait()

    def stores(group):
        return [
            pltpu.make_async_copy(term_v.at[group], term_out.at[group], store_sems.at[0, group]),
            pltpu.make_async_copy(act_v.at[group], act_out.at[group], store_sems.at[1, group]),
        ]

    def compute(group):
        rows = rows_v[group]
        cots = cot_v[group]
        down_all = down_v[...].reshape(ff, width)
        start = 0
        while start < ff:
            size = min(256, ff - start)
            tile = slice(start, start + size)
            gate = dot(rows, gate_v[..., tile].reshape(width, size))
            up = dot(rows, up_v[..., tile].reshape(width, size))
            grad_act = dot_right_t(cots, down_all[tile])
            sigmoid = 1.0 / (1.0 + jnp.exp(-gate))
            silu = gate * sigmoid
            act_v[group, :, tile] = (silu * up).astype(BF)
            slope = sigmoid * (1.0 + gate * (1.0 - sigmoid))
            ggate_v[group, :, tile] = (grad_act * up * slope).astype(BF)
            gup_v[group, :, tile] = (grad_act * silu).astype(BF)
            start += size
        ggate = ggate_v[group]
        gup = gup_v[group]
        act = act_v[group]
        tile_cols = 2 * block

        @pl.loop(0, width // tile_cols)
        def _(t):
            cols = pl.ds(pl.multiple_of(t * tile_cols, tile_cols), tile_cols)
            back = dot_right_t(ggate, gate_v[pl.ds(2 * t, 2)].reshape(tile_cols, ff))
            back += dot_right_t(gup, up_v[pl.ds(2 * t, 2)].reshape(tile_cols, ff))
            in_v[group, :, cols] = back.astype(BF)
            down = down_v[:, :, cols].reshape(ff, tile_cols)
            term_v[group, :, cols] = dot(act, down).astype(BF)

        for copy in stores(group):
            copy.start()

    @pl.loop(1, far)
    def _(step):
        for side, half in both:
            hop(step, side, half).wait_recv()

        @pl.when(step < far - 1)
        def _():
            for side, half in both:
                hop(step + 1, side, half).start()

        @pl.when(step == far - 1)
        def _():
            for side, half in ends:
                hop(far, side, half).start()

        compute(step)

    for side, half in ends:
        hop(far, side, half).wait_recv()
    compute(0)

    def back_hop(step, side, half, source):
        return pltpu.make_async_remote_copy(
            src_ref=source,
            dst_ref=got_v.at[step, side, half],
            send_sem=back_send.at[step, side, half],
            recv_sem=back_recv.at[step, side, half],
            device_id=up_device if side else down_device,
            device_id_type=MESH,
        )

    def held(step, side, half):
        return in_v.at[step, piece(side, half)]

    for side, half in ends:
        back_hop(far - 1, side, half, held(0, 1, half)).start()

    def pass_on(step, side, half, added):
        own = held(step, side, half)
        if added:
            back_hop(step, side, half, own).wait_recv()
            own[...] = (own[...].astype(F32) + got_v[step, side, half].astype(F32)).astype(BF)
        back_hop(step - 1, side, half, own).start()

    for side, half in both:
        if (side, half) not in ends:
            pass_on(far - 1, side, half, False)

    def gate_up_terms(t):
        cols = slice(t * 2 * block, (t + 1) * 2 * block)
        rows = rows_v[:, :, cols].reshape(n_batch * n_tok, 2 * block)
        for target, grads in ((gate_v, ggate_v), (up_v, gup_v)):
            term = dot_left_t(rows, grads[...].reshape(n_batch * n_tok, ff))
            target[2 * t : 2 * t + 2] = term.astype(BF).reshape(2, 4, own_rows, ff)

    def pass_all(step):
        for side, half in [(1, 0), (0, 1), (0, 0), (1, 1)]:
            if step < far - 1 or (side, half) in ends:
                pass_on(step, side, half, True)

    steps = list(range(1, far))
    outer, inner = place.outer, place.inner
    kinds = list(enumerate((gate_v, up_v)))
    near_copies, far_copies = {}, {}

    def send_near(t):
        pair = pl.ds(2 * t, 2)
        near_copies[t] = [
            parts.remote(
                target.at[pair, 2 * side + 1 - inner], gu_got.at[kind, side, pair], near_device
            )
            for side in (0, 1)
            for kind, target in kinds
        ]

    def send_far(t):
        pair = pl.ds(2 * t, 2)
        for copy in near_copies[t]:
            parts.arrive(copy)
        far_copies[t] = []
        for kind, target in kinds:
            other = target.at[pair, 2 * (1 - outer) + inner]
            added = other[...].astype(F32) + gu_got[kind, 1 - outer, pair].astype(F32)
            other[...] = added.astype(BF)
            far_copies[t].append(parts.remote(other, gu_last.at[kind, pair], far_device))

    def take_far(t):
        pair = pl.ds(2 * t, 2)
        for copy in far_copies[t]:
            parts.arrive(copy)
        for kind, target in kinds:
            kept = target.at[pair, 2 * outer + inner]
            added = kept[...].astype(F32) + gu_got[kind, outer, pair].astype(F32)
            kept[...] = (added + gu_last[kind, pair].astype(F32)).astype(BF)
            parts.local(kept, gu_out.at[pair, kind])

    def ring_step():
        if steps:
            pass_all(steps.pop())

    tiles = width // (2 * block)
    for t in range(tiles):
        gate_up_terms(t)
        send_near(t)
        if t > 0:
            send_far(t - 1)
        ring_step()
    while steps:
        ring_step()
    send_far(tiles - 1)
    for half in (0, 1):
        for side in (0, 1):
            back_hop(0, side, half, held(0, 0, half)).wait_recv()
        rows = slice(half * cut, (half + 1) * cut)
        sum_ref[rows, :] = (
            in_v[0, rows, :].astype(F32)
            + got_v[0, 0, half].astype(F32)
            + got_v[0, 1, half].astype(F32)
        )
    for t in range(tiles):
        take_far(t)
    parts.drain()

    for step in range(1, far + 1):
        for side, half in both if step < far else ends:
            hop(step, side, half).wait_send()
    for side, half in ends:
        back_hop(far - 1, side, half, held(0, 1, half)).wait_send()
    for step in range(far - 1, 0, -1):
        for side, half in both:
            back_hop(step - 1, side, half, held(step, side, half)).wait_send()
    for group in range(far):
        for copy in stores(group):
            copy.wait()


def fused_mlp(n_batch, rows, cots, gu_rows, own_down):
    n_tok, width = rows.shape
    ff = gu_rows.shape[-1]
    own_rows = gu_rows.shape[3]
    far = n_batch // 2
    pair = 2 * n_tok
    flops = 18 * n_batch * n_tok * width * ff
    return pl.pallas_call(
        functools.partial(mlp_kernel, n_batch),
        out_shape=(
            jax.ShapeDtypeStruct((n_tok, width), F32),
            jax.ShapeDtypeStruct((far, pair, ff), BF),
            jax.ShapeDtypeStruct((far, pair, width), BF),
            jax.ShapeDtypeStruct((n_batch, 2, own_rows, ff), BF),
        ),
        in_specs=[pl.BlockSpec(memory_space=pl.ANY)] * 4,
        out_specs=[pl.BlockSpec(memory_space=pltpu.VMEM)]
        + [pl.BlockSpec(memory_space=pl.ANY)] * 3,
        scratch_shapes=[
            pltpu.VMEM((far, pair, width), BF),
            pltpu.VMEM((far, pair, width), BF),
            pltpu.VMEM((n_batch, 4, own_rows, ff), BF),
            pltpu.VMEM((n_batch, 4, own_rows, ff), BF),
            pltpu.VMEM((4, ff // 4, width), BF),
            pltpu.VMEM((far, pair, ff), BF),
            pltpu.VMEM((far, pair, ff), BF),
            pltpu.VMEM((far, pair, ff), BF),
            pltpu.VMEM((far, pair, width), BF),
            pltpu.VMEM((far, pair, width), BF),
            pltpu.VMEM((far, 2, 2, n_tok // 2, width), BF),
            pltpu.VMEM((2, 2, n_batch, own_rows, ff), BF),
            pltpu.VMEM((2, n_batch, own_rows, ff), BF),
            pltpu.SemaphoreType.DMA((far + 1, 2, 2)),
            pltpu.SemaphoreType.DMA((far + 1, 2, 2)),
            pltpu.SemaphoreType.DMA((far, 2, 2)),
            pltpu.SemaphoreType.DMA((far, 2, 2)),
            pltpu.SemaphoreType.DMA((4 + n_batch,)),
            pltpu.SemaphoreType.DMA((2, far)),
            pltpu.SemaphoreType.DMA((72,)),
            pltpu.SemaphoreType.DMA((72,)),
        ],
        compiler_params=pltpu.CompilerParams(
            collective_id=1, has_side_effects=True, vmem_limit_bytes=60 * 1024 * 1024
        ),
        cost_estimate=pl.CostEstimate(
            flops=flops, bytes_accessed=24 * 1024 * 1024, transcendentals=n_batch * n_tok * ff
        ),
        name="fused_mlp",
    )(rows, gu_rows, own_down, cots)


class RingCollect:
    def __init__(self, place, block, got, send_sems, recv_sems):
        self.place, self.block, self.got = place, block, got
        self.send_sems, self.recv_sems = send_sems, recv_sems
        self.cut = got.shape[3]
        self.step = place.h
        self.sent = []

    def held(self, step, half):
        return self.block(step).at[pl.ds(half * self.cut, self.cut)]

    def hop(self, step, side, half, source):
        place = self.place
        return pltpu.make_async_remote_copy(
            src_ref=source,
            dst_ref=self.got.at[step, side, half],
            send_sem=self.send_sems.at[step, side, half],
            recv_sem=self.recv_sems.at[step, side, half],
            device_id=place.up() if side else place.down(),
            device_id_type=MESH,
        )

    def send(self, step, side, half, source):
        copy = self.hop(step, side, half, source)
        copy.start()
        self.sent.append(copy)

    def advance(self):
        far = self.place.h
        step = self.step
        self.step -= 1
        if step == far:
            for side in (0, 1):
                self.send(far - 1, side, side, self.held(far, side))
            for side in (0, 1):
                half = 1 - side
                self.send(far - 2, side, half, self.held((2 * side - 1) * (far - 1), half))
            return
        pieces = [(0, 0), (1, 1)] if step == far - 1 else [(1, 0), (0, 1), (0, 0), (1, 1)]
        for side, half in pieces:
            own = self.held((2 * side - 1) * step, half)
            self.hop(step, side, half, own).wait_recv()
            own[...] = (own[...].astype(F32) + self.got[step, side, half].astype(F32)).astype(BF)
            self.send(step - 1, side, half, own)

    def finish(self, half):
        own = self.held(0, half)
        for side in (0, 1):
            self.hop(0, side, half, own).wait_recv()
        return (
            own[...].astype(F32)
            + self.got[0, 0, half].astype(F32)
            + self.got[0, 1, half].astype(F32)
        )

    def drain(self):
        for copy in self.sent:
            copy.wait_send()


def tail_kernel(
    n_batch,
    gain_rows,
    out_ref,
    up_ref,
    rows_ref,
    gu_ref,
    packed_ref,
    back_ref,
    latent_ref,
    tokens_ref,
    hidden_ref,
    gains_ref,
    mlp_term_ref,
    cos_ref,
    sin_ref,
    out_grad,
    up_grad,
    in_grad,
    gain_grad,
    gu_grad,
    tokens_grad,
    out_v,
    up_v,
    in_v,
    out_got,
    up_got,
    in_got,
    up_sum,
    up_all,
    in_sum,
    in_all,
    ring_send,
    ring_recv,
    send_sems,
    recv_sems,
    packed_v,
    project_own,
    project_v,
    rows_v,
    gu_v,
    load_sems,
):
    place = Place(n_batch)
    copies = Copies(send_sems, recv_sems)
    b, c, n = place.b, place.c, n_batch
    own_rows = in_grad.shape[0]
    group = HeadGroup(place, out_grad.shape[0])
    ctx_peers = [(b, place.far), (b, place.near), (b, lax.rem(place.near + 2, 4))]

    loads = [
        pltpu.make_async_copy(held, kept, load_sems.at[i])
        for i, (held, kept) in enumerate([(out_ref, out_v), (up_ref, up_v), (rows_ref, rows_v), (gu_ref, gu_v), (packed_ref, packed_v)])
    ]
    for copy in loads:
        copy.start()
    barrier = greet(place, [place.up(), place.down()] + ctx_peers)

    pl.semaphore_wait(barrier, 5)

    rings = []
    for i, (kept, got) in enumerate([(out_v, out_got), (up_v, up_got), (in_v, in_got)]):
        rings.append(
            RingCollect(
                place,
                lambda step, kept=kept: kept.at[place.rank_of(step)],
                got,
                ring_send.at[i],
                ring_recv.at[i],
            )
        )
    for copy, ring in zip(loads[:2], rings):
        copy.wait()
        ring.advance()
    part_cols = project_v.shape[2]
    n_tok, width = tokens_ref.shape
    latent = latent_ref.shape[1]

    q_latent = latent_ref[...]
    inverse = rms_scale(q_latent)
    normed_query = q_latent * inverse
    grad_qn = back_ref[:, :latent]
    query_term = jnp.sum(grad_qn * normed_query, axis=0, keepdims=True)
    grad_latent = norm_back(grad_qn * gains_ref[2:3, :latent], normed_query, inverse)
    front, back = turn(back_ref[:, latent : latent + HD], cos_ref[...], -sin_ref[...])
    project = jnp.concatenate(
        [grad_latent, front, back, back_ref[:, latent + HD :]], axis=1
    ).astype(BF)
    for part in range(4):
        project_own[part] = project[:, part * part_cols : (part + 1) * part_cols]
    project_copies = [
        copies.remote(project_own.at[peer[1]], project_v.at[c], peer) for peer in ctx_peers
    ]
    project_copies.append(copies.local(project_own.at[c], project_v.at[c]))
    for ring in rings[:2]:
        ring.advance()
    loads[4].wait()
    in_cols = 4 * part_cols
    residual = tokens_ref[...].astype(F32)
    inverse = rms_scale(residual)
    normed = residual * inverse
    weights = packed_v[:, :, :, :in_cols].reshape(width, in_cols)
    grad_attn_in = dot_right_t(project, weights)
    attn_term = jnp.sum(grad_attn_in * normed, axis=0, keepdims=True)
    back = norm_back(grad_attn_in * gains_ref[0:1, :], normed, inverse)
    tokens_grad[...] = (hidden_ref[...] + back).astype(BF)
    for ring in rings[:2]:
        ring.advance()
    for copy in project_copies:
        copies.arrive(copy)
    loads[2].wait()
    project_all = project_v[...].reshape(-1, part_cols)
    part_rows = own_rows + 16
    n_all = project_all.shape[0]
    ahead = max(1, 256 // (4 * own_rows))
    chunk = ahead * 4 * own_rows

    @pl.loop(0, width // chunk)
    def _(t):
        cols = pl.ds(pl.multiple_of(t * chunk, chunk), chunk)
        term = dot_left_t(rows_v[:, :, :, cols].reshape(n_all, chunk), project_all).astype(BF)
        term = term.reshape(ahead, 4, own_rows, part_cols)
        for part in range(4):
            in_v[pl.ds(t * ahead, ahead), pl.ds(part * part_rows, own_rows), :] = term[:, part]

    none = jnp.zeros((16, part_cols), BF)
    wide = jnp.concatenate([attn_term, mlp_term_ref[...], jnp.zeros((14, width), F32)], axis=0)
    short = jnp.concatenate([jnp.zeros((2, latent), F32), query_term], axis=0)
    short = jnp.concatenate([short, jnp.zeros((13, latent), F32)], axis=0)
    for rank in range(n):
        for part in range(4):
            at = pl.ds(part * part_rows + own_rows, 16)
            device = 4 * rank + part
            in_v[rank, at, :] = none
            in_v[rank, at, :own_rows] = wide[
                :, device * own_rows : (device + 1) * own_rows
            ].astype(BF)
            more = short[:, device * gain_rows : (device + 1) * gain_rows].astype(BF)
            kept = in_v[rank, at, :gain_rows]
            in_v[rank, at, :gain_rows] = kept + more
    rings[2].advance()
    if rings[0].step > 0:
        for ring in rings[:2]:
            ring.advance()
    while rings[2].step > 0:
        for ring in rings:
            if ring.step > 0:
                ring.advance()

    loads[3].wait()
    ff = gu_v.shape[3]
    for slab_at in range(n):
        for kind in (0, 1):
            start = (kind * n + slab_at) * ff
            gu_grad[:, start : start + ff] = gu_v[slab_at, kind].astype(F32)

    in_ring, up_ring, out_ring = rings[2], rings[1], rings[0]
    out_cut, up_cut, in_cut = out_ring.cut, up_ring.cut, in_ring.cut
    for half in (0, 1):
        out_grad[half * out_cut : (half + 1) * out_cut, :] = out_ring.finish(half)
    for half in (0, 1):
        up_sum[pl.ds(half * up_cut, up_cut), :] = up_ring.finish(half).astype(BF)
    up_copies = [
        copies.remote(
            up_sum.at[pl.ds(peer[1] * gain_rows, gain_rows)], up_all.at[c], peer
        )
        for peer in ctx_peers
    ]
    up_copies.append(
        copies.local(up_sum.at[pl.ds(c * gain_rows, gain_rows)], up_all.at[c])
    )
    for half in (0, 1):
        in_sum[pl.ds(half * in_cut, in_cut), :] = in_ring.finish(half).astype(BF)
    in_copies = [
        copies.remote(in_sum.at[pl.ds(peer[1] * part_rows, part_rows)], in_all.at[c], peer)
        for peer in ctx_peers
    ]
    in_copies.append(copies.local(in_sum.at[pl.ds(c * part_rows, part_rows)], in_all.at[c]))

    for copy in up_copies:
        copies.arrive(copy)
    cols = up_all.shape[2]
    heads = cols // HD
    for part in range(4):
        for local in range(heads):
            head = group.head(part, local, heads)
            up_grad[:, head * HD : (head + 1) * HD] = up_all[
                part, :, local * HD : (local + 1) * HD
            ].astype(F32)
    for copy in in_copies:
        copies.arrive(copy)
    cols = in_all.shape[2]
    gains = jnp.zeros(gain_grad.shape, F32)
    for part in range(4):
        in_grad[:, part * cols : (part + 1) * cols] = in_all[part, :own_rows, :].astype(F32)
        gains = gains + in_all[part, own_rows:, :].astype(F32)
    gain_grad[...] = gains
    copies.drain()
    for ring in rings:
        ring.drain()


def collect_weights(n_batch, gain_rows, out_terms, up_terms, attn_in_all, grad_gu, packed, own):
    far = n_batch // 2
    out_rows, width = out_terms.shape[1:]
    up_rows, up_cols = up_terms.shape[1:]
    n_tok = own[2].shape[0]
    in_cols = own[0].shape[1] // 4
    own_rows = width // (4 * n_batch)
    in_rows = 4 * (own_rows + 16)
    shapes = [out_terms.shape[1:], up_terms.shape[1:], (in_rows, in_cols)]
    sems = 2 * n_batch + 16
    return pl.pallas_call(
        functools.partial(tail_kernel, n_batch, gain_rows),
        out_shape=(
            jax.ShapeDtypeStruct((out_rows, width), F32),
            jax.ShapeDtypeStruct((gain_rows, 4 * up_cols), F32),
            jax.ShapeDtypeStruct((own_rows, 4 * in_cols), F32),
            jax.ShapeDtypeStruct((16, in_cols), F32),
            jax.ShapeDtypeStruct((own_rows, 2 * n_batch * grad_gu.shape[3]), F32),
            jax.ShapeDtypeStruct((n_tok, width), BF),
        ),
        in_specs=[pl.BlockSpec(memory_space=pl.ANY)] * 5 + [pl.BlockSpec(memory_space=pltpu.VMEM)] * len(own),
        out_specs=[pl.BlockSpec(memory_space=pltpu.VMEM)] * 6,
        scratch_shapes=[pltpu.VMEM((n_batch,) + shape, BF) for shape in shapes]
        + [pltpu.VMEM((far, 2, 2, rows // 2, cols), BF) for rows, cols in shapes]
        + [
            pltpu.VMEM((up_rows, up_cols), BF),
            pltpu.VMEM((4, gain_rows, up_cols), BF),
            pltpu.VMEM((in_rows, in_cols), BF),
            pltpu.VMEM((4, own_rows + 16, in_cols), BF),
            pltpu.SemaphoreType.DMA((3, far, 2, 2)),
            pltpu.SemaphoreType.DMA((3, far, 2, 2)),
            pltpu.SemaphoreType.DMA((sems,)),
            pltpu.SemaphoreType.DMA((sems,)),
            pltpu.VMEM(packed.shape, BF),
            pltpu.VMEM((4, n_tok, in_cols), BF),
            pltpu.VMEM((4, n_tok, in_cols), BF),
            pltpu.VMEM(attn_in_all.shape, BF),
            pltpu.VMEM(grad_gu.shape, BF),
            pltpu.SemaphoreType.DMA((5,)),
        ],
        compiler_params=pltpu.CompilerParams(
            collective_id=2, has_side_effects=True, vmem_limit_bytes=56 * 1024 * 1024
        ),
        name="collect_weights",
    )(out_terms, up_terms, attn_in_all, grad_gu, packed, *own)


class CtxCollect:
    def __init__(self, place, copies, part, near_got, far_got):
        self.place, self.copies, self.part = place, copies, part
        self.near_got, self.far_got = near_got, far_got
        self.near = {}
        self.far = {}

    def start(self, item):
        place = self.place
        self.near[item] = [
            self.copies.remote(
                self.part.at[2 * side + 1 - place.inner, item],
                self.near_got.at[side, item],
                (place.b, place.near),
            )
            for side in (0, 1)
        ]

    def cross(self, item):
        place = self.place
        for copy in self.near[item]:
            self.copies.arrive(copy)
        other = self.part.at[2 * (1 - place.outer) + place.inner, item]
        added = other[...].astype(F32) + self.near_got[1 - place.outer, item].astype(F32)
        other[...] = added.astype(BF)
        self.far[item] = self.copies.remote(
            other, self.far_got.at[item], (place.b, place.far)
        )

    def finish(self, item):
        place = self.place
        self.copies.arrive(self.far[item])
        return (
            self.part[2 * place.outer + place.inner, item].astype(F32)
            + self.near_got[place.outer, item].astype(F32)
            + self.far_got[item].astype(F32)
        )


class CtxGather:
    def __init__(self, place, copies, everyone):
        self.place, self.copies, self.everyone = place, copies, everyone
        self.far = {}
        self.near = {}

    def start(self, item):
        place = self.place
        own = self.everyone.at[place.c, item]
        self.far[item] = self.copies.remote(own, own, (place.b, place.far))
        self.near[item] = [self.copies.remote(own, own, (place.b, place.near))]

    def cross(self, item):
        place = self.place
        self.copies.arrive(self.far[item])
        other = self.everyone.at[place.far, item]
        self.near[item].append(self.copies.remote(other, other, (place.b, place.near)))

    def finish(self, item):
        for copy in self.near[item]:
            self.copies.arrive(copy)


def greet_lines(place):
    devices = [place.up(), place.down(), (place.b, place.far), (place.b, place.near)]
    pl.semaphore_wait(greet(place, devices), 4)


def turn(values, cosine, sine):
    half_size = HD // 2
    front, back = values[:, :half_size], values[:, half_size:]
    return front * cosine - back * sine, back * cosine + front * sine


def softmax_rows(queries, keys, keep, score_scale):
    scores = dot_right_t(queries, keys) * score_scale
    rows = lax.broadcasted_iota(jnp.int32, scores.shape, 0)
    cols = lax.broadcasted_iota(jnp.int32, scores.shape, 1)
    masked = jnp.where((cols <= rows) & (keep > 0.5), scores, -1e30)
    raised = jnp.exp(masked - jnp.max(masked, axis=-1, keepdims=True))
    return raised / jnp.sum(raised, axis=-1, keepdims=True)

def head_group(n_batch, own_rows):
    return min(4, HD // own_rows)


class HeadGroup:
    def __init__(self, place, own_rows):
        self.size = head_group(place.n, own_rows)
        self.count = place.n // self.size
        if self.size == 2:
            self.me = place.inner
            self.others = [(1 - place.inner, (place.b, place.near))]
        else:
            self.me = place.c
            ranks = [place.far, place.near, lax.rem(place.near + 2, 4)]
            self.others = [(rank, (place.b, rank)) for rank in ranks]

    def blocks(self, member):
        return pl.ds(member * self.count, self.count)

    def head(self, rank, local, heads):
        if self.size == 2:
            return 2 * (heads * (rank % 2) + local) + rank // 2
        return heads * rank + local


def front_kernel(
    n_batch,
    heads,
    packed_ref,
    up_ref,
    out_ref,
    gu_ref,
    down_ref,
    tokens_ref,
    cot_ref,
    cos_ref,
    sin_ref,
    cos_own_ref,
    sin_own_ref,
    keep_ref,
    hidden,
    mlp_in,
    gains,
    latents,
    packed_out,
    up_out,
    out_out,
    gu_all,
    down_all,
    qkv_out,
    turned_out,
    mixed_out,
    rows_out,
    cot_all,
    packed_v,
    flat_v,
    gu_v,
    half_v,
    out_v,
    up_v,
    tokens_v,
    rows_v,
    down_v,
    cot_v,
    qkv_v,
    turned_v,
    mixed_v,
    part_v,
    near_got,
    far_got,
    send_sems,
    recv_sems,
):
    place = Place(n_batch)
    copies = Copies(send_sems, recv_sems)
    b, c, n = place.b, place.c, n_batch
    own_rows = packed_ref.shape[0]
    gain_rows = up_ref.shape[0]
    out_rows = out_ref.shape[0]
    n_tok, width = tokens_ref.shape
    micro, pos_dev = qkv_v.shape[1:3]
    length = 4 * pos_dev
    in_cols = qkv_v.shape[3]
    latent = in_cols - 2 * HD
    ff = gu_v.shape[3]
    score_scale = 1.0 / math.sqrt(HD)
    group = HeadGroup(place, out_rows)
    peers = [(lax.rem(b + k, n), c) for k in range(1, n)]
    ctx_peers = [(b, place.far), (b, place.near), (b, lax.rem(place.near + 2, 4))]
    far_device, near_device = ctx_peers[0], ctx_peers[1]

    barrier = greet(place, peers + ctx_peers)
    own_packed = copies.local(packed_ref, packed_v.at[b, c])
    own_out = copies.local(out_ref, half_v.at[b])
    own_tokens = copies.local(tokens_ref, tokens_v)
    own_flat = copies.local(gu_ref, flat_v)
    own_down = copies.local(down_ref, down_v)
    own_cot = copies.local(cot_ref, cot_v)

    def up_cols(rank, local):
        start = pl.multiple_of(group.head(rank, local, heads) * HD, HD)
        return up_ref.at[:, pl.ds(start, HD)]

    own_up = [
        copies.local(up_cols(c, local), up_v.at[b, c, :, pl.ds(local * HD, HD)])
        for local in range(heads)
    ]
    pl.semaphore_wait(barrier, n + 2)
    up_copies = [
        copies.remote(up_cols(peer[1], local), up_v.at[b, c, :, pl.ds(local * HD, HD)], peer)
        for peer in ctx_peers
        for local in range(heads)
    ]
    copies.arrive(own_packed)
    packed_ring = RingGather(place, copies, own_rows, lambda rank, rows: packed_v.at[rank, c, rows])
    up_ring = RingGather(place, copies, gain_rows, lambda rank, rows: up_v.at[rank, :, rows])
    out_ring = RingGather(place, copies, out_rows, lambda rank, rows: half_v.at[rank, rows])
    cot_ring = RingGather(place, copies, n_tok, lambda rank, rows: cot_all.at[rank, rows])
    packed_far = []

    def packed_step():
        packed_ring.advance()
        ranks = packed_ring.arrived() if packed_ring.step > 1 else [b]
        for rank in ranks:
            block = packed_v.at[rank, c]
            packed_far.append(copies.remote(block, block, far_device))

    packed_step()
    copies.arrive(own_down)
    copies.local(down_v, down_all.at[c])
    down_far = copies.remote(down_v, down_all.at[c], far_device)
    copies.remote(down_v, down_all.at[c], near_device)
    copies.arrive(own_flat)
    for slab_at in range(n):
        for kind in (0, 1):
            start = (kind * n + slab_at) * ff
            gu_v[slab_at, kind] = flat_v[:, start : start + ff]
    own_gu = copies.local(gu_v.at[b], gu_all.at[:, b, c])
    gu_copies = []
    gu_far = []
    waiting = []

    def send_gu(count):
        for _ in range(count):
            k = len(gu_copies) + 1
            if k < n:
                peer = peers[k - 1]
                copy = copies.remote(gu_v.at[peer[0]], gu_all.at[:, b, c], peer)
                gu_copies.append(copy)
                waiting.append((lax.rem(b - k + n, n), copy))

    def forward_gu(count):
        for _ in range(min(count, len(waiting))):
            rank, copy = waiting.pop(0)
            copies.arrive(copy)
            block = gu_all.at[:, rank, c]
            gu_far.append(copies.remote(block, block, far_device))

    for copy in own_up + up_copies:
        copies.arrive(copy)
    up_ring.advance()
    packed_step()
    send_gu(n // 2)
    up_ring.advance()
    while packed_ring.step <= place.h:
        packed_step()
        up_ring.advance()
    copies.arrive(own_out)
    out_ring.advance()
    mine = packed_v.at[:, c]
    packed_near = [copies.remote(mine, mine, near_device)]
    while up_ring.step <= place.h:
        up_ring.advance()
    copies.arrive(own_gu)
    gu_far.append(copies.remote(gu_all.at[:, b, c], gu_all.at[:, b, c], far_device))
    send_gu(n)
    out_ring.advance()
    for copy in packed_far:
        copies.arrive(copy)
    theirs = packed_v.at[:, place.far]
    packed_near.append(copies.remote(theirs, theirs, near_device))
    copies.arrive(down_far)
    copies.remote(down_all.at[place.far], down_all.at[place.far], near_device)

    copies.arrive(own_tokens)
    residual = tokens_v[...].astype(F32)
    normed = residual * rms_scale(residual)
    for copy in packed_near:
        copies.arrive(copy)
    extra = packed_v[:, :, :, in_cols:].astype(F32)
    gain_wide = jnp.transpose(extra.reshape(width, 128))
    gain_query = jnp.transpose(extra[:, :, :gain_rows].reshape(latent, 128))[2:3]
    gains[0:2, :] = gain_wide[0:2]
    gains[2:3, :latent] = gain_query
    attn_in = (normed * gain_wide[0:1]).astype(BF)
    rows_v[...] = attn_in
    tile = 512
    for start in range(0, in_cols, tile):
        weights = packed_v[:, :, :, start : start + tile].reshape(width, tile)
        part = dot(attn_in, weights)
        if start + tile <= latent:
            latents[:, start : start + tile] = part
        else:
            front, back = turn(part[:, :HD], cos_own_ref[...], sin_own_ref[...])
            half = HD // 2
            qkv_v[c, :, :, latent : latent + half] = (
                front.astype(BF).reshape(micro, pos_dev, half)
            )
            qkv_v[c, :, :, latent + half : latent + HD] = (
                back.astype(BF).reshape(micro, pos_dev, half)
            )
            qkv_v[c, :, :, latent + HD :] = part[:, HD:].astype(BF).reshape(micro, pos_dev, HD)
    q_latent = latents[...]
    q_normed = q_latent * rms_scale(q_latent) * gain_query
    qkv_v[c, :, :, :latent] = q_normed.astype(BF).reshape(micro, pos_dev, latent)
    qkv = CtxGather(place, copies, qkv_v)
    for item in range(micro):
        qkv.start(item)
    copies.local(rows_v, rows_out)
    for item in range(micro):
        qkv.cross(item)
    out_ring.advance()
    forward_gu(n // 2)
    cosine, sine = cos_ref[...], sin_ref[...]
    for item in range(micro):
        qkv.finish(item)
        q_all = qkv_v[:, item, :, :latent].reshape(length, latent)
        keys = qkv_v[:, item, :, latent : latent + HD].reshape(length, HD)
        values = qkv_v[:, item, :, latent + HD :].reshape(length, HD)
        keep = keep_ref[item]

        @pl.loop(0, heads)
        def _(head):
            base = pl.multiple_of(head * HD, HD)
            cols = pl.ds(base, HD)
            up = up_v[:, :, :, cols].reshape(latent, HD)
            front, back = turn(dot(q_all, up), cosine, sine)
            turned_v[item, :, pl.ds(base, HD // 2)] = front.astype(BF)
            upper = pl.multiple_of(base + HD // 2, HD // 2)
            turned_v[item, :, pl.ds(upper, HD // 2)] = back.astype(BF)
            weights = softmax_rows(turned_v[item, :, cols], keys, keep, score_scale)
            mixed = dot(weights.astype(BF), values).astype(BF)
            mixed_v[:, item, :, cols] = mixed.reshape(4, pos_dev, HD)

        if out_ring.step < place.h:
            out_ring.advance()
    while out_ring.step < place.h:
        out_ring.advance()

    copies.arrive(own_cot)
    copies.arrive(copies.local(cot_v, cot_all.at[b]))
    cot_ring.advance()
    out_ring.advance()
    out_swaps = [
        copies.remote(half_v.at[group.blocks(member)], out_v.at[:, group.me], device)
        for member, device in group.others
    ]
    out_swaps.append(copies.local(half_v.at[group.blocks(group.me)], out_v.at[:, group.me]))
    forward_gu(n)
    for copy in out_swaps:
        copies.arrive(copy)
    attended_sum = CtxCollect(place, copies, part_v, near_got, far_got)
    for item in range(micro):
        mixed = mixed_v[:, item].reshape(length, heads * HD)

        @pl.loop(0, width // 512)
        def _(t):
            cols = pl.ds(pl.multiple_of(t * 512, 512), 512)
            weights = out_v[:, :, :, cols].reshape(heads * HD, 512)
            part = dot(mixed, weights).astype(BF)
            part_v[:, item, :, cols] = part.reshape(4, pos_dev, 512)

        attended_sum.start(item)
        if item > 0:
            attended_sum.cross(item - 1)
    cot_ring.advance()
    attended_sum.cross(micro - 1)
    copies.local(packed_v, packed_out)
    copies.local(up_v, up_out)
    copies.local(out_v, out_out)
    copies.local(qkv_v, qkv_out)
    copies.local(turned_v, turned_out)
    copies.local(mixed_v, mixed_out)
    for item in range(micro):
        at = slice(item * pos_dev, (item + 1) * pos_dev)
        total = tokens_v[at, :].astype(F32) + attended_sum.finish(item)
        hidden[at, :] = total
        mlp_in[at, :] = (total * rms_scale(total) * gains[1:2, :]).astype(BF)
    mine = gu_all.at[:, :, c]
    copies.remote(mine, mine, near_device)
    while cot_ring.step <= place.h:
        cot_ring.advance()
    for copy in gu_far:
        copies.arrive(copy)
    theirs = gu_all.at[:, :, place.far]
    copies.remote(theirs, theirs, near_device)
    copies.drain()


def front(n_batch, heads, packed, query_up, proj_out, gate_up, down, tokens, cots, tables):
    own_rows, packed_cols = packed.shape
    in_cols = packed_cols - 128
    latent = in_cols - 2 * HD
    gain_rows = query_up.shape[0]
    out_rows, width = proj_out.shape
    n_tok = cots.shape[0]
    pos_dev = tables[0].shape[0] // 4
    micro = n_tok // pos_dev
    ff = gate_up.shape[1] // (2 * n_batch)
    size = head_group(n_batch, out_rows)
    head_cols = heads * HD
    shapes = {
        "packed": (n_batch, 4, own_rows, packed_cols),
        "up": (n_batch, 4, gain_rows, head_cols),
        "out": (n_batch // size, size, out_rows, width),
        "gu": (2, n_batch, 4, own_rows, ff),
        "down": (4,) + down.shape,
        "qkv": (4, micro, pos_dev, in_cols),
        "turned": (micro, 4 * pos_dev, head_cols),
        "mixed": (4, micro, pos_dev, head_cols),
        "rows": (n_tok, width),
        "cot": (n_batch, n_tok, width),
    }
    anywhere = pl.BlockSpec(memory_space=pl.ANY)
    near = pl.BlockSpec(memory_space=pltpu.VMEM)
    sems = 13 * n_batch + 100
    return pl.pallas_call(
        functools.partial(front_kernel, n_batch, heads),
        out_shape=(
            jax.ShapeDtypeStruct((n_tok, width), F32),
            jax.ShapeDtypeStruct((n_tok, width), BF),
            jax.ShapeDtypeStruct((8, width), F32),
            jax.ShapeDtypeStruct((n_tok, latent), F32),
        )
        + tuple(jax.ShapeDtypeStruct(shape, BF) for shape in shapes.values()),
        in_specs=[anywhere] * 7 + [near] * 5,
        out_specs=[near] * 4 + [anywhere] * len(shapes),
        scratch_shapes=[
            pltpu.VMEM(shapes["packed"], BF),
            pltpu.VMEM(gate_up.shape, BF),
            pltpu.VMEM((n_batch, 2, own_rows, ff), BF),
            pltpu.VMEM((n_batch, out_rows, width), BF),
            pltpu.VMEM(shapes["out"], BF),
            pltpu.VMEM(shapes["up"], BF),
            pltpu.VMEM((n_tok, width), BF),
            pltpu.VMEM((n_tok, width), BF),
            pltpu.VMEM(down.shape, BF),
            pltpu.VMEM((n_tok, width), BF),
            pltpu.VMEM(shapes["qkv"], BF),
            pltpu.VMEM(shapes["turned"], BF),
            pltpu.VMEM(shapes["mixed"], BF),
            pltpu.VMEM((4, micro, pos_dev, width), BF),
            pltpu.VMEM((2, micro, pos_dev, width), BF),
            pltpu.VMEM((micro, pos_dev, width), BF),
            pltpu.SemaphoreType.DMA((sems,)),
            pltpu.SemaphoreType.DMA((sems,)),
        ],
        compiler_params=pltpu.CompilerParams(
            collective_id=0, has_side_effects=True, vmem_limit_bytes=56 * 1024 * 1024
        ),
        name="front",
    )(packed, query_up, proj_out, gate_up, down, tokens, cots, *tables)


def attention_back_kernel(
    n_batch,
    heads,
    has_terms,
    grad_ref,
    qkv_ref,
    turned_ref,
    mixed_ref,
    up_ref,
    out_ref,
    gu_ref,
    down_ref,
    rows_ref,
    *refs,
):
    terms_ref, cot_ref, refs = (refs[0], refs[1], refs[2:]) if has_terms else (None, None, refs)
    (
        cos_ref,
        sin_ref,
        keep_ref,
        back_out,
        out_terms,
        up_terms,
        gu_grad,
        down_grad,
        rows_all,
    ) = refs[:9]
    terms_sum, refs = (refs[9], refs[10:]) if has_terms else (None, refs[9:])
    (
        grad_v,
        qkv_v,
        turned_v,
        mixed_v,
        up_v,
        out_v,
        qgrad_v,
        kgrad_v,
        vgrad_v,
        part_v,
        near_got,
        far_got,
        outgrad_v,
        upgrad_v,
        down_v,
        gu_v,
        rows_v,
        send_sems,
        recv_sems,
        load_sems,
    ) = refs[:20]
    place = Place(n_batch)
    copies = Copies(send_sems, recv_sems)
    b, c, n = place.b, place.c, n_batch
    micro, pos_dev, width = grad_ref.shape
    length = 4 * pos_dev
    head_cols = heads * HD
    latent = qkv_ref.shape[3] - 2 * HD
    score_scale = 1.0 / math.sqrt(HD)
    pairs = [
        (grad_ref, grad_v.at[c]),
        (out_ref, out_v),
        (qkv_ref, qkv_v),
        (turned_ref, turned_v),
        (up_ref, up_v),
        (mixed_ref, mixed_v),
    ]
    if has_terms:
        (
            terms_v,
            terms_got,
            ring_send,
            ring_recv,
            act_v,
            cot_v,
            down_all,
            down_got,
        ) = refs[20:]
        pairs += [(terms_ref, terms_v), (down_ref, act_v)]
        n_tok = terms_v.shape[1]
        spots = [(0, 0, 0), (place.h, 0, 1)]
        spots += [
            (side * step, step, (side + 1) // 2) for step in range(1, place.h) for side in (-1, 1)
        ]
        pairs += [
            (cot_ref.at[place.rank_of(step)], cot_v.at[pair, pl.ds(side * n_tok, n_tok)])
            for step, pair, side in spots
        ]
    loads = [
        pltpu.make_async_copy(source, target, load_sems.at[i])
        for i, (source, target) in enumerate(pairs)
    ]
    for copy in loads:
        copy.start()
    peers = [(lax.rem(b + k, n), c) for k in range(1, n)]
    others = peers + [(b, place.far), (b, place.near), (b, lax.rem(place.near + 2, 4))]
    pl.semaphore_wait(greet(place, others), n + 2)
    out_rows = out_terms.shape[1]
    group = HeadGroup(place, out_rows)
    loads[0].wait()
    grads = CtxGather(place, copies, grad_v)
    for item in range(micro):
        grads.start(item)
    steps = []
    if has_terms:

        def spot(step):
            return 0 if step == 0 else 1 if step == place.h else 2 * abs(step) + (step > 0)

        terms = RingCollect(
            place, lambda step: terms_v.at[spot(step)], terms_got, ring_send, ring_recv
        )
        loads[6].wait()
        steps = [terms.advance] * place.h

    def ring_step():
        if steps:
            steps.pop()()

    ring_step()
    own_gu = copies.local(gu_ref.at[b], gu_v)
    own_rows = copies.local(rows_ref, rows_v.at[c, 0])
    for peer in peers:
        copies.remote(gu_ref.at[peer[0]], gu_grad.at[b], peer)
    for item in range(micro):
        grads.cross(item)
    outer, inner = place.outer, place.inner
    if has_terms:
        for copy in loads[7:]:
            copy.wait()
        n_rows = cot_v.shape[0] * cot_v.shape[1]
        ff = act_v.shape[2]

        @pl.loop(0, width // 512)
        def _(t):
            cols = pl.ds(pl.multiple_of(t * 512, 512), 512)
            term = dot_left_t(
                act_v[...].reshape(n_rows, ff), cot_v[:, :, cols].reshape(n_rows, 512)
            )
            down_all[:, :, cols] = term.astype(BF).reshape(4, ff // 4, 512)

        down_near = [
            copies.remote(down_all.at[2 * side + 1 - inner], down_got.at[side], (b, place.near))
            for side in (0, 1)
        ]
    else:
        down_own = copies.local(down_ref.at[outer], down_v.at[0])
        down_far = copies.remote(down_ref.at[1 - outer], down_v.at[1], (b, place.far))
    for copy in loads[1:6]:
        copy.wait()
    if has_terms:
        for copy in down_near:
            copies.arrive(copy)
        other = down_all.at[2 * (1 - outer) + inner]
        other[...] = (other[...].astype(F32) + down_got[1 - outer].astype(F32)).astype(BF)
        down_far = copies.remote(other, down_v.at[1], (b, place.far))
    copies.arrive(own_rows)
    rows = CtxGather(place, copies, rows_v)
    rows.start(0)
    back_sum = CtxCollect(place, copies, part_v, near_got, far_got)
    cosine, sine = cos_ref[...], sin_ref[...]
    for item in range(micro):
        grads.finish(item)
        incoming = grad_v[:, item].reshape(length, width)
        keys = qkv_v[:, item, :, latent : latent + HD].reshape(length, HD)
        values = qkv_v[:, item, :, latent + HD :].reshape(length, HD)
        keep = keep_ref[item]
        kgrad_v[...] = jnp.zeros_like(kgrad_v)
        vgrad_v[...] = jnp.zeros_like(vgrad_v)

        @pl.loop(0, heads)
        def _(head):
            cols = pl.ds(pl.multiple_of(head * HD, HD), HD)
            grad_mixed = dot_right_t(incoming, out_v[head]).astype(BF)
            queries = turned_v[item, :, cols]
            weights = softmax_rows(queries, keys, keep, score_scale)
            grad_probs = dot_right_t(grad_mixed, values)
            row_dot = jnp.sum(weights * grad_probs, axis=-1, keepdims=True)
            grad_scores = (weights * (grad_probs - row_dot)).astype(BF)
            front, back = turn(dot(grad_scores, keys) * score_scale, cosine, -sine)
            front, back = front.astype(BF), back.astype(BF)
            base = pl.multiple_of(head * HD, HD)
            qgrad_v[:, item, :, pl.ds(base, HD // 2)] = front.reshape(4, pos_dev, HD // 2)
            base = pl.multiple_of(head * HD + HD // 2, HD // 2)
            qgrad_v[:, item, :, pl.ds(base, HD // 2)] = back.reshape(4, pos_dev, HD // 2)
            kgrad_v[...] += dot_left_t(grad_scores, queries) * score_scale
            vgrad_v[...] += dot_left_t(weights.astype(BF), grad_mixed)

        ring_step()
        qgrad = qgrad_v[:, item].reshape(length, head_cols)
        part_v[:, item, :, :latent] = (
            dot_right_t(qgrad, up_v[...]).astype(BF).reshape(4, pos_dev, latent)
        )
        part_v[:, item, :, latent : latent + HD] = (
            kgrad_v[...].astype(BF).reshape(4, pos_dev, HD)
        )
        part_v[:, item, :, latent + HD :] = vgrad_v[...].astype(BF).reshape(4, pos_dev, HD)
        back_sum.start(item)
        if item > 0:
            back_sum.cross(item - 1)
    n_all = 4 * micro * pos_dev
    back_sum.cross(micro - 1)
    ring_step()

    @pl.loop(0, width // 512)
    def _(t):
        cols = pl.ds(pl.multiple_of(t * 512, 512), 512)
        term = dot_left_t(
            mixed_v[...].reshape(n_all, head_cols), grad_v[:, :, :, cols].reshape(n_all, 512)
        )
        outgrad_v[:, :, :, cols] = term.astype(BF).reshape(group.count, group.size, out_rows, 512)

    mine = out_terms.at[group.blocks(group.me)]
    copies.local(outgrad_v.at[:, group.me], mine)
    for member, device in group.others:
        copies.remote(outgrad_v.at[:, member], mine, device)
    for item in range(micro):
        back_out[item] = back_sum.finish(item)
    ring_step()

    @pl.loop(0, head_cols // HD)
    def _(t):
        cols = pl.ds(pl.multiple_of(t * HD, HD), HD)
        term = dot_left_t(
            qkv_v[:, :, :, :latent].reshape(n_all, latent),
            qgrad_v[:, :, :, cols].reshape(n_all, HD),
        )
        upgrad_v[:, :, cols] = term.astype(BF).reshape(n, latent // n, HD)

    copies.local(upgrad_v, up_terms)
    rows.cross(0)
    rows.finish(0)
    copies.local(rows_v, rows_all)
    copies.arrive(own_gu)
    copies.local(gu_v, gu_grad.at[b])
    copies.arrive(down_far)
    if has_terms:
        down_grad[...] = (
            down_all[2 * outer + inner].astype(F32)
            + down_got[outer].astype(F32)
            + down_v[1].astype(F32)
        )
    else:
        copies.arrive(down_own)
        down_grad[...] = down_v[0].astype(F32) + down_v[1].astype(F32)
    if has_terms:
        while steps:
            ring_step()
        cut = terms.cut
        for half in (0, 1):
            terms_sum[half * cut : (half + 1) * cut, :] = terms.finish(half)
        terms.drain()
    copies.drain()


def attention_back(
    n_batch, grad_att, qkv_all, turned, mixed, own_qup, own_out, grad_gu, down_part, attn_in, terms, cots, tables
):
    micro, pos_dev, width = grad_att.shape
    n_tok = micro * pos_dev
    qkv_cols = qkv_all.shape[3]
    latent, head_cols = own_qup.shape
    own_out = own_out.reshape(head_cols // HD, HD, width)
    length = 4 * pos_dev
    far = n_batch // 2
    has_terms = terms is not None
    down_rows = down_part.shape[2] // 4 if has_terms else down_part.shape[1]
    size = head_group(n_batch, head_cols // n_batch)
    sems = 2 * n_batch + 48
    anywhere = pl.BlockSpec(memory_space=pl.ANY)
    near = pl.BlockSpec(memory_space=pltpu.VMEM)
    out_shape = [
        jax.ShapeDtypeStruct((micro, pos_dev, qkv_cols), F32),
        jax.ShapeDtypeStruct((n_batch, head_cols // n_batch, width), BF),
        jax.ShapeDtypeStruct((n_batch, latent // n_batch, head_cols), BF),
        jax.ShapeDtypeStruct(grad_gu.shape, BF),
        jax.ShapeDtypeStruct((down_rows, width), F32),
        jax.ShapeDtypeStruct((4, 1) + attn_in.shape, BF),
    ]
    out_specs = [near] + [anywhere] * 3 + [near, anywhere]
    scratch = [
        pltpu.VMEM((4, micro, pos_dev, width), BF),
        pltpu.VMEM((4, micro, pos_dev, qkv_cols), BF),
        pltpu.VMEM((micro, length, head_cols), BF),
        pltpu.VMEM((4, micro, pos_dev, head_cols), BF),
        pltpu.VMEM((latent, head_cols), BF),
        pltpu.VMEM((head_cols // HD, HD, width), BF),
        pltpu.VMEM((4, micro, pos_dev, head_cols), BF),
        pltpu.VMEM((length, HD), F32),
        pltpu.VMEM((length, HD), F32),
        pltpu.VMEM((4, micro, pos_dev, qkv_cols), BF),
        pltpu.VMEM((2, micro, pos_dev, qkv_cols), BF),
        pltpu.VMEM((micro, pos_dev, qkv_cols), BF),
        pltpu.VMEM((n_batch // size, size, head_cols // n_batch, width), BF),
        pltpu.VMEM((n_batch, latent // n_batch, head_cols), BF),
        pltpu.VMEM((2, down_rows, width), BF),
        pltpu.VMEM(grad_gu.shape[1:], BF),
        pltpu.VMEM((4, 1) + attn_in.shape, BF),
        pltpu.SemaphoreType.DMA((sems,)),
        pltpu.SemaphoreType.DMA((sems,)),
        pltpu.SemaphoreType.DMA((8 + n_batch,)),
    ]
    args = [grad_att, qkv_all, turned, mixed, own_qup, own_out, grad_gu, down_part, attn_in]
    if has_terms:
        args += [terms, cots]
        out_shape.append(jax.ShapeDtypeStruct((n_tok, width), F32))
        out_specs.append(near)
        scratch += [
            pltpu.VMEM(terms.shape, BF),
            pltpu.VMEM((far, 2, 2, n_tok // 2, width), BF),
            pltpu.SemaphoreType.DMA((far, 2, 2)),
            pltpu.SemaphoreType.DMA((far, 2, 2)),
            pltpu.VMEM(down_part.shape, BF),
            pltpu.VMEM((far, 2 * n_tok, width), BF),
            pltpu.VMEM((4, down_rows, width), BF),
            pltpu.VMEM((2, down_rows, width), BF),
        ]
    return pl.pallas_call(
        functools.partial(attention_back_kernel, n_batch, head_cols // HD, has_terms),
        out_shape=tuple(out_shape),
        in_specs=[anywhere] * len(args) + [near] * 3,
        out_specs=out_specs,
        scratch_shapes=scratch,
        compiler_params=pltpu.CompilerParams(
            collective_id=4, has_side_effects=True, vmem_limit_bytes=56 * 1024 * 1024
        ),
        name="attention_back",
    )(*args, *tables)


def permuted_mlp(ring, rows_own, cots, gu_rows, own_down):
    mlp_in = ring.spread(rows_own)
    n_tok, width = rows_own.shape
    _, n_batch, n_ctx, own_rows, ff = gu_rows.shape
    own_gate, own_up = gu_rows.reshape(2, width, ff)
    own_down = own_down.reshape(ff, width)
    far = ring.h
    groups = [[0]] + [[-step, step] for step in range(1, far)] + [[far]]
    out_terms = {}
    in_terms = {}
    kept = []
    for group in groups:
        rows = jnp.concatenate([mlp_in[step] for step in group], axis=0)
        grad_rows = jnp.concatenate([pick(cots, ring.rank_of(step)) for step in group], axis=0)
        gate_part = dot(rows, own_gate)
        up_part = dot(rows, own_up)
        sigmoid_gate = jax.nn.sigmoid(gate_part)
        silu_gate = gate_part * sigmoid_gate
        activated = (silu_gate * up_part).astype(BF)
        grad_act = dot_right_t(grad_rows, own_down)
        grad_gate = (
            grad_act * up_part * (sigmoid_gate * (1.0 + gate_part * (1.0 - sigmoid_gate)))
        ).astype(BF)
        grad_up = (grad_act * silu_gate).astype(BF)
        in_term = dot_right_t(grad_gate, own_gate) + dot_right_t(grad_up, own_up)
        out_term = dot(activated, own_down)
        for place_in, step in enumerate(group):
            cut = slice(place_in * n_tok, (place_in + 1) * n_tok)
            in_terms[step] = in_term[cut]
            out_terms[step] = out_term[cut]
        kept.append((rows, grad_rows, activated, grad_gate, grad_up))
    rows, grad_rows, activated, grad_gate, grad_up = (
        jnp.concatenate(items, axis=0) for items in zip(*kept)
    )
    grad_gu = jnp.stack([dot_left_t(rows, grad_gate), dot_left_t(rows, grad_up)])
    grad_gu = grad_gu.reshape(2, n_batch, n_ctx, own_rows, ff).transpose(2, 1, 0, 3, 4)
    grad_down = dot_left_t(activated, grad_rows)
    return (
        ring.collect(lambda step: in_terms[step]),
        near_collect(grad_down.reshape(n_ctx, ff // n_ctx, width)).astype(BF),
        out_terms,
        ctx_collect(grad_gu).astype(BF),
    )


def shards(
    tokens,
    cotangent,
    lengths,
    slot_sequence,
    proj_in,
    query_up,
    proj_out,
    attn_gain,
    query_gain,
    mlp_gain,
    gate_up,
    down_proj,
):
    n_ctx = lax.axis_size("ctx")
    n_batch = lax.axis_size("batch")
    ctx_rank = lax.axis_index("ctx")
    batch_rank = lax.axis_index("batch")
    ring = Ring()
    micro, pos_dev, width = tokens.shape
    n_tok = micro * pos_dev
    full_length = pos_dev * n_ctx
    heads = H // n_ctx
    score_scale = 1.0 / math.sqrt(HD)
    in_cols = proj_in.shape[1]

    slot_total = lengths.shape[0]
    slot_ids = jnp.arange(slot_total, dtype=jnp.int32)
    seq_lengths = jnp.sum(
        jnp.where(slot_sequence[:, None] == slot_ids[None, :], lengths[None, :], 0), axis=1
    )
    own_lengths = lax.dynamic_slice_in_dim(seq_lengths, batch_rank * micro, micro)
    query_pos = ctx_rank * pos_dev + jnp.arange(pos_dev, dtype=jnp.int32)
    key_pos = jnp.arange(full_length, dtype=jnp.int32)
    cos_all, sin_all = rope_tables(key_pos)
    cos_own, sin_own = rope_tables(query_pos)

    own_rows = proj_in.shape[0]
    gain_rows = query_gain.shape[0]
    gains = jnp.stack(
        [attn_gain, mlp_gain, jnp.pad(query_gain, (0, own_rows - gain_rows))], axis=1
    )
    packed = jnp.concatenate([proj_in, jnp.pad(gains, ((0, 0), (0, 125)))], axis=1)
    valid_rows = (query_pos[None, :] < own_lengths[:, None]).astype(F32).reshape(n_tok, 1)
    grad_out = cotangent.reshape(n_tok, width).astype(F32) * valid_rows
    keep = (key_pos[None, None, :] < own_lengths[:, None, None]).astype(F32)
    tables = (cos_all, sin_all, jnp.tile(cos_own, (micro, 1)), jnp.tile(sin_own, (micro, 1)), keep)
    (
        hidden_res,
        mlp_in,
        gains,
        q_latent,
        packed,
        own_qup,
        own_out,
        gu_rows,
        own_down,
        qkv_all,
        turned,
        mixed,
        attn_in,
        cots,
    ) = front(
        n_batch,
        heads,
        packed,
        query_up,
        proj_out,
        gate_up,
        down_proj,
        tokens.reshape(n_tok, width),
        grad_out.astype(BF),
        tables,
    )
    own_qup = own_qup.reshape(QR, heads * HD)
    gain_mlp = gains[1]

    scale_two = rms_scale(hidden_res)
    normed_two = hidden_res * scale_two
    resident = 10 * n_batch * n_tok * width <= 24 * 1024 * 1024
    if resident:
        grad_mlp_in, down_part, terms, grad_gu_own = fused_mlp(
            n_batch, mlp_in, cots, gu_rows, own_down
        )
        terms = terms.reshape(n_batch, n_tok, width)
    else:
        terms = None
        grad_mlp_in, down_part, out_terms, grad_gu_own = permuted_mlp(
            ring, mlp_in, cots, gu_rows, own_down
        )
    gain_mlp_term = jnp.sum(grad_mlp_in * normed_two, axis=0)
    grad_hidden = grad_out + norm_back(grad_mlp_in * gain_mlp, normed_two, scale_two)
    back_own, out_grads, up_grads, grad_gu_own, grad_down, attn_in_all, *sums = attention_back(
        n_batch,
        grad_hidden.astype(BF).reshape(micro, pos_dev, width),
        qkv_all,
        turned,
        mixed,
        own_qup,
        own_out,
        grad_gu_own,
        down_part,
        attn_in,
        terms,
        cots,
        (cos_all, sin_all, keep),
    )
    out_sum = sums[0] if resident else ring.collect(lambda step: out_terms[step])
    layer_out = hidden_res + out_sum
    back_own = back_own.reshape(n_tok, in_cols)
    (
        grad_proj_out,
        grad_query_up,
        grad_proj_in,
        gain_sums,
        grad_gate_up,
        grad_tokens,
    ) = collect_weights(
        n_batch,
        gain_rows,
        out_grads,
        up_grads,
        attn_in_all,
        grad_gu_own,
        packed,
        (
            back_own,
            q_latent,
            tokens.reshape(n_tok, width),
            grad_hidden,
            gains,
            gain_mlp_term[None, :],
            tables[2],
            tables[3],
        ),
    )
    gain_sums = gain_sums[:, :own_rows]

    return (
        layer_out.reshape(tokens.shape).astype(BF),
        grad_tokens.reshape(tokens.shape),
        grad_proj_in,
        grad_query_up,
        grad_proj_out,
        gain_sums[0],
        gain_sums[2, :gain_rows],
        gain_sums[1],
        grad_gate_up,
        grad_down,
    )


def solution(mesh):
    rows = P(("batch", "ctx"), None)
    vector = P(("batch", "ctx"))
    acts = P("batch", "ctx", None)
    return jax.shard_map(
        shards,
        mesh=mesh,
        in_specs=(acts, acts, P(), P(), rows, rows, rows, vector, vector, vector, rows, rows),
        out_specs=(acts, acts, rows, rows, rows, vector, vector, vector, rows, rows),
        check_vma=False,
    )
```

```python
import functools
import math

import jax
import jax.numpy as jnp
import numpy as np
from jax import lax
from jax.experimental import pallas as pl
from jax.experimental.pallas import tpu as pltpu
from jax.sharding import PartitionSpec as P

H = 16
HD = 256
QR = 1024
EPSILON = 1e-06
BF = jnp.bfloat16
F32 = jnp.float32


def rms_scale(values):
    return lax.rsqrt(jnp.mean(values * values, axis=-1, keepdims=True) + EPSILON)


def rope_tables(length):
    half_size = HD // 2
    frequency = np.float32(10000.0) ** (-(np.arange(half_size, dtype=np.float32) * 2.0 / HD))
    angles = np.arange(length, dtype=np.float32)[:, None] * frequency.astype(np.float32)[None, :]
    cosine, sine = np.cos(angles), np.sin(angles)
    return jnp.asarray(cosine, F32), jnp.asarray(sine, F32)


def rotate(values, cosine_table, sine_table):
    half_size = values.shape[-1] // 2
    front_half = values[..., :half_size]
    back_half = values[..., half_size:]
    return jnp.concatenate(
        [
            front_half * cosine_table - back_half * sine_table,
            back_half * cosine_table + front_half * sine_table,
        ],
        axis=-1,
    )


def rotate_back(values, cosine_table, sine_table):
    return rotate(values, cosine_table, -sine_table)


def dot(left_side, right_side):
    return jnp.dot(left_side, right_side, preferred_element_type=F32)


def dot_right_t(left_side, right_side):
    return lax.dot_general(
        left_side, right_side, (((1,), (1,)), ((), ())), preferred_element_type=F32
    )


def dot_left_t(left_side, right_side):
    return lax.dot_general(
        left_side, right_side, (((0,), (0,)), ((), ())), preferred_element_type=F32
    )


def norm_back(grad_normed, normed, inv_rms):
    return inv_rms * (grad_normed - normed * jnp.mean(grad_normed * normed, axis=-1, keepdims=True))


def pick(array, index, axis=0):
    return lax.dynamic_index_in_dim(array, index, axis, keepdims=False)


def place(array, block, index, axis=0):
    return lax.dynamic_update_index_in_dim(array, block, index, axis)


class Ring:
    def __init__(self):
        self.n = lax.axis_size("batch")
        self.h = self.n // 2
        rank = lax.axis_index("batch")
        self.at = jnp.where(rank % 2 == 0, rank // 2, self.n - 1 - rank // 2)
        order = [2 * i for i in range(self.h)] + [2 * i + 1 for i in reversed(range(self.h))]
        self.up = [(order[i], order[(i + 1) % self.n]) for i in range(self.n)]
        self.down = [(there, here) for here, there in self.up]

    def rank_of(self, step):
        spot = (self.at + step) % self.n
        return jnp.where(spot < self.h, 2 * spot, 2 * (self.n - 1 - spot) + 1)

    def spread(self, block):
        found = {0: block}
        upward = downward = block
        for step in range(1, self.h):
            upward = lax.ppermute(upward, "batch", self.up)
            downward = lax.ppermute(downward, "batch", self.down)
            found[-step] = upward
            found[step] = downward
        cut = block.shape[0] // 2
        found[self.h] = jnp.concatenate(
            [
                lax.ppermute(upward[:cut], "batch", self.up),
                lax.ppermute(downward[cut:], "batch", self.down),
            ],
            axis=0,
        )
        return found

    def gather(self, block):
        found = self.spread(block)
        whole = jnp.zeros((self.n,) + block.shape, block.dtype)
        for step, part in found.items():
            whole = place(whole, part, self.rank_of(step))
        return whole

    def collect(self, term):
        far = term(self.h)
        cut = far.shape[0] // 2
        downward = lax.ppermute(far[:cut].astype(BF), "batch", self.down)
        upward = lax.ppermute(far[cut:].astype(BF), "batch", self.up)
        for step in range(self.h - 1, 0, -1):
            for_lower = term(-step).astype(F32)
            for_upper = term(step).astype(F32)
            if step == self.h - 1:
                for_lower = jnp.concatenate(
                    [for_lower[:cut] + downward.astype(F32), for_lower[cut:]], axis=0
                )
                for_upper = jnp.concatenate(
                    [for_upper[:cut], for_upper[cut:] + upward.astype(F32)], axis=0
                )
            else:
                for_lower = for_lower + downward.astype(F32)
                for_upper = for_upper + upward.astype(F32)
            downward = lax.ppermute(for_lower.astype(BF), "batch", self.down)
            upward = lax.ppermute(for_upper.astype(BF), "batch", self.up)
        own = term(0).astype(F32)
        return own + downward.astype(F32) + upward.astype(F32)

    def collect_rows(self, stacked):
        return self.collect(lambda step: pick(stacked, self.rank_of(step)))


FAR = [(0, 2), (1, 3), (2, 0), (3, 1)]
NEAR = [(0, 1), (1, 0), (2, 3), (3, 2)]


def ctx_place():
    rank = lax.axis_index("ctx")
    return rank // 2, rank % 2


def in_order(mine, theirs, at):
    return jnp.where(at == 0, jnp.stack([mine, theirs]), jnp.stack([theirs, mine]))


def ctx_gather(block):
    outer, inner = ctx_place()
    pair = in_order(block, lax.ppermute(block, "ctx", FAR), outer)
    whole = in_order(pair, lax.ppermute(pair, "ctx", NEAR), inner)
    whole = jnp.swapaxes(whole, 0, 1)
    return whole.reshape((4,) + block.shape)


def near_collect(stacked):
    _, inner = ctx_place()
    parts = stacked.reshape((2, 2) + stacked.shape[1:])
    got = lax.ppermute(pick(parts, 1 - inner, 1).astype(BF), "ctx", NEAR)
    return pick(parts, inner, 1).astype(F32) + got.astype(F32)


def ctx_collect(stacked):
    outer, _ = ctx_place()
    half = near_collect(stacked)
    got = lax.ppermute(pick(half, 1 - outer).astype(BF), "ctx", FAR)
    return pick(half, outer) + got.astype(F32)


def ctx_exchange(stacked):
    outer, inner = ctx_place()
    parts = stacked.reshape((2, 2) + stacked.shape[1:])
    got = lax.ppermute(pick(parts, 1 - outer), "ctx", FAR)
    parts = in_order(pick(parts, outer), got, outer)
    got = lax.ppermute(pick(parts, 1 - inner, 1), "ctx", NEAR)
    whole = in_order(pick(parts, inner, 1), got, inner)
    return jnp.swapaxes(whole, 0, 1).reshape(stacked.shape)


MESH = pl.DeviceIdType.MESH


class Place:
    def __init__(self, n_batch):
        self.n = n_batch
        self.h = n_batch // 2
        self.b = lax.axis_index("batch")
        self.c = lax.axis_index("ctx")
        self.outer = lax.div(self.c, 2)
        self.inner = lax.rem(self.c, 2)
        self.far = lax.rem(self.c + 2, 4)
        self.near = self.c + 1 - 2 * self.inner
        odd = lax.rem(self.b, 2)
        half = lax.div(self.b, 2)
        self.at = half + odd * (self.n - 1 - 2 * half)

    def rank_of(self, step):
        spot = lax.rem(self.at + step + 2 * self.n, self.n)
        back = lax.div(spot, self.h)
        return (1 - back) * 2 * spot + back * (2 * (self.n - 1 - spot) + 1)

    def up(self):
        return (self.rank_of(1), self.c)

    def down(self):
        return (self.rank_of(-1), self.c)


class Copies:
    def __init__(self, send_sems, recv_sems):
        self.send_sems = send_sems
        self.recv_sems = recv_sems
        self.count = 0
        self.open_sends = []
        self.open_recvs = []

    def remote(self, source, target, device):
        index = self.count
        self.count += 1
        copy = pltpu.make_async_remote_copy(
            src_ref=source,
            dst_ref=target,
            send_sem=self.send_sems.at[index],
            recv_sem=self.recv_sems.at[index],
            device_id=device,
            device_id_type=MESH,
        )
        copy.start()
        self.open_sends.append(copy)
        self.open_recvs.append(copy)
        return copy

    def local(self, source, target):
        index = self.count
        self.count += 1
        copy = pltpu.make_async_copy(source, target, self.recv_sems.at[index])
        copy.start()
        self.open_recvs.append(copy)
        return copy

    def arrive(self, copy):
        if any(copy is other for other in self.open_recvs):
            self.open_recvs = [other for other in self.open_recvs if other is not copy]
            if any(copy is other for other in self.open_sends):
                copy.wait_recv()
            else:
                copy.wait()

    def drain(self):
        for copy in list(self.open_recvs):
            self.arrive(copy)
        for copy in self.open_sends:
            copy.wait_send()


def greet(place, others):
    barrier = pltpu.get_barrier_semaphore()
    for device in others:
        pl.semaphore_signal(barrier, inc=1, device_id=device, device_id_type=MESH)
    return barrier


class RingGather:
    def __init__(self, place, copies, rows, slot):
        self.place, self.copies, self.rows, self.slot = place, copies, rows, slot
        self.step = 0
        self.moving = ()

    def advance(self):
        place, copies = self.place, self.copies
        for copy in self.moving:
            copies.arrive(copy)
        self.moving = ()
        self.step += 1
        cut = self.rows // 2
        if self.step > place.h:
            return
        lower = place.rank_of(1 - self.step)
        upper = place.rank_of(self.step - 1)
        if self.step < place.h:
            whole = pl.ds(0, self.rows)
            pieces = (whole, whole)
        else:
            pieces = (pl.ds(0, cut), pl.ds(cut, self.rows - cut))
        upward, downward = self.slot(lower, pieces[0]), self.slot(upper, pieces[1])
        self.moving = (
            copies.remote(upward, upward, place.up()),
            copies.remote(downward, downward, place.down()),
        )

    def arrived(self):
        step = self.step - 1
        if step == 0:
            return []
        if step == self.place.h:
            return [self.place.rank_of(step)]
        return [self.place.rank_of(-step), self.place.rank_of(step)]


def mlp_kernel(
    n_batch,
    rows_ref,
    gu_ref,
    down_ref,
    cot_ref,
    *refs,
):
    (
        sum_ref,
        act_out,
        term_out,
        gu_out,
        rows_v,
        cot_v,
        gate_v,
        up_v,
        down_v,
        act_v,
        ggate_v,
        gup_v,
        in_v,
        term_v,
        got_v,
        gu_got,
        gu_last,
        send_sems,
        recv_sems,
        back_send,
        back_recv,
        load_sems,
        store_sems,
        part_send,
        part_recv,
    ) = refs
    place = Place(n_batch)
    far = place.h
    n_tok = rows_ref.shape[0]
    cut = n_tok // 2
    width = rows_ref.shape[1]
    ff = gu_ref.shape[-1]
    up_device, down_device = place.up(), place.down()
    far_device, near_device = (place.b, place.far), (place.b, place.near)
    barrier = greet(place, [up_device, down_device, far_device, near_device])
    parts = Copies(part_send, part_recv)
    own_rows = gate_v.shape[2]
    block = 4 * own_rows

    load_rows = pltpu.make_async_copy(rows_ref, rows_v.at[0, pl.ds(0, n_tok)], load_sems.at[0])
    load_rows.start()
    loads = [
        pltpu.make_async_copy(source, target, load_sems.at[1 + i])
        for i, (source, target) in enumerate(
            [(gu_ref.at[0], gate_v), (gu_ref.at[1], up_v), (down_ref, down_v)]
        )
    ]
    spots = [(0, 0, 0), (far, 0, 1)]
    spots += [(side * step, step, (side + 1) // 2) for step in range(1, far) for side in (-1, 1)]
    for i, (distance, group, side) in enumerate(spots):
        loads.append(
            pltpu.make_async_copy(
                cot_ref.at[place.rank_of(distance)], cot_v.at[group, pl.ds(side * n_tok, n_tok)], load_sems.at[4 + i]
            )
        )
    for copy in loads:
        copy.start()
    load_rows.wait()
    pl.semaphore_wait(barrier, 4)

    def piece(side, half):
        return pl.ds(side * n_tok + half * cut, cut)

    def hop(step, side, half):
        source_group, source_side = step - 1, side
        target_group, target_side = step, side
        if isinstance(step, int) and step == 1:
            source_side = 0
        if isinstance(step, int) and step == far:
            target_group, target_side = 0, 1
        return pltpu.make_async_remote_copy(
            src_ref=rows_v.at[source_group, piece(source_side, half)],
            dst_ref=rows_v.at[target_group, piece(target_side, half)],
            send_sem=send_sems.at[step, side, half],
            recv_sem=recv_sems.at[step, side, half],
            device_id=down_device if side else up_device,
            device_id_type=MESH,
        )

    both = [(side, half) for half in (0, 1) for side in (0, 1)]
    ends = [(0, 0), (1, 1)]
    for side, half in both:
        hop(1, side, half).start()
    for copy in loads:
        copy.wait()

    def stores(group):
        return [
            pltpu.make_async_copy(term_v.at[group], term_out.at[group], store_sems.at[0, group]),
            pltpu.make_async_copy(act_v.at[group], act_out.at[group], store_sems.at[1, group]),
        ]

    def compute(group):
        rows = rows_v[group]
        cots = cot_v[group]
        down_all = down_v[...].reshape(ff, width)
        start = 0
        while start < ff:
            size = min(256, ff - start)
            tile = slice(start, start + size)
            gate = dot(rows, gate_v[..., tile].reshape(width, size))
            up = dot(rows, up_v[..., tile].reshape(width, size))
            grad_act = dot_right_t(cots, down_all[tile])
            sigmoid = 1.0 / (1.0 + jnp.exp(-gate))
            silu = gate * sigmoid
            act_v[group, :, tile] = (silu * up).astype(BF)
            slope = sigmoid * (1.0 + gate * (1.0 - sigmoid))
            ggate_v[group, :, tile] = (grad_act * up * slope).astype(BF)
            gup_v[group, :, tile] = (grad_act * silu).astype(BF)
            start += size
        ggate = ggate_v[group]
        gup = gup_v[group]
        act = act_v[group]
        tile_cols = 2 * block

        @pl.loop(0, width // tile_cols)
        def _(t):
            cols = pl.ds(pl.multiple_of(t * tile_cols, tile_cols), tile_cols)
            back = dot_right_t(ggate, gate_v[pl.ds(2 * t, 2)].reshape(tile_cols, ff))
            back += dot_right_t(gup, up_v[pl.ds(2 * t, 2)].reshape(tile_cols, ff))
            in_v[group, :, cols] = back.astype(BF)
            down = down_v[:, :, cols].reshape(ff, tile_cols)
            term_v[group, :, cols] = dot(act, down).astype(BF)

        for copy in stores(group):
            copy.start()

    @pl.loop(1, far)
    def _(step):
        for side, half in both:
            hop(step, side, half).wait_recv()

            @pl.when(step < far - 1)
            def _():
                hop(step + 1, side, half).start()

            if (side, half) in ends:

                @pl.when(step == far - 1)
                def _():
                    hop(far, side, half).start()

        compute(step)

    for side, half in ends:
        hop(far, side, half).wait_recv()
    compute(0)

    def back_hop(step, side, half, source):
        return pltpu.make_async_remote_copy(
            src_ref=source,
            dst_ref=got_v.at[step, side, half],
            send_sem=back_send.at[step, side, half],
            recv_sem=back_recv.at[step, side, half],
            device_id=up_device if side else down_device,
            device_id_type=MESH,
        )

    def held(step, side, half):
        return in_v.at[step, piece(side, half)]

    for side, half in ends:
        back_hop(far - 1, side, half, held(0, 1, half)).start()

    def pass_on(step, side, half, added):
        own = held(step, side, half)
        if added:
            back_hop(step, side, half, own).wait_recv()
            own[...] = (own[...].astype(F32) + got_v[step, side, half].astype(F32)).astype(BF)
        back_hop(step - 1, side, half, own).start()

    for side, half in both:
        if (side, half) not in ends:
            pass_on(far - 1, side, half, False)

    def gate_up_terms(t):
        cols = slice(t * 2 * block, (t + 1) * 2 * block)
        rows = rows_v[:, :, cols].reshape(n_batch * n_tok, 2 * block)
        for target, grads in ((gate_v, ggate_v), (up_v, gup_v)):
            term = dot_left_t(rows, grads[...].reshape(n_batch * n_tok, ff))
            target[2 * t : 2 * t + 2] = term.astype(BF).reshape(2, 4, own_rows, ff)

    def pass_all(step):
        for side, half in [(1, 0), (0, 1), (0, 0), (1, 1)]:
            if step < far - 1 or (side, half) in ends:
                pass_on(step, side, half, True)

    steps = list(range(1, far))
    outer, inner = place.outer, place.inner
    kinds = list(enumerate((gate_v, up_v)))
    near_copies, far_copies = {}, {}

    def send_near(t):
        pair = pl.ds(2 * t, 2)
        near_copies[t] = [
            parts.remote(
                target.at[pair, 2 * side + 1 - inner], gu_got.at[kind, side, pair], near_device
            )
            for side in (0, 1)
            for kind, target in kinds
        ]

    def send_far(t):
        pair = pl.ds(2 * t, 2)
        for copy in near_copies[t]:
            parts.arrive(copy)
        far_copies[t] = []
        for kind, target in kinds:
            other = target.at[pair, 2 * (1 - outer) + inner]
            added = other[...].astype(F32) + gu_got[kind, 1 - outer, pair].astype(F32)
            other[...] = added.astype(BF)
            far_copies[t].append(parts.remote(other, gu_last.at[kind, pair], far_device))

    def take_far(t):
        pair = pl.ds(2 * t, 2)
        for copy in far_copies[t]:
            parts.arrive(copy)
        for kind, target in kinds:
            kept = target.at[pair, 2 * outer + inner]
            added = kept[...].astype(F32) + gu_got[kind, outer, pair].astype(F32)
            kept[...] = (added + gu_last[kind, pair].astype(F32)).astype(BF)
            parts.local(kept, gu_out.at[pair, kind])

    def ring_step():
        if steps:
            pass_all(steps.pop())

    tiles = width // (2 * block)
    for t in range(tiles):
        gate_up_terms(t)
        send_near(t)
        if t > 0:
            send_far(t - 1)
        ring_step()
    while steps:
        ring_step()
    send_far(tiles - 1)
    for half in (0, 1):
        for side in (0, 1):
            back_hop(0, side, half, held(0, 0, half)).wait_recv()
        rows = slice(half * cut, (half + 1) * cut)
        sum_ref[rows, :] = (
            in_v[0, rows, :].astype(F32)
            + got_v[0, 0, half].astype(F32)
            + got_v[0, 1, half].astype(F32)
        )
    for t in range(tiles):
        take_far(t)
    parts.drain()

    for step in range(1, far + 1):
        for side, half in both if step < far else ends:
            hop(step, side, half).wait_send()
    for side, half in ends:
        back_hop(far - 1, side, half, held(0, 1, half)).wait_send()
    for step in range(far - 1, 0, -1):
        for side, half in both:
            back_hop(step - 1, side, half, held(step, side, half)).wait_send()
    for group in range(far):
        for copy in stores(group):
            copy.wait()


def fused_mlp(n_batch, rows, cots, gu_rows, own_down):
    n_tok, width = rows.shape
    ff = gu_rows.shape[-1]
    own_rows = gu_rows.shape[3]
    far = n_batch // 2
    pair = 2 * n_tok
    flops = 18 * n_batch * n_tok * width * ff
    return pl.pallas_call(
        functools.partial(mlp_kernel, n_batch),
        out_shape=(
            jax.ShapeDtypeStruct((n_tok, width), F32),
            jax.ShapeDtypeStruct((far, pair, ff), BF),
            jax.ShapeDtypeStruct((far, pair, width), BF),
            jax.ShapeDtypeStruct((n_batch, 2, own_rows, ff), BF),
        ),
        in_specs=[pl.BlockSpec(memory_space=pl.ANY)] * 4,
        out_specs=[pl.BlockSpec(memory_space=pltpu.VMEM)]
        + [pl.BlockSpec(memory_space=pl.ANY)] * 3,
        scratch_shapes=[
            pltpu.VMEM((far, pair, width), BF),
            pltpu.VMEM((far, pair, width), BF),
            pltpu.VMEM((n_batch, 4, own_rows, ff), BF),
            pltpu.VMEM((n_batch, 4, own_rows, ff), BF),
            pltpu.VMEM((4, ff // 4, width), BF),
            pltpu.VMEM((far, pair, ff), BF),
            pltpu.VMEM((far, pair, ff), BF),
            pltpu.VMEM((far, pair, ff), BF),
            pltpu.VMEM((far, pair, width), BF),
            pltpu.VMEM((far, pair, width), BF),
            pltpu.VMEM((far, 2, 2, n_tok // 2, width), BF),
            pltpu.VMEM((2, 2, n_batch, own_rows, ff), BF),
            pltpu.VMEM((2, n_batch, own_rows, ff), BF),
            pltpu.SemaphoreType.DMA((far + 1, 2, 2)),
            pltpu.SemaphoreType.DMA((far + 1, 2, 2)),
            pltpu.SemaphoreType.DMA((far, 2, 2)),
            pltpu.SemaphoreType.DMA((far, 2, 2)),
            pltpu.SemaphoreType.DMA((4 + n_batch,)),
            pltpu.SemaphoreType.DMA((2, far)),
            pltpu.SemaphoreType.DMA((72,)),
            pltpu.SemaphoreType.DMA((72,)),
        ],
        compiler_params=pltpu.CompilerParams(
            collective_id=1, has_side_effects=True, vmem_limit_bytes=60 * 1024 * 1024
        ),
        cost_estimate=pl.CostEstimate(
            flops=flops, bytes_accessed=24 * 1024 * 1024, transcendentals=n_batch * n_tok * ff
        ),
        name="fused_mlp",
    )(rows, gu_rows, own_down, cots)


class RingCollect:
    def __init__(self, place, block, got, send_sems, recv_sems):
        self.place, self.block, self.got = place, block, got
        self.send_sems, self.recv_sems = send_sems, recv_sems
        self.cut = got.shape[3]
        self.step = place.h
        self.sent = []

    def held(self, step, half):
        return self.block(step).at[pl.ds(half * self.cut, self.cut)]

    def hop(self, step, side, half, source):
        place = self.place
        return pltpu.make_async_remote_copy(
            src_ref=source,
            dst_ref=self.got.at[step, side, half],
            send_sem=self.send_sems.at[step, side, half],
            recv_sem=self.recv_sems.at[step, side, half],
            device_id=place.up() if side else place.down(),
            device_id_type=MESH,
        )

    def send(self, step, side, half, source):
        copy = self.hop(step, side, half, source)
        copy.start()
        self.sent.append(copy)

    def advance(self):
        far = self.place.h
        step = self.step
        self.step -= 1
        if step == far:
            for side in (0, 1):
                self.send(far - 1, side, side, self.held(far, side))
            for side in (0, 1):
                half = 1 - side
                self.send(far - 2, side, half, self.held((2 * side - 1) * (far - 1), half))
            return
        pieces = [(0, 0), (1, 1)] if step == far - 1 else [(1, 0), (0, 1), (0, 0), (1, 1)]
        for side, half in pieces:
            own = self.held((2 * side - 1) * step, half)
            self.hop(step, side, half, own).wait_recv()
            own[...] = (own[...].astype(F32) + self.got[step, side, half].astype(F32)).astype(BF)
            self.send(step - 1, side, half, own)

    def finish(self, half):
        own = self.held(0, half)
        for side in (0, 1):
            self.hop(0, side, half, own).wait_recv()
        return (
            own[...].astype(F32)
            + self.got[0, 0, half].astype(F32)
            + self.got[0, 1, half].astype(F32)
        )

    def drain(self):
        for copy in self.sent:
            copy.wait_send()


def tail_kernel(
    n_batch,
    gain_rows,
    out_ref,
    up_ref,
    rows_ref,
    gu_ref,
    packed_ref,
    back_ref,
    latent_ref,
    tokens_ref,
    hidden_ref,
    gains_ref,
    mlp_term_ref,
    cos_ref,
    sin_ref,
    out_grad,
    up_grad,
    in_grad,
    gain_grad,
    gu_grad,
    tokens_grad,
    out_v,
    up_v,
    in_v,
    out_got,
    up_got,
    in_got,
    up_sum,
    up_all,
    in_sum,
    in_all,
    ring_send,
    ring_recv,
    send_sems,
    recv_sems,
    packed_v,
    project_own,
    project_v,
    rows_v,
    gu_v,
    load_sems,
):
    place = Place(n_batch)
    copies = Copies(send_sems, recv_sems)
    b, c, n = place.b, place.c, n_batch
    own_rows = in_grad.shape[0]
    group = HeadGroup(place, out_grad.shape[0])
    ctx_peers = [(b, place.far), (b, place.near), (b, lax.rem(place.near + 2, 4))]

    loads = [
        pltpu.make_async_copy(held, kept, load_sems.at[i])
        for i, (held, kept) in enumerate([(out_ref, out_v), (up_ref, up_v), (rows_ref, rows_v), (gu_ref, gu_v), (packed_ref, packed_v)])
    ]
    for copy in loads:
        copy.start()
    barrier = greet(place, [place.up(), place.down()] + ctx_peers)

    pl.semaphore_wait(barrier, 5)

    rings = []
    for i, (kept, got) in enumerate([(out_v, out_got), (up_v, up_got), (in_v, in_got)]):
        rings.append(
            RingCollect(
                place,
                lambda step, kept=kept: kept.at[place.rank_of(step)],
                got,
                ring_send.at[i],
                ring_recv.at[i],
            )
        )
    for copy, ring in zip(loads[:2], rings):
        copy.wait()
        ring.advance()
    part_cols = project_v.shape[2]
    n_tok, width = tokens_ref.shape
    pos_dev = cos_ref.shape[0] // 4
    own_at = pl.ds(pl.multiple_of(c * pos_dev, pos_dev), pos_dev)
    cos_own = jnp.concatenate([cos_ref[own_at, :]] * (n_tok // pos_dev), axis=0)
    sin_own = jnp.concatenate([sin_ref[own_at, :]] * (n_tok // pos_dev), axis=0)
    latent = latent_ref.shape[1]

    q_latent = latent_ref[...]
    inverse = rms_scale(q_latent)
    normed_query = q_latent * inverse
    grad_qn = back_ref[:, :latent]
    query_term = jnp.sum(grad_qn * normed_query, axis=0, keepdims=True)
    grad_latent = norm_back(grad_qn * gains_ref[2:3, :latent], normed_query, inverse)
    front, back = turn(back_ref[:, latent : latent + HD], cos_own, -sin_own)
    project = jnp.concatenate(
        [grad_latent, front, back, back_ref[:, latent + HD :]], axis=1
    ).astype(BF)
    for part in range(4):
        project_own[part] = project[:, part * part_cols : (part + 1) * part_cols]
    project_copies = [
        copies.remote(project_own.at[peer[1]], project_v.at[c], peer) for peer in ctx_peers
    ]
    project_copies.append(copies.local(project_own.at[c], project_v.at[c]))
    for ring in rings[:2]:
        ring.advance()
    loads[4].wait()
    in_cols = 4 * part_cols
    residual = tokens_ref[...].astype(F32)
    inverse = rms_scale(residual)
    normed = residual * inverse
    weights = packed_v[:, :, :, :in_cols].reshape(width, in_cols)
    grad_attn_in = dot_right_t(project, weights)
    attn_term = jnp.sum(grad_attn_in * normed, axis=0, keepdims=True)
    back = norm_back(grad_attn_in * gains_ref[0:1, :], normed, inverse)
    tokens_grad[...] = (hidden_ref[...] + back).astype(BF)
    for ring in rings[:2]:
        ring.advance()
    for copy in project_copies:
        copies.arrive(copy)
    loads[2].wait()
    project_all = project_v[...].reshape(-1, part_cols)
    part_rows = own_rows + 16
    n_all = project_all.shape[0]
    ahead = max(1, 256 // (4 * own_rows))
    chunk = ahead * 4 * own_rows

    @pl.loop(0, width // chunk)
    def _(t):
        cols = pl.ds(pl.multiple_of(t * chunk, chunk), chunk)
        term = dot_left_t(rows_v[:, :, :, cols].reshape(n_all, chunk), project_all).astype(BF)
        term = term.reshape(ahead, 4, own_rows, part_cols)
        for part in range(4):
            in_v[pl.ds(t * ahead, ahead), pl.ds(part * part_rows, own_rows), :] = term[:, part]

    none = jnp.zeros((16, part_cols), BF)
    wide = jnp.concatenate([attn_term, mlp_term_ref[...], jnp.zeros((14, width), F32)], axis=0)
    short = jnp.concatenate([jnp.zeros((2, latent), F32), query_term], axis=0)
    short = jnp.concatenate([short, jnp.zeros((13, latent), F32)], axis=0)
    for rank in range(n):
        for part in range(4):
            at = pl.ds(part * part_rows + own_rows, 16)
            device = 4 * rank + part
            in_v[rank, at, :] = none
            in_v[rank, at, :own_rows] = wide[
                :, device * own_rows : (device + 1) * own_rows
            ].astype(BF)
            more = short[:, device * gain_rows : (device + 1) * gain_rows].astype(BF)
            kept = in_v[rank, at, :gain_rows]
            in_v[rank, at, :gain_rows] = kept + more
    rings[2].advance()
    if rings[0].step > 0:
        for ring in rings[:2]:
            ring.advance()
    while rings[2].step > 0:
        for ring in rings:
            if ring.step > 0:
                ring.advance()

    loads[3].wait()
    ff = gu_v.shape[3]
    for slab_at in range(n):
        for kind in (0, 1):
            start = (kind * n + slab_at) * ff
            gu_grad[:, start : start + ff] = gu_v[slab_at, kind].astype(F32)

    in_ring, up_ring, out_ring = rings[2], rings[1], rings[0]
    out_cut, up_cut, in_cut = out_ring.cut, up_ring.cut, in_ring.cut
    for half in (0, 1):
        out_grad[half * out_cut : (half + 1) * out_cut, :] = out_ring.finish(half)
    for half in (0, 1):
        up_sum[pl.ds(half * up_cut, up_cut), :] = up_ring.finish(half).astype(BF)
    up_copies = [
        copies.remote(
            up_sum.at[pl.ds(peer[1] * gain_rows, gain_rows)], up_all.at[c], peer
        )
        for peer in ctx_peers
    ]
    up_copies.append(
        copies.local(up_sum.at[pl.ds(c * gain_rows, gain_rows)], up_all.at[c])
    )
    for half in (0, 1):
        in_sum[pl.ds(half * in_cut, in_cut), :] = in_ring.finish(half).astype(BF)
    in_copies = [
        copies.remote(in_sum.at[pl.ds(peer[1] * part_rows, part_rows)], in_all.at[c], peer)
        for peer in ctx_peers
    ]
    in_copies.append(copies.local(in_sum.at[pl.ds(c * part_rows, part_rows)], in_all.at[c]))

    for copy in up_copies:
        copies.arrive(copy)
    cols = up_all.shape[2]
    heads = cols // HD
    for part in range(4):
        for local in range(heads):
            head = group.head(part, local, heads)
            up_grad[:, head * HD : (head + 1) * HD] = up_all[
                part, :, local * HD : (local + 1) * HD
            ].astype(F32)
    for copy in in_copies:
        copies.arrive(copy)
    cols = in_all.shape[2]
    gains = jnp.zeros(gain_grad.shape, F32)
    for part in range(4):
        in_grad[:, part * cols : (part + 1) * cols] = in_all[part, :own_rows, :].astype(F32)
        gains = gains + in_all[part, own_rows:, :].astype(F32)
    gain_grad[...] = gains
    copies.drain()
    for ring in rings:
        ring.drain()


def collect_weights(n_batch, gain_rows, out_terms, up_terms, attn_in_all, grad_gu, packed, own):
    far = n_batch // 2
    out_rows, width = out_terms.shape[1:]
    up_rows, up_cols = up_terms.shape[1:]
    n_tok = own[2].shape[0]
    in_cols = own[0].shape[1] // 4
    own_rows = width // (4 * n_batch)
    in_rows = 4 * (own_rows + 16)
    shapes = [out_terms.shape[1:], up_terms.shape[1:], (in_rows, in_cols)]
    sems = 2 * n_batch + 16
    return pl.pallas_call(
        functools.partial(tail_kernel, n_batch, gain_rows),
        out_shape=(
            jax.ShapeDtypeStruct((out_rows, width), F32),
            jax.ShapeDtypeStruct((gain_rows, 4 * up_cols), F32),
            jax.ShapeDtypeStruct((own_rows, 4 * in_cols), F32),
            jax.ShapeDtypeStruct((16, in_cols), F32),
            jax.ShapeDtypeStruct((own_rows, 2 * n_batch * grad_gu.shape[3]), F32),
            jax.ShapeDtypeStruct((n_tok, width), BF),
        ),
        in_specs=[pl.BlockSpec(memory_space=pl.ANY)] * 5 + [pl.BlockSpec(memory_space=pltpu.VMEM)] * len(own),
        out_specs=[pl.BlockSpec(memory_space=pltpu.VMEM)] * 6,
        scratch_shapes=[pltpu.VMEM((n_batch,) + shape, BF) for shape in shapes]
        + [pltpu.VMEM((far, 2, 2, rows // 2, cols), BF) for rows, cols in shapes]
        + [
            pltpu.VMEM((up_rows, up_cols), BF),
            pltpu.VMEM((4, gain_rows, up_cols), BF),
            pltpu.VMEM((in_rows, in_cols), BF),
            pltpu.VMEM((4, own_rows + 16, in_cols), BF),
            pltpu.SemaphoreType.DMA((3, far, 2, 2)),
            pltpu.SemaphoreType.DMA((3, far, 2, 2)),
            pltpu.SemaphoreType.DMA((sems,)),
            pltpu.SemaphoreType.DMA((sems,)),
            pltpu.VMEM(packed.shape, BF),
            pltpu.VMEM((4, n_tok, in_cols), BF),
            pltpu.VMEM((4, n_tok, in_cols), BF),
            pltpu.VMEM(attn_in_all.shape, BF),
            pltpu.VMEM(grad_gu.shape, BF),
            pltpu.SemaphoreType.DMA((5,)),
        ],
        compiler_params=pltpu.CompilerParams(
            collective_id=2, has_side_effects=True, vmem_limit_bytes=56 * 1024 * 1024
        ),
        name="collect_weights",
    )(out_terms, up_terms, attn_in_all, grad_gu, packed, *own)


class CtxCollect:
    def __init__(self, place, copies, part, near_got, far_got):
        self.place, self.copies, self.part = place, copies, part
        self.near_got, self.far_got = near_got, far_got
        self.near = {}
        self.far = {}

    def start(self, item):
        place = self.place
        self.near[item] = [
            self.copies.remote(
                self.part.at[2 * side + 1 - place.inner, item],
                self.near_got.at[side, item],
                (place.b, place.near),
            )
            for side in (0, 1)
        ]

    def cross(self, item):
        place = self.place
        for copy in self.near[item]:
            self.copies.arrive(copy)
        other = self.part.at[2 * (1 - place.outer) + place.inner, item]
        added = other[...].astype(F32) + self.near_got[1 - place.outer, item].astype(F32)
        other[...] = added.astype(BF)
        self.far[item] = self.copies.remote(
            other, self.far_got.at[item], (place.b, place.far)
        )

    def finish(self, item):
        place = self.place
        self.copies.arrive(self.far[item])
        return (
            self.part[2 * place.outer + place.inner, item].astype(F32)
            + self.near_got[place.outer, item].astype(F32)
            + self.far_got[item].astype(F32)
        )


class CtxGather:
    def __init__(self, place, copies, everyone):
        self.place, self.copies, self.everyone = place, copies, everyone
        self.far = {}
        self.near = {}

    def start(self, item):
        place = self.place
        own = self.everyone.at[place.c, item]
        self.far[item] = self.copies.remote(own, own, (place.b, place.far))
        self.near[item] = [self.copies.remote(own, own, (place.b, place.near))]

    def cross(self, item):
        place = self.place
        self.copies.arrive(self.far[item])
        other = self.everyone.at[place.far, item]
        self.near[item].append(self.copies.remote(other, other, (place.b, place.near)))

    def finish(self, item):
        for copy in self.near[item]:
            self.copies.arrive(copy)


def greet_lines(place):
    devices = [place.up(), place.down(), (place.b, place.far), (place.b, place.near)]
    pl.semaphore_wait(greet(place, devices), 4)


def turn(values, cosine, sine):
    half_size = HD // 2
    front, back = values[:, :half_size], values[:, half_size:]
    return front * cosine - back * sine, back * cosine + front * sine


def softmax_rows(queries, keys, keep, score_scale):
    scores = dot_right_t(queries, keys) * score_scale
    rows = lax.broadcasted_iota(jnp.int32, scores.shape, 0)
    cols = lax.broadcasted_iota(jnp.int32, scores.shape, 1)
    masked = jnp.where((cols <= rows) & (keep > 0.5), scores, -1e30)
    raised = jnp.exp(masked - jnp.max(masked, axis=-1, keepdims=True))
    return raised / jnp.sum(raised, axis=-1, keepdims=True)

def head_group(n_batch, own_rows):
    return min(4, HD // own_rows)


class HeadGroup:
    def __init__(self, place, own_rows):
        self.size = head_group(place.n, own_rows)
        self.count = place.n // self.size
        if self.size == 2:
            self.me = place.inner
            self.others = [(1 - place.inner, (place.b, place.near))]
        else:
            self.me = place.c
            ranks = [place.far, place.near, lax.rem(place.near + 2, 4)]
            self.others = [(rank, (place.b, rank)) for rank in ranks]

    def blocks(self, member):
        return pl.ds(member * self.count, self.count)

    def head(self, rank, local, heads):
        if self.size == 2:
            return 2 * (heads * (rank % 2) + local) + rank // 2
        return heads * rank + local


def front_kernel(
    n_batch,
    heads,
    proj_ref,
    gain_ref,
    up_ref,
    out_ref,
    gu_ref,
    down_ref,
    tokens_ref,
    cot_ref,
    cos_ref,
    sin_ref,
    keep_ref,
    valid_ref,
    hidden,
    mlp_in,
    gains,
    latents,
    packed_out,
    up_out,
    out_out,
    gu_all,
    down_all,
    qkv_out,
    turned_out,
    mixed_out,
    rows_out,
    cot_all,
    packed_v,
    flat_v,
    gu_v,
    half_v,
    out_v,
    up_v,
    tokens_v,
    rows_v,
    down_v,
    cot_v,
    qkv_v,
    turned_v,
    mixed_v,
    part_v,
    near_got,
    far_got,
    send_sems,
    recv_sems,
):
    place = Place(n_batch)
    copies = Copies(send_sems, recv_sems)
    b, c, n = place.b, place.c, n_batch
    own_rows = proj_ref.shape[0]
    gain_rows = up_ref.shape[0]
    out_rows = out_ref.shape[0]
    n_tok, width = tokens_ref.shape
    micro, pos_dev = qkv_v.shape[1:3]
    length = 4 * pos_dev
    in_cols = qkv_v.shape[3]
    latent = in_cols - 2 * HD
    ff = gu_v.shape[3]
    score_scale = 1.0 / math.sqrt(HD)
    group = HeadGroup(place, out_rows)
    peers = [(lax.rem(b + k, n), c) for k in range(1, n)]
    ctx_peers = [(b, place.far), (b, place.near), (b, lax.rem(place.near + 2, 4))]
    far_device, near_device = ctx_peers[0], ctx_peers[1]

    barrier = greet(place, peers + ctx_peers)
    own_packed = [
        copies.local(proj_ref, packed_v.at[b, c, :, pl.ds(0, in_cols)]),
        copies.local(gain_ref, packed_v.at[b, c, :, pl.ds(in_cols, 128)]),
    ]
    own_out = copies.local(out_ref, half_v.at[b])
    own_tokens = copies.local(tokens_ref, tokens_v)
    own_flat = copies.local(gu_ref, flat_v)
    own_down = copies.local(down_ref, down_v)
    own_cot = copies.local(cot_ref, cot_v)

    def up_cols(rank, local):
        start = pl.multiple_of(group.head(rank, local, heads) * HD, HD)
        return up_ref.at[:, pl.ds(start, HD)]

    own_up = [
        copies.local(up_cols(c, local), up_v.at[b, c, :, pl.ds(local * HD, HD)])
        for local in range(heads)
    ]
    pl.semaphore_wait(barrier, n + 2)
    up_copies = [
        copies.remote(up_cols(peer[1], local), up_v.at[b, c, :, pl.ds(local * HD, HD)], peer)
        for peer in ctx_peers
        for local in range(heads)
    ]
    for copy in own_packed:
        copies.arrive(copy)
    packed_ring = RingGather(place, copies, own_rows, lambda rank, rows: packed_v.at[rank, c, rows])
    up_ring = RingGather(place, copies, gain_rows, lambda rank, rows: up_v.at[rank, :, rows])
    out_ring = RingGather(place, copies, out_rows, lambda rank, rows: half_v.at[rank, rows])
    cot_ring = RingGather(place, copies, n_tok, lambda rank, rows: cot_all.at[rank, rows])
    packed_far = []

    def packed_step():
        packed_ring.advance()
        ranks = packed_ring.arrived() if packed_ring.step > 1 else [b]
        for rank in ranks:
            block = packed_v.at[rank, c]
            packed_far.append(copies.remote(block, block, far_device))

    packed_step()
    copies.arrive(own_down)
    copies.local(down_v, down_all.at[c])
    down_far = copies.remote(down_v, down_all.at[c], far_device)
    copies.remote(down_v, down_all.at[c], near_device)
    copies.arrive(own_flat)
    for slab_at in range(n):
        for kind in (0, 1):
            start = (kind * n + slab_at) * ff
            gu_v[slab_at, kind] = flat_v[:, start : start + ff]
    own_gu = copies.local(gu_v.at[b], gu_all.at[:, b, c])
    gu_copies = []
    gu_far = []
    waiting = []

    def send_gu(count):
        for _ in range(count):
            k = len(gu_copies) + 1
            if k < n:
                peer = peers[k - 1]
                copy = copies.remote(gu_v.at[peer[0]], gu_all.at[:, b, c], peer)
                gu_copies.append(copy)
                waiting.append((lax.rem(b - k + n, n), copy))

    def forward_gu(count):
        for _ in range(min(count, len(waiting))):
            rank, copy = waiting.pop(0)
            copies.arrive(copy)
            block = gu_all.at[:, rank, c]
            gu_far.append(copies.remote(block, block, far_device))

    for copy in own_up + up_copies:
        copies.arrive(copy)
    up_ring.advance()
    packed_step()
    send_gu(n // 2)
    copies.arrive(own_out)
    out_ring.advance()
    up_ring.advance()
    while packed_ring.step <= place.h:
        packed_step()
        up_ring.advance()
    mine = packed_v.at[:, c]
    packed_near = [copies.remote(mine, mine, near_device)]
    while up_ring.step <= place.h:
        up_ring.advance()
    copies.arrive(own_gu)
    gu_far.append(copies.remote(gu_all.at[:, b, c], gu_all.at[:, b, c], far_device))
    send_gu(n)
    out_ring.advance()
    forward_gu(2)
    for copy in packed_far:
        copies.arrive(copy)
    theirs = packed_v.at[:, place.far]
    packed_near.append(copies.remote(theirs, theirs, near_device))

    copies.arrive(own_tokens)
    own_at = pl.ds(pl.multiple_of(c * pos_dev, pos_dev), pos_dev)
    cos_own = jnp.concatenate([cos_ref[own_at, :]] * micro, axis=0)
    sin_own = jnp.concatenate([sin_ref[own_at, :]] * micro, axis=0)
    residual = tokens_v[...].astype(F32)
    normed = residual * rms_scale(residual)
    for copy in packed_near:
        copies.arrive(copy)
    extra = packed_v[:, :, :, in_cols:].astype(F32)
    gain_wide = jnp.transpose(extra.reshape(width, 128))
    gain_query = jnp.transpose(extra[:, :, :gain_rows].reshape(latent, 128))[2:3]
    gains[0:2, :] = gain_wide[0:2]
    gains[2:3, :latent] = gain_query
    attn_in = (normed * gain_wide[0:1]).astype(BF)
    rows_v[...] = attn_in
    tile = 512
    for start in range(0, in_cols, tile):
        weights = packed_v[:, :, :, start : start + tile].reshape(width, tile)
        part = dot(attn_in, weights)
        if start + tile <= latent:
            latents[:, start : start + tile] = part
        else:
            front, back = turn(part[:, :HD], cos_own, sin_own)
            half = HD // 2
            qkv_v[c, :, :, latent : latent + half] = (
                front.astype(BF).reshape(micro, pos_dev, half)
            )
            qkv_v[c, :, :, latent + half : latent + HD] = (
                back.astype(BF).reshape(micro, pos_dev, half)
            )
            qkv_v[c, :, :, latent + HD :] = part[:, HD:].astype(BF).reshape(micro, pos_dev, HD)
    q_latent = latents[...]
    q_normed = q_latent * rms_scale(q_latent) * gain_query
    qkv_v[c, :, :, :latent] = q_normed.astype(BF).reshape(micro, pos_dev, latent)
    qkv = CtxGather(place, copies, qkv_v)
    for item in range(micro):
        qkv.start(item)
    copies.local(rows_v, rows_out)
    copies.arrive(own_cot)
    cot_v[...] = (cot_v[...].astype(F32) * valid_ref[...]).astype(BF)
    copies.arrive(copies.local(cot_v, cot_all.at[b]))
    cot_ring.advance()
    for item in range(micro):
        qkv.cross(item)
    if out_ring.step < place.h:
        out_ring.advance()
    forward_gu(n // 2)
    cosine, sine = cos_ref[...], sin_ref[...]
    for item in range(micro):
        qkv.finish(item)
        q_all = qkv_v[:, item, :, :latent].reshape(length, latent)
        keys = qkv_v[:, item, :, latent : latent + HD].reshape(length, HD)
        values = qkv_v[:, item, :, latent + HD :].reshape(length, HD)
        keep = keep_ref[item]

        @pl.loop(0, heads)
        def _(head):
            base = pl.multiple_of(head * HD, HD)
            cols = pl.ds(base, HD)
            up = up_v[:, :, :, cols].reshape(latent, HD)
            front, back = turn(dot(q_all, up), cosine, sine)
            turned_v[item, :, pl.ds(base, HD // 2)] = front.astype(BF)
            upper = pl.multiple_of(base + HD // 2, HD // 2)
            turned_v[item, :, pl.ds(upper, HD // 2)] = back.astype(BF)
            weights = softmax_rows(turned_v[item, :, cols], keys, keep, score_scale)
            mixed = dot(weights.astype(BF), values).astype(BF)
            mixed_v[:, item, :, cols] = mixed.reshape(4, pos_dev, HD)

        if out_ring.step < place.h:
            out_ring.advance()
    while out_ring.step < place.h:
        out_ring.advance()

    cot_ring.advance()
    while out_ring.step <= place.h:
        out_ring.advance()
    out_swaps = [
        copies.remote(half_v.at[group.blocks(member)], out_v.at[:, group.me], device)
        for member, device in group.others
    ]
    out_swaps.append(copies.local(half_v.at[group.blocks(group.me)], out_v.at[:, group.me]))
    forward_gu(n)
    for copy in out_swaps:
        copies.arrive(copy)
    copies.arrive(down_far)
    copies.remote(down_all.at[place.far], down_all.at[place.far], near_device)
    attended_sum = CtxCollect(place, copies, part_v, near_got, far_got)
    for item in range(micro):
        mixed = mixed_v[:, item].reshape(length, heads * HD)

        @pl.loop(0, width // 512)
        def _(t):
            cols = pl.ds(pl.multiple_of(t * 512, 512), 512)
            weights = out_v[:, :, :, cols].reshape(heads * HD, 512)
            part = dot(mixed, weights).astype(BF)
            part_v[:, item, :, cols] = part.reshape(4, pos_dev, 512)

        attended_sum.start(item)
        if item > 0:
            attended_sum.cross(item - 1)
    cot_ring.advance()
    attended_sum.cross(micro - 1)
    copies.local(packed_v, packed_out)
    copies.local(up_v, up_out)
    copies.local(out_v, out_out)
    copies.local(qkv_v, qkv_out)
    copies.local(turned_v, turned_out)
    copies.local(mixed_v, mixed_out)
    for item in range(micro):
        at = slice(item * pos_dev, (item + 1) * pos_dev)
        total = tokens_v[at, :].astype(F32) + attended_sum.finish(item)
        hidden[at, :] = total
        mlp_in[at, :] = (total * rms_scale(total) * gains[1:2, :]).astype(BF)
    mine = gu_all.at[:, :, c]
    copies.remote(mine, mine, near_device)
    while cot_ring.step <= place.h:
        cot_ring.advance()
    for copy in gu_far:
        copies.arrive(copy)
    theirs = gu_all.at[:, :, place.far]
    copies.remote(theirs, theirs, near_device)
    copies.drain()


def front(n_batch, heads, proj_in, gain_cols, query_up, proj_out, gate_up, down, tokens, cots, tables):
    own_rows, in_cols = proj_in.shape
    packed_cols = in_cols + 128
    latent = in_cols - 2 * HD
    gain_rows = query_up.shape[0]
    out_rows, width = proj_out.shape
    n_tok = cots.shape[0]
    pos_dev = tables[0].shape[0] // 4
    micro = n_tok // pos_dev
    ff = gate_up.shape[1] // (2 * n_batch)
    size = head_group(n_batch, out_rows)
    head_cols = heads * HD
    shapes = {
        "packed": (n_batch, 4, own_rows, packed_cols),
        "up": (n_batch, 4, gain_rows, head_cols),
        "out": (n_batch // size, size, out_rows, width),
        "gu": (2, n_batch, 4, own_rows, ff),
        "down": (4,) + down.shape,
        "qkv": (4, micro, pos_dev, in_cols),
        "turned": (micro, 4 * pos_dev, head_cols),
        "mixed": (4, micro, pos_dev, head_cols),
        "rows": (n_tok, width),
        "cot": (n_batch, n_tok, width),
    }
    anywhere = pl.BlockSpec(memory_space=pl.ANY)
    near = pl.BlockSpec(memory_space=pltpu.VMEM)
    sems = 13 * n_batch + 100
    return pl.pallas_call(
        functools.partial(front_kernel, n_batch, heads),
        out_shape=(
            jax.ShapeDtypeStruct((n_tok, width), F32),
            jax.ShapeDtypeStruct((n_tok, width), BF),
            jax.ShapeDtypeStruct((8, width), F32),
            jax.ShapeDtypeStruct((n_tok, latent), F32),
        )
        + tuple(jax.ShapeDtypeStruct(shape, BF) for shape in shapes.values()),
        in_specs=[anywhere] * 8 + [near] * 4,
        out_specs=[near] * 4 + [anywhere] * len(shapes),
        scratch_shapes=[
            pltpu.VMEM(shapes["packed"], BF),
            pltpu.VMEM(gate_up.shape, BF),
            pltpu.VMEM((n_batch, 2, own_rows, ff), BF),
            pltpu.VMEM((n_batch, out_rows, width), BF),
            pltpu.VMEM(shapes["out"], BF),
            pltpu.VMEM(shapes["up"], BF),
            pltpu.VMEM((n_tok, width), BF),
            pltpu.VMEM((n_tok, width), BF),
            pltpu.VMEM(down.shape, BF),
            pltpu.VMEM((n_tok, width), BF),
            pltpu.VMEM(shapes["qkv"], BF),
            pltpu.VMEM(shapes["turned"], BF),
            pltpu.VMEM(shapes["mixed"], BF),
            pltpu.VMEM((4, micro, pos_dev, width), BF),
            pltpu.VMEM((2, micro, pos_dev, width), BF),
            pltpu.VMEM((micro, pos_dev, width), BF),
            pltpu.SemaphoreType.DMA((sems,)),
            pltpu.SemaphoreType.DMA((sems,)),
        ],
        compiler_params=pltpu.CompilerParams(
            collective_id=0, has_side_effects=True, vmem_limit_bytes=56 * 1024 * 1024
        ),
        name="front",
    )(proj_in, gain_cols, query_up, proj_out, gate_up, down, tokens, cots, *tables)


def attention_back_kernel(
    n_batch,
    heads,
    has_terms,
    grad_ref,
    qkv_ref,
    turned_ref,
    mixed_ref,
    up_ref,
    out_ref,
    gu_ref,
    down_ref,
    rows_ref,
    *refs,
):
    terms_ref, cot_ref, refs = (refs[0], refs[1], refs[2:]) if has_terms else (None, None, refs)
    (
        cos_ref,
        sin_ref,
        keep_ref,
        back_out,
        out_terms,
        up_terms,
        gu_grad,
        down_grad,
        rows_all,
    ) = refs[:9]
    terms_sum, refs = (refs[9], refs[10:]) if has_terms else (None, refs[9:])
    (
        grad_v,
        qkv_v,
        turned_v,
        mixed_v,
        up_v,
        out_v,
        qgrad_v,
        kgrad_v,
        vgrad_v,
        part_v,
        near_got,
        far_got,
        outgrad_v,
        upgrad_v,
        down_v,
        gu_v,
        rows_v,
        send_sems,
        recv_sems,
        load_sems,
    ) = refs[:20]
    place = Place(n_batch)
    copies = Copies(send_sems, recv_sems)
    b, c, n = place.b, place.c, n_batch
    micro, pos_dev, width = grad_ref.shape
    length = 4 * pos_dev
    head_cols = heads * HD
    latent = qkv_ref.shape[3] - 2 * HD
    score_scale = 1.0 / math.sqrt(HD)
    pairs = [
        (grad_ref, grad_v.at[c]),
        (out_ref, out_v),
        (qkv_ref, qkv_v),
        (turned_ref, turned_v),
        (up_ref, up_v),
        (mixed_ref, mixed_v),
    ]
    if has_terms:
        (
            terms_v,
            terms_got,
            ring_send,
            ring_recv,
            act_v,
            cot_v,
            down_all,
            down_got,
        ) = refs[20:]
        pairs += [(terms_ref, terms_v), (down_ref, act_v)]
        n_tok = terms_v.shape[1]
        spots = [(0, 0, 0), (place.h, 0, 1)]
        spots += [
            (side * step, step, (side + 1) // 2) for step in range(1, place.h) for side in (-1, 1)
        ]
        pairs += [
            (cot_ref.at[place.rank_of(step)], cot_v.at[pair, pl.ds(side * n_tok, n_tok)])
            for step, pair, side in spots
        ]
    loads = [
        pltpu.make_async_copy(source, target, load_sems.at[i])
        for i, (source, target) in enumerate(pairs)
    ]
    for copy in loads:
        copy.start()
    peers = [(lax.rem(b + k, n), c) for k in range(1, n)]
    others = peers + [(b, place.far), (b, place.near), (b, lax.rem(place.near + 2, 4))]
    pl.semaphore_wait(greet(place, others), n + 2)
    out_rows = out_terms.shape[1]
    group = HeadGroup(place, out_rows)
    loads[0].wait()
    grads = CtxGather(place, copies, grad_v)
    for item in range(micro):
        grads.start(item)
    steps = []
    if has_terms:

        def spot(step):
            return 0 if step == 0 else 1 if step == place.h else 2 * abs(step) + (step > 0)

        terms = RingCollect(
            place, lambda step: terms_v.at[spot(step)], terms_got, ring_send, ring_recv
        )
        loads[6].wait()
        steps = [terms.advance] * place.h

    def ring_step():
        if steps:
            steps.pop()()

    ring_step()
    own_gu = copies.local(gu_ref.at[b], gu_v)
    own_rows = copies.local(rows_ref, rows_v.at[c, 0])
    for peer in peers:
        copies.remote(gu_ref.at[peer[0]], gu_grad.at[b], peer)
    for item in range(micro):
        grads.cross(item)
    outer, inner = place.outer, place.inner
    if has_terms:
        for copy in loads[7:]:
            copy.wait()
        n_rows = cot_v.shape[0] * cot_v.shape[1]
        ff = act_v.shape[2]

        @pl.loop(0, width // 512)
        def _(t):
            cols = pl.ds(pl.multiple_of(t * 512, 512), 512)
            term = dot_left_t(
                act_v[...].reshape(n_rows, ff), cot_v[:, :, cols].reshape(n_rows, 512)
            )
            down_all[:, :, cols] = term.astype(BF).reshape(4, ff // 4, 512)

        down_near = [
            copies.remote(down_all.at[2 * side + 1 - inner], down_got.at[side], (b, place.near))
            for side in (0, 1)
        ]
    else:
        down_own = copies.local(down_ref.at[outer], down_v.at[0])
        down_far = copies.remote(down_ref.at[1 - outer], down_v.at[1], (b, place.far))
    for copy in loads[1:6]:
        copy.wait()
    if has_terms:
        for copy in down_near:
            copies.arrive(copy)
        other = down_all.at[2 * (1 - outer) + inner]
        other[...] = (other[...].astype(F32) + down_got[1 - outer].astype(F32)).astype(BF)
        down_far = copies.remote(other, down_v.at[1], (b, place.far))
    copies.arrive(own_rows)
    rows = CtxGather(place, copies, rows_v)
    rows.start(0)
    back_sum = CtxCollect(place, copies, part_v, near_got, far_got)
    cosine, sine = cos_ref[...], sin_ref[...]
    for item in range(micro):
        grads.finish(item)
        incoming = grad_v[:, item].reshape(length, width)
        keys = qkv_v[:, item, :, latent : latent + HD].reshape(length, HD)
        values = qkv_v[:, item, :, latent + HD :].reshape(length, HD)
        keep = keep_ref[item]
        kgrad_v[...] = jnp.zeros_like(kgrad_v)
        vgrad_v[...] = jnp.zeros_like(vgrad_v)

        @pl.loop(0, heads)
        def _(head):
            cols = pl.ds(pl.multiple_of(head * HD, HD), HD)
            grad_mixed = dot_right_t(incoming, out_v[head]).astype(BF)
            queries = turned_v[item, :, cols]
            weights = softmax_rows(queries, keys, keep, score_scale)
            grad_probs = dot_right_t(grad_mixed, values)
            row_dot = jnp.sum(weights * grad_probs, axis=-1, keepdims=True)
            grad_scores = (weights * (grad_probs - row_dot)).astype(BF)
            front, back = turn(dot(grad_scores, keys) * score_scale, cosine, -sine)
            front, back = front.astype(BF), back.astype(BF)
            base = pl.multiple_of(head * HD, HD)
            qgrad_v[:, item, :, pl.ds(base, HD // 2)] = front.reshape(4, pos_dev, HD // 2)
            base = pl.multiple_of(head * HD + HD // 2, HD // 2)
            qgrad_v[:, item, :, pl.ds(base, HD // 2)] = back.reshape(4, pos_dev, HD // 2)
            kgrad_v[...] += dot_left_t(grad_scores, queries) * score_scale
            vgrad_v[...] += dot_left_t(weights.astype(BF), grad_mixed)

        ring_step()
        qgrad = qgrad_v[:, item].reshape(length, head_cols)
        part_v[:, item, :, :latent] = (
            dot_right_t(qgrad, up_v[...]).astype(BF).reshape(4, pos_dev, latent)
        )
        part_v[:, item, :, latent : latent + HD] = (
            kgrad_v[...].astype(BF).reshape(4, pos_dev, HD)
        )
        part_v[:, item, :, latent + HD :] = vgrad_v[...].astype(BF).reshape(4, pos_dev, HD)
        back_sum.start(item)
        if item > 0:
            back_sum.cross(item - 1)
    n_all = 4 * micro * pos_dev
    back_sum.cross(micro - 1)
    ring_step()

    @pl.loop(0, width // 512)
    def _(t):
        cols = pl.ds(pl.multiple_of(t * 512, 512), 512)
        term = dot_left_t(
            mixed_v[...].reshape(n_all, head_cols), grad_v[:, :, :, cols].reshape(n_all, 512)
        )
        outgrad_v[:, :, :, cols] = term.astype(BF).reshape(group.count, group.size, out_rows, 512)

    mine = out_terms.at[group.blocks(group.me)]
    copies.local(outgrad_v.at[:, group.me], mine)
    for member, device in group.others:
        copies.remote(outgrad_v.at[:, member], mine, device)
    for item in range(micro):
        back_out[item] = back_sum.finish(item)
    ring_step()

    @pl.loop(0, head_cols // HD)
    def _(t):
        cols = pl.ds(pl.multiple_of(t * HD, HD), HD)
        term = dot_left_t(
            qkv_v[:, :, :, :latent].reshape(n_all, latent),
            qgrad_v[:, :, :, cols].reshape(n_all, HD),
        )
        upgrad_v[:, :, cols] = term.astype(BF).reshape(n, latent // n, HD)

    copies.local(upgrad_v, up_terms)
    rows.cross(0)
    rows.finish(0)
    copies.local(rows_v, rows_all)
    copies.arrive(own_gu)
    copies.local(gu_v, gu_grad.at[b])
    copies.arrive(down_far)
    if has_terms:
        down_grad[...] = (
            down_all[2 * outer + inner].astype(F32)
            + down_got[outer].astype(F32)
            + down_v[1].astype(F32)
        )
    else:
        copies.arrive(down_own)
        down_grad[...] = down_v[0].astype(F32) + down_v[1].astype(F32)
    if has_terms:
        while steps:
            ring_step()
        cut = terms.cut
        for half in (0, 1):
            terms_sum[half * cut : (half + 1) * cut, :] = terms.finish(half)
        terms.drain()
    copies.drain()


def attention_back(
    n_batch, grad_att, qkv_all, turned, mixed, own_qup, own_out, grad_gu, down_part, attn_in, terms, cots, tables
):
    micro, pos_dev, width = grad_att.shape
    n_tok = micro * pos_dev
    qkv_cols = qkv_all.shape[3]
    latent, head_cols = own_qup.shape
    own_out = own_out.reshape(head_cols // HD, HD, width)
    length = 4 * pos_dev
    far = n_batch // 2
    has_terms = terms is not None
    down_rows = down_part.shape[2] // 4 if has_terms else down_part.shape[1]
    size = head_group(n_batch, head_cols // n_batch)
    sems = 2 * n_batch + 48
    anywhere = pl.BlockSpec(memory_space=pl.ANY)
    near = pl.BlockSpec(memory_space=pltpu.VMEM)
    out_shape = [
        jax.ShapeDtypeStruct((micro, pos_dev, qkv_cols), F32),
        jax.ShapeDtypeStruct((n_batch, head_cols // n_batch, width), BF),
        jax.ShapeDtypeStruct((n_batch, latent // n_batch, head_cols), BF),
        jax.ShapeDtypeStruct(grad_gu.shape, BF),
        jax.ShapeDtypeStruct((down_rows, width), F32),
        jax.ShapeDtypeStruct((4, 1) + attn_in.shape, BF),
    ]
    out_specs = [near] + [anywhere] * 3 + [near, anywhere]
    scratch = [
        pltpu.VMEM((4, micro, pos_dev, width), BF),
        pltpu.VMEM((4, micro, pos_dev, qkv_cols), BF),
        pltpu.VMEM((micro, length, head_cols), BF),
        pltpu.VMEM((4, micro, pos_dev, head_cols), BF),
        pltpu.VMEM((latent, head_cols), BF),
        pltpu.VMEM((head_cols // HD, HD, width), BF),
        pltpu.VMEM((4, micro, pos_dev, head_cols), BF),
        pltpu.VMEM((length, HD), F32),
        pltpu.VMEM((length, HD), F32),
        pltpu.VMEM((4, micro, pos_dev, qkv_cols), BF),
        pltpu.VMEM((2, micro, pos_dev, qkv_cols), BF),
        pltpu.VMEM((micro, pos_dev, qkv_cols), BF),
        pltpu.VMEM((n_batch // size, size, head_cols // n_batch, width), BF),
        pltpu.VMEM((n_batch, latent // n_batch, head_cols), BF),
        pltpu.VMEM((2, down_rows, width), BF),
        pltpu.VMEM(grad_gu.shape[1:], BF),
        pltpu.VMEM((4, 1) + attn_in.shape, BF),
        pltpu.SemaphoreType.DMA((sems,)),
        pltpu.SemaphoreType.DMA((sems,)),
        pltpu.SemaphoreType.DMA((8 + n_batch,)),
    ]
    args = [grad_att, qkv_all, turned, mixed, own_qup, own_out, grad_gu, down_part, attn_in]
    if has_terms:
        args += [terms, cots]
        out_shape.append(jax.ShapeDtypeStruct((n_tok, width), F32))
        out_specs.append(near)
        scratch += [
            pltpu.VMEM(terms.shape, BF),
            pltpu.VMEM((far, 2, 2, n_tok // 2, width), BF),
            pltpu.SemaphoreType.DMA((far, 2, 2)),
            pltpu.SemaphoreType.DMA((far, 2, 2)),
            pltpu.VMEM(down_part.shape, BF),
            pltpu.VMEM((far, 2 * n_tok, width), BF),
            pltpu.VMEM((4, down_rows, width), BF),
            pltpu.VMEM((2, down_rows, width), BF),
        ]
    return pl.pallas_call(
        functools.partial(attention_back_kernel, n_batch, head_cols // HD, has_terms),
        out_shape=tuple(out_shape),
        in_specs=[anywhere] * len(args) + [near] * 3,
        out_specs=out_specs,
        scratch_shapes=scratch,
        compiler_params=pltpu.CompilerParams(
            collective_id=4, has_side_effects=True, vmem_limit_bytes=56 * 1024 * 1024
        ),
        name="attention_back",
    )(*args, *tables)


def permuted_mlp(ring, rows_own, cots, gu_rows, own_down):
    mlp_in = ring.spread(rows_own)
    n_tok, width = rows_own.shape
    _, n_batch, n_ctx, own_rows, ff = gu_rows.shape
    own_gate, own_up = gu_rows.reshape(2, width, ff)
    own_down = own_down.reshape(ff, width)
    far = ring.h
    groups = [[0]] + [[-step, step] for step in range(1, far)] + [[far]]
    out_terms = {}
    in_terms = {}
    kept = []
    for group in groups:
        rows = jnp.concatenate([mlp_in[step] for step in group], axis=0)
        grad_rows = jnp.concatenate([pick(cots, ring.rank_of(step)) for step in group], axis=0)
        gate_part = dot(rows, own_gate)
        up_part = dot(rows, own_up)
        sigmoid_gate = jax.nn.sigmoid(gate_part)
        silu_gate = gate_part * sigmoid_gate
        activated = (silu_gate * up_part).astype(BF)
        grad_act = dot_right_t(grad_rows, own_down)
        grad_gate = (
            grad_act * up_part * (sigmoid_gate * (1.0 + gate_part * (1.0 - sigmoid_gate)))
        ).astype(BF)
        grad_up = (grad_act * silu_gate).astype(BF)
        in_term = dot_right_t(grad_gate, own_gate) + dot_right_t(grad_up, own_up)
        out_term = dot(activated, own_down)
        for place_in, step in enumerate(group):
            cut = slice(place_in * n_tok, (place_in + 1) * n_tok)
            in_terms[step] = in_term[cut]
            out_terms[step] = out_term[cut]
        kept.append((rows, grad_rows, activated, grad_gate, grad_up))
    rows, grad_rows, activated, grad_gate, grad_up = (
        jnp.concatenate(items, axis=0) for items in zip(*kept)
    )
    grad_gu = jnp.stack([dot_left_t(rows, grad_gate), dot_left_t(rows, grad_up)])
    grad_gu = grad_gu.reshape(2, n_batch, n_ctx, own_rows, ff).transpose(2, 1, 0, 3, 4)
    grad_down = dot_left_t(activated, grad_rows)
    return (
        ring.collect(lambda step: in_terms[step]),
        near_collect(grad_down.reshape(n_ctx, ff // n_ctx, width)).astype(BF),
        out_terms,
        ctx_collect(grad_gu).astype(BF),
    )


def shards(
    tokens,
    cotangent,
    lengths,
    slot_sequence,
    proj_in,
    query_up,
    proj_out,
    attn_gain,
    query_gain,
    mlp_gain,
    gate_up,
    down_proj,
):
    n_ctx = lax.axis_size("ctx")
    n_batch = lax.axis_size("batch")
    ctx_rank = lax.axis_index("ctx")
    batch_rank = lax.axis_index("batch")
    ring = Ring()
    micro, pos_dev, width = tokens.shape
    n_tok = micro * pos_dev
    full_length = pos_dev * n_ctx
    heads = H // n_ctx
    score_scale = 1.0 / math.sqrt(HD)
    in_cols = proj_in.shape[1]

    slot_total = lengths.shape[0]
    slot_ids = jnp.arange(slot_total, dtype=jnp.int32)
    seq_lengths = jnp.sum(
        jnp.where(slot_sequence[:, None] == slot_ids[None, :], lengths[None, :], 0), axis=1
    )
    own_lengths = lax.dynamic_slice_in_dim(seq_lengths, batch_rank * micro, micro)
    query_pos = ctx_rank * pos_dev + jnp.arange(pos_dev, dtype=jnp.int32)
    key_pos = jnp.arange(full_length, dtype=jnp.int32)
    cos_all, sin_all = rope_tables(full_length)

    own_rows = proj_in.shape[0]
    gain_rows = query_gain.shape[0]
    gains = jnp.stack(
        [attn_gain, mlp_gain, jnp.pad(query_gain, (0, own_rows - gain_rows))], axis=1
    )
    gain_cols = jnp.pad(gains, ((0, 0), (0, 125)))
    valid_rows = (query_pos[None, :] < own_lengths[:, None]).astype(F32).reshape(n_tok, 1)
    grad_out = cotangent.reshape(n_tok, width).astype(F32) * valid_rows
    keep = (key_pos[None, None, :] < own_lengths[:, None, None]).astype(F32)
    (
        hidden_res,
        mlp_in,
        gains,
        q_latent,
        packed,
        own_qup,
        own_out,
        gu_rows,
        own_down,
        qkv_all,
        turned,
        mixed,
        attn_in,
        cots,
    ) = front(
        n_batch,
        heads,
        proj_in,
        gain_cols,
        query_up,
        proj_out,
        gate_up,
        down_proj,
        tokens.reshape(n_tok, width),
        cotangent.reshape(n_tok, width),
        (cos_all, sin_all, keep, valid_rows),
    )
    own_qup = own_qup.reshape(QR, heads * HD)
    gain_mlp = gains[1]

    scale_two = rms_scale(hidden_res)
    normed_two = hidden_res * scale_two
    resident = 10 * n_batch * n_tok * width <= 24 * 1024 * 1024
    if resident:
        grad_mlp_in, down_part, terms, grad_gu_own = fused_mlp(
            n_batch, mlp_in, cots, gu_rows, own_down
        )
        terms = terms.reshape(n_batch, n_tok, width)
    else:
        terms = None
        grad_mlp_in, down_part, out_terms, grad_gu_own = permuted_mlp(
            ring, mlp_in, cots, gu_rows, own_down
        )
    gain_mlp_term = jnp.sum(grad_mlp_in * normed_two, axis=0)
    grad_hidden = grad_out + norm_back(grad_mlp_in * gain_mlp, normed_two, scale_two)
    back_own, out_grads, up_grads, grad_gu_own, grad_down, attn_in_all, *sums = attention_back(
        n_batch,
        grad_hidden.astype(BF).reshape(micro, pos_dev, width),
        qkv_all,
        turned,
        mixed,
        own_qup,
        own_out,
        grad_gu_own,
        down_part,
        attn_in,
        terms,
        cots,
        (cos_all, sin_all, keep),
    )
    out_sum = sums[0] if resident else ring.collect(lambda step: out_terms[step])
    layer_out = hidden_res + out_sum
    back_own = back_own.reshape(n_tok, in_cols)
    (
        grad_proj_out,
        grad_query_up,
        grad_proj_in,
        gain_sums,
        grad_gate_up,
        grad_tokens,
    ) = collect_weights(
        n_batch,
        gain_rows,
        out_grads,
        up_grads,
        attn_in_all,
        grad_gu_own,
        packed,
        (
            back_own,
            q_latent,
            tokens.reshape(n_tok, width),
            grad_hidden,
            gains,
            gain_mlp_term[None, :],
            cos_all,
            sin_all,
        ),
    )
    gain_sums = gain_sums[:, :own_rows]

    return (
        layer_out.reshape(tokens.shape).astype(BF),
        grad_tokens.reshape(tokens.shape),
        grad_proj_in,
        grad_query_up,
        grad_proj_out,
        gain_sums[0],
        gain_sums[2, :gain_rows],
        gain_sums[1],
        grad_gate_up,
        grad_down,
    )


def solution(mesh):
    rows = P(("batch", "ctx"), None)
    vector = P(("batch", "ctx"))
    acts = P("batch", "ctx", None)
    return jax.shard_map(
        shards,
        mesh=mesh,
        in_specs=(acts, acts, P(), P(), rows, rows, rows, vector, vector, vector, rows, rows),
        out_specs=(acts, acts, rows, rows, rows, vector, vector, vector, rows, rows),
        check_vma=False,
    )
```

```python
import functools
import math

import jax
import jax.numpy as jnp
import numpy as np
from jax import lax
from jax.experimental import pallas as pl
from jax.experimental.pallas import tpu as pltpu
from jax.sharding import PartitionSpec as P

H = 16
HD = 256
QR = 1024
EPSILON = 1e-06
BF = jnp.bfloat16
F32 = jnp.float32


def rms_scale(values):
    return lax.rsqrt(jnp.mean(values * values, axis=-1, keepdims=True) + EPSILON)


def rope_tables(length):
    half_size = HD // 2
    frequency = np.float32(10000.0) ** (-(np.arange(half_size, dtype=np.float32) * 2.0 / HD))
    angles = np.arange(length, dtype=np.float32)[:, None] * frequency.astype(np.float32)[None, :]
    cosine, sine = np.cos(angles), np.sin(angles)
    return jnp.asarray(cosine, F32), jnp.asarray(sine, F32)


def rotate(values, cosine_table, sine_table):
    half_size = values.shape[-1] // 2
    front_half = values[..., :half_size]
    back_half = values[..., half_size:]
    return jnp.concatenate(
        [
            front_half * cosine_table - back_half * sine_table,
            back_half * cosine_table + front_half * sine_table,
        ],
        axis=-1,
    )


def rotate_back(values, cosine_table, sine_table):
    return rotate(values, cosine_table, -sine_table)


def dot(left_side, right_side):
    return jnp.dot(left_side, right_side, preferred_element_type=F32)


def dot_right_t(left_side, right_side):
    return lax.dot_general(
        left_side, right_side, (((1,), (1,)), ((), ())), preferred_element_type=F32
    )


def dot_left_t(left_side, right_side):
    return lax.dot_general(
        left_side, right_side, (((0,), (0,)), ((), ())), preferred_element_type=F32
    )


def norm_back(grad_normed, normed, inv_rms):
    return inv_rms * (grad_normed - normed * jnp.mean(grad_normed * normed, axis=-1, keepdims=True))


def pick(array, index, axis=0):
    return lax.dynamic_index_in_dim(array, index, axis, keepdims=False)


def place(array, block, index, axis=0):
    return lax.dynamic_update_index_in_dim(array, block, index, axis)


class Ring:
    def __init__(self):
        self.n = lax.axis_size("batch")
        self.h = self.n // 2
        rank = lax.axis_index("batch")
        self.at = jnp.where(rank % 2 == 0, rank // 2, self.n - 1 - rank // 2)
        order = [2 * i for i in range(self.h)] + [2 * i + 1 for i in reversed(range(self.h))]
        self.up = [(order[i], order[(i + 1) % self.n]) for i in range(self.n)]
        self.down = [(there, here) for here, there in self.up]

    def rank_of(self, step):
        spot = (self.at + step) % self.n
        return jnp.where(spot < self.h, 2 * spot, 2 * (self.n - 1 - spot) + 1)

    def spread(self, block):
        found = {0: block}
        upward = downward = block
        for step in range(1, self.h):
            upward = lax.ppermute(upward, "batch", self.up)
            downward = lax.ppermute(downward, "batch", self.down)
            found[-step] = upward
            found[step] = downward
        cut = block.shape[0] // 2
        found[self.h] = jnp.concatenate(
            [
                lax.ppermute(upward[:cut], "batch", self.up),
                lax.ppermute(downward[cut:], "batch", self.down),
            ],
            axis=0,
        )
        return found

    def gather(self, block):
        found = self.spread(block)
        whole = jnp.zeros((self.n,) + block.shape, block.dtype)
        for step, part in found.items():
            whole = place(whole, part, self.rank_of(step))
        return whole

    def collect(self, term):
        far = term(self.h)
        cut = far.shape[0] // 2
        downward = lax.ppermute(far[:cut].astype(BF), "batch", self.down)
        upward = lax.ppermute(far[cut:].astype(BF), "batch", self.up)
        for step in range(self.h - 1, 0, -1):
            for_lower = term(-step).astype(F32)
            for_upper = term(step).astype(F32)
            if step == self.h - 1:
                for_lower = jnp.concatenate(
                    [for_lower[:cut] + downward.astype(F32), for_lower[cut:]], axis=0
                )
                for_upper = jnp.concatenate(
                    [for_upper[:cut], for_upper[cut:] + upward.astype(F32)], axis=0
                )
            else:
                for_lower = for_lower + downward.astype(F32)
                for_upper = for_upper + upward.astype(F32)
            downward = lax.ppermute(for_lower.astype(BF), "batch", self.down)
            upward = lax.ppermute(for_upper.astype(BF), "batch", self.up)
        own = term(0).astype(F32)
        return own + downward.astype(F32) + upward.astype(F32)

    def collect_rows(self, stacked):
        return self.collect(lambda step: pick(stacked, self.rank_of(step)))


FAR = [(0, 2), (1, 3), (2, 0), (3, 1)]
NEAR = [(0, 1), (1, 0), (2, 3), (3, 2)]


def ctx_place():
    rank = lax.axis_index("ctx")
    return rank // 2, rank % 2


def in_order(mine, theirs, at):
    return jnp.where(at == 0, jnp.stack([mine, theirs]), jnp.stack([theirs, mine]))


def ctx_gather(block):
    outer, inner = ctx_place()
    pair = in_order(block, lax.ppermute(block, "ctx", FAR), outer)
    whole = in_order(pair, lax.ppermute(pair, "ctx", NEAR), inner)
    whole = jnp.swapaxes(whole, 0, 1)
    return whole.reshape((4,) + block.shape)


def near_collect(stacked):
    _, inner = ctx_place()
    parts = stacked.reshape((2, 2) + stacked.shape[1:])
    got = lax.ppermute(pick(parts, 1 - inner, 1).astype(BF), "ctx", NEAR)
    return pick(parts, inner, 1).astype(F32) + got.astype(F32)


def ctx_collect(stacked):
    outer, _ = ctx_place()
    half = near_collect(stacked)
    got = lax.ppermute(pick(half, 1 - outer).astype(BF), "ctx", FAR)
    return pick(half, outer) + got.astype(F32)


def ctx_exchange(stacked):
    outer, inner = ctx_place()
    parts = stacked.reshape((2, 2) + stacked.shape[1:])
    got = lax.ppermute(pick(parts, 1 - outer), "ctx", FAR)
    parts = in_order(pick(parts, outer), got, outer)
    got = lax.ppermute(pick(parts, 1 - inner, 1), "ctx", NEAR)
    whole = in_order(pick(parts, inner, 1), got, inner)
    return jnp.swapaxes(whole, 0, 1).reshape(stacked.shape)


MESH = pl.DeviceIdType.MESH


class Place:
    def __init__(self, n_batch):
        self.n = n_batch
        self.h = n_batch // 2
        self.b = lax.axis_index("batch")
        self.c = lax.axis_index("ctx")
        self.outer = lax.div(self.c, 2)
        self.inner = lax.rem(self.c, 2)
        self.far = lax.rem(self.c + 2, 4)
        self.near = self.c + 1 - 2 * self.inner
        odd = lax.rem(self.b, 2)
        half = lax.div(self.b, 2)
        self.at = half + odd * (self.n - 1 - 2 * half)

    def rank_of(self, step):
        spot = lax.rem(self.at + step + 2 * self.n, self.n)
        back = lax.div(spot, self.h)
        return (1 - back) * 2 * spot + back * (2 * (self.n - 1 - spot) + 1)

    def up(self):
        return (self.rank_of(1), self.c)

    def down(self):
        return (self.rank_of(-1), self.c)


class Copies:
    def __init__(self, send_sems, recv_sems):
        self.send_sems = send_sems
        self.recv_sems = recv_sems
        self.count = 0
        self.open_sends = []
        self.open_recvs = []

    def remote(self, source, target, device):
        index = self.count
        self.count += 1
        copy = pltpu.make_async_remote_copy(
            src_ref=source,
            dst_ref=target,
            send_sem=self.send_sems.at[index],
            recv_sem=self.recv_sems.at[index],
            device_id=device,
            device_id_type=MESH,
        )
        copy.start()
        self.open_sends.append(copy)
        self.open_recvs.append(copy)
        return copy

    def local(self, source, target):
        index = self.count
        self.count += 1
        copy = pltpu.make_async_copy(source, target, self.recv_sems.at[index])
        copy.start()
        self.open_recvs.append(copy)
        return copy

    def arrive(self, copy):
        if any(copy is other for other in self.open_recvs):
            self.open_recvs = [other for other in self.open_recvs if other is not copy]
            if any(copy is other for other in self.open_sends):
                copy.wait_recv()
            else:
                copy.wait()

    def drain(self):
        for copy in list(self.open_recvs):
            self.arrive(copy)
        for copy in self.open_sends:
            copy.wait_send()


def greet(place, others):
    barrier = pltpu.get_barrier_semaphore()
    for device in others:
        pl.semaphore_signal(barrier, inc=1, device_id=device, device_id_type=MESH)
    return barrier


class RingGather:
    def __init__(self, place, copies, rows, slot):
        self.place, self.copies, self.rows, self.slot = place, copies, rows, slot
        self.step = 0
        self.moving = ()

    def advance(self):
        place, copies = self.place, self.copies
        for copy in self.moving:
            copies.arrive(copy)
        self.moving = ()
        self.step += 1
        cut = self.rows // 2
        if self.step > place.h:
            return
        lower = place.rank_of(1 - self.step)
        upper = place.rank_of(self.step - 1)
        if self.step < place.h:
            whole = pl.ds(0, self.rows)
            pieces = (whole, whole)
        else:
            pieces = (pl.ds(0, cut), pl.ds(cut, self.rows - cut))
        upward, downward = self.slot(lower, pieces[0]), self.slot(upper, pieces[1])
        self.moving = (
            copies.remote(upward, upward, place.up()),
            copies.remote(downward, downward, place.down()),
        )

    def arrived(self):
        step = self.step - 1
        if step == 0:
            return []
        if step == self.place.h:
            return [self.place.rank_of(step)]
        return [self.place.rank_of(-step), self.place.rank_of(step)]


def mlp_kernel(
    n_batch,
    rows_ref,
    gu_ref,
    down_ref,
    cot_ref,
    hidden_ref,
    gains_ref,
    *refs,
):
    (
        grad_ref,
        low_ref,
        gain_term,
        act_out,
        term_out,
        gu_out,
        rows_v,
        cot_v,
        gate_v,
        up_v,
        down_v,
        act_v,
        ggate_v,
        gup_v,
        in_v,
        term_v,
        got_v,
        gu_got,
        gu_last,
        send_sems,
        recv_sems,
        back_send,
        back_recv,
        load_sems,
        store_sems,
        part_send,
        part_recv,
    ) = refs
    place = Place(n_batch)
    far = place.h
    n_tok = rows_ref.shape[0]
    cut = n_tok // 2
    width = rows_ref.shape[1]
    ff = gu_ref.shape[-1]
    up_device, down_device = place.up(), place.down()
    far_device, near_device = (place.b, place.far), (place.b, place.near)
    barrier = greet(place, [up_device, down_device, far_device, near_device])
    parts = Copies(part_send, part_recv)
    own_rows = gate_v.shape[2]
    block = 4 * own_rows

    load_rows = pltpu.make_async_copy(rows_ref, rows_v.at[0, pl.ds(0, n_tok)], load_sems.at[0])
    load_rows.start()
    loads = [
        pltpu.make_async_copy(source, target, load_sems.at[1 + i])
        for i, (source, target) in enumerate(
            [(gu_ref.at[0], gate_v), (gu_ref.at[1], up_v), (down_ref, down_v)]
        )
    ]
    spots = [(0, 0, 0), (far, 0, 1)]
    spots += [(side * step, step, (side + 1) // 2) for step in range(1, far) for side in (-1, 1)]
    for i, (distance, group, side) in enumerate(spots):
        loads.append(
            pltpu.make_async_copy(
                cot_ref.at[place.rank_of(distance)], cot_v.at[group, pl.ds(side * n_tok, n_tok)], load_sems.at[4 + i]
            )
        )
    for copy in loads:
        copy.start()
    load_rows.wait()
    pl.semaphore_wait(barrier, 4)

    def piece(side, half):
        return pl.ds(side * n_tok + half * cut, cut)

    def hop(step, side, half):
        source_group, source_side = step - 1, side
        target_group, target_side = step, side
        if isinstance(step, int) and step == 1:
            source_side = 0
        if isinstance(step, int) and step == far:
            target_group, target_side = 0, 1
        return pltpu.make_async_remote_copy(
            src_ref=rows_v.at[source_group, piece(source_side, half)],
            dst_ref=rows_v.at[target_group, piece(target_side, half)],
            send_sem=send_sems.at[step, side, half],
            recv_sem=recv_sems.at[step, side, half],
            device_id=down_device if side else up_device,
            device_id_type=MESH,
        )

    both = [(side, half) for half in (0, 1) for side in (0, 1)]
    ends = [(0, 0), (1, 1)]
    for side, half in both:
        hop(1, side, half).start()
    for copy in loads:
        copy.wait()

    def stores(group):
        return [
            pltpu.make_async_copy(term_v.at[group], term_out.at[group], store_sems.at[0, group]),
            pltpu.make_async_copy(act_v.at[group], act_out.at[group], store_sems.at[1, group]),
        ]

    def compute(group):
        rows = rows_v[group]
        cots = cot_v[group]
        down_all = down_v[...].reshape(ff, width)
        start = 0
        while start < ff:
            size = min(256, ff - start)
            tile = slice(start, start + size)
            gate = dot(rows, gate_v[..., tile].reshape(width, size))
            up = dot(rows, up_v[..., tile].reshape(width, size))
            grad_act = dot_right_t(cots, down_all[tile])
            sigmoid = 1.0 / (1.0 + jnp.exp(-gate))
            silu = gate * sigmoid
            act_v[group, :, tile] = (silu * up).astype(BF)
            slope = sigmoid * (1.0 + gate * (1.0 - sigmoid))
            ggate_v[group, :, tile] = (grad_act * up * slope).astype(BF)
            gup_v[group, :, tile] = (grad_act * silu).astype(BF)
            start += size
        ggate = ggate_v[group]
        gup = gup_v[group]
        act = act_v[group]
        tile_cols = 2 * block

        @pl.loop(0, width // tile_cols)
        def _(t):
            cols = pl.ds(pl.multiple_of(t * tile_cols, tile_cols), tile_cols)
            back = dot_right_t(ggate, gate_v[pl.ds(2 * t, 2)].reshape(tile_cols, ff))
            back += dot_right_t(gup, up_v[pl.ds(2 * t, 2)].reshape(tile_cols, ff))
            in_v[group, :, cols] = back.astype(BF)
            down = down_v[:, :, cols].reshape(ff, tile_cols)
            term_v[group, :, cols] = dot(act, down).astype(BF)

        for copy in stores(group):
            copy.start()

    @pl.loop(1, far)
    def _(step):
        for side, half in both:
            hop(step, side, half).wait_recv()

            @pl.when(step < far - 1)
            def _():
                hop(step + 1, side, half).start()

            if (side, half) in ends:

                @pl.when(step == far - 1)
                def _():
                    hop(far, side, half).start()

        compute(step)

    for side, half in ends:
        hop(far, side, half).wait_recv()
    compute(0)

    def back_hop(step, side, half, source):
        return pltpu.make_async_remote_copy(
            src_ref=source,
            dst_ref=got_v.at[step, side, half],
            send_sem=back_send.at[step, side, half],
            recv_sem=back_recv.at[step, side, half],
            device_id=up_device if side else down_device,
            device_id_type=MESH,
        )

    def held(step, side, half):
        return in_v.at[step, piece(side, half)]

    for side, half in ends:
        back_hop(far - 1, side, half, held(0, 1, half)).start()

    def pass_on(step, side, half, added):
        own = held(step, side, half)
        if added:
            back_hop(step, side, half, own).wait_recv()
            own[...] = (own[...].astype(F32) + got_v[step, side, half].astype(F32)).astype(BF)
        back_hop(step - 1, side, half, own).start()

    for side, half in both:
        if (side, half) not in ends:
            pass_on(far - 1, side, half, False)

    def gate_up_terms(t):
        cols = slice(t * 2 * block, (t + 1) * 2 * block)
        rows = rows_v[:, :, cols].reshape(n_batch * n_tok, 2 * block)
        for target, grads in ((gate_v, ggate_v), (up_v, gup_v)):
            term = dot_left_t(rows, grads[...].reshape(n_batch * n_tok, ff))
            target[2 * t : 2 * t + 2] = term.astype(BF).reshape(2, 4, own_rows, ff)

    def pass_all(step):
        for side, half in [(1, 0), (0, 1), (0, 0), (1, 1)]:
            if step < far - 1 or (side, half) in ends:
                pass_on(step, side, half, True)

    steps = list(range(1, far))
    outer, inner = place.outer, place.inner
    kinds = list(enumerate((gate_v, up_v)))
    near_copies, far_copies = {}, {}

    def send_near(t):
        pair = pl.ds(2 * t, 2)
        near_copies[t] = [
            parts.remote(
                target.at[pair, 2 * side + 1 - inner], gu_got.at[kind, side, pair], near_device
            )
            for side in (0, 1)
            for kind, target in kinds
        ]

    def send_far(t):
        pair = pl.ds(2 * t, 2)
        for copy in near_copies[t]:
            parts.arrive(copy)
        far_copies[t] = []
        for kind, target in kinds:
            other = target.at[pair, 2 * (1 - outer) + inner]
            added = other[...].astype(F32) + gu_got[kind, 1 - outer, pair].astype(F32)
            other[...] = added.astype(BF)
            far_copies[t].append(parts.remote(other, gu_last.at[kind, pair], far_device))

    def take_far(t):
        pair = pl.ds(2 * t, 2)
        for copy in far_copies[t]:
            parts.arrive(copy)
        for kind, target in kinds:
            kept = target.at[pair, 2 * outer + inner]
            added = kept[...].astype(F32) + gu_got[kind, outer, pair].astype(F32)
            kept[...] = (added + gu_last[kind, pair].astype(F32)).astype(BF)
            parts.local(kept, gu_out.at[pair, kind])

    def ring_step():
        if steps:
            pass_all(steps.pop())

    tiles = width // (2 * block)
    for t in range(tiles):
        gate_up_terms(t)
        send_near(t)
        if t > 0:
            send_far(t - 1)
        ring_step()
    while steps:
        ring_step()
    send_far(tiles - 1)
    totals = []
    for half in (0, 1):
        for side in (0, 1):
            back_hop(0, side, half, held(0, 0, half)).wait_recv()
        totals.append(
            in_v[0, half * cut : (half + 1) * cut, :].astype(F32)
            + got_v[0, 0, half].astype(F32)
            + got_v[0, 1, half].astype(F32)
        )
    total = jnp.concatenate(totals, axis=0)
    hidden = hidden_ref[...]
    inverse = rms_scale(hidden)
    normed = hidden * inverse
    gain_term[...] = jnp.sum(total * normed, axis=0, keepdims=True)
    back = norm_back(total * gains_ref[1:2, :], normed, inverse)
    grad_hidden = cot_v[0, :n_tok, :].astype(F32) + back
    grad_ref[...] = grad_hidden
    low_ref[...] = grad_hidden.astype(BF)
    for t in range(tiles):
        take_far(t)
    parts.drain()

    for step in range(1, far + 1):
        for side, half in both if step < far else ends:
            hop(step, side, half).wait_send()
    for side, half in ends:
        back_hop(far - 1, side, half, held(0, 1, half)).wait_send()
    for step in range(far - 1, 0, -1):
        for side, half in both:
            back_hop(step - 1, side, half, held(step, side, half)).wait_send()
    for group in range(far):
        for copy in stores(group):
            copy.wait()


def fused_mlp(n_batch, rows, cots, hidden_res, gains, gu_rows, own_down):
    n_tok, width = rows.shape
    ff = gu_rows.shape[-1]
    own_rows = gu_rows.shape[3]
    far = n_batch // 2
    pair = 2 * n_tok
    flops = 18 * n_batch * n_tok * width * ff
    return pl.pallas_call(
        functools.partial(mlp_kernel, n_batch),
        out_shape=(
            jax.ShapeDtypeStruct((n_tok, width), F32),
            jax.ShapeDtypeStruct((n_tok, width), BF),
            jax.ShapeDtypeStruct((1, width), F32),
            jax.ShapeDtypeStruct((far, pair, ff), BF),
            jax.ShapeDtypeStruct((far, pair, width), BF),
            jax.ShapeDtypeStruct((n_batch, 2, own_rows, ff), BF),
        ),
        in_specs=[pl.BlockSpec(memory_space=pl.ANY)] * 4
        + [pl.BlockSpec(memory_space=pltpu.VMEM)] * 2,
        out_specs=[pl.BlockSpec(memory_space=pltpu.VMEM)] * 3
        + [pl.BlockSpec(memory_space=pl.ANY)] * 3,
        scratch_shapes=[
            pltpu.VMEM((far, pair, width), BF),
            pltpu.VMEM((far, pair, width), BF),
            pltpu.VMEM((n_batch, 4, own_rows, ff), BF),
            pltpu.VMEM((n_batch, 4, own_rows, ff), BF),
            pltpu.VMEM((4, ff // 4, width), BF),
            pltpu.VMEM((far, pair, ff), BF),
            pltpu.VMEM((far, pair, ff), BF),
            pltpu.VMEM((far, pair, ff), BF),
            pltpu.VMEM((far, pair, width), BF),
            pltpu.VMEM((far, pair, width), BF),
            pltpu.VMEM((far, 2, 2, n_tok // 2, width), BF),
            pltpu.VMEM((2, 2, n_batch, own_rows, ff), BF),
            pltpu.VMEM((2, n_batch, own_rows, ff), BF),
            pltpu.SemaphoreType.DMA((far + 1, 2, 2)),
            pltpu.SemaphoreType.DMA((far + 1, 2, 2)),
            pltpu.SemaphoreType.DMA((far, 2, 2)),
            pltpu.SemaphoreType.DMA((far, 2, 2)),
            pltpu.SemaphoreType.DMA((4 + n_batch,)),
            pltpu.SemaphoreType.DMA((2, far)),
            pltpu.SemaphoreType.DMA((72,)),
            pltpu.SemaphoreType.DMA((72,)),
        ],
        compiler_params=pltpu.CompilerParams(
            collective_id=1, has_side_effects=True, vmem_limit_bytes=60 * 1024 * 1024
        ),
        cost_estimate=pl.CostEstimate(
            flops=flops, bytes_accessed=24 * 1024 * 1024, transcendentals=n_batch * n_tok * ff
        ),
        name="fused_mlp",
    )(rows, gu_rows, own_down, cots, hidden_res, gains)


class RingCollect:
    def __init__(self, place, block, got, send_sems, recv_sems):
        self.place, self.block, self.got = place, block, got
        self.send_sems, self.recv_sems = send_sems, recv_sems
        self.cut = got.shape[3]
        self.step = place.h
        self.sent = []

    def held(self, step, half):
        return self.block(step).at[pl.ds(half * self.cut, self.cut)]

    def hop(self, step, side, half, source):
        place = self.place
        return pltpu.make_async_remote_copy(
            src_ref=source,
            dst_ref=self.got.at[step, side, half],
            send_sem=self.send_sems.at[step, side, half],
            recv_sem=self.recv_sems.at[step, side, half],
            device_id=place.up() if side else place.down(),
            device_id_type=MESH,
        )

    def send(self, step, side, half, source):
        copy = self.hop(step, side, half, source)
        copy.start()
        self.sent.append(copy)

    def advance(self):
        far = self.place.h
        step = self.step
        self.step -= 1
        if step == far:
            for side in (0, 1):
                self.send(far - 1, side, side, self.held(far, side))
            for side in (0, 1):
                half = 1 - side
                self.send(far - 2, side, half, self.held((2 * side - 1) * (far - 1), half))
            return
        pieces = [(0, 0), (1, 1)] if step == far - 1 else [(1, 0), (0, 1), (0, 0), (1, 1)]
        for side, half in pieces:
            own = self.held((2 * side - 1) * step, half)
            self.hop(step, side, half, own).wait_recv()
            own[...] = (own[...].astype(F32) + self.got[step, side, half].astype(F32)).astype(BF)
            self.send(step - 1, side, half, own)

    def finish(self, half):
        own = self.held(0, half)
        for side in (0, 1):
            self.hop(0, side, half, own).wait_recv()
        return (
            own[...].astype(F32)
            + self.got[0, 0, half].astype(F32)
            + self.got[0, 1, half].astype(F32)
        )

    def drain(self):
        for copy in self.sent:
            copy.wait_send()


def tail_kernel(
    n_batch,
    gain_rows,
    out_ref,
    up_ref,
    rows_ref,
    gu_ref,
    packed_ref,
    back_ref,
    latent_ref,
    tokens_ref,
    hidden_ref,
    gains_ref,
    mlp_term_ref,
    cos_ref,
    sin_ref,
    out_grad,
    up_grad,
    in_grad,
    attn_gain_grad,
    query_gain_grad,
    mlp_gain_grad,
    gu_grad,
    tokens_grad,
    out_v,
    up_v,
    in_v,
    out_got,
    up_got,
    in_got,
    up_sum,
    up_all,
    in_sum,
    in_all,
    ring_send,
    ring_recv,
    send_sems,
    recv_sems,
    packed_v,
    project_own,
    project_v,
    rows_v,
    gu_v,
    load_sems,
):
    place = Place(n_batch)
    copies = Copies(send_sems, recv_sems)
    b, c, n = place.b, place.c, n_batch
    own_rows = in_grad.shape[0]
    group = HeadGroup(place, out_grad.shape[0])
    ctx_peers = [(b, place.far), (b, place.near), (b, lax.rem(place.near + 2, 4))]

    loads = [
        pltpu.make_async_copy(held, kept, load_sems.at[i])
        for i, (held, kept) in enumerate([(out_ref, out_v), (up_ref, up_v), (rows_ref, rows_v), (gu_ref, gu_v), (packed_ref, packed_v)])
    ]
    for copy in loads:
        copy.start()
    barrier = greet(place, [place.up(), place.down()] + ctx_peers)

    pl.semaphore_wait(barrier, 5)

    rings = []
    for i, (kept, got) in enumerate([(out_v, out_got), (up_v, up_got), (in_v, in_got)]):
        rings.append(
            RingCollect(
                place,
                lambda step, kept=kept: kept.at[place.rank_of(step)],
                got,
                ring_send.at[i],
                ring_recv.at[i],
            )
        )
    for copy, ring in zip(loads[:2], rings):
        copy.wait()
        ring.advance()
    part_cols = project_v.shape[2]
    n_tok, width = tokens_ref.shape
    pos_dev = cos_ref.shape[0] // 4
    own_at = pl.ds(pl.multiple_of(c * pos_dev, pos_dev), pos_dev)
    cos_own = jnp.concatenate([cos_ref[own_at, :]] * (n_tok // pos_dev), axis=0)
    sin_own = jnp.concatenate([sin_ref[own_at, :]] * (n_tok // pos_dev), axis=0)
    latent = latent_ref.shape[1]

    q_latent = latent_ref[...]
    inverse = rms_scale(q_latent)
    normed_query = q_latent * inverse
    grad_qn = back_ref[:, :latent]
    query_term = jnp.sum(grad_qn * normed_query, axis=0, keepdims=True)
    grad_latent = norm_back(grad_qn * gains_ref[2:3, :latent], normed_query, inverse)
    front, back = turn(back_ref[:, latent : latent + HD], cos_own, -sin_own)
    project = jnp.concatenate(
        [grad_latent, front, back, back_ref[:, latent + HD :]], axis=1
    ).astype(BF)
    for part in range(4):
        project_own[part] = project[:, part * part_cols : (part + 1) * part_cols]
    project_copies = [
        copies.remote(project_own.at[peer[1]], project_v.at[c], peer) for peer in ctx_peers
    ]
    project_copies.append(copies.local(project_own.at[c], project_v.at[c]))
    for ring in rings[:2]:
        ring.advance()
    loads[4].wait()
    in_cols = 4 * part_cols
    residual = tokens_ref[...].astype(F32)
    inverse = rms_scale(residual)
    normed = residual * inverse
    weights = packed_v[:, :, :, :in_cols].reshape(width, in_cols)
    grad_attn_in = dot_right_t(project, weights)
    attn_term = jnp.sum(grad_attn_in * normed, axis=0, keepdims=True)
    back = norm_back(grad_attn_in * gains_ref[0:1, :], normed, inverse)
    tokens_grad[...] = (hidden_ref[...] + back).astype(BF)
    for ring in rings[:2]:
        ring.advance()
    for copy in project_copies:
        copies.arrive(copy)
    loads[2].wait()
    project_all = project_v[...].reshape(-1, part_cols)
    part_rows = own_rows + 16
    n_all = project_all.shape[0]
    ahead = max(1, 256 // (4 * own_rows))
    chunk = ahead * 4 * own_rows

    @pl.loop(0, width // chunk)
    def _(t):
        cols = pl.ds(pl.multiple_of(t * chunk, chunk), chunk)
        term = dot_left_t(rows_v[:, :, :, cols].reshape(n_all, chunk), project_all).astype(BF)
        term = term.reshape(ahead, 4, own_rows, part_cols)
        for part in range(4):
            in_v[pl.ds(t * ahead, ahead), pl.ds(part * part_rows, own_rows), :] = term[:, part]

    none = jnp.zeros((16, part_cols), BF)
    wide = jnp.concatenate([attn_term, mlp_term_ref[...], jnp.zeros((14, width), F32)], axis=0)
    short = jnp.concatenate([jnp.zeros((2, latent), F32), query_term], axis=0)
    short = jnp.concatenate([short, jnp.zeros((13, latent), F32)], axis=0)
    for rank in range(n):
        for part in range(4):
            at = pl.ds(part * part_rows + own_rows, 16)
            device = 4 * rank + part
            in_v[rank, at, :] = none
            in_v[rank, at, :own_rows] = wide[
                :, device * own_rows : (device + 1) * own_rows
            ].astype(BF)
            more = short[:, device * gain_rows : (device + 1) * gain_rows].astype(BF)
            kept = in_v[rank, at, :gain_rows]
            in_v[rank, at, :gain_rows] = kept + more
    rings[2].advance()
    if rings[0].step > 0:
        for ring in rings[:2]:
            ring.advance()
    while rings[2].step > 0:
        for ring in rings:
            if ring.step > 0:
                ring.advance()

    loads[3].wait()
    ff = gu_v.shape[3]
    for slab_at in range(n):
        for kind in (0, 1):
            start = (kind * n + slab_at) * ff
            gu_grad[:, start : start + ff] = gu_v[slab_at, kind].astype(F32)

    in_ring, up_ring, out_ring = rings[2], rings[1], rings[0]
    out_cut, up_cut, in_cut = out_ring.cut, up_ring.cut, in_ring.cut
    for half in (0, 1):
        out_grad[half * out_cut : (half + 1) * out_cut, :] = out_ring.finish(half)
    for half in (0, 1):
        up_sum[pl.ds(half * up_cut, up_cut), :] = up_ring.finish(half).astype(BF)
    up_copies = [
        copies.remote(
            up_sum.at[pl.ds(peer[1] * gain_rows, gain_rows)], up_all.at[c], peer
        )
        for peer in ctx_peers
    ]
    up_copies.append(
        copies.local(up_sum.at[pl.ds(c * gain_rows, gain_rows)], up_all.at[c])
    )
    for half in (0, 1):
        in_sum[pl.ds(half * in_cut, in_cut), :] = in_ring.finish(half).astype(BF)
    in_copies = [
        copies.remote(in_sum.at[pl.ds(peer[1] * part_rows, part_rows)], in_all.at[c], peer)
        for peer in ctx_peers
    ]
    in_copies.append(copies.local(in_sum.at[pl.ds(c * part_rows, part_rows)], in_all.at[c]))

    for copy in up_copies:
        copies.arrive(copy)
    cols = up_all.shape[2]
    heads = cols // HD
    for part in range(4):
        for local in range(heads):
            head = group.head(part, local, heads)
            up_grad[:, head * HD : (head + 1) * HD] = up_all[
                part, :, local * HD : (local + 1) * HD
            ].astype(F32)
    for copy in in_copies:
        copies.arrive(copy)
    cols = in_all.shape[2]
    gains = jnp.zeros((16, cols), F32)
    for part in range(4):
        in_grad[:, part * cols : (part + 1) * cols] = in_all[part, :own_rows, :].astype(F32)
        gains = gains + in_all[part, own_rows:, :].astype(F32)
    attn_gain_grad[...] = gains[0:1, :own_rows]
    mlp_gain_grad[...] = gains[1:2, :own_rows]
    query_gain_grad[...] = gains[2:3, :gain_rows]
    copies.drain()
    for ring in rings:
        ring.drain()


def collect_weights(n_batch, gain_rows, out_terms, up_terms, attn_in_all, grad_gu, packed, own):
    far = n_batch // 2
    out_rows, width = out_terms.shape[1:]
    up_rows, up_cols = up_terms.shape[1:]
    n_tok = own[2].shape[0]
    in_cols = own[0].shape[1] // 4
    own_rows = width // (4 * n_batch)
    in_rows = 4 * (own_rows + 16)
    shapes = [out_terms.shape[1:], up_terms.shape[1:], (in_rows, in_cols)]
    sems = 2 * n_batch + 16
    return pl.pallas_call(
        functools.partial(tail_kernel, n_batch, gain_rows),
        out_shape=(
            jax.ShapeDtypeStruct((out_rows, width), F32),
            jax.ShapeDtypeStruct((gain_rows, 4 * up_cols), F32),
            jax.ShapeDtypeStruct((own_rows, 4 * in_cols), F32),
            jax.ShapeDtypeStruct((1, own_rows), F32),
            jax.ShapeDtypeStruct((1, gain_rows), F32),
            jax.ShapeDtypeStruct((1, own_rows), F32),
            jax.ShapeDtypeStruct((own_rows, 2 * n_batch * grad_gu.shape[3]), F32),
            jax.ShapeDtypeStruct((n_tok, width), BF),
        ),
        in_specs=[pl.BlockSpec(memory_space=pl.ANY)] * 5 + [pl.BlockSpec(memory_space=pltpu.VMEM)] * len(own),
        out_specs=[pl.BlockSpec(memory_space=pltpu.VMEM)] * 8,
        scratch_shapes=[pltpu.VMEM((n_batch,) + shape, BF) for shape in shapes]
        + [pltpu.VMEM((far, 2, 2, rows // 2, cols), BF) for rows, cols in shapes]
        + [
            pltpu.VMEM((up_rows, up_cols), BF),
            pltpu.VMEM((4, gain_rows, up_cols), BF),
            pltpu.VMEM((in_rows, in_cols), BF),
            pltpu.VMEM((4, own_rows + 16, in_cols), BF),
            pltpu.SemaphoreType.DMA((3, far, 2, 2)),
            pltpu.SemaphoreType.DMA((3, far, 2, 2)),
            pltpu.SemaphoreType.DMA((sems,)),
            pltpu.SemaphoreType.DMA((sems,)),
            pltpu.VMEM(packed.shape, BF),
            pltpu.VMEM((4, n_tok, in_cols), BF),
            pltpu.VMEM((4, n_tok, in_cols), BF),
            pltpu.VMEM(attn_in_all.shape, BF),
            pltpu.VMEM(grad_gu.shape, BF),
            pltpu.SemaphoreType.DMA((5,)),
        ],
        compiler_params=pltpu.CompilerParams(
            collective_id=2, has_side_effects=True, vmem_limit_bytes=56 * 1024 * 1024
        ),
        name="collect_weights",
    )(out_terms, up_terms, attn_in_all, grad_gu, packed, *own)


class CtxCollect:
    def __init__(self, place, copies, part, near_got, far_got):
        self.place, self.copies, self.part = place, copies, part
        self.near_got, self.far_got = near_got, far_got
        self.near = {}
        self.far = {}

    def start(self, item):
        place = self.place
        self.near[item] = [
            self.copies.remote(
                self.part.at[2 * side + 1 - place.inner, item],
                self.near_got.at[side, item],
                (place.b, place.near),
            )
            for side in (0, 1)
        ]

    def cross(self, item):
        place = self.place
        for copy in self.near[item]:
            self.copies.arrive(copy)
        other = self.part.at[2 * (1 - place.outer) + place.inner, item]
        added = other[...].astype(F32) + self.near_got[1 - place.outer, item].astype(F32)
        other[...] = added.astype(BF)
        self.far[item] = self.copies.remote(
            other, self.far_got.at[item], (place.b, place.far)
        )

    def finish(self, item):
        place = self.place
        self.copies.arrive(self.far[item])
        return (
            self.part[2 * place.outer + place.inner, item].astype(F32)
            + self.near_got[place.outer, item].astype(F32)
            + self.far_got[item].astype(F32)
        )


class CtxGather:
    def __init__(self, place, copies, everyone):
        self.place, self.copies, self.everyone = place, copies, everyone
        self.far = {}
        self.near = {}

    def start(self, item):
        place = self.place
        own = self.everyone.at[place.c, item]
        self.far[item] = self.copies.remote(own, own, (place.b, place.far))
        self.near[item] = [self.copies.remote(own, own, (place.b, place.near))]

    def cross(self, item):
        place = self.place
        self.copies.arrive(self.far[item])
        other = self.everyone.at[place.far, item]
        self.near[item].append(self.copies.remote(other, other, (place.b, place.near)))

    def finish(self, item):
        for copy in self.near[item]:
            self.copies.arrive(copy)


def greet_lines(place):
    devices = [place.up(), place.down(), (place.b, place.far), (place.b, place.near)]
    pl.semaphore_wait(greet(place, devices), 4)


def turn(values, cosine, sine):
    half_size = HD // 2
    front, back = values[:, :half_size], values[:, half_size:]
    return front * cosine - back * sine, back * cosine + front * sine


def softmax_rows(queries, keys, keep, score_scale):
    scores = dot_right_t(queries, keys) * score_scale
    rows = lax.broadcasted_iota(jnp.int32, scores.shape, 0)
    cols = lax.broadcasted_iota(jnp.int32, scores.shape, 1)
    masked = jnp.where((cols <= rows) & (keep > 0.5), scores, -1e30)
    raised = jnp.exp(masked - jnp.max(masked, axis=-1, keepdims=True))
    return raised / jnp.sum(raised, axis=-1, keepdims=True)

def head_group(n_batch, own_rows):
    return min(4, HD // own_rows)


class HeadGroup:
    def __init__(self, place, own_rows):
        self.size = head_group(place.n, own_rows)
        self.count = place.n // self.size
        if self.size == 2:
            self.me = place.inner
            self.others = [(1 - place.inner, (place.b, place.near))]
        else:
            self.me = place.c
            ranks = [place.far, place.near, lax.rem(place.near + 2, 4)]
            self.others = [(rank, (place.b, rank)) for rank in ranks]

    def blocks(self, member):
        return pl.ds(member * self.count, self.count)

    def head(self, rank, local, heads):
        if self.size == 2:
            return 2 * (heads * (rank % 2) + local) + rank // 2
        return heads * rank + local


def front_kernel(
    n_batch,
    heads,
    proj_ref,
    gain_ref,
    up_ref,
    out_ref,
    gu_ref,
    down_ref,
    tokens_ref,
    cot_ref,
    cos_ref,
    sin_ref,
    keep_ref,
    valid_ref,
    hidden,
    mlp_in,
    gains,
    latents,
    packed_out,
    up_out,
    out_out,
    gu_all,
    down_all,
    qkv_out,
    turned_out,
    mixed_out,
    rows_out,
    cot_all,
    packed_v,
    flat_v,
    gu_v,
    half_v,
    out_v,
    up_v,
    tokens_v,
    rows_v,
    down_v,
    cot_v,
    qkv_v,
    turned_v,
    mixed_v,
    part_v,
    near_got,
    far_got,
    send_sems,
    recv_sems,
):
    place = Place(n_batch)
    copies = Copies(send_sems, recv_sems)
    b, c, n = place.b, place.c, n_batch
    own_rows = proj_ref.shape[0]
    gain_rows = up_ref.shape[0]
    out_rows = out_ref.shape[0]
    n_tok, width = tokens_ref.shape
    micro, pos_dev = qkv_v.shape[1:3]
    length = 4 * pos_dev
    in_cols = qkv_v.shape[3]
    latent = in_cols - 2 * HD
    ff = gu_v.shape[3]
    score_scale = 1.0 / math.sqrt(HD)
    group = HeadGroup(place, out_rows)
    peers = [(lax.rem(b + k, n), c) for k in range(1, n)]
    ctx_peers = [(b, place.far), (b, place.near), (b, lax.rem(place.near + 2, 4))]
    far_device, near_device = ctx_peers[0], ctx_peers[1]

    barrier = greet(place, peers + ctx_peers)
    own_packed = [
        copies.local(proj_ref, packed_v.at[b, c, :, pl.ds(0, in_cols)]),
        copies.local(gain_ref, packed_v.at[b, c, :, pl.ds(in_cols, 128)]),
    ]
    own_out = copies.local(out_ref, half_v.at[b])
    own_tokens = copies.local(tokens_ref, tokens_v)
    own_flat = copies.local(gu_ref, flat_v)
    own_down = copies.local(down_ref, down_v)
    own_cot = copies.local(cot_ref, cot_v)

    def up_cols(rank, local):
        start = pl.multiple_of(group.head(rank, local, heads) * HD, HD)
        return up_ref.at[:, pl.ds(start, HD)]

    own_up = [
        copies.local(up_cols(c, local), up_v.at[b, c, :, pl.ds(local * HD, HD)])
        for local in range(heads)
    ]
    pl.semaphore_wait(barrier, n + 2)
    up_copies = [
        copies.remote(up_cols(peer[1], local), up_v.at[b, c, :, pl.ds(local * HD, HD)], peer)
        for peer in ctx_peers
        for local in range(heads)
    ]
    for copy in own_packed:
        copies.arrive(copy)
    packed_ring = RingGather(place, copies, own_rows, lambda rank, rows: packed_v.at[rank, c, rows])
    up_ring = RingGather(place, copies, gain_rows, lambda rank, rows: up_v.at[rank, :, rows])
    out_ring = RingGather(place, copies, out_rows, lambda rank, rows: half_v.at[rank, rows])
    cot_ring = RingGather(place, copies, n_tok, lambda rank, rows: cot_all.at[rank, rows])
    packed_far = []

    def packed_step():
        packed_ring.advance()
        ranks = packed_ring.arrived() if packed_ring.step > 1 else [b]
        for rank in ranks:
            block = packed_v.at[rank, c]
            packed_far.append(copies.remote(block, block, far_device))

    packed_step()
    copies.arrive(own_down)
    copies.local(down_v, down_all.at[c])
    down_far = copies.remote(down_v, down_all.at[c], far_device)
    copies.remote(down_v, down_all.at[c], near_device)
    copies.arrive(own_flat)
    for slab_at in range(n):
        for kind in (0, 1):
            start = (kind * n + slab_at) * ff
            gu_v[slab_at, kind] = flat_v[:, start : start + ff]
    own_gu = copies.local(gu_v.at[b], gu_all.at[:, b, c])
    gu_copies = []
    gu_far = []
    waiting = []

    def send_gu(count):
        for _ in range(count):
            k = len(gu_copies) + 1
            if k < n:
                peer = peers[k - 1]
                copy = copies.remote(gu_v.at[peer[0]], gu_all.at[:, b, c], peer)
                gu_copies.append(copy)
                waiting.append((lax.rem(b - k + n, n), copy))

    def forward_gu(count):
        for _ in range(min(count, len(waiting))):
            rank, copy = waiting.pop(0)
            copies.arrive(copy)
            block = gu_all.at[:, rank, c]
            gu_far.append(copies.remote(block, block, far_device))

    for copy in own_up + up_copies:
        copies.arrive(copy)
    up_ring.advance()
    packed_step()
    send_gu(n // 2)
    copies.arrive(own_out)
    out_ring.advance()
    up_ring.advance()
    while packed_ring.step <= place.h:
        packed_step()
        up_ring.advance()
    mine = packed_v.at[:, c]
    packed_near = [copies.remote(mine, mine, near_device)]
    while up_ring.step <= place.h:
        up_ring.advance()
    copies.arrive(own_gu)
    gu_far.append(copies.remote(gu_all.at[:, b, c], gu_all.at[:, b, c], far_device))
    send_gu(n)
    out_ring.advance()
    forward_gu(2)
    for copy in packed_far:
        copies.arrive(copy)
    theirs = packed_v.at[:, place.far]
    packed_near.append(copies.remote(theirs, theirs, near_device))

    copies.arrive(own_tokens)
    own_at = pl.ds(pl.multiple_of(c * pos_dev, pos_dev), pos_dev)
    cos_own = jnp.concatenate([cos_ref[own_at, :]] * micro, axis=0)
    sin_own = jnp.concatenate([sin_ref[own_at, :]] * micro, axis=0)
    residual = tokens_v[...].astype(F32)
    normed = residual * rms_scale(residual)
    for copy in packed_near:
        copies.arrive(copy)
    extra = packed_v[:, :, :, in_cols:].astype(F32)
    gain_wide = jnp.transpose(extra.reshape(width, 128))
    gain_query = jnp.transpose(extra[:, :, :gain_rows].reshape(latent, 128))[2:3]
    gains[0:2, :] = gain_wide[0:2]
    gains[2:3, :latent] = gain_query
    attn_in = (normed * gain_wide[0:1]).astype(BF)
    rows_v[...] = attn_in
    tile = 512
    for start in range(0, in_cols, tile):
        weights = packed_v[:, :, :, start : start + tile].reshape(width, tile)
        part = dot(attn_in, weights)
        if start + tile <= latent:
            latents[:, start : start + tile] = part
        else:
            front, back = turn(part[:, :HD], cos_own, sin_own)
            half = HD // 2
            qkv_v[c, :, :, latent : latent + half] = (
                front.astype(BF).reshape(micro, pos_dev, half)
            )
            qkv_v[c, :, :, latent + half : latent + HD] = (
                back.astype(BF).reshape(micro, pos_dev, half)
            )
            qkv_v[c, :, :, latent + HD :] = part[:, HD:].astype(BF).reshape(micro, pos_dev, HD)
    q_latent = latents[...]
    q_normed = q_latent * rms_scale(q_latent) * gain_query
    qkv_v[c, :, :, :latent] = q_normed.astype(BF).reshape(micro, pos_dev, latent)
    qkv = CtxGather(place, copies, qkv_v)
    for item in range(micro):
        qkv.start(item)
    copies.local(rows_v, rows_out)
    copies.arrive(own_cot)
    cot_v[...] = (cot_v[...].astype(F32) * valid_ref[...]).astype(BF)
    copies.arrive(copies.local(cot_v, cot_all.at[b]))
    cot_ring.advance()
    for item in range(micro):
        qkv.cross(item)
    if out_ring.step < place.h:
        out_ring.advance()
    forward_gu(n // 2)
    cosine, sine = cos_ref[...], sin_ref[...]
    for item in range(micro):
        qkv.finish(item)
        q_all = qkv_v[:, item, :, :latent].reshape(length, latent)
        keys = qkv_v[:, item, :, latent : latent + HD].reshape(length, HD)
        values = qkv_v[:, item, :, latent + HD :].reshape(length, HD)
        keep = keep_ref[item]

        @pl.loop(0, heads)
        def _(head):
            base = pl.multiple_of(head * HD, HD)
            cols = pl.ds(base, HD)
            up = up_v[:, :, :, cols].reshape(latent, HD)
            front, back = turn(dot(q_all, up), cosine, sine)
            turned_v[item, :, pl.ds(base, HD // 2)] = front.astype(BF)
            upper = pl.multiple_of(base + HD // 2, HD // 2)
            turned_v[item, :, pl.ds(upper, HD // 2)] = back.astype(BF)
            weights = softmax_rows(turned_v[item, :, cols], keys, keep, score_scale)
            mixed = dot(weights.astype(BF), values).astype(BF)
            mixed_v[:, item, :, cols] = mixed.reshape(4, pos_dev, HD)

        if out_ring.step < place.h:
            out_ring.advance()
    while out_ring.step < place.h:
        out_ring.advance()

    cot_ring.advance()
    while out_ring.step <= place.h:
        out_ring.advance()
    out_swaps = [
        copies.remote(half_v.at[group.blocks(member)], out_v.at[:, group.me], device)
        for member, device in group.others
    ]
    out_swaps.append(copies.local(half_v.at[group.blocks(group.me)], out_v.at[:, group.me]))
    forward_gu(n)
    for copy in out_swaps:
        copies.arrive(copy)
    copies.arrive(down_far)
    copies.remote(down_all.at[place.far], down_all.at[place.far], near_device)
    attended_sum = CtxCollect(place, copies, part_v, near_got, far_got)
    for item in range(micro):
        mixed = mixed_v[:, item].reshape(length, heads * HD)

        @pl.loop(0, width // 512)
        def _(t):
            cols = pl.ds(pl.multiple_of(t * 512, 512), 512)
            weights = out_v[:, :, :, cols].reshape(heads * HD, 512)
            part = dot(mixed, weights).astype(BF)
            part_v[:, item, :, cols] = part.reshape(4, pos_dev, 512)

        attended_sum.start(item)
        if item > 0:
            attended_sum.cross(item - 1)
    cot_ring.advance()
    attended_sum.cross(micro - 1)
    copies.local(packed_v, packed_out)
    copies.local(up_v, up_out)
    copies.local(out_v, out_out)
    copies.local(qkv_v, qkv_out)
    copies.local(turned_v, turned_out)
    copies.local(mixed_v, mixed_out)
    for item in range(micro):
        at = slice(item * pos_dev, (item + 1) * pos_dev)
        total = tokens_v[at, :].astype(F32) + attended_sum.finish(item)
        hidden[at, :] = total
        mlp_in[at, :] = (total * rms_scale(total) * gains[1:2, :]).astype(BF)
    mine = gu_all.at[:, :, c]
    copies.remote(mine, mine, near_device)
    while cot_ring.step <= place.h:
        cot_ring.advance()
    for copy in gu_far:
        copies.arrive(copy)
    theirs = gu_all.at[:, :, place.far]
    copies.remote(theirs, theirs, near_device)
    copies.drain()


def front(n_batch, heads, proj_in, gain_cols, query_up, proj_out, gate_up, down, tokens, cots, tables):
    own_rows, in_cols = proj_in.shape
    packed_cols = in_cols + 128
    latent = in_cols - 2 * HD
    gain_rows = query_up.shape[0]
    out_rows, width = proj_out.shape
    n_tok = cots.shape[0]
    pos_dev = tables[0].shape[0] // 4
    micro = n_tok // pos_dev
    ff = gate_up.shape[1] // (2 * n_batch)
    size = head_group(n_batch, out_rows)
    head_cols = heads * HD
    shapes = {
        "packed": (n_batch, 4, own_rows, packed_cols),
        "up": (n_batch, 4, gain_rows, head_cols),
        "out": (n_batch // size, size, out_rows, width),
        "gu": (2, n_batch, 4, own_rows, ff),
        "down": (4,) + down.shape,
        "qkv": (4, micro, pos_dev, in_cols),
        "turned": (micro, 4 * pos_dev, head_cols),
        "mixed": (4, micro, pos_dev, head_cols),
        "rows": (n_tok, width),
        "cot": (n_batch, n_tok, width),
    }
    anywhere = pl.BlockSpec(memory_space=pl.ANY)
    near = pl.BlockSpec(memory_space=pltpu.VMEM)
    sems = 13 * n_batch + 100
    return pl.pallas_call(
        functools.partial(front_kernel, n_batch, heads),
        out_shape=(
            jax.ShapeDtypeStruct((n_tok, width), F32),
            jax.ShapeDtypeStruct((n_tok, width), BF),
            jax.ShapeDtypeStruct((8, width), F32),
            jax.ShapeDtypeStruct((n_tok, latent), F32),
        )
        + tuple(jax.ShapeDtypeStruct(shape, BF) for shape in shapes.values()),
        in_specs=[anywhere] * 8 + [near] * 4,
        out_specs=[near] * 4 + [anywhere] * len(shapes),
        scratch_shapes=[
            pltpu.VMEM(shapes["packed"], BF),
            pltpu.VMEM(gate_up.shape, BF),
            pltpu.VMEM((n_batch, 2, own_rows, ff), BF),
            pltpu.VMEM((n_batch, out_rows, width), BF),
            pltpu.VMEM(shapes["out"], BF),
            pltpu.VMEM(shapes["up"], BF),
            pltpu.VMEM((n_tok, width), BF),
            pltpu.VMEM((n_tok, width), BF),
            pltpu.VMEM(down.shape, BF),
            pltpu.VMEM((n_tok, width), BF),
            pltpu.VMEM(shapes["qkv"], BF),
            pltpu.VMEM(shapes["turned"], BF),
            pltpu.VMEM(shapes["mixed"], BF),
            pltpu.VMEM((4, micro, pos_dev, width), BF),
            pltpu.VMEM((2, micro, pos_dev, width), BF),
            pltpu.VMEM((micro, pos_dev, width), BF),
            pltpu.SemaphoreType.DMA((sems,)),
            pltpu.SemaphoreType.DMA((sems,)),
        ],
        compiler_params=pltpu.CompilerParams(
            collective_id=0, has_side_effects=True, vmem_limit_bytes=56 * 1024 * 1024
        ),
        name="front",
    )(proj_in, gain_cols, query_up, proj_out, gate_up, down, tokens, cots, *tables)


def attention_back_kernel(
    n_batch,
    heads,
    has_terms,
    grad_ref,
    qkv_ref,
    turned_ref,
    mixed_ref,
    up_ref,
    out_ref,
    gu_ref,
    down_ref,
    rows_ref,
    *refs,
):
    terms_ref, cot_ref, refs = (refs[0], refs[1], refs[2:]) if has_terms else (None, None, refs)
    (
        cos_ref,
        sin_ref,
        keep_ref,
        back_out,
        out_terms,
        up_terms,
        gu_grad,
        down_grad,
        rows_all,
    ) = refs[:9]
    terms_sum, refs = (refs[9], refs[10:]) if has_terms else (None, refs[9:])
    (
        grad_v,
        qkv_v,
        turned_v,
        mixed_v,
        up_v,
        out_v,
        qgrad_v,
        kgrad_v,
        vgrad_v,
        part_v,
        near_got,
        far_got,
        outgrad_v,
        upgrad_v,
        down_v,
        gu_v,
        rows_v,
        send_sems,
        recv_sems,
        load_sems,
    ) = refs[:20]
    place = Place(n_batch)
    copies = Copies(send_sems, recv_sems)
    b, c, n = place.b, place.c, n_batch
    micro, pos_dev, width = grad_ref.shape
    length = 4 * pos_dev
    head_cols = heads * HD
    latent = qkv_ref.shape[3] - 2 * HD
    score_scale = 1.0 / math.sqrt(HD)
    pairs = [
        (grad_ref, grad_v.at[c]),
        (out_ref, out_v),
        (qkv_ref, qkv_v),
        (turned_ref, turned_v),
        (up_ref, up_v),
        (mixed_ref, mixed_v),
    ]
    if has_terms:
        (
            terms_v,
            terms_got,
            ring_send,
            ring_recv,
            act_v,
            cot_v,
            down_all,
            down_got,
        ) = refs[20:]
        pairs += [(terms_ref, terms_v), (down_ref, act_v)]
        n_tok = terms_v.shape[1]
        spots = [(0, 0, 0), (place.h, 0, 1)]
        spots += [
            (side * step, step, (side + 1) // 2) for step in range(1, place.h) for side in (-1, 1)
        ]
        pairs += [
            (cot_ref.at[place.rank_of(step)], cot_v.at[pair, pl.ds(side * n_tok, n_tok)])
            for step, pair, side in spots
        ]
    loads = [
        pltpu.make_async_copy(source, target, load_sems.at[i])
        for i, (source, target) in enumerate(pairs)
    ]
    for copy in loads:
        copy.start()
    peers = [(lax.rem(b + k, n), c) for k in range(1, n)]
    others = peers + [(b, place.far), (b, place.near), (b, lax.rem(place.near + 2, 4))]
    pl.semaphore_wait(greet(place, others), n + 2)
    out_rows = out_terms.shape[1]
    group = HeadGroup(place, out_rows)
    loads[0].wait()
    grads = CtxGather(place, copies, grad_v)
    for item in range(micro):
        grads.start(item)
    steps = []
    if has_terms:

        def spot(step):
            return 0 if step == 0 else 1 if step == place.h else 2 * abs(step) + (step > 0)

        terms = RingCollect(
            place, lambda step: terms_v.at[spot(step)], terms_got, ring_send, ring_recv
        )
        loads[6].wait()
        steps = [terms.advance] * place.h

    def ring_step():
        if steps:
            steps.pop()()

    ring_step()
    own_gu = copies.local(gu_ref.at[b], gu_v)
    own_rows = copies.local(rows_ref, rows_v.at[c, 0])
    for peer in peers:
        copies.remote(gu_ref.at[peer[0]], gu_grad.at[b], peer)
    for item in range(micro):
        grads.cross(item)
    outer, inner = place.outer, place.inner
    if has_terms:
        for copy in loads[7:]:
            copy.wait()
        n_rows = cot_v.shape[0] * cot_v.shape[1]
        ff = act_v.shape[2]

        @pl.loop(0, width // 512)
        def _(t):
            cols = pl.ds(pl.multiple_of(t * 512, 512), 512)
            term = dot_left_t(
                act_v[...].reshape(n_rows, ff), cot_v[:, :, cols].reshape(n_rows, 512)
            )
            down_all[:, :, cols] = term.astype(BF).reshape(4, ff // 4, 512)

        down_near = [
            copies.remote(down_all.at[2 * side + 1 - inner], down_got.at[side], (b, place.near))
            for side in (0, 1)
        ]
    else:
        down_own = copies.local(down_ref.at[outer], down_v.at[0])
        down_far = copies.remote(down_ref.at[1 - outer], down_v.at[1], (b, place.far))
    for copy in loads[1:6]:
        copy.wait()
    if has_terms:
        for copy in down_near:
            copies.arrive(copy)
        other = down_all.at[2 * (1 - outer) + inner]
        other[...] = (other[...].astype(F32) + down_got[1 - outer].astype(F32)).astype(BF)
        down_far = copies.remote(other, down_v.at[1], (b, place.far))
    copies.arrive(own_rows)
    rows = CtxGather(place, copies, rows_v)
    rows.start(0)
    back_sum = CtxCollect(place, copies, part_v, near_got, far_got)
    cosine, sine = cos_ref[...], sin_ref[...]
    for item in range(micro):
        grads.finish(item)
        incoming = grad_v[:, item].reshape(length, width)
        keys = qkv_v[:, item, :, latent : latent + HD].reshape(length, HD)
        values = qkv_v[:, item, :, latent + HD :].reshape(length, HD)
        keep = keep_ref[item]
        kgrad_v[...] = jnp.zeros_like(kgrad_v)
        vgrad_v[...] = jnp.zeros_like(vgrad_v)

        @pl.loop(0, heads)
        def _(head):
            cols = pl.ds(pl.multiple_of(head * HD, HD), HD)
            grad_mixed = dot_right_t(incoming, out_v[head]).astype(BF)
            queries = turned_v[item, :, cols]
            weights = softmax_rows(queries, keys, keep, score_scale)
            grad_probs = dot_right_t(grad_mixed, values)
            row_dot = jnp.sum(weights * grad_probs, axis=-1, keepdims=True)
            grad_scores = (weights * (grad_probs - row_dot)).astype(BF)
            front, back = turn(dot(grad_scores, keys) * score_scale, cosine, -sine)
            front, back = front.astype(BF), back.astype(BF)
            base = pl.multiple_of(head * HD, HD)
            qgrad_v[:, item, :, pl.ds(base, HD // 2)] = front.reshape(4, pos_dev, HD // 2)
            base = pl.multiple_of(head * HD + HD // 2, HD // 2)
            qgrad_v[:, item, :, pl.ds(base, HD // 2)] = back.reshape(4, pos_dev, HD // 2)
            kgrad_v[...] += dot_left_t(grad_scores, queries) * score_scale
            vgrad_v[...] += dot_left_t(weights.astype(BF), grad_mixed)

        ring_step()
        qgrad = qgrad_v[:, item].reshape(length, head_cols)
        part_v[:, item, :, :latent] = (
            dot_right_t(qgrad, up_v[...]).astype(BF).reshape(4, pos_dev, latent)
        )
        part_v[:, item, :, latent : latent + HD] = (
            kgrad_v[...].astype(BF).reshape(4, pos_dev, HD)
        )
        part_v[:, item, :, latent + HD :] = vgrad_v[...].astype(BF).reshape(4, pos_dev, HD)
        back_sum.start(item)
        if item > 0:
            back_sum.cross(item - 1)
    n_all = 4 * micro * pos_dev
    back_sum.cross(micro - 1)
    ring_step()

    @pl.loop(0, width // 512)
    def _(t):
        cols = pl.ds(pl.multiple_of(t * 512, 512), 512)
        term = dot_left_t(
            mixed_v[...].reshape(n_all, head_cols), grad_v[:, :, :, cols].reshape(n_all, 512)
        )
        outgrad_v[:, :, :, cols] = term.astype(BF).reshape(group.count, group.size, out_rows, 512)

    mine = out_terms.at[group.blocks(group.me)]
    copies.local(outgrad_v.at[:, group.me], mine)
    for member, device in group.others:
        copies.remote(outgrad_v.at[:, member], mine, device)
    for item in range(micro):
        back_out[item] = back_sum.finish(item)
    ring_step()

    @pl.loop(0, head_cols // HD)
    def _(t):
        cols = pl.ds(pl.multiple_of(t * HD, HD), HD)
        term = dot_left_t(
            qkv_v[:, :, :, :latent].reshape(n_all, latent),
            qgrad_v[:, :, :, cols].reshape(n_all, HD),
        )
        upgrad_v[:, :, cols] = term.astype(BF).reshape(n, latent // n, HD)

    copies.local(upgrad_v, up_terms)
    rows.cross(0)
    rows.finish(0)
    copies.local(rows_v, rows_all)
    copies.arrive(own_gu)
    copies.local(gu_v, gu_grad.at[b])
    copies.arrive(down_far)
    if has_terms:
        down_grad[...] = (
            down_all[2 * outer + inner].astype(F32)
            + down_got[outer].astype(F32)
            + down_v[1].astype(F32)
        )
    else:
        copies.arrive(down_own)
        down_grad[...] = down_v[0].astype(F32) + down_v[1].astype(F32)
    if has_terms:
        while steps:
            ring_step()
        cut = terms.cut
        for half in (0, 1):
            terms_sum[half * cut : (half + 1) * cut, :] = terms.finish(half)
        terms.drain()
    copies.drain()


def attention_back(
    n_batch, grad_att, qkv_all, turned, mixed, own_qup, own_out, grad_gu, down_part, attn_in, terms, cots, tables
):
    micro, pos_dev, width = grad_att.shape
    n_tok = micro * pos_dev
    qkv_cols = qkv_all.shape[3]
    latent, head_cols = own_qup.shape
    own_out = own_out.reshape(head_cols // HD, HD, width)
    length = 4 * pos_dev
    far = n_batch // 2
    has_terms = terms is not None
    down_rows = down_part.shape[2] // 4 if has_terms else down_part.shape[1]
    size = head_group(n_batch, head_cols // n_batch)
    sems = 2 * n_batch + 48
    anywhere = pl.BlockSpec(memory_space=pl.ANY)
    near = pl.BlockSpec(memory_space=pltpu.VMEM)
    out_shape = [
        jax.ShapeDtypeStruct((micro, pos_dev, qkv_cols), F32),
        jax.ShapeDtypeStruct((n_batch, head_cols // n_batch, width), BF),
        jax.ShapeDtypeStruct((n_batch, latent // n_batch, head_cols), BF),
        jax.ShapeDtypeStruct(grad_gu.shape, BF),
        jax.ShapeDtypeStruct((down_rows, width), F32),
        jax.ShapeDtypeStruct((4, 1) + attn_in.shape, BF),
    ]
    out_specs = [near] + [anywhere] * 3 + [near, anywhere]
    scratch = [
        pltpu.VMEM((4, micro, pos_dev, width), BF),
        pltpu.VMEM((4, micro, pos_dev, qkv_cols), BF),
        pltpu.VMEM((micro, length, head_cols), BF),
        pltpu.VMEM((4, micro, pos_dev, head_cols), BF),
        pltpu.VMEM((latent, head_cols), BF),
        pltpu.VMEM((head_cols // HD, HD, width), BF),
        pltpu.VMEM((4, micro, pos_dev, head_cols), BF),
        pltpu.VMEM((length, HD), F32),
        pltpu.VMEM((length, HD), F32),
        pltpu.VMEM((4, micro, pos_dev, qkv_cols), BF),
        pltpu.VMEM((2, micro, pos_dev, qkv_cols), BF),
        pltpu.VMEM((micro, pos_dev, qkv_cols), BF),
        pltpu.VMEM((n_batch // size, size, head_cols // n_batch, width), BF),
        pltpu.VMEM((n_batch, latent // n_batch, head_cols), BF),
        pltpu.VMEM((2, down_rows, width), BF),
        pltpu.VMEM(grad_gu.shape[1:], BF),
        pltpu.VMEM((4, 1) + attn_in.shape, BF),
        pltpu.SemaphoreType.DMA((sems,)),
        pltpu.SemaphoreType.DMA((sems,)),
        pltpu.SemaphoreType.DMA((8 + n_batch,)),
    ]
    args = [grad_att, qkv_all, turned, mixed, own_qup, own_out, grad_gu, down_part, attn_in]
    if has_terms:
        args += [terms, cots]
        out_shape.append(jax.ShapeDtypeStruct((n_tok, width), F32))
        out_specs.append(near)
        scratch += [
            pltpu.VMEM(terms.shape, BF),
            pltpu.VMEM((far, 2, 2, n_tok // 2, width), BF),
            pltpu.SemaphoreType.DMA((far, 2, 2)),
            pltpu.SemaphoreType.DMA((far, 2, 2)),
            pltpu.VMEM(down_part.shape, BF),
            pltpu.VMEM((far, 2 * n_tok, width), BF),
            pltpu.VMEM((4, down_rows, width), BF),
            pltpu.VMEM((2, down_rows, width), BF),
        ]
    return pl.pallas_call(
        functools.partial(attention_back_kernel, n_batch, head_cols // HD, has_terms),
        out_shape=tuple(out_shape),
        in_specs=[anywhere] * len(args) + [near] * 3,
        out_specs=out_specs,
        scratch_shapes=scratch,
        compiler_params=pltpu.CompilerParams(
            collective_id=4, has_side_effects=True, vmem_limit_bytes=56 * 1024 * 1024
        ),
        name="attention_back",
    )(*args, *tables)


def permuted_mlp(ring, rows_own, cots, gu_rows, own_down):
    mlp_in = ring.spread(rows_own)
    n_tok, width = rows_own.shape
    _, n_batch, n_ctx, own_rows, ff = gu_rows.shape
    own_gate, own_up = gu_rows.reshape(2, width, ff)
    own_down = own_down.reshape(ff, width)
    far = ring.h
    groups = [[0]] + [[-step, step] for step in range(1, far)] + [[far]]
    out_terms = {}
    in_terms = {}
    kept = []
    for group in groups:
        rows = jnp.concatenate([mlp_in[step] for step in group], axis=0)
        grad_rows = jnp.concatenate([pick(cots, ring.rank_of(step)) for step in group], axis=0)
        gate_part = dot(rows, own_gate)
        up_part = dot(rows, own_up)
        sigmoid_gate = jax.nn.sigmoid(gate_part)
        silu_gate = gate_part * sigmoid_gate
        activated = (silu_gate * up_part).astype(BF)
        grad_act = dot_right_t(grad_rows, own_down)
        grad_gate = (
            grad_act * up_part * (sigmoid_gate * (1.0 + gate_part * (1.0 - sigmoid_gate)))
        ).astype(BF)
        grad_up = (grad_act * silu_gate).astype(BF)
        in_term = dot_right_t(grad_gate, own_gate) + dot_right_t(grad_up, own_up)
        out_term = dot(activated, own_down)
        for place_in, step in enumerate(group):
            cut = slice(place_in * n_tok, (place_in + 1) * n_tok)
            in_terms[step] = in_term[cut]
            out_terms[step] = out_term[cut]
        kept.append((rows, grad_rows, activated, grad_gate, grad_up))
    rows, grad_rows, activated, grad_gate, grad_up = (
        jnp.concatenate(items, axis=0) for items in zip(*kept)
    )
    grad_gu = jnp.stack([dot_left_t(rows, grad_gate), dot_left_t(rows, grad_up)])
    grad_gu = grad_gu.reshape(2, n_batch, n_ctx, own_rows, ff).transpose(2, 1, 0, 3, 4)
    grad_down = dot_left_t(activated, grad_rows)
    return (
        ring.collect(lambda step: in_terms[step]),
        near_collect(grad_down.reshape(n_ctx, ff // n_ctx, width)).astype(BF),
        out_terms,
        ctx_collect(grad_gu).astype(BF),
    )


def shards(
    tokens,
    cotangent,
    lengths,
    slot_sequence,
    proj_in,
    query_up,
    proj_out,
    attn_gain,
    query_gain,
    mlp_gain,
    gate_up,
    down_proj,
):
    n_ctx = lax.axis_size("ctx")
    n_batch = lax.axis_size("batch")
    ctx_rank = lax.axis_index("ctx")
    batch_rank = lax.axis_index("batch")
    ring = Ring()
    micro, pos_dev, width = tokens.shape
    n_tok = micro * pos_dev
    full_length = pos_dev * n_ctx
    heads = H // n_ctx
    score_scale = 1.0 / math.sqrt(HD)
    in_cols = proj_in.shape[1]

    slot_total = lengths.shape[0]
    slot_ids = jnp.arange(slot_total, dtype=jnp.int32)
    seq_lengths = jnp.sum(
        jnp.where(slot_sequence[:, None] == slot_ids[None, :], lengths[None, :], 0), axis=1
    )
    own_lengths = lax.dynamic_slice_in_dim(seq_lengths, batch_rank * micro, micro)
    query_pos = ctx_rank * pos_dev + jnp.arange(pos_dev, dtype=jnp.int32)
    key_pos = jnp.arange(full_length, dtype=jnp.int32)
    cos_all, sin_all = rope_tables(full_length)

    own_rows = proj_in.shape[0]
    gain_rows = query_gain.shape[0]
    gains = jnp.stack(
        [attn_gain, mlp_gain, jnp.pad(query_gain, (0, own_rows - gain_rows))], axis=1
    )
    gain_cols = jnp.pad(gains, ((0, 0), (0, 125)))
    valid_rows = (query_pos[None, :] < own_lengths[:, None]).astype(F32).reshape(n_tok, 1)
    keep = (key_pos[None, None, :] < own_lengths[:, None, None]).astype(F32)
    (
        hidden_res,
        mlp_in,
        gains,
        q_latent,
        packed,
        own_qup,
        own_out,
        gu_rows,
        own_down,
        qkv_all,
        turned,
        mixed,
        attn_in,
        cots,
    ) = front(
        n_batch,
        heads,
        proj_in,
        gain_cols,
        query_up,
        proj_out,
        gate_up,
        down_proj,
        tokens.reshape(n_tok, width),
        cotangent.reshape(n_tok, width),
        (cos_all, sin_all, keep, valid_rows),
    )
    own_qup = own_qup.reshape(QR, heads * HD)

    resident = 10 * n_batch * n_tok * width <= 24 * 1024 * 1024
    if resident:
        grad_hidden, grad_att, gain_mlp_term, down_part, terms, grad_gu_own = fused_mlp(
            n_batch, mlp_in, cots, hidden_res, gains, gu_rows, own_down
        )
        terms = terms.reshape(n_batch, n_tok, width)
    else:
        terms = None
        scale_two = rms_scale(hidden_res)
        normed_two = hidden_res * scale_two
        grad_mlp_in, down_part, out_terms, grad_gu_own = permuted_mlp(
            ring, mlp_in, cots, gu_rows, own_down
        )
        gain_mlp_term = jnp.sum(grad_mlp_in * normed_two, axis=0)[None, :]
        grad_hidden = cotangent.reshape(n_tok, width).astype(F32) * valid_rows
        grad_hidden += norm_back(grad_mlp_in * gains[1], normed_two, scale_two)
        grad_att = grad_hidden.astype(BF)
    back_own, out_grads, up_grads, grad_gu_own, grad_down, attn_in_all, *sums = attention_back(
        n_batch,
        grad_att.reshape(micro, pos_dev, width),
        qkv_all,
        turned,
        mixed,
        own_qup,
        own_out,
        grad_gu_own,
        down_part,
        attn_in,
        terms,
        cots,
        (cos_all, sin_all, keep),
    )
    out_sum = sums[0] if resident else ring.collect(lambda step: out_terms[step])
    layer_out = hidden_res + out_sum
    back_own = back_own.reshape(n_tok, in_cols)
    (
        grad_proj_out,
        grad_query_up,
        grad_proj_in,
        grad_attn_gain,
        grad_query_gain,
        grad_mlp_gain,
        grad_gate_up,
        grad_tokens,
    ) = collect_weights(
        n_batch,
        gain_rows,
        out_grads,
        up_grads,
        attn_in_all,
        grad_gu_own,
        packed,
        (
            back_own,
            q_latent,
            tokens.reshape(n_tok, width),
            grad_hidden,
            gains,
            gain_mlp_term,
            cos_all,
            sin_all,
        ),
    )
    return (
        layer_out.reshape(tokens.shape).astype(BF),
        grad_tokens.reshape(tokens.shape),
        grad_proj_in,
        grad_query_up,
        grad_proj_out,
        grad_attn_gain.reshape(-1),
        grad_query_gain.reshape(-1),
        grad_mlp_gain.reshape(-1),
        grad_gate_up,
        grad_down,
    )


def solution(mesh):
    rows = P(("batch", "ctx"), None)
    vector = P(("batch", "ctx"))
    acts = P("batch", "ctx", None)
    return jax.shard_map(
        shards,
        mesh=mesh,
        in_specs=(acts, acts, P(), P(), rows, rows, rows, vector, vector, vector, rows, rows),
        out_specs=(acts, acts, rows, rows, rows, vector, vector, vector, rows, rows),
        check_vma=False,
    )
```

```python
import functools
import math

import jax
import jax.numpy as jnp
import numpy as np
from jax import lax
from jax.experimental import pallas as pl
from jax.experimental.pallas import tpu as pltpu
from jax.sharding import PartitionSpec as P

H = 16
HD = 256
QR = 1024
EPSILON = 1e-06
BF = jnp.bfloat16
F32 = jnp.float32


def rms_scale(values):
    return lax.rsqrt(jnp.mean(values * values, axis=-1, keepdims=True) + EPSILON)


def rope_tables(length):
    half_size = HD // 2
    frequency = np.float32(10000.0) ** (-(np.arange(half_size, dtype=np.float32) * 2.0 / HD))
    angles = np.arange(length, dtype=np.float32)[:, None] * frequency.astype(np.float32)[None, :]
    cosine, sine = np.cos(angles), np.sin(angles)
    return jnp.asarray(cosine, F32), jnp.asarray(sine, F32)


def rotate(values, cosine_table, sine_table):
    half_size = values.shape[-1] // 2
    front_half = values[..., :half_size]
    back_half = values[..., half_size:]
    return jnp.concatenate(
        [
            front_half * cosine_table - back_half * sine_table,
            back_half * cosine_table + front_half * sine_table,
        ],
        axis=-1,
    )


def rotate_back(values, cosine_table, sine_table):
    return rotate(values, cosine_table, -sine_table)


def dot(left_side, right_side):
    return jnp.dot(left_side, right_side, preferred_element_type=F32)


def dot_right_t(left_side, right_side):
    return lax.dot_general(
        left_side, right_side, (((1,), (1,)), ((), ())), preferred_element_type=F32
    )


def dot_left_t(left_side, right_side):
    return lax.dot_general(
        left_side, right_side, (((0,), (0,)), ((), ())), preferred_element_type=F32
    )


def norm_back(grad_normed, normed, inv_rms):
    return inv_rms * (grad_normed - normed * jnp.mean(grad_normed * normed, axis=-1, keepdims=True))


def pick(array, index, axis=0):
    return lax.dynamic_index_in_dim(array, index, axis, keepdims=False)


def place(array, block, index, axis=0):
    return lax.dynamic_update_index_in_dim(array, block, index, axis)


class Ring:
    def __init__(self):
        self.n = lax.axis_size("batch")
        self.h = self.n // 2
        rank = lax.axis_index("batch")
        self.at = jnp.where(rank % 2 == 0, rank // 2, self.n - 1 - rank // 2)
        order = [2 * i for i in range(self.h)] + [2 * i + 1 for i in reversed(range(self.h))]
        self.up = [(order[i], order[(i + 1) % self.n]) for i in range(self.n)]
        self.down = [(there, here) for here, there in self.up]

    def rank_of(self, step):
        spot = (self.at + step) % self.n
        return jnp.where(spot < self.h, 2 * spot, 2 * (self.n - 1 - spot) + 1)

    def spread(self, block):
        found = {0: block}
        upward = downward = block
        for step in range(1, self.h):
            upward = lax.ppermute(upward, "batch", self.up)
            downward = lax.ppermute(downward, "batch", self.down)
            found[-step] = upward
            found[step] = downward
        cut = block.shape[0] // 2
        found[self.h] = jnp.concatenate(
            [
                lax.ppermute(upward[:cut], "batch", self.up),
                lax.ppermute(downward[cut:], "batch", self.down),
            ],
            axis=0,
        )
        return found

    def gather(self, block):
        found = self.spread(block)
        whole = jnp.zeros((self.n,) + block.shape, block.dtype)
        for step, part in found.items():
            whole = place(whole, part, self.rank_of(step))
        return whole

    def collect(self, term):
        far = term(self.h)
        cut = far.shape[0] // 2
        downward = lax.ppermute(far[:cut].astype(BF), "batch", self.down)
        upward = lax.ppermute(far[cut:].astype(BF), "batch", self.up)
        for step in range(self.h - 1, 0, -1):
            for_lower = term(-step).astype(F32)
            for_upper = term(step).astype(F32)
            if step == self.h - 1:
                for_lower = jnp.concatenate(
                    [for_lower[:cut] + downward.astype(F32), for_lower[cut:]], axis=0
                )
                for_upper = jnp.concatenate(
                    [for_upper[:cut], for_upper[cut:] + upward.astype(F32)], axis=0
                )
            else:
                for_lower = for_lower + downward.astype(F32)
                for_upper = for_upper + upward.astype(F32)
            downward = lax.ppermute(for_lower.astype(BF), "batch", self.down)
            upward = lax.ppermute(for_upper.astype(BF), "batch", self.up)
        own = term(0).astype(F32)
        return own + downward.astype(F32) + upward.astype(F32)

    def collect_rows(self, stacked):
        return self.collect(lambda step: pick(stacked, self.rank_of(step)))


FAR = [(0, 2), (1, 3), (2, 0), (3, 1)]
NEAR = [(0, 1), (1, 0), (2, 3), (3, 2)]


def ctx_place():
    rank = lax.axis_index("ctx")
    return rank // 2, rank % 2


def in_order(mine, theirs, at):
    return jnp.where(at == 0, jnp.stack([mine, theirs]), jnp.stack([theirs, mine]))


def ctx_gather(block):
    outer, inner = ctx_place()
    pair = in_order(block, lax.ppermute(block, "ctx", FAR), outer)
    whole = in_order(pair, lax.ppermute(pair, "ctx", NEAR), inner)
    whole = jnp.swapaxes(whole, 0, 1)
    return whole.reshape((4,) + block.shape)


def near_collect(stacked):
    _, inner = ctx_place()
    parts = stacked.reshape((2, 2) + stacked.shape[1:])
    got = lax.ppermute(pick(parts, 1 - inner, 1).astype(BF), "ctx", NEAR)
    return pick(parts, inner, 1).astype(F32) + got.astype(F32)


def ctx_collect(stacked):
    outer, _ = ctx_place()
    half = near_collect(stacked)
    got = lax.ppermute(pick(half, 1 - outer).astype(BF), "ctx", FAR)
    return pick(half, outer) + got.astype(F32)


def ctx_exchange(stacked):
    outer, inner = ctx_place()
    parts = stacked.reshape((2, 2) + stacked.shape[1:])
    got = lax.ppermute(pick(parts, 1 - outer), "ctx", FAR)
    parts = in_order(pick(parts, outer), got, outer)
    got = lax.ppermute(pick(parts, 1 - inner, 1), "ctx", NEAR)
    whole = in_order(pick(parts, inner, 1), got, inner)
    return jnp.swapaxes(whole, 0, 1).reshape(stacked.shape)


MESH = pl.DeviceIdType.MESH


class Place:
    def __init__(self, n_batch):
        self.n = n_batch
        self.h = n_batch // 2
        self.b = lax.axis_index("batch")
        self.c = lax.axis_index("ctx")
        self.outer = lax.div(self.c, 2)
        self.inner = lax.rem(self.c, 2)
        self.far = lax.rem(self.c + 2, 4)
        self.near = self.c + 1 - 2 * self.inner
        odd = lax.rem(self.b, 2)
        half = lax.div(self.b, 2)
        self.at = half + odd * (self.n - 1 - 2 * half)

    def rank_of(self, step):
        spot = lax.rem(self.at + step + 2 * self.n, self.n)
        back = lax.div(spot, self.h)
        return (1 - back) * 2 * spot + back * (2 * (self.n - 1 - spot) + 1)

    def up(self):
        return (self.rank_of(1), self.c)

    def down(self):
        return (self.rank_of(-1), self.c)


class Copies:
    def __init__(self, send_sems, recv_sems):
        self.send_sems = send_sems
        self.recv_sems = recv_sems
        self.count = 0
        self.open_sends = []
        self.open_recvs = []

    def remote(self, source, target, device):
        index = self.count
        self.count += 1
        copy = pltpu.make_async_remote_copy(
            src_ref=source,
            dst_ref=target,
            send_sem=self.send_sems.at[index],
            recv_sem=self.recv_sems.at[index],
            device_id=device,
            device_id_type=MESH,
        )
        copy.start()
        self.open_sends.append(copy)
        self.open_recvs.append(copy)
        return copy

    def local(self, source, target):
        index = self.count
        self.count += 1
        copy = pltpu.make_async_copy(source, target, self.recv_sems.at[index])
        copy.start()
        self.open_recvs.append(copy)
        return copy

    def arrive(self, copy):
        if any(copy is other for other in self.open_recvs):
            self.open_recvs = [other for other in self.open_recvs if other is not copy]
            if any(copy is other for other in self.open_sends):
                copy.wait_recv()
            else:
                copy.wait()

    def drain(self):
        for copy in list(self.open_recvs):
            self.arrive(copy)
        for copy in self.open_sends:
            copy.wait_send()


def greet(place, others):
    barrier = pltpu.get_barrier_semaphore()
    for device in others:
        pl.semaphore_signal(barrier, inc=1, device_id=device, device_id_type=MESH)
    return barrier


class RingGather:
    def __init__(self, place, copies, rows, slot):
        self.place, self.copies, self.rows, self.slot = place, copies, rows, slot
        self.step = 0
        self.moving = ()

    def advance(self):
        place, copies = self.place, self.copies
        for copy in self.moving:
            copies.arrive(copy)
        self.moving = ()
        self.step += 1
        cut = self.rows // 2
        if self.step > place.h:
            return
        lower = place.rank_of(1 - self.step)
        upper = place.rank_of(self.step - 1)
        if self.step < place.h:
            whole = pl.ds(0, self.rows)
            pieces = (whole, whole)
        else:
            pieces = (pl.ds(0, cut), pl.ds(cut, self.rows - cut))
        upward, downward = self.slot(lower, pieces[0]), self.slot(upper, pieces[1])
        self.moving = (
            copies.remote(upward, upward, place.up()),
            copies.remote(downward, downward, place.down()),
        )

    def arrived(self):
        step = self.step - 1
        if step == 0:
            return []
        if step == self.place.h:
            return [self.place.rank_of(step)]
        return [self.place.rank_of(-step), self.place.rank_of(step)]


def mlp_kernel(
    n_batch,
    rows_ref,
    gu_ref,
    down_ref,
    cot_ref,
    hidden_ref,
    gains_ref,
    *refs,
):
    (
        grad_ref,
        low_ref,
        gain_term,
        act_out,
        term_out,
        gu_out,
        rows_v,
        cot_v,
        gate_v,
        up_v,
        down_v,
        act_v,
        ggate_v,
        gup_v,
        in_v,
        term_v,
        got_v,
        gu_got,
        gu_last,
        send_sems,
        recv_sems,
        back_send,
        back_recv,
        load_sems,
        store_sems,
        part_send,
        part_recv,
    ) = refs
    place = Place(n_batch)
    far = place.h
    n_tok = rows_ref.shape[0]
    cut = n_tok // 2
    width = rows_ref.shape[1]
    ff = gu_ref.shape[-1]
    up_device, down_device = place.up(), place.down()
    far_device, near_device = (place.b, place.far), (place.b, place.near)
    barrier = greet(place, [up_device, down_device, far_device, near_device])
    parts = Copies(part_send, part_recv)
    own_rows = gate_v.shape[2]
    block = 4 * own_rows

    load_rows = pltpu.make_async_copy(rows_ref, rows_v.at[0, pl.ds(0, n_tok)], load_sems.at[0])
    load_rows.start()
    loads = [
        pltpu.make_async_copy(source, target, load_sems.at[1 + i])
        for i, (source, target) in enumerate(
            [(gu_ref.at[0], gate_v), (gu_ref.at[1], up_v), (down_ref, down_v)]
        )
    ]
    spots = [(0, 0, 0), (far, 0, 1)]
    spots += [(side * step, step, (side + 1) // 2) for step in range(1, far) for side in (-1, 1)]
    for i, (distance, group, side) in enumerate(spots):
        loads.append(
            pltpu.make_async_copy(
                cot_ref.at[place.rank_of(distance)], cot_v.at[group, pl.ds(side * n_tok, n_tok)], load_sems.at[4 + i]
            )
        )
    for copy in loads:
        copy.start()
    load_rows.wait()
    pl.semaphore_wait(barrier, 4)

    def piece(side, half):
        return pl.ds(side * n_tok + half * cut, cut)

    def hop(step, side, half):
        source_group, source_side = step - 1, side
        target_group, target_side = step, side
        if isinstance(step, int) and step == 1:
            source_side = 0
        if isinstance(step, int) and step == far:
            target_group, target_side = 0, 1
        return pltpu.make_async_remote_copy(
            src_ref=rows_v.at[source_group, piece(source_side, half)],
            dst_ref=rows_v.at[target_group, piece(target_side, half)],
            send_sem=send_sems.at[step, side, half],
            recv_sem=recv_sems.at[step, side, half],
            device_id=down_device if side else up_device,
            device_id_type=MESH,
        )

    both = [(side, half) for half in (0, 1) for side in (0, 1)]
    ends = [(0, 0), (1, 1)]
    for side, half in both:
        hop(1, side, half).start()
    for copy in loads:
        copy.wait()

    def stores(group):
        return [
            pltpu.make_async_copy(term_v.at[group], term_out.at[group], store_sems.at[0, group]),
            pltpu.make_async_copy(act_v.at[group], act_out.at[group], store_sems.at[1, group]),
        ]

    def compute(group):
        rows = rows_v[group]
        cots = cot_v[group]
        down_all = down_v[...].reshape(ff, width)
        start = 0
        while start < ff:
            size = min(256, ff - start)
            tile = slice(start, start + size)
            gate = dot(rows, gate_v[..., tile].reshape(width, size))
            up = dot(rows, up_v[..., tile].reshape(width, size))
            grad_act = dot_right_t(cots, down_all[tile])
            sigmoid = 1.0 / (1.0 + jnp.exp(-gate))
            silu = gate * sigmoid
            act_v[group, :, tile] = (silu * up).astype(BF)
            slope = sigmoid * (1.0 + gate * (1.0 - sigmoid))
            ggate_v[group, :, tile] = (grad_act * up * slope).astype(BF)
            gup_v[group, :, tile] = (grad_act * silu).astype(BF)
            start += size
        ggate = ggate_v[group]
        gup = gup_v[group]
        act = act_v[group]
        tile_cols = 2 * block

        @pl.loop(0, width // tile_cols)
        def _(t):
            cols = pl.ds(pl.multiple_of(t * tile_cols, tile_cols), tile_cols)
            back = dot_right_t(ggate, gate_v[pl.ds(2 * t, 2)].reshape(tile_cols, ff))
            back += dot_right_t(gup, up_v[pl.ds(2 * t, 2)].reshape(tile_cols, ff))
            in_v[group, :, cols] = back.astype(BF)
            down = down_v[:, :, cols].reshape(ff, tile_cols)
            term_v[group, :, cols] = dot(act, down).astype(BF)

        for copy in stores(group):
            copy.start()

    @pl.loop(1, far)
    def _(step):
        for side, half in both:
            hop(step, side, half).wait_recv()

            @pl.when(step < far - 1)
            def _():
                hop(step + 1, side, half).start()

            if (side, half) in ends:

                @pl.when(step == far - 1)
                def _():
                    hop(far, side, half).start()

        compute(step)

    for side, half in ends:
        hop(far, side, half).wait_recv()
    compute(0)

    def back_hop(step, side, half, source):
        return pltpu.make_async_remote_copy(
            src_ref=source,
            dst_ref=got_v.at[step, side, half],
            send_sem=back_send.at[step, side, half],
            recv_sem=back_recv.at[step, side, half],
            device_id=up_device if side else down_device,
            device_id_type=MESH,
        )

    def held(step, side, half):
        return in_v.at[step, piece(side, half)]

    for side, half in ends:
        back_hop(far - 1, side, half, held(0, 1, half)).start()

    def pass_on(step, side, half, added):
        own = held(step, side, half)
        if added:
            back_hop(step, side, half, own).wait_recv()
            own[...] = (own[...].astype(F32) + got_v[step, side, half].astype(F32)).astype(BF)
        back_hop(step - 1, side, half, own).start()

    for side, half in both:
        if (side, half) not in ends:
            pass_on(far - 1, side, half, False)

    def gate_up_terms(t):
        cols = slice(t * 2 * block, (t + 1) * 2 * block)
        rows = rows_v[:, :, cols].reshape(n_batch * n_tok, 2 * block)
        for target, grads in ((gate_v, ggate_v), (up_v, gup_v)):
            term = dot_left_t(rows, grads[...].reshape(n_batch * n_tok, ff))
            target[2 * t : 2 * t + 2] = term.astype(BF).reshape(2, 4, own_rows, ff)

    def pass_all(step):
        for side, half in [(1, 0), (0, 1), (0, 0), (1, 1)]:
            if step < far - 1 or (side, half) in ends:
                pass_on(step, side, half, True)

    steps = list(range(1, far))
    outer, inner = place.outer, place.inner
    kinds = list(enumerate((gate_v, up_v)))
    near_copies, far_copies = {}, {}

    def send_near(t):
        pair = pl.ds(2 * t, 2)
        near_copies[t] = [
            parts.remote(
                target.at[pair, 2 * side + 1 - inner], gu_got.at[kind, side, pair], near_device
            )
            for side in (0, 1)
            for kind, target in kinds
        ]

    def send_far(t):
        pair = pl.ds(2 * t, 2)
        for copy in near_copies[t]:
            parts.arrive(copy)
        far_copies[t] = []
        for kind, target in kinds:
            other = target.at[pair, 2 * (1 - outer) + inner]
            added = other[...].astype(F32) + gu_got[kind, 1 - outer, pair].astype(F32)
            other[...] = added.astype(BF)
            far_copies[t].append(parts.remote(other, gu_last.at[kind, pair], far_device))

    def take_far(t):
        pair = pl.ds(2 * t, 2)
        for copy in far_copies[t]:
            parts.arrive(copy)
        for kind, target in kinds:
            kept = target.at[pair, 2 * outer + inner]
            added = kept[...].astype(F32) + gu_got[kind, outer, pair].astype(F32)
            kept[...] = (added + gu_last[kind, pair].astype(F32)).astype(BF)
            parts.local(kept, gu_out.at[pair, kind])

    def ring_step():
        if steps:
            pass_all(steps.pop())

    tiles = width // (2 * block)
    for t in range(tiles):
        gate_up_terms(t)
        send_near(t)
        if t > 0:
            send_far(t - 1)
        ring_step()
    while steps:
        ring_step()
    send_far(tiles - 1)
    totals = []
    for half in (0, 1):
        for side in (0, 1):
            back_hop(0, side, half, held(0, 0, half)).wait_recv()
        totals.append(
            in_v[0, half * cut : (half + 1) * cut, :].astype(F32)
            + got_v[0, 0, half].astype(F32)
            + got_v[0, 1, half].astype(F32)
        )
    total = jnp.concatenate(totals, axis=0)
    hidden = hidden_ref[...]
    inverse = rms_scale(hidden)
    normed = hidden * inverse
    gain_term[...] = jnp.sum(total * normed, axis=0, keepdims=True)
    back = norm_back(total * gains_ref[1:2, :], normed, inverse)
    grad_hidden = cot_v[0, :n_tok, :].astype(F32) + back
    grad_ref[...] = grad_hidden
    low_ref[...] = grad_hidden.astype(BF)
    for t in range(tiles):
        take_far(t)
    parts.drain()

    for step in range(1, far + 1):
        for side, half in both if step < far else ends:
            hop(step, side, half).wait_send()
    for side, half in ends:
        back_hop(far - 1, side, half, held(0, 1, half)).wait_send()
    for step in range(far - 1, 0, -1):
        for side, half in both:
            back_hop(step - 1, side, half, held(step, side, half)).wait_send()
    for group in range(far):
        for copy in stores(group):
            copy.wait()


def fused_mlp(n_batch, rows, cots, hidden_res, gains, gu_rows, own_down):
    n_tok, width = rows.shape
    ff = gu_rows.shape[-1]
    own_rows = gu_rows.shape[3]
    far = n_batch // 2
    pair = 2 * n_tok
    flops = 18 * n_batch * n_tok * width * ff
    return pl.pallas_call(
        functools.partial(mlp_kernel, n_batch),
        out_shape=(
            jax.ShapeDtypeStruct((n_tok, width), F32),
            jax.ShapeDtypeStruct((n_tok, width), BF),
            jax.ShapeDtypeStruct((1, width), F32),
            jax.ShapeDtypeStruct((far, pair, ff), BF),
            jax.ShapeDtypeStruct((far, pair, width), BF),
            jax.ShapeDtypeStruct((n_batch, 2, own_rows, ff), BF),
        ),
        in_specs=[pl.BlockSpec(memory_space=pl.ANY)] * 4
        + [pl.BlockSpec(memory_space=pltpu.VMEM)] * 2,
        out_specs=[pl.BlockSpec(memory_space=pltpu.VMEM)] * 3
        + [pl.BlockSpec(memory_space=pl.ANY)] * 3,
        scratch_shapes=[
            pltpu.VMEM((far, pair, width), BF),
            pltpu.VMEM((far, pair, width), BF),
            pltpu.VMEM((n_batch, 4, own_rows, ff), BF),
            pltpu.VMEM((n_batch, 4, own_rows, ff), BF),
            pltpu.VMEM((4, ff // 4, width), BF),
            pltpu.VMEM((far, pair, ff), BF),
            pltpu.VMEM((far, pair, ff), BF),
            pltpu.VMEM((far, pair, ff), BF),
            pltpu.VMEM((far, pair, width), BF),
            pltpu.VMEM((far, pair, width), BF),
            pltpu.VMEM((far, 2, 2, n_tok // 2, width), BF),
            pltpu.VMEM((2, 2, n_batch, own_rows, ff), BF),
            pltpu.VMEM((2, n_batch, own_rows, ff), BF),
            pltpu.SemaphoreType.DMA((far + 1, 2, 2)),
            pltpu.SemaphoreType.DMA((far + 1, 2, 2)),
            pltpu.SemaphoreType.DMA((far, 2, 2)),
            pltpu.SemaphoreType.DMA((far, 2, 2)),
            pltpu.SemaphoreType.DMA((4 + n_batch,)),
            pltpu.SemaphoreType.DMA((2, far)),
            pltpu.SemaphoreType.DMA((72,)),
            pltpu.SemaphoreType.DMA((72,)),
        ],
        compiler_params=pltpu.CompilerParams(
            collective_id=1, has_side_effects=True, vmem_limit_bytes=60 * 1024 * 1024
        ),
        cost_estimate=pl.CostEstimate(
            flops=flops, bytes_accessed=24 * 1024 * 1024, transcendentals=n_batch * n_tok * ff
        ),
        name="fused_mlp",
    )(rows, gu_rows, own_down, cots, hidden_res, gains)


class RingCollect:
    def __init__(self, place, block, got, send_sems, recv_sems):
        self.place, self.block, self.got = place, block, got
        self.send_sems, self.recv_sems = send_sems, recv_sems
        self.cut = got.shape[3]
        self.step = place.h
        self.sent = []

    def held(self, step, half):
        return self.block(step).at[pl.ds(half * self.cut, self.cut)]

    def hop(self, step, side, half, source):
        place = self.place
        return pltpu.make_async_remote_copy(
            src_ref=source,
            dst_ref=self.got.at[step, side, half],
            send_sem=self.send_sems.at[step, side, half],
            recv_sem=self.recv_sems.at[step, side, half],
            device_id=place.up() if side else place.down(),
            device_id_type=MESH,
        )

    def send(self, step, side, half, source):
        copy = self.hop(step, side, half, source)
        copy.start()
        self.sent.append(copy)

    def advance(self):
        far = self.place.h
        step = self.step
        self.step -= 1
        if step == far:
            for side in (0, 1):
                self.send(far - 1, side, side, self.held(far, side))
            for side in (0, 1):
                half = 1 - side
                self.send(far - 2, side, half, self.held((2 * side - 1) * (far - 1), half))
            return
        pieces = [(0, 0), (1, 1)] if step == far - 1 else [(1, 0), (0, 1), (0, 0), (1, 1)]
        for side, half in pieces:
            own = self.held((2 * side - 1) * step, half)
            self.hop(step, side, half, own).wait_recv()
            own[...] = (own[...].astype(F32) + self.got[step, side, half].astype(F32)).astype(BF)
            self.send(step - 1, side, half, own)

    def finish(self, half):
        own = self.held(0, half)
        for side in (0, 1):
            self.hop(0, side, half, own).wait_recv()
        return (
            own[...].astype(F32)
            + self.got[0, 0, half].astype(F32)
            + self.got[0, 1, half].astype(F32)
        )

    def drain(self):
        for copy in self.sent:
            copy.wait_send()


def tail_kernel(
    n_batch,
    gain_rows,
    out_ref,
    up_ref,
    rows_ref,
    gu_ref,
    packed_ref,
    back_ref,
    latent_ref,
    tokens_ref,
    hidden_ref,
    gains_ref,
    mlp_term_ref,
    cos_ref,
    sin_ref,
    out_grad,
    up_grad,
    in_grad,
    attn_gain_grad,
    query_gain_grad,
    mlp_gain_grad,
    gu_grad,
    tokens_grad,
    out_v,
    up_v,
    in_v,
    out_got,
    up_got,
    in_got,
    up_sum,
    up_all,
    in_sum,
    in_all,
    ring_send,
    ring_recv,
    send_sems,
    recv_sems,
    packed_v,
    project_own,
    project_v,
    rows_v,
    gu_v,
    load_sems,
):
    place = Place(n_batch)
    copies = Copies(send_sems, recv_sems)
    b, c, n = place.b, place.c, n_batch
    own_rows = in_grad.shape[0]
    group = HeadGroup(place, out_grad.shape[0])
    ctx_peers = [(b, place.far), (b, place.near), (b, lax.rem(place.near + 2, 4))]

    loads = [
        pltpu.make_async_copy(held, kept, load_sems.at[i])
        for i, (held, kept) in enumerate([(out_ref, out_v), (up_ref, up_v), (rows_ref, rows_v), (gu_ref, gu_v), (packed_ref, packed_v)])
    ]
    for copy in (loads[1], loads[0], *loads[2:]):
        copy.start()
    barrier = greet(place, [place.up(), place.down()] + ctx_peers)

    pl.semaphore_wait(barrier, 5)

    rings = []
    for i, (kept, got) in enumerate([(out_v, out_got), (up_v, up_got), (in_v, in_got)]):
        rings.append(
            RingCollect(
                place,
                lambda step, kept=kept: kept.at[place.rank_of(step)],
                got,
                ring_send.at[i],
                ring_recv.at[i],
            )
        )
    for at in (1, 0):
        loads[at].wait()
        rings[at].advance()
    part_cols = project_v.shape[2]
    n_tok, width = tokens_ref.shape
    pos_dev = cos_ref.shape[0] // 4
    own_at = pl.ds(pl.multiple_of(c * pos_dev, pos_dev), pos_dev)
    cos_own = jnp.concatenate([cos_ref[own_at, :]] * (n_tok // pos_dev), axis=0)
    sin_own = jnp.concatenate([sin_ref[own_at, :]] * (n_tok // pos_dev), axis=0)
    latent = latent_ref.shape[1]

    q_latent = latent_ref[...]
    inverse = rms_scale(q_latent)
    normed_query = q_latent * inverse
    grad_qn = back_ref[:, :latent]
    query_term = jnp.sum(grad_qn * normed_query, axis=0, keepdims=True)
    grad_latent = norm_back(grad_qn * gains_ref[2:3, :latent], normed_query, inverse)
    front, back = turn(back_ref[:, latent : latent + HD], cos_own, -sin_own)
    project = jnp.concatenate(
        [grad_latent, front, back, back_ref[:, latent + HD :]], axis=1
    ).astype(BF)
    for part in range(4):
        project_own[part] = project[:, part * part_cols : (part + 1) * part_cols]
    project_copies = [
        copies.remote(project_own.at[peer[1]], project_v.at[c], peer) for peer in ctx_peers
    ]
    project_copies.append(copies.local(project_own.at[c], project_v.at[c]))
    for ring in rings[:2]:
        ring.advance()
    loads[4].wait()
    in_cols = 4 * part_cols
    residual = tokens_ref[...].astype(F32)
    inverse = rms_scale(residual)
    normed = residual * inverse
    weights = packed_v[:, :, :, :in_cols].reshape(width, in_cols)
    grad_attn_in = dot_right_t(project, weights)
    attn_term = jnp.sum(grad_attn_in * normed, axis=0, keepdims=True)
    back = norm_back(grad_attn_in * gains_ref[0:1, :], normed, inverse)
    tokens_grad[...] = (hidden_ref[...] + back).astype(BF)
    for ring in rings[:2]:
        ring.advance()
    for copy in project_copies:
        copies.arrive(copy)
    loads[2].wait()
    project_all = project_v[...].reshape(-1, part_cols)
    part_rows = own_rows + 16
    n_all = project_all.shape[0]
    ahead = max(1, 256 // (4 * own_rows))
    chunk = ahead * 4 * own_rows

    @pl.loop(0, width // chunk)
    def _(t):
        cols = pl.ds(pl.multiple_of(t * chunk, chunk), chunk)
        term = dot_left_t(rows_v[:, :, :, cols].reshape(n_all, chunk), project_all).astype(BF)
        term = term.reshape(ahead, 4, own_rows, part_cols)
        for part in range(4):
            in_v[pl.ds(t * ahead, ahead), pl.ds(part * part_rows, own_rows), :] = term[:, part]

    none = jnp.zeros((16, part_cols), BF)
    wide = jnp.concatenate([attn_term, mlp_term_ref[...], jnp.zeros((14, width), F32)], axis=0)
    short = jnp.concatenate([jnp.zeros((2, latent), F32), query_term], axis=0)
    short = jnp.concatenate([short, jnp.zeros((13, latent), F32)], axis=0)
    for rank in range(n):
        for part in range(4):
            at = pl.ds(part * part_rows + own_rows, 16)
            device = 4 * rank + part
            in_v[rank, at, :] = none
            in_v[rank, at, :own_rows] = wide[
                :, device * own_rows : (device + 1) * own_rows
            ].astype(BF)
            more = short[:, device * gain_rows : (device + 1) * gain_rows].astype(BF)
            kept = in_v[rank, at, :gain_rows]
            in_v[rank, at, :gain_rows] = kept + more
    rings[2].advance()
    if rings[0].step > 0:
        for ring in rings[:2]:
            ring.advance()
    while rings[2].step > 0:
        for ring in rings:
            if ring.step > 0:
                ring.advance()

    loads[3].wait()
    ff = gu_v.shape[3]
    for slab_at in range(n):
        for kind in (0, 1):
            start = (kind * n + slab_at) * ff
            gu_grad[:, start : start + ff] = gu_v[slab_at, kind].astype(F32)

    in_ring, up_ring, out_ring = rings[2], rings[1], rings[0]
    out_cut, up_cut, in_cut = out_ring.cut, up_ring.cut, in_ring.cut
    for half in (0, 1):
        out_grad[half * out_cut : (half + 1) * out_cut, :] = out_ring.finish(half)
    for half in (0, 1):
        up_sum[pl.ds(half * up_cut, up_cut), :] = up_ring.finish(half).astype(BF)
    up_copies = [
        copies.remote(
            up_sum.at[pl.ds(peer[1] * gain_rows, gain_rows)], up_all.at[c], peer
        )
        for peer in ctx_peers
    ]
    up_copies.append(
        copies.local(up_sum.at[pl.ds(c * gain_rows, gain_rows)], up_all.at[c])
    )
    for half in (0, 1):
        in_sum[pl.ds(half * in_cut, in_cut), :] = in_ring.finish(half).astype(BF)
    in_copies = [
        copies.remote(in_sum.at[pl.ds(peer[1] * part_rows, part_rows)], in_all.at[c], peer)
        for peer in ctx_peers
    ]
    in_copies.append(copies.local(in_sum.at[pl.ds(c * part_rows, part_rows)], in_all.at[c]))

    for copy in up_copies:
        copies.arrive(copy)
    cols = up_all.shape[2]
    heads = cols // HD
    for part in range(4):
        for local in range(heads):
            head = group.head(part, local, heads)
            up_grad[:, head * HD : (head + 1) * HD] = up_all[
                part, :, local * HD : (local + 1) * HD
            ].astype(F32)
    for copy in in_copies:
        copies.arrive(copy)
    cols = in_all.shape[2]
    gains = jnp.zeros((16, cols), F32)
    for part in range(4):
        in_grad[:, part * cols : (part + 1) * cols] = in_all[part, :own_rows, :].astype(F32)
        gains = gains + in_all[part, own_rows:, :].astype(F32)
    attn_gain_grad[...] = gains[0:1, :own_rows]
    mlp_gain_grad[...] = gains[1:2, :own_rows]
    query_gain_grad[...] = gains[2:3, :gain_rows]
    copies.drain()
    for ring in rings:
        ring.drain()


def collect_weights(n_batch, gain_rows, out_terms, up_terms, attn_in_all, grad_gu, packed, own):
    far = n_batch // 2
    out_rows, width = out_terms.shape[1:]
    up_rows, up_cols = up_terms.shape[1:]
    n_tok = own[2].shape[0]
    in_cols = own[0].shape[1] // 4
    own_rows = width // (4 * n_batch)
    in_rows = 4 * (own_rows + 16)
    shapes = [out_terms.shape[1:], up_terms.shape[1:], (in_rows, in_cols)]
    sems = 2 * n_batch + 16
    return pl.pallas_call(
        functools.partial(tail_kernel, n_batch, gain_rows),
        out_shape=(
            jax.ShapeDtypeStruct((out_rows, width), F32),
            jax.ShapeDtypeStruct((gain_rows, 4 * up_cols), F32),
            jax.ShapeDtypeStruct((own_rows, 4 * in_cols), F32),
            jax.ShapeDtypeStruct((1, own_rows), F32),
            jax.ShapeDtypeStruct((1, gain_rows), F32),
            jax.ShapeDtypeStruct((1, own_rows), F32),
            jax.ShapeDtypeStruct((own_rows, 2 * n_batch * grad_gu.shape[3]), F32),
            jax.ShapeDtypeStruct((n_tok, width), BF),
        ),
        in_specs=[pl.BlockSpec(memory_space=pl.ANY)] * 5 + [pl.BlockSpec(memory_space=pltpu.VMEM)] * len(own),
        out_specs=[pl.BlockSpec(memory_space=pltpu.VMEM)] * 8,
        scratch_shapes=[pltpu.VMEM((n_batch,) + shape, BF) for shape in shapes]
        + [pltpu.VMEM((far, 2, 2, rows // 2, cols), BF) for rows, cols in shapes]
        + [
            pltpu.VMEM((up_rows, up_cols), BF),
            pltpu.VMEM((4, gain_rows, up_cols), BF),
            pltpu.VMEM((in_rows, in_cols), BF),
            pltpu.VMEM((4, own_rows + 16, in_cols), BF),
            pltpu.SemaphoreType.DMA((3, far, 2, 2)),
            pltpu.SemaphoreType.DMA((3, far, 2, 2)),
            pltpu.SemaphoreType.DMA((sems,)),
            pltpu.SemaphoreType.DMA((sems,)),
            pltpu.VMEM(packed.shape, BF),
            pltpu.VMEM((4, n_tok, in_cols), BF),
            pltpu.VMEM((4, n_tok, in_cols), BF),
            pltpu.VMEM(attn_in_all.shape, BF),
            pltpu.VMEM(grad_gu.shape, BF),
            pltpu.SemaphoreType.DMA((5,)),
        ],
        compiler_params=pltpu.CompilerParams(
            collective_id=2, has_side_effects=True, vmem_limit_bytes=56 * 1024 * 1024
        ),
        name="collect_weights",
    )(out_terms, up_terms, attn_in_all, grad_gu, packed, *own)


class CtxCollect:
    def __init__(self, place, copies, part, near_got, far_got):
        self.place, self.copies, self.part = place, copies, part
        self.near_got, self.far_got = near_got, far_got
        self.near = {}
        self.far = {}

    def start(self, item):
        place = self.place
        self.near[item] = [
            self.copies.remote(
                self.part.at[2 * side + 1 - place.inner, item],
                self.near_got.at[side, item],
                (place.b, place.near),
            )
            for side in (0, 1)
        ]

    def cross(self, item):
        place = self.place
        for copy in self.near[item]:
            self.copies.arrive(copy)
        other = self.part.at[2 * (1 - place.outer) + place.inner, item]
        added = other[...].astype(F32) + self.near_got[1 - place.outer, item].astype(F32)
        other[...] = added.astype(BF)
        self.far[item] = self.copies.remote(
            other, self.far_got.at[item], (place.b, place.far)
        )

    def finish(self, item):
        place = self.place
        self.copies.arrive(self.far[item])
        return (
            self.part[2 * place.outer + place.inner, item].astype(F32)
            + self.near_got[place.outer, item].astype(F32)
            + self.far_got[item].astype(F32)
        )


class CtxGather:
    def __init__(self, place, copies, everyone):
        self.place, self.copies, self.everyone = place, copies, everyone
        self.far = {}
        self.near = {}

    def start(self, item):
        place = self.place
        own = self.everyone.at[place.c, item]
        self.far[item] = self.copies.remote(own, own, (place.b, place.far))
        self.near[item] = [self.copies.remote(own, own, (place.b, place.near))]

    def cross(self, item):
        place = self.place
        self.copies.arrive(self.far[item])
        other = self.everyone.at[place.far, item]
        self.near[item].append(self.copies.remote(other, other, (place.b, place.near)))

    def finish(self, item):
        for copy in self.near[item]:
            self.copies.arrive(copy)


def greet_lines(place):
    devices = [place.up(), place.down(), (place.b, place.far), (place.b, place.near)]
    pl.semaphore_wait(greet(place, devices), 4)


def turn(values, cosine, sine):
    half_size = HD // 2
    front, back = values[:, :half_size], values[:, half_size:]
    return front * cosine - back * sine, back * cosine + front * sine


def softmax_rows(queries, keys, keep, score_scale):
    scores = dot_right_t(queries, keys) * score_scale
    rows = lax.broadcasted_iota(jnp.int32, scores.shape, 0)
    cols = lax.broadcasted_iota(jnp.int32, scores.shape, 1)
    masked = jnp.where((cols <= rows) & (keep > 0.5), scores, -1e30)
    raised = jnp.exp(masked - jnp.max(masked, axis=-1, keepdims=True))
    return raised / jnp.sum(raised, axis=-1, keepdims=True)

def head_group(n_batch, own_rows):
    return min(4, HD // own_rows)


class HeadGroup:
    def __init__(self, place, own_rows):
        self.size = head_group(place.n, own_rows)
        self.count = place.n // self.size
        if self.size == 2:
            self.me = place.inner
            self.others = [(1 - place.inner, (place.b, place.near))]
        else:
            self.me = place.c
            ranks = [place.far, place.near, lax.rem(place.near + 2, 4)]
            self.others = [(rank, (place.b, rank)) for rank in ranks]

    def blocks(self, member):
        return pl.ds(member * self.count, self.count)

    def head(self, rank, local, heads):
        if self.size == 2:
            return 2 * (heads * (rank % 2) + local) + rank // 2
        return heads * rank + local


def front_kernel(
    n_batch,
    heads,
    proj_ref,
    gain_ref,
    up_ref,
    out_ref,
    gu_ref,
    down_ref,
    tokens_ref,
    cot_ref,
    cos_ref,
    sin_ref,
    keep_ref,
    valid_ref,
    hidden,
    mlp_in,
    gains,
    latents,
    packed_out,
    up_out,
    out_out,
    gu_all,
    down_all,
    qkv_out,
    turned_out,
    mixed_out,
    rows_out,
    cot_all,
    packed_v,
    flat_v,
    gu_v,
    half_v,
    out_v,
    up_v,
    tokens_v,
    rows_v,
    down_v,
    cot_v,
    qkv_v,
    turned_v,
    mixed_v,
    part_v,
    near_got,
    far_got,
    send_sems,
    recv_sems,
):
    place = Place(n_batch)
    copies = Copies(send_sems, recv_sems)
    b, c, n = place.b, place.c, n_batch
    own_rows = proj_ref.shape[0]
    gain_rows = up_ref.shape[0]
    out_rows = out_ref.shape[0]
    n_tok, width = tokens_ref.shape
    micro, pos_dev = qkv_v.shape[1:3]
    length = 4 * pos_dev
    in_cols = qkv_v.shape[3]
    latent = in_cols - 2 * HD
    ff = gu_v.shape[3]
    score_scale = 1.0 / math.sqrt(HD)
    group = HeadGroup(place, out_rows)
    peers = [(lax.rem(b + k, n), c) for k in range(1, n)]
    ctx_peers = [(b, place.far), (b, place.near), (b, lax.rem(place.near + 2, 4))]
    far_device, near_device = ctx_peers[0], ctx_peers[1]

    barrier = greet(place, peers + ctx_peers)
    own_packed = [
        copies.local(proj_ref, packed_v.at[b, c, :, pl.ds(0, in_cols)]),
        copies.local(gain_ref, packed_v.at[b, c, :, pl.ds(in_cols, 128)]),
    ]
    own_out = copies.local(out_ref, half_v.at[b])
    own_tokens = copies.local(tokens_ref, tokens_v)
    own_flat = copies.local(gu_ref, flat_v)
    own_down = copies.local(down_ref, down_v)
    own_cot = copies.local(cot_ref, cot_v)

    def up_cols(rank, local):
        start = pl.multiple_of(group.head(rank, local, heads) * HD, HD)
        return up_ref.at[:, pl.ds(start, HD)]

    own_up = [
        copies.local(up_cols(c, local), up_v.at[b, c, :, pl.ds(local * HD, HD)])
        for local in range(heads)
    ]
    pl.semaphore_wait(barrier, n + 2)
    up_copies = [
        copies.remote(up_cols(peer[1], local), up_v.at[b, c, :, pl.ds(local * HD, HD)], peer)
        for peer in ctx_peers
        for local in range(heads)
    ]
    for copy in own_packed:
        copies.arrive(copy)
    packed_ring = RingGather(place, copies, own_rows, lambda rank, rows: packed_v.at[rank, c, rows])
    up_ring = RingGather(place, copies, gain_rows, lambda rank, rows: up_v.at[rank, :, rows])
    out_ring = RingGather(place, copies, out_rows, lambda rank, rows: half_v.at[rank, rows])
    cot_ring = RingGather(place, copies, n_tok, lambda rank, rows: cot_all.at[rank, rows])
    packed_far = []

    def packed_step():
        packed_ring.advance()
        ranks = packed_ring.arrived() if packed_ring.step > 1 else [b]
        for rank in ranks:
            block = packed_v.at[rank, c]
            packed_far.append(copies.remote(block, block, far_device))

    packed_step()
    copies.arrive(own_down)
    copies.local(down_v, down_all.at[c])
    down_far = copies.remote(down_v, down_all.at[c], far_device)
    copies.remote(down_v, down_all.at[c], near_device)
    copies.arrive(own_flat)
    for slab_at in range(n):
        for kind in (0, 1):
            start = (kind * n + slab_at) * ff
            gu_v[slab_at, kind] = flat_v[:, start : start + ff]
    own_gu = copies.local(gu_v.at[b], gu_all.at[:, b, c])
    gu_copies = []
    gu_far = []
    waiting = []

    def send_gu(count):
        for _ in range(count):
            k = len(gu_copies) + 1
            if k < n:
                peer = peers[k - 1]
                copy = copies.remote(gu_v.at[peer[0]], gu_all.at[:, b, c], peer)
                gu_copies.append(copy)
                waiting.append((lax.rem(b - k + n, n), copy))

    def forward_gu(count):
        for _ in range(min(count, len(waiting))):
            rank, copy = waiting.pop(0)
            copies.arrive(copy)
            block = gu_all.at[:, rank, c]
            gu_far.append(copies.remote(block, block, far_device))

    for copy in own_up + up_copies:
        copies.arrive(copy)
    up_ring.advance()
    packed_step()
    send_gu(n // 2)
    copies.arrive(own_out)
    out_ring.advance()
    up_ring.advance()
    while packed_ring.step <= place.h:
        packed_step()
        up_ring.advance()
    mine = packed_v.at[:, c]
    packed_near = [copies.remote(mine, mine, near_device)]
    while up_ring.step <= place.h:
        up_ring.advance()
    copies.arrive(own_gu)
    gu_far.append(copies.remote(gu_all.at[:, b, c], gu_all.at[:, b, c], far_device))
    send_gu(n)
    out_ring.advance()
    forward_gu(2)
    for copy in packed_far:
        copies.arrive(copy)
    theirs = packed_v.at[:, place.far]
    packed_near.append(copies.remote(theirs, theirs, near_device))

    copies.arrive(own_tokens)
    own_at = pl.ds(pl.multiple_of(c * pos_dev, pos_dev), pos_dev)
    cos_own = jnp.concatenate([cos_ref[own_at, :]] * micro, axis=0)
    sin_own = jnp.concatenate([sin_ref[own_at, :]] * micro, axis=0)
    residual = tokens_v[...].astype(F32)
    normed = residual * rms_scale(residual)
    for copy in packed_near:
        copies.arrive(copy)
    extra = packed_v[:, :, :, in_cols:].astype(F32)
    gain_wide = jnp.transpose(extra.reshape(width, 128))
    gain_query = jnp.transpose(extra[:, :, :gain_rows].reshape(latent, 128))[2:3]
    gains[0:2, :] = gain_wide[0:2]
    gains[2:3, :latent] = gain_query
    attn_in = (normed * gain_wide[0:1]).astype(BF)
    rows_v[...] = attn_in
    tile = 512
    for start in range(0, in_cols, tile):
        weights = packed_v[:, :, :, start : start + tile].reshape(width, tile)
        part = dot(attn_in, weights)
        if start + tile <= latent:
            latents[:, start : start + tile] = part
        else:
            front, back = turn(part[:, :HD], cos_own, sin_own)
            half = HD // 2
            qkv_v[c, :, :, latent : latent + half] = (
                front.astype(BF).reshape(micro, pos_dev, half)
            )
            qkv_v[c, :, :, latent + half : latent + HD] = (
                back.astype(BF).reshape(micro, pos_dev, half)
            )
            qkv_v[c, :, :, latent + HD :] = part[:, HD:].astype(BF).reshape(micro, pos_dev, HD)
    q_latent = latents[...]
    q_normed = q_latent * rms_scale(q_latent) * gain_query
    qkv_v[c, :, :, :latent] = q_normed.astype(BF).reshape(micro, pos_dev, latent)
    qkv = CtxGather(place, copies, qkv_v)
    for item in range(micro):
        qkv.start(item)
    copies.local(rows_v, rows_out)
    copies.arrive(own_cot)
    cot_v[...] = (cot_v[...].astype(F32) * valid_ref[...]).astype(BF)
    copies.arrive(copies.local(cot_v, cot_all.at[b]))
    cot_ring.advance()
    for item in range(micro):
        qkv.cross(item)
    if out_ring.step < place.h:
        out_ring.advance()
    forward_gu(n // 2)
    cosine, sine = cos_ref[...], sin_ref[...]
    for item in range(micro):
        qkv.finish(item)
        q_all = qkv_v[:, item, :, :latent].reshape(length, latent)
        keys = qkv_v[:, item, :, latent : latent + HD].reshape(length, HD)
        values = qkv_v[:, item, :, latent + HD :].reshape(length, HD)
        keep = keep_ref[item]

        @pl.loop(0, heads)
        def _(head):
            base = pl.multiple_of(head * HD, HD)
            cols = pl.ds(base, HD)
            up = up_v[:, :, :, cols].reshape(latent, HD)
            front, back = turn(dot(q_all, up), cosine, sine)
            turned_v[item, :, pl.ds(base, HD // 2)] = front.astype(BF)
            upper = pl.multiple_of(base + HD // 2, HD // 2)
            turned_v[item, :, pl.ds(upper, HD // 2)] = back.astype(BF)
            weights = softmax_rows(turned_v[item, :, cols], keys, keep, score_scale)
            mixed = dot(weights.astype(BF), values).astype(BF)
            mixed_v[:, item, :, cols] = mixed.reshape(4, pos_dev, HD)

        if out_ring.step < place.h:
            out_ring.advance()
    while out_ring.step < place.h:
        out_ring.advance()

    cot_ring.advance()
    while out_ring.step <= place.h:
        out_ring.advance()
    out_swaps = [
        copies.remote(half_v.at[group.blocks(member)], out_v.at[:, group.me], device)
        for member, device in group.others
    ]
    out_swaps.append(copies.local(half_v.at[group.blocks(group.me)], out_v.at[:, group.me]))
    forward_gu(n)
    for copy in out_swaps:
        copies.arrive(copy)
    copies.arrive(down_far)
    copies.remote(down_all.at[place.far], down_all.at[place.far], near_device)
    attended_sum = CtxCollect(place, copies, part_v, near_got, far_got)
    for item in range(micro):
        mixed = mixed_v[:, item].reshape(length, heads * HD)

        @pl.loop(0, width // 512)
        def _(t):
            cols = pl.ds(pl.multiple_of(t * 512, 512), 512)
            weights = out_v[:, :, :, cols].reshape(heads * HD, 512)
            part = dot(mixed, weights).astype(BF)
            part_v[:, item, :, cols] = part.reshape(4, pos_dev, 512)

        attended_sum.start(item)
        if item > 0:
            attended_sum.cross(item - 1)
    cot_ring.advance()
    attended_sum.cross(micro - 1)
    copies.local(packed_v, packed_out)
    copies.local(up_v, up_out)
    copies.local(out_v, out_out)
    copies.local(qkv_v, qkv_out)
    copies.local(turned_v, turned_out)
    copies.local(mixed_v, mixed_out)
    for item in range(micro):
        at = slice(item * pos_dev, (item + 1) * pos_dev)
        total = tokens_v[at, :].astype(F32) + attended_sum.finish(item)
        hidden[at, :] = total
        mlp_in[at, :] = (total * rms_scale(total) * gains[1:2, :]).astype(BF)
    mine = gu_all.at[:, :, c]
    copies.remote(mine, mine, near_device)
    while cot_ring.step <= place.h:
        cot_ring.advance()
    for copy in gu_far:
        copies.arrive(copy)
    theirs = gu_all.at[:, :, place.far]
    copies.remote(theirs, theirs, near_device)
    copies.drain()


def front(n_batch, heads, proj_in, gain_cols, query_up, proj_out, gate_up, down, tokens, cots, tables):
    own_rows, in_cols = proj_in.shape
    packed_cols = in_cols + 128
    latent = in_cols - 2 * HD
    gain_rows = query_up.shape[0]
    out_rows, width = proj_out.shape
    n_tok = cots.shape[0]
    pos_dev = tables[0].shape[0] // 4
    micro = n_tok // pos_dev
    ff = gate_up.shape[1] // (2 * n_batch)
    size = head_group(n_batch, out_rows)
    head_cols = heads * HD
    shapes = {
        "packed": (n_batch, 4, own_rows, packed_cols),
        "up": (n_batch, 4, gain_rows, head_cols),
        "out": (n_batch // size, size, out_rows, width),
        "gu": (2, n_batch, 4, own_rows, ff),
        "down": (4,) + down.shape,
        "qkv": (4, micro, pos_dev, in_cols),
        "turned": (micro, 4 * pos_dev, head_cols),
        "mixed": (4, micro, pos_dev, head_cols),
        "rows": (n_tok, width),
        "cot": (n_batch, n_tok, width),
    }
    anywhere = pl.BlockSpec(memory_space=pl.ANY)
    near = pl.BlockSpec(memory_space=pltpu.VMEM)
    sems = 13 * n_batch + 100
    return pl.pallas_call(
        functools.partial(front_kernel, n_batch, heads),
        out_shape=(
            jax.ShapeDtypeStruct((n_tok, width), F32),
            jax.ShapeDtypeStruct((n_tok, width), BF),
            jax.ShapeDtypeStruct((8, width), F32),
            jax.ShapeDtypeStruct((n_tok, latent), F32),
        )
        + tuple(jax.ShapeDtypeStruct(shape, BF) for shape in shapes.values()),
        in_specs=[anywhere] * 8 + [near] * 4,
        out_specs=[near] * 4 + [anywhere] * len(shapes),
        scratch_shapes=[
            pltpu.VMEM(shapes["packed"], BF),
            pltpu.VMEM(gate_up.shape, BF),
            pltpu.VMEM((n_batch, 2, own_rows, ff), BF),
            pltpu.VMEM((n_batch, out_rows, width), BF),
            pltpu.VMEM(shapes["out"], BF),
            pltpu.VMEM(shapes["up"], BF),
            pltpu.VMEM((n_tok, width), BF),
            pltpu.VMEM((n_tok, width), BF),
            pltpu.VMEM(down.shape, BF),
            pltpu.VMEM((n_tok, width), BF),
            pltpu.VMEM(shapes["qkv"], BF),
            pltpu.VMEM(shapes["turned"], BF),
            pltpu.VMEM(shapes["mixed"], BF),
            pltpu.VMEM((4, micro, pos_dev, width), BF),
            pltpu.VMEM((2, micro, pos_dev, width), BF),
            pltpu.VMEM((micro, pos_dev, width), BF),
            pltpu.SemaphoreType.DMA((sems,)),
            pltpu.SemaphoreType.DMA((sems,)),
        ],
        compiler_params=pltpu.CompilerParams(
            collective_id=0, has_side_effects=True, vmem_limit_bytes=56 * 1024 * 1024
        ),
        name="front",
    )(proj_in, gain_cols, query_up, proj_out, gate_up, down, tokens, cots, *tables)


def attention_back_kernel(
    n_batch,
    heads,
    has_terms,
    grad_ref,
    qkv_ref,
    turned_ref,
    mixed_ref,
    up_ref,
    out_ref,
    gu_ref,
    down_ref,
    rows_ref,
    *refs,
):
    terms_ref, cot_ref, refs = (refs[0], refs[1], refs[2:]) if has_terms else (None, None, refs)
    (
        cos_ref,
        sin_ref,
        keep_ref,
        back_out,
        out_terms,
        up_terms,
        gu_grad,
        down_grad,
        rows_all,
    ) = refs[:9]
    terms_sum, refs = (refs[9], refs[10:]) if has_terms else (None, refs[9:])
    (
        grad_v,
        qkv_v,
        turned_v,
        mixed_v,
        up_v,
        out_v,
        qgrad_v,
        kgrad_v,
        vgrad_v,
        part_v,
        near_got,
        far_got,
        outgrad_v,
        upgrad_v,
        down_v,
        gu_v,
        rows_v,
        send_sems,
        recv_sems,
        load_sems,
    ) = refs[:20]
    place = Place(n_batch)
    copies = Copies(send_sems, recv_sems)
    b, c, n = place.b, place.c, n_batch
    micro, pos_dev, width = grad_ref.shape
    length = 4 * pos_dev
    head_cols = heads * HD
    latent = qkv_ref.shape[3] - 2 * HD
    score_scale = 1.0 / math.sqrt(HD)
    pairs = [
        (grad_ref, grad_v.at[c]),
        (out_ref, out_v),
        (qkv_ref, qkv_v),
        (turned_ref, turned_v),
        (up_ref, up_v),
        (mixed_ref, mixed_v),
    ]
    if has_terms:
        (
            terms_v,
            terms_got,
            ring_send,
            ring_recv,
            act_v,
            cot_v,
            down_all,
            down_got,
        ) = refs[20:]
        pairs += [(terms_ref, terms_v), (down_ref, act_v)]
        n_tok = terms_v.shape[1]
        spots = [(0, 0, 0), (place.h, 0, 1)]
        spots += [
            (side * step, step, (side + 1) // 2) for step in range(1, place.h) for side in (-1, 1)
        ]
        pairs += [
            (cot_ref.at[place.rank_of(step)], cot_v.at[pair, pl.ds(side * n_tok, n_tok)])
            for step, pair, side in spots
        ]
    loads = [
        pltpu.make_async_copy(source, target, load_sems.at[i])
        for i, (source, target) in enumerate(pairs)
    ]
    for copy in loads[:1] + loads[6:] + loads[1:6]:
        copy.start()
    peers = [(lax.rem(b + k, n), c) for k in range(1, n)]
    others = peers + [(b, place.far), (b, place.near), (b, lax.rem(place.near + 2, 4))]
    pl.semaphore_wait(greet(place, others), n + 2)
    out_rows = out_terms.shape[1]
    group = HeadGroup(place, out_rows)
    loads[0].wait()
    grads = CtxGather(place, copies, grad_v)
    for item in range(micro):
        grads.start(item)
    steps = []
    if has_terms:

        def spot(step):
            return 0 if step == 0 else 1 if step == place.h else 2 * abs(step) + (step > 0)

        terms = RingCollect(
            place, lambda step: terms_v.at[spot(step)], terms_got, ring_send, ring_recv
        )
        loads[6].wait()
        steps = [terms.advance] * place.h

    def ring_step():
        if steps:
            steps.pop()()

    ring_step()
    own_gu = copies.local(gu_ref.at[b], gu_v)
    own_rows = copies.local(rows_ref, rows_v.at[c, 0])
    for peer in peers:
        copies.remote(gu_ref.at[peer[0]], gu_grad.at[b], peer)
    for item in range(micro):
        grads.cross(item)
    outer, inner = place.outer, place.inner
    if has_terms:
        for copy in loads[7:]:
            copy.wait()
        n_rows = cot_v.shape[0] * cot_v.shape[1]
        ff = act_v.shape[2]

        @pl.loop(0, width // 512)
        def _(t):
            cols = pl.ds(pl.multiple_of(t * 512, 512), 512)
            term = dot_left_t(
                act_v[...].reshape(n_rows, ff), cot_v[:, :, cols].reshape(n_rows, 512)
            )
            down_all[:, :, cols] = term.astype(BF).reshape(4, ff // 4, 512)

        down_near = [
            copies.remote(down_all.at[2 * side + 1 - inner], down_got.at[side], (b, place.near))
            for side in (0, 1)
        ]
    else:
        down_own = copies.local(down_ref.at[outer], down_v.at[0])
        down_far = copies.remote(down_ref.at[1 - outer], down_v.at[1], (b, place.far))
    for copy in loads[1:6]:
        copy.wait()
    if has_terms:
        for copy in down_near:
            copies.arrive(copy)
        other = down_all.at[2 * (1 - outer) + inner]
        other[...] = (other[...].astype(F32) + down_got[1 - outer].astype(F32)).astype(BF)
        down_far = copies.remote(other, down_v.at[1], (b, place.far))
    copies.arrive(own_rows)
    rows = CtxGather(place, copies, rows_v)
    rows.start(0)
    back_sum = CtxCollect(place, copies, part_v, near_got, far_got)
    cosine, sine = cos_ref[...], sin_ref[...]
    for item in range(micro):
        grads.finish(item)
        incoming = grad_v[:, item].reshape(length, width)
        keys = qkv_v[:, item, :, latent : latent + HD].reshape(length, HD)
        values = qkv_v[:, item, :, latent + HD :].reshape(length, HD)
        keep = keep_ref[item]
        kgrad_v[...] = jnp.zeros_like(kgrad_v)
        vgrad_v[...] = jnp.zeros_like(vgrad_v)

        @pl.loop(0, heads)
        def _(head):
            cols = pl.ds(pl.multiple_of(head * HD, HD), HD)
            grad_mixed = dot_right_t(incoming, out_v[head]).astype(BF)
            queries = turned_v[item, :, cols]
            weights = softmax_rows(queries, keys, keep, score_scale)
            grad_probs = dot_right_t(grad_mixed, values)
            row_dot = jnp.sum(weights * grad_probs, axis=-1, keepdims=True)
            grad_scores = (weights * (grad_probs - row_dot)).astype(BF)
            front, back = turn(dot(grad_scores, keys) * score_scale, cosine, -sine)
            front, back = front.astype(BF), back.astype(BF)
            base = pl.multiple_of(head * HD, HD)
            qgrad_v[:, item, :, pl.ds(base, HD // 2)] = front.reshape(4, pos_dev, HD // 2)
            base = pl.multiple_of(head * HD + HD // 2, HD // 2)
            qgrad_v[:, item, :, pl.ds(base, HD // 2)] = back.reshape(4, pos_dev, HD // 2)
            kgrad_v[...] += dot_left_t(grad_scores, queries) * score_scale
            vgrad_v[...] += dot_left_t(weights.astype(BF), grad_mixed)

        ring_step()
        qgrad = qgrad_v[:, item].reshape(length, head_cols)
        part_v[:, item, :, :latent] = (
            dot_right_t(qgrad, up_v[...]).astype(BF).reshape(4, pos_dev, latent)
        )
        part_v[:, item, :, latent : latent + HD] = (
            kgrad_v[...].astype(BF).reshape(4, pos_dev, HD)
        )
        part_v[:, item, :, latent + HD :] = vgrad_v[...].astype(BF).reshape(4, pos_dev, HD)
        back_sum.start(item)
        if item > 0:
            back_sum.cross(item - 1)
    n_all = 4 * micro * pos_dev
    back_sum.cross(micro - 1)
    ring_step()

    @pl.loop(0, width // 512)
    def _(t):
        cols = pl.ds(pl.multiple_of(t * 512, 512), 512)
        term = dot_left_t(
            mixed_v[...].reshape(n_all, head_cols), grad_v[:, :, :, cols].reshape(n_all, 512)
        )
        outgrad_v[:, :, :, cols] = term.astype(BF).reshape(group.count, group.size, out_rows, 512)

    mine = out_terms.at[group.blocks(group.me)]
    copies.local(outgrad_v.at[:, group.me], mine)
    for member, device in group.others:
        copies.remote(outgrad_v.at[:, member], mine, device)
    for item in range(micro):
        back_out[item] = back_sum.finish(item)
    ring_step()

    @pl.loop(0, head_cols // HD)
    def _(t):
        cols = pl.ds(pl.multiple_of(t * HD, HD), HD)
        term = dot_left_t(
            qkv_v[:, :, :, :latent].reshape(n_all, latent),
            qgrad_v[:, :, :, cols].reshape(n_all, HD),
        )
        upgrad_v[:, :, cols] = term.astype(BF).reshape(n, latent // n, HD)

    copies.local(upgrad_v, up_terms)
    rows.cross(0)
    rows.finish(0)
    copies.local(rows_v, rows_all)
    copies.arrive(own_gu)
    copies.local(gu_v, gu_grad.at[b])
    copies.arrive(down_far)
    if has_terms:
        down_grad[...] = (
            down_all[2 * outer + inner].astype(F32)
            + down_got[outer].astype(F32)
            + down_v[1].astype(F32)
        )
    else:
        copies.arrive(down_own)
        down_grad[...] = down_v[0].astype(F32) + down_v[1].astype(F32)
    if has_terms:
        while steps:
            ring_step()
        cut = terms.cut
        for half in (0, 1):
            terms_sum[half * cut : (half + 1) * cut, :] = terms.finish(half)
        terms.drain()
    copies.drain()


def attention_back(
    n_batch, grad_att, qkv_all, turned, mixed, own_qup, own_out, grad_gu, down_part, attn_in, terms, cots, tables
):
    micro, pos_dev, width = grad_att.shape
    n_tok = micro * pos_dev
    qkv_cols = qkv_all.shape[3]
    latent, head_cols = own_qup.shape
    own_out = own_out.reshape(head_cols // HD, HD, width)
    length = 4 * pos_dev
    far = n_batch // 2
    has_terms = terms is not None
    down_rows = down_part.shape[2] // 4 if has_terms else down_part.shape[1]
    size = head_group(n_batch, head_cols // n_batch)
    sems = 2 * n_batch + 48
    anywhere = pl.BlockSpec(memory_space=pl.ANY)
    near = pl.BlockSpec(memory_space=pltpu.VMEM)
    out_shape = [
        jax.ShapeDtypeStruct((micro, pos_dev, qkv_cols), F32),
        jax.ShapeDtypeStruct((n_batch, head_cols // n_batch, width), BF),
        jax.ShapeDtypeStruct((n_batch, latent // n_batch, head_cols), BF),
        jax.ShapeDtypeStruct(grad_gu.shape, BF),
        jax.ShapeDtypeStruct((down_rows, width), F32),
        jax.ShapeDtypeStruct((4, 1) + attn_in.shape, BF),
    ]
    out_specs = [near] + [anywhere] * 3 + [near, anywhere]
    scratch = [
        pltpu.VMEM((4, micro, pos_dev, width), BF),
        pltpu.VMEM((4, micro, pos_dev, qkv_cols), BF),
        pltpu.VMEM((micro, length, head_cols), BF),
        pltpu.VMEM((4, micro, pos_dev, head_cols), BF),
        pltpu.VMEM((latent, head_cols), BF),
        pltpu.VMEM((head_cols // HD, HD, width), BF),
        pltpu.VMEM((4, micro, pos_dev, head_cols), BF),
        pltpu.VMEM((length, HD), F32),
        pltpu.VMEM((length, HD), F32),
        pltpu.VMEM((4, micro, pos_dev, qkv_cols), BF),
        pltpu.VMEM((2, micro, pos_dev, qkv_cols), BF),
        pltpu.VMEM((micro, pos_dev, qkv_cols), BF),
        pltpu.VMEM((n_batch // size, size, head_cols // n_batch, width), BF),
        pltpu.VMEM((n_batch, latent // n_batch, head_cols), BF),
        pltpu.VMEM((2, down_rows, width), BF),
        pltpu.VMEM(grad_gu.shape[1:], BF),
        pltpu.VMEM((4, 1) + attn_in.shape, BF),
        pltpu.SemaphoreType.DMA((sems,)),
        pltpu.SemaphoreType.DMA((sems,)),
        pltpu.SemaphoreType.DMA((8 + n_batch,)),
    ]
    args = [grad_att, qkv_all, turned, mixed, own_qup, own_out, grad_gu, down_part, attn_in]
    if has_terms:
        args += [terms, cots]
        out_shape.append(jax.ShapeDtypeStruct((n_tok, width), F32))
        out_specs.append(near)
        scratch += [
            pltpu.VMEM(terms.shape, BF),
            pltpu.VMEM((far, 2, 2, n_tok // 2, width), BF),
            pltpu.SemaphoreType.DMA((far, 2, 2)),
            pltpu.SemaphoreType.DMA((far, 2, 2)),
            pltpu.VMEM(down_part.shape, BF),
            pltpu.VMEM((far, 2 * n_tok, width), BF),
            pltpu.VMEM((4, down_rows, width), BF),
            pltpu.VMEM((2, down_rows, width), BF),
        ]
    return pl.pallas_call(
        functools.partial(attention_back_kernel, n_batch, head_cols // HD, has_terms),
        out_shape=tuple(out_shape),
        in_specs=[anywhere] * len(args) + [near] * 3,
        out_specs=out_specs,
        scratch_shapes=scratch,
        compiler_params=pltpu.CompilerParams(
            collective_id=4, has_side_effects=True, vmem_limit_bytes=56 * 1024 * 1024
        ),
        name="attention_back",
    )(*args, *tables)


def permuted_mlp(ring, rows_own, cots, gu_rows, own_down):
    mlp_in = ring.spread(rows_own)
    n_tok, width = rows_own.shape
    _, n_batch, n_ctx, own_rows, ff = gu_rows.shape
    own_gate, own_up = gu_rows.reshape(2, width, ff)
    own_down = own_down.reshape(ff, width)
    far = ring.h
    groups = [[0]] + [[-step, step] for step in range(1, far)] + [[far]]
    out_terms = {}
    in_terms = {}
    kept = []
    for group in groups:
        rows = jnp.concatenate([mlp_in[step] for step in group], axis=0)
        grad_rows = jnp.concatenate([pick(cots, ring.rank_of(step)) for step in group], axis=0)
        gate_part = dot(rows, own_gate)
        up_part = dot(rows, own_up)
        sigmoid_gate = jax.nn.sigmoid(gate_part)
        silu_gate = gate_part * sigmoid_gate
        activated = (silu_gate * up_part).astype(BF)
        grad_act = dot_right_t(grad_rows, own_down)
        grad_gate = (
            grad_act * up_part * (sigmoid_gate * (1.0 + gate_part * (1.0 - sigmoid_gate)))
        ).astype(BF)
        grad_up = (grad_act * silu_gate).astype(BF)
        in_term = dot_right_t(grad_gate, own_gate) + dot_right_t(grad_up, own_up)
        out_term = dot(activated, own_down)
        for place_in, step in enumerate(group):
            cut = slice(place_in * n_tok, (place_in + 1) * n_tok)
            in_terms[step] = in_term[cut]
            out_terms[step] = out_term[cut]
        kept.append((rows, grad_rows, activated, grad_gate, grad_up))
    rows, grad_rows, activated, grad_gate, grad_up = (
        jnp.concatenate(items, axis=0) for items in zip(*kept)
    )
    grad_gu = jnp.stack([dot_left_t(rows, grad_gate), dot_left_t(rows, grad_up)])
    grad_gu = grad_gu.reshape(2, n_batch, n_ctx, own_rows, ff).transpose(2, 1, 0, 3, 4)
    grad_down = dot_left_t(activated, grad_rows)
    return (
        ring.collect(lambda step: in_terms[step]),
        near_collect(grad_down.reshape(n_ctx, ff // n_ctx, width)).astype(BF),
        out_terms,
        ctx_collect(grad_gu).astype(BF),
    )


def shards(
    tokens,
    cotangent,
    lengths,
    slot_sequence,
    proj_in,
    query_up,
    proj_out,
    attn_gain,
    query_gain,
    mlp_gain,
    gate_up,
    down_proj,
):
    n_ctx = lax.axis_size("ctx")
    n_batch = lax.axis_size("batch")
    ctx_rank = lax.axis_index("ctx")
    batch_rank = lax.axis_index("batch")
    ring = Ring()
    micro, pos_dev, width = tokens.shape
    n_tok = micro * pos_dev
    full_length = pos_dev * n_ctx
    heads = H // n_ctx
    score_scale = 1.0 / math.sqrt(HD)
    in_cols = proj_in.shape[1]

    slot_total = lengths.shape[0]
    slot_ids = jnp.arange(slot_total, dtype=jnp.int32)
    seq_lengths = jnp.sum(
        jnp.where(slot_sequence[:, None] == slot_ids[None, :], lengths[None, :], 0), axis=1
    )
    own_lengths = lax.dynamic_slice_in_dim(seq_lengths, batch_rank * micro, micro)
    query_pos = ctx_rank * pos_dev + jnp.arange(pos_dev, dtype=jnp.int32)
    key_pos = jnp.arange(full_length, dtype=jnp.int32)
    cos_all, sin_all = rope_tables(full_length)

    own_rows = proj_in.shape[0]
    gain_rows = query_gain.shape[0]
    gains = jnp.stack(
        [attn_gain, mlp_gain, jnp.pad(query_gain, (0, own_rows - gain_rows))], axis=1
    )
    gain_cols = jnp.pad(gains, ((0, 0), (0, 125)))
    valid_rows = (query_pos[None, :] < own_lengths[:, None]).astype(F32).reshape(n_tok, 1)
    keep = (key_pos[None, None, :] < own_lengths[:, None, None]).astype(F32)
    (
        hidden_res,
        mlp_in,
        gains,
        q_latent,
        packed,
        own_qup,
        own_out,
        gu_rows,
        own_down,
        qkv_all,
        turned,
        mixed,
        attn_in,
        cots,
    ) = front(
        n_batch,
        heads,
        proj_in,
        gain_cols,
        query_up,
        proj_out,
        gate_up,
        down_proj,
        tokens.reshape(n_tok, width),
        cotangent.reshape(n_tok, width),
        (cos_all, sin_all, keep, valid_rows),
    )
    own_qup = own_qup.reshape(QR, heads * HD)

    resident = 10 * n_batch * n_tok * width <= 24 * 1024 * 1024
    if resident:
        grad_hidden, grad_att, gain_mlp_term, down_part, terms, grad_gu_own = fused_mlp(
            n_batch, mlp_in, cots, hidden_res, gains, gu_rows, own_down
        )
        terms = terms.reshape(n_batch, n_tok, width)
    else:
        terms = None
        scale_two = rms_scale(hidden_res)
        normed_two = hidden_res * scale_two
        grad_mlp_in, down_part, out_terms, grad_gu_own = permuted_mlp(
            ring, mlp_in, cots, gu_rows, own_down
        )
        gain_mlp_term = jnp.sum(grad_mlp_in * normed_two, axis=0)[None, :]
        grad_hidden = cotangent.reshape(n_tok, width).astype(F32) * valid_rows
        grad_hidden += norm_back(grad_mlp_in * gains[1], normed_two, scale_two)
        grad_att = grad_hidden.astype(BF)
    back_own, out_grads, up_grads, grad_gu_own, grad_down, attn_in_all, *sums = attention_back(
        n_batch,
        grad_att.reshape(micro, pos_dev, width),
        qkv_all,
        turned,
        mixed,
        own_qup,
        own_out,
        grad_gu_own,
        down_part,
        attn_in,
        terms,
        cots,
        (cos_all, sin_all, keep),
    )
    out_sum = sums[0] if resident else ring.collect(lambda step: out_terms[step])
    layer_out = hidden_res + out_sum
    back_own = back_own.reshape(n_tok, in_cols)
    (
        grad_proj_out,
        grad_query_up,
        grad_proj_in,
        grad_attn_gain,
        grad_query_gain,
        grad_mlp_gain,
        grad_gate_up,
        grad_tokens,
    ) = collect_weights(
        n_batch,
        gain_rows,
        out_grads,
        up_grads,
        attn_in_all,
        grad_gu_own,
        packed,
        (
            back_own,
            q_latent,
            tokens.reshape(n_tok, width),
            grad_hidden,
            gains,
            gain_mlp_term,
            cos_all,
            sin_all,
        ),
    )
    return (
        layer_out.reshape(tokens.shape).astype(BF),
        grad_tokens.reshape(tokens.shape),
        grad_proj_in,
        grad_query_up,
        grad_proj_out,
        grad_attn_gain.reshape(-1),
        grad_query_gain.reshape(-1),
        grad_mlp_gain.reshape(-1),
        grad_gate_up,
        grad_down,
    )


def solution(mesh):
    rows = P(("batch", "ctx"), None)
    vector = P(("batch", "ctx"))
    acts = P("batch", "ctx", None)
    return jax.shard_map(
        shards,
        mesh=mesh,
        in_specs=(acts, acts, P(), P(), rows, rows, rows, vector, vector, vector, rows, rows),
        out_specs=(acts, acts, rows, rows, rows, vector, vector, vector, rows, rows),
        check_vma=False,
    )
```
